32 devices in a mesh: ctx: 16 (over z, x, core), fsdp: 2 (over y).
Axes of the slice: x: 2, y: 2, z: 4, core: 2. Of those that a mesh axis runs over, the one named last changes fastest.
Arguments:
- hidden_in: bfloat16 [2, 2048, 1024], P('fsdp', 'ctx'), may hold values from -6 to 6
- doc_lengths: int32 [2, 8], P('fsdp'), may hold values from 1 to 1920, as said below
- attn_gain: float32 [1024], replicated, may hold values from 0.5 to 1.5
- query_gain: float32 [64], replicated, may hold values from 0.5 to 1.5
- key_norm_gain: float32 [64], replicated, may hold values from 0.5 to 1.5
- ffn_gain: float32 [1024], replicated, may hold values from 0.5 to 1.5
- query_proj: float32 [1024, 1024], P('fsdp'), may hold values from -0.1875 to 0.1875
- key_weight: float32 [1024, 512], P('fsdp'), may hold values from -0.1875 to 0.1875
- value_weight: float32 [1024, 512], P('fsdp'), may hold values from -0.1875 to 0.1875
- attn_proj: float32 [1024, 1024], P('fsdp'), may hold values from -3 to 3
- gate_proj: float32 [1024, 4608], P('fsdp'), may hold values from -0.1875 to 0.1875
- up_proj: float32 [1024, 4608], P('fsdp'), may hold values from -0.1875 to 0.1875
- down_proj: float32 [4608, 1024], P('fsdp'), may hold values from -0.09375 to 0.09375
- out_cotangent: bfloat16 [2, 2048, 1024], P('fsdp', 'ctx'), may hold values from -6 to 6
Outputs:
- hidden_out: float32 [2, 2048, 1024], P('fsdp', 'ctx')
- input_grad: float32 [2, 2048, 1024], P('fsdp', 'ctx')
- attn_gain_grad: float32 [1024], replicated
- query_gain_grad: float32 [64], replicated
- key_gain_grad: float32 [64], replicated
- ffn_gain_grad: float32 [1024], replicated
- query_grad: float32 [1024, 1024], P('fsdp', 'ctx')
- key_grad: float32 [1024, 512], P('fsdp', 'ctx')
- value_grad: float32 [1024, 512], P('fsdp', 'ctx')
- attn_grad: float32 [1024, 1024], P('fsdp', 'ctx')
- gate_grad: float32 [1024, 4608], P('fsdp', 'ctx')
- up_grad: float32 [1024, 4608], P('fsdp', 'ctx')
- down_grad: float32 [4608, 1024], P('fsdp', 'ctx')
The draws below stay inside these ranges and needn't reach their ends.
Inputs may be any that keep to these rules, and one draw needn't show every extreme that they name: `doc_lengths`: each stream's 8 document lengths sum to 2048; in every stream exactly one document has 1920 tokens, and it is neither the first nor the last of its stream.
All inputs are finite; a program needn't handle non-finite values.
Results may differ from the reference program's by a relative error of at most 0.014.
Values may be sent and summed in bfloat16 or wider, within the bound.
A program may use at most 320 MiB of HBM per device.

```python
import jax
import jax.numpy as jnp
from jax import lax

MODEL_WIDTH = 1024
QUERY_HEADS = 16
KEY_VALUE_HEADS = 8
HEAD_SIZE = 64
FF = 4608
TOK_DEV = 128
DOCS = 8
STREAMS = 2
TOKENS = 2048
DOC_MOST = 1920


def draw_doc_lengths(key, part):
    rows_list = []
    for stream in range(STREAMS):
        stream_key = jax.random.fold_in(key, 1701 + stream)
        first_key, second_key = jax.random.split(stream_key)
        spare_tokens = TOK_DEV - (DOCS - 1)
        chosen = jax.random.randint(first_key, (spare_tokens,), 0, DOCS - 1)
        smalls = 1 + jnp.sum((chosen[:, None] == jnp.arange(DOCS - 1, dtype=jnp.int32)[None, :]).astype(jnp.int32), axis=0)
        before_count = jax.random.randint(second_key, (), 1, DOCS - 1)
        places = jnp.arange(DOCS, dtype=jnp.int32)
        source_index = jnp.clip(jnp.where(places < before_count, places, places - 1), 0, DOCS - 2)
        lengths = jnp.where(places == before_count, DOC_MOST, smalls[source_index])
        rows_list.append(lengths.astype(jnp.int32))
    return jnp.stack(rows_list).astype(jnp.int32)


def shard_levels(rng, dims, pieces, least, largest):
    level = 1.0
    for axis_at, blocks in pieces:
        heights = jax.random.uniform(jax.random.fold_in(jax.random.fold_in(rng, 6), axis_at), (blocks,), jnp.float32, least / len(pieces), largest / len(pieces))
        level = level * jnp.repeat(jnp.exp(heights), dims[axis_at] // blocks).reshape((-1,) + (1,) * (len(dims) - 1 - axis_at))
    return level


def normal_values(key, dims, spread, bound, cuts=(), kind=jnp.bfloat16):
    factor_of = shard_levels(key, dims, cuts, -0.22, 0.18) if cuts else 1.0
    drawn = jax.random.normal(key, dims, jnp.float32) * spread * factor_of
    return jnp.minimum(jnp.maximum(drawn, -bound), bound).astype(kind)


def setup_inputs(seed: int = 0) -> dict:
    key_list = jax.random.split(jax.random.key(seed), 15)
    hidden_in = normal_values(key_list[0], (STREAMS, TOKENS, MODEL_WIDTH), 1.0, 6.0, ((0, 2), (1, 16)))
    doc_lengths = draw_doc_lengths(jax.random.fold_in(key_list[14], 71), 0)
    attn_gain = jnp.clip(1.0 + 0.1 * jax.random.normal(key_list[2], (MODEL_WIDTH,), jnp.float32), 0.5, 1.5)
    query_gain = jnp.clip(1.0 + 0.1 * jax.random.normal(key_list[3], (HEAD_SIZE,), jnp.float32), 0.5, 1.5)
    key_norm_gain = jnp.clip(1.0 + 0.1 * jax.random.normal(key_list[4], (HEAD_SIZE,), jnp.float32), 0.5, 1.5)
    ffn_gain = jnp.clip(1.0 + 0.1 * jax.random.normal(key_list[5], (MODEL_WIDTH,), jnp.float32), 0.5, 1.5)
    query_proj = normal_values(key_list[6], (MODEL_WIDTH, QUERY_HEADS * HEAD_SIZE), MODEL_WIDTH ** -0.5, 0.1875, ((0, 2),), jnp.float32)
    key_weight = normal_values(key_list[7], (MODEL_WIDTH, KEY_VALUE_HEADS * HEAD_SIZE), MODEL_WIDTH ** -0.5, 0.1875, ((0, 2),), jnp.float32)
    value_weight = normal_values(key_list[8], (MODEL_WIDTH, KEY_VALUE_HEADS * HEAD_SIZE), MODEL_WIDTH ** -0.5, 0.1875, ((0, 2),), jnp.float32)
    attn_proj = normal_values(key_list[9], (QUERY_HEADS * HEAD_SIZE, MODEL_WIDTH), 4 ** -0.5, 3.0, ((0, 2),), jnp.float32)
    gate_proj = normal_values(key_list[10], (MODEL_WIDTH, FF), MODEL_WIDTH ** -0.5, 0.1875, ((0, 2),), jnp.float32)
    up_proj = normal_values(key_list[11], (MODEL_WIDTH, FF), MODEL_WIDTH ** -0.5, 0.1875, ((0, 2),), jnp.float32)
    down_proj = normal_values(key_list[12], (FF, MODEL_WIDTH), FF ** -0.5, 0.09375, ((0, 2),), jnp.float32)
    out_cotangent = normal_values(key_list[13], (STREAMS, TOKENS, MODEL_WIDTH), 1.0, 6.0, ((0, 2), (1, 16)))
    return {"hidden_in": hidden_in, "doc_lengths": doc_lengths, "attn_gain": attn_gain, "query_gain": query_gain, "key_norm_gain": key_norm_gain, "ffn_gain": ffn_gain, "query_proj": query_proj, "key_weight": key_weight, "value_weight": value_weight, "attn_proj": attn_proj, "gate_proj": gate_proj, "up_proj": up_proj, "down_proj": down_proj, "out_cotangent": out_cotangent}


epsilon = 1e-05
rope_base = 1000000.0
highest = lax.Precision.HIGHEST

@jax.custom_vjp
def low(v):
    return lax.optimization_barrier(v.astype(jnp.bfloat16)).astype(jnp.float32)

@jax.custom_vjp
def low_back(v):
    return v

def low_keep(v):
    return (low(v), None)

def low_pass(kept, grad):
    return (grad,)

def back_keep(v):
    return (v, None)

def back_low(kept, grad):
    return (low(grad),)
low.defvjp(low_keep, low_pass)
low_back.defvjp(back_keep, back_low)

def root_mean_norm(value_rows, gain):
    return value_rows * lax.rsqrt(lax.optimization_barrier(jnp.mean(value_rows * value_rows, axis=-1, keepdims=True)) + epsilon) * gain

def apply_rotary(value_rows, token_positions):
    halfway = value_rows.shape[-1] // 2
    freqs = rope_base ** (-2.0 * jnp.arange(halfway, dtype=jnp.float32) / value_rows.shape[-1])
    angles = token_positions.astype(jnp.float32)[:, None] * freqs[None, :]
    cosine = jnp.cos(angles)[:, None, :]
    sine_part = jnp.sin(angles)[:, None, :]
    leading = value_rows[..., :halfway]
    trailing = value_rows[..., halfway:]
    return jnp.concatenate([leading * cosine - trailing * sine_part, leading * sine_part + trailing * cosine], axis=-1)

def locate(token_index, starts):
    after = token_index[:, None] >= starts[None, :]
    document_index = lax.optimization_barrier(jnp.sum(after.astype(jnp.int32), axis=1)).astype(jnp.int32)
    begins = lax.optimization_barrier(jnp.max(jnp.where(after, starts[None, :], 0), axis=1)).astype(jnp.int32)
    return (document_index, (token_index - begins).astype(jnp.int32))

def attend_blocks(query_rows, key_rows, value_rows, document_index, token_index):
    query_per_key = QUERY_HEADS // KEY_VALUE_HEADS
    keys_all = jnp.repeat(key_rows, query_per_key, axis=1)
    values_all = jnp.repeat(value_rows, query_per_key, axis=1)
    length = query_rows.shape[0]
    segment_length = min(512, length)
    blocks = length // segment_length

    def one_block(inputs):
        query_block, doc_block, index_block = inputs
        scores = low_back(jnp.einsum('qhd,khd->hqk', query_block, keys_all, precision=highest))
        allowed = (doc_block[:, None] == document_index[None, :]) & (index_block[:, None] >= token_index[None, :])
        weights = jnp.where(allowed[None, :, :], jnp.exp(scores), 0.0)
        totals = lax.optimization_barrier(jnp.sum(weights, axis=-1))
        summed = low_back(jnp.einsum('hqk,khd->qhd', low(weights), values_all, precision=highest))
        return summed / jnp.transpose(totals)[:, :, None]
    mixed_heads = lax.map(jax.checkpoint(one_block), (query_rows.reshape(blocks, segment_length, QUERY_HEADS, HEAD_SIZE), document_index.reshape(blocks, segment_length), token_index.reshape(blocks, segment_length)))
    return mixed_heads.reshape(length, QUERY_HEADS * HEAD_SIZE)

def block_forward(resid, gains, mats, document_index, token_positions, token_index):
    attn_gain, query_gain, key_norm_gain, ffn_gain = gains
    query_w, key_w, value_w, attn_w, gate_w, up_w, down_w = mats
    token_rows = resid.shape[0]
    normed = low(root_mean_norm(resid, attn_gain))
    query_pre = low_back(jnp.dot(normed, query_w, precision=highest, preferred_element_type=jnp.float32))
    key_before_norm = low_back(jnp.dot(normed, key_w, precision=highest, preferred_element_type=jnp.float32))
    value_rows = low_back(low(jnp.dot(normed, value_w, precision=highest, preferred_element_type=jnp.float32)))
    query_rows = low(apply_rotary(root_mean_norm(query_pre.reshape(token_rows, QUERY_HEADS, HEAD_SIZE), query_gain), token_positions) * HEAD_SIZE ** (-0.5))
    key_rows = low(apply_rotary(root_mean_norm(key_before_norm.reshape(token_rows, KEY_VALUE_HEADS, HEAD_SIZE), key_norm_gain), token_positions))
    mixed_heads = attend_blocks(query_rows, key_rows, value_rows.reshape(token_rows, KEY_VALUE_HEADS, HEAD_SIZE), document_index, token_index)
    middle = resid + low_back(jnp.dot(low(mixed_heads), attn_w, precision=highest, preferred_element_type=jnp.float32))
    normed_ffn = low(root_mean_norm(middle, ffn_gain))
    gate = low_back(jnp.dot(normed_ffn, gate_w, precision=highest, preferred_element_type=jnp.float32))
    up_part = low_back(jnp.dot(normed_ffn, up_w, precision=highest, preferred_element_type=jnp.float32))
    hidden = low(jax.nn.silu(gate) * up_part)
    return middle + jnp.dot(hidden, down_w, precision=highest, preferred_element_type=jnp.float32)

def reference(hidden_in, doc_lengths, attn_gain, query_gain, key_norm_gain, ffn_gain, query_proj, key_weight, value_weight, attn_proj, gate_proj, up_proj, down_proj, out_cotangent):
    token_index = jnp.arange(TOKENS, dtype=jnp.int32)
    starts = (jnp.cumsum(doc_lengths, axis=1) - doc_lengths).astype(jnp.int32)
    located = [locate(token_index, starts[stream]) for stream in range(STREAMS)]

    def whole(resid_all, gains, mats):
        lowered = tuple((low(matrix) for matrix in mats))
        outputs = [block_forward(resid_all[stream], gains, lowered, located[stream][0], located[stream][1], token_index) for stream in range(STREAMS)]
        return jnp.stack(outputs)
    gains = (attn_gain, query_gain, key_norm_gain, ffn_gain)
    mats = (query_proj, key_weight, value_weight, attn_proj, gate_proj, up_proj, down_proj)
    result, backward = jax.vjp(whole, hidden_in.astype(jnp.float32), gains, mats)
    grad_in, grad_gains, grad_mats = backward(out_cotangent.astype(jnp.float32))
    return (result, grad_in, grad_gains[0], grad_gains[1], grad_gains[2], grad_gains[3], grad_mats[0], grad_mats[1], grad_mats[2], grad_mats[3], grad_mats[4], grad_mats[5], grad_mats[6])
```

```python
import functools

import jax
import jax.numpy as jnp
from jax import lax
from jax.experimental import pallas as pl
from jax.experimental.pallas import tpu as pltpu
from jax.sharding import PartitionSpec as P

QUERY_HEADS = 16
KEY_VALUE_HEADS = 8
HEAD_SIZE = 64
FF = 4608
WIDTH = 1024
GROUP = 4
ROWS = 128

epsilon = 1e-05
rope_base = 1000000.0
MESH = pl.DeviceIdType.MESH
ANY = pl.ANY
bf16 = jnp.bfloat16
f32 = jnp.float32


def who():
    c = lax.axis_index("ctx")
    f = lax.axis_index("fsdp")
    return c, f, lax.rem(c, GROUP)


def flip(l, k):
    if k == 0:
        return l
    if k == 1:
        return l + 1 - 2 * lax.rem(l, 2)
    return lax.rem(l + 2, GROUP)


KINDS = ((2, 0), (0, 1), (2, 1))


def slot(l, f):
    return f * GROUP + l


def enter(peers):
    bar = pltpu.get_barrier_semaphore()
    for p in peers:
        pl.semaphore_signal(bar, inc=1, device_id=p, device_id_type=MESH)
    pl.semaphore_wait(bar, len(peers))


def rcopy(src, dst, s, r, dev):
    return pltpu.make_async_remote_copy(
        src_ref=src, dst_ref=dst, send_sem=s, recv_sem=r, device_id=dev, device_id_type=MESH
    )


def gather8_kernel(x_ref, o_ref, ss, rs, ls):
    c, f, l = who()
    base = c - l
    sib = (base + flip(l, 1), f)
    peers = [(base + flip(l, a), lax.rem(f + b, 2)) for a, b in KINDS]
    me = slot(l, f)
    own = pltpu.make_async_copy(x_ref, o_ref.at[me], ls)
    own.start()
    enter([sib] + peers)
    first = []
    for k, p in enumerate(peers):
        cp = rcopy(x_ref, o_ref.at[me], ss.at[k], rs.at[k], p)
        cp.start()
        first.append(cp)
    cp0 = rcopy(x_ref, o_ref.at[me], ss.at[3], rs.at[3], sib)
    cp0.start()
    fw = []
    for k, (a, b) in enumerate(KINDS):
        sl = slot(flip(l, a), lax.rem(f + b, 2))
        first[k].wait_recv()
        cp = rcopy(o_ref.at[sl], o_ref.at[sl], ss.at[4 + k], rs.at[4 + k], sib)
        cp.start()
        fw.append(cp)
    for cp in fw + [cp0]:
        cp.wait_recv()
    for cp in first + [cp0] + fw:
        cp.wait_send()
    own.wait()


def comm_params(cid):
    return pltpu.CompilerParams(collective_id=cid, has_side_effects=True)


def any_specs(n):
    return [pl.BlockSpec(memory_space=ANY)] * n


def gather8(x, cid):
    return pl.pallas_call(
        gather8_kernel,
        out_shape=jax.ShapeDtypeStruct((8,) + x.shape, x.dtype),
        in_specs=any_specs(1),
        out_specs=any_specs(1)[0],
        scratch_shapes=[
            pltpu.SemaphoreType.DMA((7,)),
            pltpu.SemaphoreType.DMA((7,)),
            pltpu.SemaphoreType.DMA,
        ],
        compiler_params=comm_params(cid),
        name="gather8_%d" % cid,
    )(x)


def line_kernel(n, same, x_ref, o_ref, ss, rs, ls):
    c, f, l = who()
    t = lax.div(c, GROUP)
    peers = [(lax.rem(t + s, n) * GROUP + l, f) for s in range(1, n)]

    def src(tt):
        return x_ref if same else x_ref.at[tt]

    own = pltpu.make_async_copy(src(t), o_ref.at[t], ls)
    own.start()
    enter(peers)
    cps = []
    for s in range(1, n):
        cp = rcopy(src(lax.rem(t + s, n)), o_ref.at[t], ss.at[s - 1], rs.at[s - 1], peers[s - 1])
        cp.start()
        cps.append(cp)
    for cp in cps:
        cp.wait_recv()
    for cp in cps:
        cp.wait_send()
    own.wait()


def line(x, n, same, cid):
    shp = x.shape if same else x.shape[1:]
    return pl.pallas_call(
        functools.partial(line_kernel, n, same),
        out_shape=jax.ShapeDtypeStruct((n,) + shp, x.dtype),
        in_specs=any_specs(1),
        out_specs=any_specs(1)[0],
        scratch_shapes=[
            pltpu.SemaphoreType.DMA((n - 1,)),
            pltpu.SemaphoreType.DMA((n - 1,)),
            pltpu.SemaphoreType.DMA,
        ],
        compiler_params=comm_params(cid),
        name="line_%d" % cid,
    )(x)


def scatter8_kernel(x_ref, o_ref, a, b, s_buf, d, ls, s1, r1, s2, r2):
    c, f, l = who()
    base = c - l
    sl = flip(l, 1)
    sib = (base + sl, f)
    peers = [(base + flip(l, i), lax.rem(f + j, 2)) for i, j in KINDS]
    kinds = list(KINDS) + [(0, 0)]
    loads = []
    for k, (i, j) in enumerate(kinds):
        cp = pltpu.make_async_copy(
            x_ref.at[slot(flip(l, i), lax.rem(f + j, 2))], a.at[k], ls.at[k]
        )
        cp.start()
        loads.append(cp)
    enter([sib] + peers)
    ones = []
    for k, (i, j) in enumerate(kinds):
        cp = rcopy(
            x_ref.at[slot(flip(sl, i), lax.rem(f + j, 2))], b.at[k], s1.at[k], r1.at[k], sib
        )
        cp.start()
        ones.append(cp)
    twos = []
    for k in range(3):
        loads[k].wait()
        ones[k].wait_recv()
        s_buf[k] = (a[k].astype(f32) + b[k].astype(f32)).astype(s_buf.dtype)
        cp = rcopy(s_buf.at[k], d.at[k], s2.at[k], r2.at[k], peers[k])
        cp.start()
        twos.append(cp)
    loads[3].wait()
    ones[3].wait_recv()
    total = a[3].astype(f32) + b[3].astype(f32)
    for k in range(3):
        twos[k].wait_recv()
        total = total + d[k].astype(f32)
    o_ref[...] = total
    for cp in ones + twos:
        cp.wait_send()


def scatter8(x, cid):
    shp = x.shape[1:]
    return pl.pallas_call(
        scatter8_kernel,
        out_shape=jax.ShapeDtypeStruct(shp, f32),
        in_specs=any_specs(1),
        out_specs=pl.BlockSpec(memory_space=pltpu.VMEM),
        scratch_shapes=[
            pltpu.VMEM((4,) + shp, x.dtype),
            pltpu.VMEM((4,) + shp, x.dtype),
            pltpu.VMEM((3,) + shp, x.dtype),
            pltpu.VMEM((3,) + shp, x.dtype),
            pltpu.SemaphoreType.DMA((4,)),
            pltpu.SemaphoreType.DMA((4,)),
            pltpu.SemaphoreType.DMA((4,)),
            pltpu.SemaphoreType.DMA((3,)),
            pltpu.SemaphoreType.DMA((3,)),
        ],
        compiler_params=comm_params(cid),
        name="scatter8_%d" % cid,
    )(x)


def swap8_kernel(x_ref, o_ref, ss, rs, ls):
    c, f, l = who()
    base = c - l
    me = slot(l, f)
    own = pltpu.make_async_copy(x_ref.at[me], o_ref.at[me], ls)
    own.start()
    others = [(i, j) for j in range(2) for i in range(4) if i + j]
    peers = [(base + lax.rem(l + i, GROUP), lax.rem(f + j, 2)) for i, j in others]
    enter(peers)
    cps = []
    for k, (i, j) in enumerate(others):
        to = slot(lax.rem(l + i, GROUP), lax.rem(f + j, 2))
        cp = rcopy(x_ref.at[to], o_ref.at[me], ss.at[k], rs.at[k], peers[k])
        cp.start()
        cps.append(cp)
    for cp in cps:
        cp.wait_recv()
    for cp in cps:
        cp.wait_send()
    own.wait()


def swap8(x, cid):
    return pl.pallas_call(
        swap8_kernel,
        out_shape=jax.ShapeDtypeStruct(x.shape, x.dtype),
        in_specs=any_specs(1),
        out_specs=any_specs(1)[0],
        scratch_shapes=[
            pltpu.SemaphoreType.DMA((7,)),
            pltpu.SemaphoreType.DMA((7,)),
            pltpu.SemaphoreType.DMA,
        ],
        compiler_params=comm_params(cid),
        name="swap8_%d" % cid,
    )(x)


def back_product(left, right):
    return lax.dot_general(
        left, right, (((1,), (1,)), ((), ())), preferred_element_type=f32
    )


def lead_sum(left, right):
    return lax.dot_general(
        left, right, (((0,), (0,)), ((), ())), preferred_element_type=f32
    )


def dot(left, right):
    return jnp.dot(left, right, preferred_element_type=f32)


def allowed_block(begin_ref, tok0, key0, rows, keys):
    token = tok0 + lax.broadcasted_iota(jnp.int32, (rows, keys), 0)
    key = key0 + lax.broadcasted_iota(jnp.int32, (rows, keys), 1)
    return (key >= begin_ref) & (key <= token)


def attend_kernel(t_ref, q_ref, kv_ref, begin_ref, sum_ref, tot_ref):
    t = t_ref[0]
    half = q_ref.shape[0] // 2
    qb = 256
    for s in range(2):
        for h in range(2):
            for b in range(half // qb):
                r0 = s * half + b * qb
                q = q_ref[r0 : r0 + qb, h * 64 : h * 64 + 64]
                begin = begin_ref[r0 : r0 + qb, :]

                def step(tt, carry):
                    acc, tot = carry
                    kb = kv_ref[tt, s * half : (s + 1) * half, :]
                    sc = back_product(q, kb[:, :64])
                    ok = allowed_block(begin, t * half + b * qb, tt * half, qb, half)
                    e = jnp.where(ok, jnp.exp(sc), 0.0)
                    acc = acc + dot(e.astype(bf16), kb[:, 64:])
                    tot = tot + jnp.sum(e, axis=1, keepdims=True)
                    return acc, tot

                acc, tot = lax.fori_loop(
                    0,
                    t + 1,
                    step,
                    (jnp.zeros((qb, 64), f32), jnp.zeros((qb, 1), f32)),
                )
                sum_ref[r0 : r0 + qb, h * 64 : h * 64 + 64] = acc
                tot_ref[r0 : r0 + qb, h * 64 : h * 64 + 64] = jnp.broadcast_to(tot, (qb, 64))


VM = pltpu.VMEM


def vspecs(n):
    return [pl.BlockSpec(memory_space=VM)] * n


def attend(t, q, kv, begin):
    n = q.shape[0]
    return pl.pallas_call(
        attend_kernel,
        out_shape=(jax.ShapeDtypeStruct((n, 128), f32), jax.ShapeDtypeStruct((n, 128), f32)),
        in_specs=[pl.BlockSpec(memory_space=pltpu.SMEM)] + vspecs(3),
        out_specs=tuple(vspecs(2)),
        cost_estimate=pl.CostEstimate(flops=2**31, bytes_accessed=2**22, transcendentals=2**22),
        compiler_params=pltpu.CompilerParams(vmem_limit_bytes=40 * 2**20),
        name="attend",
    )(t, q, kv, begin)


def attend_back_kernel(t_ref, q_ref, kv_ref, begin_ref, g_ref, delta_ref, dq_ref, dkv_ref):
    t = t_ref[0]
    half = q_ref.shape[0] // 2
    qb = 256
    T = kv_ref.shape[0]

    def clear(tt, _):
        dkv_ref[tt] = jnp.zeros(dkv_ref.shape[1:], dkv_ref.dtype)
        return 0

    lax.fori_loop(t + 1, T, clear, 0)
    dq_ref[...] = jnp.zeros_like(dq_ref)
    for s in range(2):

        def step(tt, _):
            kb = kv_ref[tt, s * half : (s + 1) * half, :]
            dk = jnp.zeros((half, 64), f32)
            dv = jnp.zeros((half, 64), f32)
            for h in range(2):
                for b in range(half // qb):
                    r0 = s * half + b * qb
                    rows = slice(r0, r0 + qb)
                    lanes = slice(h * 64, h * 64 + 64)
                    q = q_ref[rows, lanes]
                    g = g_ref[rows, lanes]
                    sc = back_product(q, kb[:, :64])
                    ok = allowed_block(
                        begin_ref[rows, :], t * half + b * qb, tt * half, qb, half
                    )
                    e = jnp.where(ok, jnp.exp(sc), 0.0)
                    dp = back_product(g, kb[:, 64:])
                    ds = (e * (dp - delta_ref[rows, h * 64 : h * 64 + 1])).astype(bf16)
                    dq_ref[rows, lanes] += dot(ds, kb[:, :64])
                    dk = dk + lead_sum(ds, q)
                    dv = dv + lead_sum(e.astype(bf16), g)
            dkv_ref[tt, s * half : (s + 1) * half, :] = jnp.concatenate([dk, dv], axis=1).astype(
                dkv_ref.dtype
            )
            return 0

        lax.fori_loop(0, t + 1, step, 0)


def attend_back(t, q, kv, begin, g, delta):
    n = q.shape[0]
    return pl.pallas_call(
        attend_back_kernel,
        out_shape=(jax.ShapeDtypeStruct((n, 128), f32), jax.ShapeDtypeStruct(kv.shape, bf16)),
        in_specs=[pl.BlockSpec(memory_space=pltpu.SMEM)] + vspecs(5),
        out_specs=tuple(vspecs(2)),
        cost_estimate=pl.CostEstimate(flops=2**33, bytes_accessed=2**23, transcendentals=2**22),
        compiler_params=pltpu.CompilerParams(vmem_limit_bytes=48 * 2**20),
        name="attend_back",
    )(t, q, kv, begin, g, delta)


def root_mean_norm(rows, gain):
    return (
        rows * lax.rsqrt(jnp.mean(rows * rows, axis=-1, keepdims=True) + epsilon) * gain
    )


def rotary(rows, cosine, sine):
    halfway = rows.shape[-1] // 2
    leading = rows[..., :halfway]
    trailing = rows[..., halfway:]
    return jnp.concatenate(
        [leading * cosine - trailing * sine, leading * sine + trailing * cosine], axis=-1
    )


SWAP = [(0, 1), (1, 0)]


def halves(f, own, other, axis):
    return jnp.where(
        f == 0,
        jnp.concatenate([own, other], axis=axis),
        jnp.concatenate([other, own], axis=axis),
    )


def local(
    hidden_in,
    doc_lengths,
    attn_gain,
    query_gain,
    key_norm_gain,
    ffn_gain,
    query_proj,
    key_weight,
    value_weight,
    attn_proj,
    gate_proj,
    up_proj,
    down_proj,
    out_cotangent,
):
    n_ctx = lax.axis_size("ctx")
    T = n_ctx // GROUP
    c = lax.axis_index("ctx")
    f = lax.axis_index("fsdp")
    t = c // GROUP
    l = c % GROUP
    head = slot(l, f)
    other_head = slot(l, 1 - f)
    tokens = 8 * ROWS
    half_tokens = tokens // 2
    segment = FF // n_ctx // 2
    columns = T * segment
    half_width = WIDTH // 2

    def head_columns(j):
        return jnp.concatenate(
            [
                lax.dynamic_slice(query_proj, (0, j * 128), (half_width, 128)),
                lax.dynamic_slice(key_weight, (0, j * 64), (half_width, 64)),
                lax.dynamic_slice(value_weight, (0, j * 64), (half_width, 64)),
            ],
            axis=1,
        ).astype(bf16)

    def ff_columns(ff):
        parts = []
        for w in (gate_proj, up_proj):
            for tt in range(T):
                parts.append(
                    lax.dynamic_slice(
                        w,
                        (0, (GROUP * tt + l) * 2 * segment + ff * segment),
                        (half_width, segment),
                    )
                )
        return jnp.concatenate(parts, axis=1).astype(bf16)

    def ff_rows(ff):
        parts = [
            lax.dynamic_slice(
                down_proj, ((GROUP * tt + l) * 2 * segment + ff * segment, 0), (segment, WIDTH)
            )
            for tt in range(T // 2)
        ]
        return jnp.concatenate(parts, axis=0).astype(bf16)

    w_heads = halves(
        f, head_columns(head), lax.ppermute(head_columns(other_head), "fsdp", SWAP), 0
    )
    out_own = attn_proj.astype(bf16)
    w_out = halves(f, out_own, lax.ppermute(out_own, "fsdp", SWAP), 0)
    w_glu = halves(f, ff_columns(f), lax.ppermute(ff_columns(1 - f), "fsdp", SWAP), 0)
    w_down = halves(f, ff_rows(f), lax.ppermute(ff_rows(1 - f), "fsdp", SWAP), 0)

    lengths_other = lax.ppermute(doc_lengths, "fsdp", SWAP)
    lengths = halves(f, doc_lengths, lengths_other, 0)
    starts = jnp.cumsum(lengths, axis=1) - lengths
    token_index = t * half_tokens + jnp.arange(half_tokens, dtype=jnp.int32)
    after = token_index[None, :, None] >= starts[:, None, :]
    begins = jnp.max(jnp.where(after, starts[:, None, :], 0), axis=2).reshape(tokens, 1)
    place = jnp.concatenate([token_index, token_index])[:, None] - begins
    freqs = rope_base ** (-2.0 * jnp.arange(32, dtype=f32) / 64)
    angles = place.astype(f32) * freqs[None, :]
    cosine = jnp.cos(angles)[:, None, :]
    sine = jnp.sin(angles)[:, None, :]

    both = gather8(jnp.stack([hidden_in[0], out_cotangent[0]]), 1)
    x_all = both[:, 0].reshape(tokens, WIDTH).astype(f32)
    c_all = both[:, 1].reshape(tokens, WIDTH)

    normed = root_mean_norm(x_all, attn_gain).astype(bf16)
    stacked = dot(normed, w_heads)

    def rotate(q_in, k_in, q_gain, k_gain):
        q_out = (
            rotary(root_mean_norm(q_in.reshape(tokens, 2, HEAD_SIZE), q_gain), cosine, sine)
            * HEAD_SIZE ** (-0.5)
        )
        k_out = rotary(root_mean_norm(k_in.reshape(tokens, 1, HEAD_SIZE), k_gain), cosine, sine)
        return q_out.reshape(tokens, 128), k_out.reshape(tokens, 64)

    (q_rot, k_rot), heads_back = jax.vjp(
        rotate, stacked[:, :128], stacked[:, 128:192], query_gain, key_norm_gain
    )
    q_rows = q_rot.astype(bf16)
    kv_rows = jnp.concatenate([k_rot, stacked[:, 192:]], axis=1).astype(bf16)
    kv_all = line(kv_rows, T, True, 2)
    t_arr = jnp.full((1,), t, jnp.int32)
    summed, totals = attend(t_arr, q_rows, kv_all, begins)
    attended = gather8((summed / totals).astype(bf16), 3)
    attended = jnp.transpose(attended, (1, 0, 2)).reshape(tokens, WIDTH)
    middle = x_all + dot(attended, w_out)
    normed_ffn = root_mean_norm(middle, ffn_gain).astype(bf16)
    glu = dot(normed_ffn, w_glu)
    gate = glu[:, :columns]
    up = glu[:, columns:]
    sig = 1.0 / (1.0 + jnp.exp(-gate))
    silu = gate * sig
    hidden = (silu * up).astype(bf16)
    grad_hidden = back_product(c_all, w_down)
    grad_gate = (grad_hidden * up * (sig * (1.0 + gate * (1.0 - sig)))).astype(bf16)
    grad_up = (grad_hidden * silu).astype(bf16)
    grad_glu = jnp.concatenate([grad_gate, grad_up], axis=1)
    part_in = back_product(grad_glu, w_glu)
    part_out = dot(hidden, w_down)
    parts = jnp.stack(
        [part_in.reshape(8, ROWS, WIDTH), part_out.reshape(8, ROWS, WIDTH)], axis=1
    ).astype(bf16)
    own_sums = scatter8(parts, 4)

    own = lax.dynamic_slice(middle, (head * ROWS, 0), (ROWS, WIDTH))
    output = own + own_sums[1]
    _, ffn_back = jax.vjp(root_mean_norm, own, ffn_gain)
    grad_mid_norm, ffn_gain_part = ffn_back(own_sums[0])
    grad_middle = out_cotangent[0].astype(f32) + grad_mid_norm
    branch = gather8(grad_middle.astype(bf16), 5).reshape(tokens, WIDTH)

    w_out_head = lax.dynamic_slice(out_own, (l * 128, 0), (128, WIDTH))
    grad_mixed = back_product(branch, w_out_head)
    grad_summed = (grad_mixed / totals).astype(bf16)
    weighted = (grad_mixed * summed / (totals * totals)).reshape(tokens, 2, 64)
    delta = jnp.broadcast_to(
        jnp.sum(weighted, axis=2, keepdims=True), (tokens, 2, 64)
    ).reshape(tokens, 128)
    grad_q, dkv = attend_back(t_arr, q_rows, kv_all, begins, grad_summed, delta)
    dkv = jnp.sum(line(dkv, T, False, 6).astype(f32), axis=0)
    gq_pre, gk_pre, q_gain_part, k_gain_part = heads_back((grad_q, dkv[:, :64]))
    grad_stacked = jnp.concatenate([gq_pre, gk_pre, dkv[:, 64:]], axis=1).astype(bf16)
    part_normed = back_product(grad_stacked, w_heads).reshape(8, ROWS, WIDTH).astype(bf16)
    grad_normed = scatter8(part_normed, 7)
    _, attn_back = jax.vjp(root_mean_norm, hidden_in[0].astype(f32), attn_gain)
    grad_resid, attn_gain_part = attn_back(grad_normed)
    input_grad = grad_middle + grad_resid

    glu_part = lead_sum(grad_glu, normed_ffn)
    glu_part = jnp.transpose(
        glu_part.reshape(2, T, segment, WIDTH).astype(bf16), (1, 0, 2, 3)
    )
    down_part = lead_sum(hidden, c_all)
    down_part = jnp.transpose(
        down_part.astype(bf16).reshape(columns, T, WIDTH // T), (1, 0, 2)
    )
    glu_sum = jnp.sum(line(glu_part, T, False, 8).astype(f32), axis=0)
    down_sum = jnp.sum(line(down_part, T, False, 9).astype(f32), axis=0)
    keep = lax.dynamic_slice(glu_sum, (0, 0, f * half_width), (2, segment, half_width))
    give = lax.dynamic_slice(glu_sum, (0, 0, (1 - f) * half_width), (2, segment, half_width))
    glu_grad = halves(f, keep, lax.ppermute(give, "fsdp", SWAP), 1)
    gate_grad = jnp.transpose(glu_grad[0])
    up_grad = jnp.transpose(glu_grad[1])

    each = WIDTH // n_ctx
    pieces = down_sum.reshape(2, columns // 2, GROUP, each)
    pieces = jnp.transpose(pieces, (0, 2, 1, 3)).reshape(8, columns // 2, each)
    got = swap8(pieces, 10).reshape(2, GROUP, T // 2, segment, each)
    down_grad = jnp.transpose(got, (2, 1, 0, 3, 4)).reshape(FF // 2, each)

    attended_half = lax.dynamic_slice(attended, (0, f * half_width), (tokens, half_width))
    branch_columns = lax.dynamic_slice(
        branch.reshape(tokens, T, GROUP, each), (0, 0, l, 0), (tokens, T, 1, each)
    ).reshape(tokens, T * each)
    attn_part = lead_sum(attended_half, branch_columns).astype(bf16)
    attn_part = jnp.transpose(attn_part.reshape(half_width, T, each), (1, 0, 2))
    attn_grad = jnp.sum(line(attn_part, T, False, 11).astype(f32), axis=0)

    heads_part = lead_sum(normed, grad_stacked).astype(bf16).reshape(T, WIDTH // T, 256)
    heads_sum = jnp.sum(line(heads_part, T, False, 12).astype(f32), axis=0)
    many = T // 2
    kw = 64 // many
    q_pieces = heads_sum[:, :128].reshape(WIDTH // T, many, 128 // many)
    k_pieces = heads_sum[:, 128:192].reshape(WIDTH // T, many, kw)
    v_pieces = heads_sum[:, 192:].reshape(WIDTH // T, many, kw)
    all_pieces = jnp.transpose(
        jnp.concatenate([q_pieces, k_pieces, v_pieces], axis=2), (1, 0, 2)
    )
    rows_of = []
    for i in range(many):
        perm = []
        for src_t in range(T):
            for src_l in range(GROUP):
                for src_f in range(2):
                    to_ctx = slot(src_l, src_f) * many + (i + src_t) % many
                    perm.append(((src_t * GROUP + src_l) * 2 + src_f, to_ctx * 2 + src_t // many))
        piece = lax.dynamic_index_in_dim(all_pieces, (i + t) % many, 0, keepdims=False)
        rows_of.append(lax.ppermute(piece, ("ctx", "fsdp"), perm))
    got_rows = jnp.stack(rows_of)
    order = (c - jnp.arange(many)) % many
    heads_grad = jnp.take(got_rows, order, axis=0).reshape(half_width, 256 // many)
    query_grad = heads_grad[:, : 128 // many]
    key_grad = heads_grad[:, 128 // many : 128 // many + kw]
    value_grad = heads_grad[:, 128 // many + kw :]

    gains = jnp.concatenate([attn_gain_part, ffn_gain_part, q_gain_part, k_gain_part])
    gains = jnp.sum(gather8(gains.reshape(17, 128), 13), axis=0)
    gains = jnp.sum(line(gains, T, True, 14), axis=0).reshape(-1)
    return (
        output[None],
        input_grad[None],
        gains[:WIDTH],
        gains[2 * WIDTH : 2 * WIDTH + 64],
        gains[2 * WIDTH + 64 :],
        gains[WIDTH : 2 * WIDTH],
        query_grad,
        key_grad,
        value_grad,
        attn_grad,
        gate_grad,
        up_grad,
        down_grad,
    )


def solution(mesh):
    in_specs = (
        P("fsdp", "ctx", None),
        P("fsdp", None),
        P(),
        P(),
        P(),
        P(),
        P("fsdp", None),
        P("fsdp", None),
        P("fsdp", None),
        P("fsdp", None),
        P("fsdp", None),
        P("fsdp", None),
        P("fsdp", None),
        P("fsdp", "ctx", None),
    )
    out_specs = (
        P("fsdp", "ctx", None),
        P("fsdp", "ctx", None),
        P(),
        P(),
        P(),
        P(),
        P("fsdp", "ctx"),
        P("fsdp", "ctx"),
        P("fsdp", "ctx"),
        P("fsdp", "ctx"),
        P("fsdp", "ctx"),
        P("fsdp", "ctx"),
        P("fsdp", "ctx"),
    )
    return jax.shard_map(local, mesh=mesh, in_specs=in_specs, out_specs=out_specs, check_vma=False)
```

```python
import functools

import jax
import jax.numpy as jnp
from jax import lax
from jax.experimental import pallas as pl
from jax.experimental.pallas import tpu as pltpu
from jax.sharding import PartitionSpec as P

QUERY_HEADS = 16
KEY_VALUE_HEADS = 8
HEAD_SIZE = 64
FF = 4608
WIDTH = 1024
ROWS = 128

epsilon = 1e-05
rope_base = 1000000.0
MESH = pl.DeviceIdType.MESH
ANY = pl.ANY
bf16 = jnp.bfloat16
f32 = jnp.float32


def who():
    n = lax.axis_size("ctx")
    c = lax.axis_index("ctx")
    f = lax.axis_index("fsdp")
    q = n // 4
    return c // q, (c % q) // 2, c % 2, f


def dev(z, m, core, f):
    return (z * (lax.axis_size("ctx") // 4) + m * 2 + core, f)


def slot(z, core):
    return z * 2 + core


def enter(peers):
    bar = pltpu.get_barrier_semaphore()
    for p in peers:
        pl.semaphore_signal(bar, inc=1, device_id=p, device_id_type=MESH)
    pl.semaphore_wait(bar, len(peers))


def rcopy(src, dst, s, r, to):
    return pltpu.make_async_remote_copy(
        src_ref=src, dst_ref=dst, send_sem=s, recv_sem=r, device_id=to, device_id_type=MESH
    )


def comm_params(cid):
    return pltpu.CompilerParams(collective_id=cid, has_side_effects=True)


def any_specs(n):
    return [pl.BlockSpec(memory_space=ANY)] * n


def gather8_kernel(x_ref, o_ref, ss, rs, ls):
    z, m, core, f = who()
    sib = dev(z, m, 1 - core, f)
    peers = [dev((z + s) % 4, m, core, f) for s in (1, 2, 3)]
    me = slot(z, core)
    own = pltpu.make_async_copy(x_ref, o_ref.at[me], ls)
    own.start()
    enter([sib] + peers)
    first = []
    for k in (1, 0, 2):
        cp = rcopy(x_ref, o_ref.at[me], ss.at[k], rs.at[k], peers[k])
        cp.start()
        first.append((k, cp))
    cp0 = rcopy(x_ref, o_ref.at[me], ss.at[3], rs.at[3], sib)
    cp0.start()
    fw = []
    for k, cp in first:
        sl = slot((z + 3 - k) % 4, core)
        cp.wait_recv()
        cp = rcopy(o_ref.at[sl], o_ref.at[sl], ss.at[4 + k], rs.at[4 + k], sib)
        cp.start()
        fw.append(cp)
    for cp in fw + [cp0]:
        cp.wait_recv()
    for cp in [cp for _, cp in first] + [cp0] + fw:
        cp.wait_send()
    own.wait()


def gather8(x, cid):
    return pl.pallas_call(
        gather8_kernel,
        out_shape=jax.ShapeDtypeStruct((8,) + x.shape, x.dtype),
        in_specs=any_specs(1),
        out_specs=any_specs(1)[0],
        scratch_shapes=[
            pltpu.SemaphoreType.DMA((7,)),
            pltpu.SemaphoreType.DMA((7,)),
            pltpu.SemaphoreType.DMA,
        ],
        compiler_params=comm_params(cid),
        name="gather8_%d" % cid,
    )(x)


def across_kernel(both, same, x_ref, o_ref, ss, rs, ls):
    z, m, core, f = who()
    M = lax.axis_size("ctx") // 8
    count = M * 2 if both else M
    me = m * 2 + f if both else m
    others = [(me + s) % count for s in range(1, count)]
    peers = [dev(z, o // 2, core, o % 2) if both else dev(z, o, core, f) for o in others]

    def src(k):
        return x_ref if same else x_ref.at[k]

    own = pltpu.make_async_copy(src(me), o_ref.at[me], ls)
    own.start()
    enter(peers)
    cps = []
    for s in range(count - 1):
        cp = rcopy(src(others[s]), o_ref.at[me], ss.at[s], rs.at[s], peers[s])
        cp.start()
        cps.append(cp)
    for cp in cps:
        cp.wait_recv()
    for cp in cps:
        cp.wait_send()
    own.wait()


def across(x, both, same, cid):
    shp = x.shape if same else x.shape[1:]
    count = lax.axis_size("ctx") // (4 if both else 8)
    return pl.pallas_call(
        functools.partial(across_kernel, both, same),
        out_shape=jax.ShapeDtypeStruct((count,) + shp, x.dtype),
        in_specs=any_specs(1),
        out_specs=any_specs(1)[0],
        scratch_shapes=[
            pltpu.SemaphoreType.DMA((count - 1,)),
            pltpu.SemaphoreType.DMA((count - 1,)),
            pltpu.SemaphoreType.DMA,
        ],
        compiler_params=comm_params(cid),
        name="across_%d" % cid,
    )(x)


def scatter8_kernel(x_ref, o_ref, a, b, s_buf, d, ls, s1, r1, s2, r2):
    z, m, core, f = who()
    sib = dev(z, m, 1 - core, f)
    to = [(z + s) % 4 for s in (1, 2, 3, 0)]
    peers = [dev(zz, m, core, f) for zz in to[:3]]
    loads = []
    for k in range(4):
        cp = pltpu.make_async_copy(x_ref.at[slot(to[k], core)], a.at[k], ls.at[k])
        cp.start()
        loads.append(cp)
    enter([sib] + peers)
    ones = []
    for k in range(4):
        cp = rcopy(x_ref.at[slot(to[k], 1 - core)], b.at[k], s1.at[k], r1.at[k], sib)
        cp.start()
        ones.append(cp)
    twos = []
    for k in range(3):
        loads[k].wait()
        ones[k].wait_recv()
        s_buf[k] = (a[k].astype(f32) + b[k].astype(f32)).astype(s_buf.dtype)
        cp = rcopy(s_buf.at[k], d.at[k], s2.at[k], r2.at[k], peers[k])
        cp.start()
        twos.append(cp)
    loads[3].wait()
    ones[3].wait_recv()
    total = a[3].astype(f32) + b[3].astype(f32)
    for k in range(3):
        twos[k].wait_recv()
        total = total + d[k].astype(f32)
    o_ref[...] = total
    for cp in ones + twos:
        cp.wait_send()


def scatter8(x, cid):
    shp = x.shape[1:]
    return pl.pallas_call(
        scatter8_kernel,
        out_shape=jax.ShapeDtypeStruct(shp, f32),
        in_specs=any_specs(1),
        out_specs=pl.BlockSpec(memory_space=pltpu.VMEM),
        scratch_shapes=[
            pltpu.VMEM((4,) + shp, x.dtype),
            pltpu.VMEM((4,) + shp, x.dtype),
            pltpu.VMEM((3,) + shp, x.dtype),
            pltpu.VMEM((3,) + shp, x.dtype),
            pltpu.SemaphoreType.DMA((4,)),
            pltpu.SemaphoreType.DMA((4,)),
            pltpu.SemaphoreType.DMA((4,)),
            pltpu.SemaphoreType.DMA((3,)),
            pltpu.SemaphoreType.DMA((3,)),
        ],
        compiler_params=comm_params(cid),
        name="scatter8_%d" % cid,
    )(x)


def back_product(left, right):
    return lax.dot_general(
        left, right, (((1,), (1,)), ((), ())), preferred_element_type=f32
    )


def lead_sum(left, right):
    return lax.dot_general(
        left, right, (((0,), (0,)), ((), ())), preferred_element_type=f32
    )


def dot(left, right):
    return jnp.dot(left, right, preferred_element_type=f32)


BLOCK = 2 * ROWS


def block_weights(q, k, begin, z, m, mm, span):
    keys = (z + 1) * BLOCK
    key = lax.broadcasted_iota(jnp.int32, (1, keys), 1)
    key = key // BLOCK * span + key % BLOCK + mm * BLOCK
    token = z * span + m * BLOCK + lax.broadcasted_iota(jnp.int32, (BLOCK, 1), 0)
    e = jnp.exp(back_product(q, k))
    return jnp.where((key >= begin) & (key <= token), e, 0.0)


def attend_kernel(span, m_ref, q_ref, kv_ref, begin_ref, sum_ref, tot_ref):
    m = m_ref[0]
    for z in range(4):
        rows = slice(z * BLOCK, (z + 1) * BLOCK)
        keys = (z + 1) * BLOCK
        for h in range(2):
            lanes = slice(h * 64, h * 64 + 64)
            acc = jnp.zeros((BLOCK, 64), f32)
            tot = jnp.zeros((BLOCK, 1), f32)
            q = q_ref[rows, lanes]

            def step(mm, carry):
                acc, tot = carry
                e = block_weights(q, kv_ref[mm, :keys, :64], begin_ref[rows, :], z, m, mm, span)
                acc = acc + dot(e.astype(bf16), kv_ref[mm, :keys, 64:])
                return acc, tot + jnp.sum(e, axis=1, keepdims=True)

            acc, tot = lax.fori_loop(0, kv_ref.shape[0], step, (acc, tot))
            sum_ref[rows, lanes] = acc
            tot_ref[rows, lanes] = jnp.broadcast_to(tot, (BLOCK, 64))


VM = pltpu.VMEM


def vspecs(n):
    return [pl.BlockSpec(memory_space=VM)] * n


def attend(m, q, kv, begin, span):
    n = q.shape[0]
    return pl.pallas_call(
        functools.partial(attend_kernel, span),
        out_shape=(jax.ShapeDtypeStruct((n, 128), f32), jax.ShapeDtypeStruct((n, 128), f32)),
        in_specs=[pl.BlockSpec(memory_space=pltpu.SMEM)] + vspecs(3),
        out_specs=tuple(vspecs(2)),
        cost_estimate=pl.CostEstimate(flops=2**31, bytes_accessed=2**22, transcendentals=2**22),
        compiler_params=pltpu.CompilerParams(vmem_limit_bytes=40 * 2**20),
        name="attend",
    )(m, q, kv, begin)


def attend_back_kernel(span, m_ref, q_ref, kv_ref, begin_ref, g_ref, delta_ref, dq_ref, dkv_ref, acc_ref):
    m = m_ref[0]
    dq_ref[...] = jnp.zeros_like(dq_ref)

    def step(mm, _):
        acc_ref[...] = jnp.zeros_like(acc_ref)
        for z in range(4):
            rows = slice(z * BLOCK, (z + 1) * BLOCK)
            keys = (z + 1) * BLOCK
            for h in range(2):
                lanes = slice(h * 64, h * 64 + 64)
                q = q_ref[rows, lanes]
                g = g_ref[rows, lanes]
                k = kv_ref[mm, :keys, :64]
                v = kv_ref[mm, :keys, 64:]
                e = block_weights(q, k, begin_ref[rows, :], z, m, mm, span)
                dp = back_product(g, v)
                ds = (e * (dp - delta_ref[rows, h * 64 : h * 64 + 1])).astype(bf16)
                dq_ref[rows, lanes] += dot(ds, k)
                acc_ref[:keys, :64] += lead_sum(ds, q)
                acc_ref[:keys, 64:] += lead_sum(e.astype(bf16), g)
        dkv_ref[mm] = acc_ref[...].astype(dkv_ref.dtype)
        return 0

    lax.fori_loop(0, kv_ref.shape[0], step, 0)


def attend_back(m, q, kv, begin, g, delta, span):
    n = q.shape[0]
    return pl.pallas_call(
        functools.partial(attend_back_kernel, span),
        out_shape=(jax.ShapeDtypeStruct((n, 128), f32), jax.ShapeDtypeStruct(kv.shape, bf16)),
        in_specs=[pl.BlockSpec(memory_space=pltpu.SMEM)] + vspecs(5),
        out_specs=tuple(vspecs(2)),
        scratch_shapes=[pltpu.VMEM((n, 128), f32)],
        cost_estimate=pl.CostEstimate(flops=2**33, bytes_accessed=2**23, transcendentals=2**22),
        compiler_params=pltpu.CompilerParams(vmem_limit_bytes=48 * 2**20),
        name="attend_back",
    )(m, q, kv, begin, g, delta)


def root_mean_norm(rows, gain):
    return (
        rows * lax.rsqrt(jnp.mean(rows * rows, axis=-1, keepdims=True) + epsilon) * gain
    )


def rotary(rows, cosine, sine):
    halfway = rows.shape[-1] // 2
    leading = rows[..., :halfway]
    trailing = rows[..., halfway:]
    return jnp.concatenate(
        [leading * cosine - trailing * sine, leading * sine + trailing * cosine], axis=-1
    )


SWAP = [(0, 1), (1, 0)]


def halves(f, own, other, axis):
    return jnp.where(
        f == 0,
        jnp.concatenate([own, other], axis=axis),
        jnp.concatenate([other, own], axis=axis),
    )


def local(
    hidden_in,
    doc_lengths,
    attn_gain,
    query_gain,
    key_norm_gain,
    ffn_gain,
    query_proj,
    key_weight,
    value_weight,
    attn_proj,
    gate_proj,
    up_proj,
    down_proj,
    out_cotangent,
):
    n_ctx = lax.axis_size("ctx")
    M = n_ctx // 8
    T = 2 * M
    z, m, core, f = who()
    head = slot(z, core)
    tokens = 8 * ROWS
    span = n_ctx // 4 * ROWS
    segment = FF // n_ctx
    columns = M * segment
    half_width = WIDTH // 2
    each = WIDTH // n_ctx

    heads_own = jnp.concatenate(
        [
            lax.dynamic_slice(query_proj, (0, head * 128), (half_width, 128)),
            lax.dynamic_slice(key_weight, (0, head * 64), (half_width, 64)),
            lax.dynamic_slice(value_weight, (0, head * 64), (half_width, 64)),
        ],
        axis=1,
    ).astype(bf16)
    first = z * (n_ctx // 4) + core
    glu_own = jnp.concatenate(
        [
            lax.dynamic_slice(w, (0, (first + 2 * mm) * segment), (half_width, segment)).astype(bf16)
            for w in (gate_proj, up_proj)
            for mm in range(M)
        ],
        axis=1,
    )
    down_own = jnp.concatenate(
        [
            lax.dynamic_slice(
                down_proj, ((first + 2 * mm) * segment - f * (FF // 2), 0), (segment, WIDTH)
            )
            for mm in range(M)
        ],
        axis=0,
    ).astype(bf16)
    out_own = attn_proj.astype(bf16)

    def swap(v):
        return lax.ppermute(v, "fsdp", SWAP)

    w_heads = halves(f, heads_own, swap(heads_own), 0)
    x_all = gather8(hidden_in[0], 1).reshape(tokens, WIDTH).astype(f32)
    heads_own, glu_own, down_own, out_own, cotangent, x_all = lax.optimization_barrier(
        (heads_own, glu_own, down_own, out_own, out_cotangent[0], x_all)
    )
    w_out = halves(f, out_own, swap(out_own), 0)
    w_glu = halves(f, glu_own, swap(glu_own), 0)
    w_down = jnp.where(f == z // 2, down_own, swap(down_own))

    starts = jnp.cumsum(doc_lengths[0]) - doc_lengths[0]
    token_index = (
        jnp.arange(4, dtype=jnp.int32)[:, None] * span
        + m * BLOCK
        + jnp.arange(BLOCK, dtype=jnp.int32)[None, :]
    ).reshape(tokens, 1)
    after = token_index >= starts[None, :]
    begins = jnp.max(jnp.where(after, starts[None, :], 0), axis=1, keepdims=True)
    place = token_index - begins
    freqs = rope_base ** (-2.0 * jnp.arange(32, dtype=f32) / 64)
    angles = place.astype(f32) * freqs[None, :]
    cosine = jnp.cos(angles)[:, None, :]
    sine = jnp.sin(angles)[:, None, :]

    normed = root_mean_norm(x_all, attn_gain).astype(bf16)
    stacked = dot(normed, w_heads)

    def rotate(q_in, k_in, q_gain, k_gain):
        q_out = (
            rotary(root_mean_norm(q_in.reshape(tokens, 2, HEAD_SIZE), q_gain), cosine, sine)
            * HEAD_SIZE ** (-0.5)
        )
        k_out = rotary(root_mean_norm(k_in.reshape(tokens, 1, HEAD_SIZE), k_gain), cosine, sine)
        return q_out.reshape(tokens, 128), k_out.reshape(tokens, 64)

    (q_rot, k_rot), heads_back = jax.vjp(
        rotate, stacked[:, :128], stacked[:, 128:192], query_gain, key_norm_gain
    )
    q_rows = q_rot.astype(bf16)
    kv_rows = jnp.concatenate([k_rot, stacked[:, 192:]], axis=1).astype(bf16)
    kv_all = across(kv_rows, False, True, 2)
    m_arr = jnp.full((1,), m, jnp.int32)
    summed, totals = attend(m_arr, q_rows, kv_all, begins, span)
    attended = gather8((summed / totals).astype(bf16), 3)
    attended = jnp.transpose(attended, (1, 0, 2)).reshape(tokens, WIDTH)
    c_all = gather8(cotangent, 15).reshape(tokens, WIDTH)
    middle = x_all + dot(attended, w_out)
    normed_ffn = root_mean_norm(middle, ffn_gain).astype(bf16)
    glu = dot(normed_ffn, w_glu)
    gate = glu[:, :columns]
    up = glu[:, columns:]
    sig = 1.0 / (1.0 + jnp.exp(-gate))
    silu = gate * sig
    hidden = (silu * up).astype(bf16)
    grad_hidden = back_product(c_all, w_down)
    grad_gate = (grad_hidden * up * (sig * (1.0 + gate * (1.0 - sig)))).astype(bf16)
    grad_up = (grad_hidden * silu).astype(bf16)
    grad_glu = jnp.concatenate([grad_gate, grad_up], axis=1)
    part_in = back_product(grad_glu, w_glu)
    part_out = dot(hidden, w_down)
    parts = jnp.stack(
        [part_in.reshape(8, ROWS, WIDTH), part_out.reshape(8, ROWS, WIDTH)], axis=1
    ).astype(bf16)
    own_sums = scatter8(parts, 4)

    own = lax.dynamic_slice(middle, (head * ROWS, 0), (ROWS, WIDTH))
    output = own + own_sums[1]
    _, ffn_back = jax.vjp(root_mean_norm, own, ffn_gain)
    grad_mid_norm, ffn_gain_part = ffn_back(own_sums[0])
    grad_middle = out_cotangent[0].astype(f32) + grad_mid_norm
    branch = gather8(grad_middle.astype(bf16), 5).reshape(tokens, WIDTH)

    w_out_head = lax.dynamic_slice(w_out, (head * 128, 0), (128, WIDTH))
    grad_mixed = back_product(branch, w_out_head)
    grad_summed = (grad_mixed / totals).astype(bf16)
    weighted = (grad_mixed * summed / (totals * totals)).reshape(tokens, 2, 64)
    delta = jnp.broadcast_to(
        jnp.sum(weighted, axis=2, keepdims=True), (tokens, 2, 64)
    ).reshape(tokens, 128)
    grad_q, dkv = attend_back(m_arr, q_rows, kv_all, begins, grad_summed, delta, span)
    dkv = jnp.sum(across(dkv, False, False, 6).astype(f32), axis=0)
    gq_pre, gk_pre, q_gain_part, k_gain_part = heads_back((grad_q, dkv[:, :64]))
    grad_stacked = jnp.concatenate([gq_pre, gk_pre, dkv[:, 64:]], axis=1).astype(bf16)
    part_normed = back_product(grad_stacked, w_heads).reshape(8, ROWS, WIDTH).astype(bf16)
    grad_normed = scatter8(part_normed, 7)
    _, attn_back = jax.vjp(root_mean_norm, hidden_in[0].astype(f32), attn_gain)
    grad_resid, attn_gain_part = attn_back(grad_normed)
    input_grad = grad_middle + grad_resid

    glu_part = lead_sum(grad_glu, normed_ffn).astype(bf16)
    glu_part = jnp.transpose(
        glu_part.reshape(2, M, segment, 2, half_width), (1, 3, 0, 2, 4)
    ).reshape(T, 2, segment, half_width)
    down_part = lead_sum(hidden, c_all).astype(bf16)
    down_part = jnp.transpose(
        down_part.reshape(columns, 2, 2, M, 2, each), (3, 1, 0, 2, 4, 5)
    ).reshape(T, columns, 4 * each)
    glu_grad = jnp.sum(across(glu_part, True, False, 8).astype(f32), axis=0)
    down_sum = jnp.sum(across(down_part, True, False, 9).astype(f32), axis=0)
    gate_grad = jnp.transpose(glu_grad[0])
    up_grad = jnp.transpose(glu_grad[1])

    devices = [
        (zz, mm, cc, ff) for zz in range(4) for mm in range(M) for cc in range(2) for ff in range(2)
    ]

    def number(zz, mm, cc, ff):
        return (zz * (n_ctx // 4) + mm * 2 + cc) * 2 + ff

    down_pieces = down_sum.reshape(columns, 2, 2, each)
    got = [[None, None], [None, None]]
    rounds = []
    for dz in range(2):
        for dc in range(2):
            piece = lax.dynamic_slice(
                down_pieces, (0, (z + dz) % 2, (core + dc) % 2, 0), (columns, 1, 1, each)
            ).reshape(columns, each)
            perm = [
                (number(zz, mm, cc, ff), number(2 * ff + (zz + dz) % 2, mm, (cc + dc) % 2, zz // 2))
                for zz, mm, cc, ff in devices
            ]
            rounds.append(lax.ppermute(piece, ("ctx", "fsdp"), perm))
    rounds = jnp.stack(rounds).reshape(2, 2, columns, each)
    rounds = jnp.where(z % 2 == 0, rounds, rounds[::-1])
    rounds = jnp.where(core == 0, rounds, rounds[:, ::-1])
    down_grad = jnp.transpose(
        rounds.reshape(2, 2, M, segment, each), (0, 2, 1, 3, 4)
    ).reshape(FF // 2, each)

    branch_columns = lax.dynamic_slice(
        branch.reshape(tokens, 4, M, 2, each), (0, z, 0, core, 0), (tokens, 1, M, 1, each)
    ).reshape(tokens, M * each)
    attn_part = lead_sum(attended, branch_columns).astype(bf16)
    attn_part = jnp.transpose(
        attn_part.reshape(2, half_width, M, each), (2, 0, 1, 3)
    ).reshape(T, half_width, each)
    attn_grad = jnp.sum(across(attn_part, True, False, 11).astype(f32), axis=0)

    heads_part = lead_sum(normed, grad_stacked).astype(bf16)
    qw, kw = 128 // M, 64 // M
    heads_part = jnp.concatenate(
        [
            heads_part[:, :128].reshape(2, half_width, M, qw),
            heads_part[:, 128:192].reshape(2, half_width, M, kw),
            heads_part[:, 192:].reshape(2, half_width, M, kw),
        ],
        axis=3,
    )
    heads_part = jnp.transpose(heads_part, (2, 0, 1, 3)).reshape(T, half_width, 256 // M)
    heads_grad = jnp.sum(across(heads_part, True, False, 12).astype(f32), axis=0)
    perm = [
        (number(zz, mm, cc, ff), number(zz, (cc * M + mm) // 2, (cc * M + mm) % 2, ff))
        for zz, mm, cc, ff in devices
    ]
    heads_grad = lax.ppermute(heads_grad, ("ctx", "fsdp"), perm)
    query_grad = heads_grad[:, :qw]
    key_grad = heads_grad[:, qw : qw + kw]
    value_grad = heads_grad[:, qw + kw :]

    gains = jnp.concatenate([attn_gain_part, ffn_gain_part, q_gain_part, k_gain_part])
    gains = jnp.sum(gather8(gains.reshape(17, 128), 13), axis=0)
    gains = jnp.sum(across(gains, True, True, 14), axis=0).reshape(-1)
    return (
        output[None],
        input_grad[None],
        gains[:WIDTH],
        gains[2 * WIDTH : 2 * WIDTH + 64],
        gains[2 * WIDTH + 64 :],
        gains[WIDTH : 2 * WIDTH],
        query_grad,
        key_grad,
        value_grad,
        attn_grad,
        gate_grad,
        up_grad,
        down_grad,
    )


def solution(mesh):
    in_specs = (
        P("fsdp", "ctx", None),
        P("fsdp", None),
        P(),
        P(),
        P(),
        P(),
        P("fsdp", None),
        P("fsdp", None),
        P("fsdp", None),
        P("fsdp", None),
        P("fsdp", None),
        P("fsdp", None),
        P("fsdp", None),
        P("fsdp", "ctx", None),
    )
    out_specs = (
        P("fsdp", "ctx", None),
        P("fsdp", "ctx", None),
        P(),
        P(),
        P(),
        P(),
        P("fsdp", "ctx"),
        P("fsdp", "ctx"),
        P("fsdp", "ctx"),
        P("fsdp", "ctx"),
        P("fsdp", "ctx"),
        P("fsdp", "ctx"),
        P("fsdp", "ctx"),
    )
    return jax.shard_map(local, mesh=mesh, in_specs=in_specs, out_specs=out_specs, check_vma=False)
```

```python
import functools

import jax
import jax.numpy as jnp
from jax import lax
from jax.experimental import pallas as pl
from jax.experimental.pallas import tpu as pltpu
from jax.sharding import PartitionSpec as P

QUERY_HEADS = 16
KEY_VALUE_HEADS = 8
HEAD_SIZE = 64
FF = 4608
WIDTH = 1024
ROWS = 128

epsilon = 1e-05
rope_base = 1000000.0
MESH = pl.DeviceIdType.MESH
ANY = pl.ANY
bf16 = jnp.bfloat16
f32 = jnp.float32


def who():
    n = lax.axis_size("ctx")
    c = lax.axis_index("ctx")
    f = lax.axis_index("fsdp")
    q = n // 4
    return c // q, (c % q) // 2, c % 2, f


def dev(z, m, core, f):
    return (z * (lax.axis_size("ctx") // 4) + m * 2 + core, f)


def slot(z, core):
    return z * 2 + core


def enter(peers):
    bar = pltpu.get_barrier_semaphore()
    for p in peers:
        pl.semaphore_signal(bar, inc=1, device_id=p, device_id_type=MESH)
    pl.semaphore_wait(bar, len(peers))


def rcopy(src, dst, s, r, to):
    return pltpu.make_async_remote_copy(
        src_ref=src, dst_ref=dst, send_sem=s, recv_sem=r, device_id=to, device_id_type=MESH
    )


def comm_params(cid):
    return pltpu.CompilerParams(collective_id=cid, has_side_effects=True)


def any_specs(n):
    return [pl.BlockSpec(memory_space=ANY)] * n


def gather8_kernel(x_ref, o_ref, ss, rs, ls):
    z, m, core, f = who()
    sib = dev(z, m, 1 - core, f)
    peers = [dev((z + s) % 4, m, core, f) for s in (1, 2, 3)]
    me = slot(z, core)
    own = pltpu.make_async_copy(x_ref, o_ref.at[me], ls)
    own.start()
    enter([sib] + peers)
    first = []
    for k in (1, 0, 2):
        cp = rcopy(x_ref, o_ref.at[me], ss.at[k], rs.at[k], peers[k])
        cp.start()
        first.append((k, cp))
    cp0 = rcopy(x_ref, o_ref.at[me], ss.at[3], rs.at[3], sib)
    cp0.start()
    fw = []
    for k, cp in first:
        sl = slot((z + 3 - k) % 4, core)
        cp.wait_recv()
        cp = rcopy(o_ref.at[sl], o_ref.at[sl], ss.at[4 + k], rs.at[4 + k], sib)
        cp.start()
        fw.append(cp)
    for cp in fw + [cp0]:
        cp.wait_recv()
    for cp in [cp for _, cp in first] + [cp0] + fw:
        cp.wait_send()
    own.wait()


def gather8(x, cid):
    return pl.pallas_call(
        gather8_kernel,
        out_shape=jax.ShapeDtypeStruct((8,) + x.shape, x.dtype),
        in_specs=any_specs(1),
        out_specs=any_specs(1)[0],
        scratch_shapes=[
            pltpu.SemaphoreType.DMA((7,)),
            pltpu.SemaphoreType.DMA((7,)),
            pltpu.SemaphoreType.DMA,
        ],
        compiler_params=comm_params(cid),
        name="gather8_%d" % cid,
    )(x)


def across_kernel(both, same, x_ref, o_ref, ss, rs, ls):
    z, m, core, f = who()
    M = lax.axis_size("ctx") // 8
    count = M * 2 if both else M
    me = m * 2 + f if both else m
    others = [(me + s) % count for s in range(1, count)]
    peers = [dev(z, o // 2, core, o % 2) if both else dev(z, o, core, f) for o in others]

    def src(k):
        return x_ref if same else x_ref.at[k]

    own = pltpu.make_async_copy(src(me), o_ref.at[me], ls)
    own.start()
    enter(peers)
    cps = []
    for s in range(count - 1):
        cp = rcopy(src(others[s]), o_ref.at[me], ss.at[s], rs.at[s], peers[s])
        cp.start()
        cps.append(cp)
    for cp in cps:
        cp.wait_recv()
    for cp in cps:
        cp.wait_send()
    own.wait()


def across(x, both, same, cid):
    shp = x.shape if same else x.shape[1:]
    count = lax.axis_size("ctx") // (4 if both else 8)
    return pl.pallas_call(
        functools.partial(across_kernel, both, same),
        out_shape=jax.ShapeDtypeStruct((count,) + shp, x.dtype),
        in_specs=any_specs(1),
        out_specs=any_specs(1)[0],
        scratch_shapes=[
            pltpu.SemaphoreType.DMA((count - 1,)),
            pltpu.SemaphoreType.DMA((count - 1,)),
            pltpu.SemaphoreType.DMA,
        ],
        compiler_params=comm_params(cid),
        name="across_%d" % cid,
    )(x)


def scatter8_kernel(x_ref, o_ref, a, b, s_buf, d, ls, s1, r1, s2, r2):
    z, m, core, f = who()
    sib = dev(z, m, 1 - core, f)
    to = [(z + s) % 4 for s in (1, 2, 3, 0)]
    peers = [dev(zz, m, core, f) for zz in to[:3]]
    loads = []
    for k in range(4):
        cp = pltpu.make_async_copy(x_ref.at[slot(to[k], core)], a.at[k], ls.at[k])
        cp.start()
        loads.append(cp)
    enter([sib] + peers)
    ones = []
    for k in range(4):
        cp = rcopy(x_ref.at[slot(to[k], 1 - core)], b.at[k], s1.at[k], r1.at[k], sib)
        cp.start()
        ones.append(cp)
    twos = []
    for k in range(3):
        loads[k].wait()
        ones[k].wait_recv()
        s_buf[k] = (a[k].astype(f32) + b[k].astype(f32)).astype(s_buf.dtype)
        cp = rcopy(s_buf.at[k], d.at[k], s2.at[k], r2.at[k], peers[k])
        cp.start()
        twos.append(cp)
    loads[3].wait()
    ones[3].wait_recv()
    total = a[3].astype(f32) + b[3].astype(f32)
    for k in range(3):
        twos[k].wait_recv()
        total = total + d[k].astype(f32)
    o_ref[...] = total
    for cp in ones + twos:
        cp.wait_send()


def scatter8(x, cid):
    shp = x.shape[1:]
    return pl.pallas_call(
        scatter8_kernel,
        out_shape=jax.ShapeDtypeStruct(shp, f32),
        in_specs=any_specs(1),
        out_specs=pl.BlockSpec(memory_space=pltpu.VMEM),
        scratch_shapes=[
            pltpu.VMEM((4,) + shp, x.dtype),
            pltpu.VMEM((4,) + shp, x.dtype),
            pltpu.VMEM((3,) + shp, x.dtype),
            pltpu.VMEM((3,) + shp, x.dtype),
            pltpu.SemaphoreType.DMA((4,)),
            pltpu.SemaphoreType.DMA((4,)),
            pltpu.SemaphoreType.DMA((4,)),
            pltpu.SemaphoreType.DMA((3,)),
            pltpu.SemaphoreType.DMA((3,)),
        ],
        compiler_params=comm_params(cid),
        name="scatter8_%d" % cid,
    )(x)


def back_product(left, right):
    return lax.dot_general(
        left, right, (((1,), (1,)), ((), ())), preferred_element_type=f32
    )


def lead_sum(left, right):
    return lax.dot_general(
        left, right, (((0,), (0,)), ((), ())), preferred_element_type=f32
    )


def dot(left, right):
    return jnp.dot(left, right, preferred_element_type=f32)


BLOCK = 2 * ROWS


def block_weights(q, k, begin, z, m, mm, span):
    keys = (z + 1) * BLOCK
    key = lax.broadcasted_iota(jnp.int32, (1, keys), 1)
    key = key // BLOCK * span + key % BLOCK + mm * BLOCK
    token = z * span + m * BLOCK + lax.broadcasted_iota(jnp.int32, (BLOCK, 1), 0)
    e = jnp.exp(back_product(q, k))
    return jnp.where((key >= begin) & (key <= token), e, 0.0)


def attend_kernel(span, m_ref, q_ref, kv_ref, begin_ref, sum_ref, tot_ref):
    m = m_ref[0]
    for z in range(4):
        rows = slice(z * BLOCK, (z + 1) * BLOCK)
        keys = (z + 1) * BLOCK
        for h in range(2):
            lanes = slice(h * 64, h * 64 + 64)
            acc = jnp.zeros((BLOCK, 64), f32)
            tot = jnp.zeros((BLOCK, 1), f32)
            q = q_ref[rows, lanes]

            def step(mm, carry):
                acc, tot = carry
                e = block_weights(q, kv_ref[mm, :keys, :64], begin_ref[rows, :], z, m, mm, span)
                acc = acc + dot(e.astype(bf16), kv_ref[mm, :keys, 64:])
                return acc, tot + jnp.sum(e, axis=1, keepdims=True)

            acc, tot = lax.fori_loop(0, kv_ref.shape[0], step, (acc, tot))
            sum_ref[rows, lanes] = acc
            tot_ref[rows, lanes] = jnp.broadcast_to(tot, (BLOCK, 64))


VM = pltpu.VMEM


def vspecs(n):
    return [pl.BlockSpec(memory_space=VM)] * n


def attend(m, q, kv, begin, span):
    n = q.shape[0]
    return pl.pallas_call(
        functools.partial(attend_kernel, span),
        out_shape=(jax.ShapeDtypeStruct((n, 128), f32), jax.ShapeDtypeStruct((n, 128), f32)),
        in_specs=[pl.BlockSpec(memory_space=pltpu.SMEM)] + vspecs(3),
        out_specs=tuple(vspecs(2)),
        cost_estimate=pl.CostEstimate(flops=2**31, bytes_accessed=2**22, transcendentals=2**22),
        compiler_params=pltpu.CompilerParams(vmem_limit_bytes=40 * 2**20),
        name="attend",
    )(m, q, kv, begin)


def attend_back_kernel(span, m_ref, q_ref, kv_ref, begin_ref, g_ref, delta_ref, dq_ref, dkv_ref, acc_ref):
    m = m_ref[0]
    dq_ref[...] = jnp.zeros_like(dq_ref)

    def step(mm, _):
        acc_ref[...] = jnp.zeros_like(acc_ref)
        for z in range(4):
            rows = slice(z * BLOCK, (z + 1) * BLOCK)
            keys = (z + 1) * BLOCK
            for h in range(2):
                lanes = slice(h * 64, h * 64 + 64)
                q = q_ref[rows, lanes]
                g = g_ref[rows, lanes]
                k = kv_ref[mm, :keys, :64]
                v = kv_ref[mm, :keys, 64:]
                e = block_weights(q, k, begin_ref[rows, :], z, m, mm, span)
                dp = back_product(g, v)
                ds = (e * (dp - delta_ref[rows, h * 64 : h * 64 + 1])).astype(bf16)
                dq_ref[rows, lanes] += dot(ds, k)
                acc_ref[:keys, :64] += lead_sum(ds, q)
                acc_ref[:keys, 64:] += lead_sum(e.astype(bf16), g)
        dkv_ref[mm] = acc_ref[...].astype(dkv_ref.dtype)
        return 0

    lax.fori_loop(0, kv_ref.shape[0], step, 0)


def attend_back(m, q, kv, begin, g, delta, span):
    n = q.shape[0]
    return pl.pallas_call(
        functools.partial(attend_back_kernel, span),
        out_shape=(jax.ShapeDtypeStruct((n, 128), f32), jax.ShapeDtypeStruct(kv.shape, bf16)),
        in_specs=[pl.BlockSpec(memory_space=pltpu.SMEM)] + vspecs(5),
        out_specs=tuple(vspecs(2)),
        scratch_shapes=[pltpu.VMEM((n, 128), f32)],
        cost_estimate=pl.CostEstimate(flops=2**33, bytes_accessed=2**23, transcendentals=2**22),
        compiler_params=pltpu.CompilerParams(vmem_limit_bytes=48 * 2**20),
        name="attend_back",
    )(m, q, kv, begin, g, delta)


def ffn_kernel(
    att_ref, x_hbm, c_hbm, own_c_ref, wo_hbm, wg_hbm, wu_hbm, wd_hbm, gain_ref,
    att_all, branch_ref, gmid_ref, mid_ref, dpart_ref, gpart_ref, glu_rx, down_rx,
    x_v, c_v, wo_v, wg_v, wu_v, wd_v, normed, hid, gg, gu, mid_b, p_out, p_sib, p_sum, p_rx,
    glu_tx, down_tx, br_own,
    ld, s_att, r_att, s_sib, r_sib, s_rs, r_rs, s_br, r_br, s_x, r_x, l_x,
):
    z, m, core, f = who()
    M = lax.axis_size("ctx") // 8
    T = 2 * M
    seg = glu_tx.shape[2]
    each = WIDTH // lax.axis_size("ctx")
    half_width = WIDTH // 2
    sib = dev(z, m, 1 - core, f)
    zs = [(z + s) % 4 for s in (1, 2, 3)]
    zpeers = [dev(zz, m, core, f) for zz in zs]
    group = m * 2 + f
    others = [(group + s) % T for s in range(1, T)]
    tpeers = [dev(z, o // 2, core, o % 2) for o in others]

    loads = []
    for k, (a, b) in enumerate(
        ((wo_hbm, wo_v), (x_hbm, x_v), (wg_hbm, wg_v), (wu_hbm, wu_v), (c_hbm, c_v), (wd_hbm, wd_v))
    ):
        cp = pltpu.make_async_copy(a, b, ld.at[k])
        cp.start()
        loads.append(cp)
    enter([sib] + zpeers + tpeers)

    def lanes(j):
        return pl.ds(pl.multiple_of(j * 128, 128), 128)

    me = slot(z, core)

    def send_att(s, i):
        b = (zs[s] + 1 + i) % 4
        return rcopy(
            att_ref.at[b], att_all.at[b, :, lanes(me)], s_att.at[s, i], r_att.at[s, i], zpeers[s]
        )

    def got_att(s, i):
        b = (z + 1 + i) % 4
        j = slot((z + 3 - s) % 4, core)
        return rcopy(
            att_ref.at[b], att_all.at[b, :, lanes(j)], s_att.at[s, i], r_att.at[s, i], zpeers[s]
        )

    def sib_att(k, i):
        b = (z + 1 + i) % 4
        j = me if k == 3 else slot((z + 3 - k) % 4, core)
        src = att_ref.at[b] if k == 3 else att_all.at[b, :, lanes(j)]
        return rcopy(src, att_all.at[b, :, lanes(j)], s_sib.at[k, i], r_sib.at[k, i], sib)

    def from_sib(k, i):
        b = (z + 1 + i) % 4
        j = slot(z, 1 - core) if k == 3 else slot((z + 3 - k) % 4, 1 - core)
        return rcopy(att_ref.at[b], att_all.at[b, :, lanes(j)], s_sib.at[k, i], r_sib.at[k, i], sib)

    for i in range(4):
        for s in (1, 0, 2):
            send_att(s, i).start()
        sib_att(3, i).start()
    for b in range(4):
        att_all[b, :, lanes(me)] = att_ref[b]

    def forward(i):
        for s in range(3):
            got_att(s, i).wait_recv()
            sib_att(s, i).start()

    def p_copy(i):
        return rcopy(p_out.at[i, 1 - core], p_sib.at[i], s_rs.at[i], r_rs.at[i], sib)

    def rs_copy(i):
        return rcopy(p_sum.at[i], p_rx.at[i], s_rs.at[4 + i], r_rs.at[4 + i], zpeers[i])

    def reduce_block(i):
        p_copy(i).wait_recv()
        p_sum[i] = (p_out[i, core].astype(f32) + p_sib[i].astype(f32)).astype(bf16)
        rs_copy(i).start()

    forward(0)
    gain = gain_ref[...]
    for cp in loads:
        cp.wait()
    for i in range(4):
        b = (z + 1 + i) % 4
        for k in range(4):
            from_sib(k, i).wait_recv()
        mid = x_v[b].astype(f32) + dot(att_all[b], wo_v[...])
        nb = (
            mid * lax.rsqrt(jnp.mean(mid * mid, axis=-1, keepdims=True) + epsilon) * gain
        ).astype(bf16)
        normed[b] = nb
        if i == 3:
            mid_b[0] = mid[:ROWS]
            mid_b[1] = mid[ROWS:]
        if i < 3:
            forward(i + 1)
        gate = dot(nb, wg_v[...])
        up = dot(nb, wu_v[...])
        sig = 1.0 / (1.0 + jnp.exp(-gate))
        silu = gate * sig
        hb = (silu * up).astype(bf16)
        hid[b] = hb
        gh = back_product(c_v[b], wd_v[...])
        ggb = (gh * up * (sig * (1.0 + gate * (1.0 - sig)))).astype(bf16)
        gub = (gh * silu).astype(bf16)
        gg[b] = ggb
        gu[b] = gub
        pb = (back_product(ggb, wg_v[...]) + back_product(gub, wu_v[...])).astype(bf16)
        p_out[i, 0] = pb[:ROWS]
        p_out[i, 1] = pb[ROWS:]
        p_copy(i).start()
        if i > 0:
            reduce_block(i - 1)
        db = dot(hb, wd_v[...]).astype(bf16)
        dpart_ref[b, 0] = db[:ROWS]
        dpart_ref[b, 1] = db[ROWS:]

    def x_copy(which, s):
        tx, rx = (glu_tx, glu_rx) if which < 2 else (down_tx, down_rx)
        if which < 2:
            src, dst = tx.at[others[s], which], rx.at[group, which]
        else:
            src, dst = tx.at[others[s]], rx.at[group]
        return rcopy(src, dst, s_x.at[which, s], r_x.at[which, s], tpeers[s])

    def x_own(which):
        if which < 2:
            return pltpu.make_async_copy(
                glu_tx.at[group, which], glu_rx.at[group, which], l_x.at[which]
            )
        return pltpu.make_async_copy(down_tx.at[group], down_rx.at[group], l_x.at[which])

    def flat(ref):
        return ref[...].reshape(8 * ROWS, ref.shape[-1])

    def glu_grads(which):
        prod = lead_sum(flat((gg, gu)[which]), flat(normed)).astype(bf16)
        for mm in range(M):
            for ff in range(2):
                glu_tx[mm * 2 + ff, which] = prod[
                    mm * seg : (mm + 1) * seg, ff * half_width : (ff + 1) * half_width
                ]
        for s in range(T - 1):
            x_copy(which, s).start()
        x_own(which).start()

    def down_grads():
        prod = lead_sum(flat(hid), flat(c_v))
        for mm in range(M):
            for ff in range(2):
                down_tx[mm * 2 + ff] = jnp.concatenate(
                    [
                        prod[:, blk * each : (blk + 1) * each]
                        for zl in range(2)
                        for cc in range(2)
                        for blk in [(2 * ff + zl) * 2 * M + mm * 2 + cc]
                    ],
                    axis=1,
                ).astype(bf16)
        for s in range(T - 1):
            x_copy(2, s).start()
        x_own(2).start()

    glu_grads(0)

    p_copy(3).wait_recv()
    dy = p_out[3, core].astype(f32) + p_sib[3].astype(f32)
    for i in range(3):
        rs_copy(i).wait_recv()
        dy = dy + p_rx[i].astype(f32)
    mid = mid_b[core]
    r = lax.rsqrt(jnp.mean(mid * mid, axis=-1, keepdims=True) + epsilon)
    gdy = gain * dy
    dv = r * gdy - mid * (r * r * r) * jnp.mean(mid * gdy, axis=-1, keepdims=True)
    gmid = own_c_ref[...].astype(f32) + dv
    gmid_ref[...] = gmid
    mid_ref[...] = mid
    gpart_ref[...] = jnp.sum(dy * mid * r, axis=0, keepdims=True)
    br_own[...] = gmid.astype(bf16)
    branch_ref[me] = br_own[...]

    def br_copy(k):
        if k < 3:
            return rcopy(br_own, branch_ref.at[me], s_br.at[k], r_br.at[k], zpeers[k])
        j = me if k == 3 else slot((z + 3 - (k - 4)) % 4, core)
        return rcopy(
            br_own if k == 3 else branch_ref.at[j], branch_ref.at[j], s_br.at[k], r_br.at[k], sib
        )

    for k in (1, 0, 2, 3):
        br_copy(k).start()
    glu_grads(1)
    down_grads()
    for k in range(3):
        br_copy(k).wait_recv()
        br_copy(k + 4).start()
    for k in range(3, 7):
        br_copy(k).wait_recv()
    for which in range(3):
        x_own(which).wait()
        for s in range(T - 1):
            x_copy(which, s).wait_recv()
    for i in range(4):
        for s in range(3):
            send_att(s, i).wait_send()
        for k in range(4):
            sib_att(k, i).wait_send()
        p_copy(i).wait_send()
    for i in range(3):
        rs_copy(i).wait_send()
    for k in range(7):
        br_copy(k).wait_send()
    for which in range(3):
        for s in range(T - 1):
            x_copy(which, s).wait_send()


def feed_forward(att, x_all, c_all, own_c, w_out, w_gate, w_up, w_down, gain, cid):
    n = lax.axis_size("ctx")
    T, seg, each = n // 4, FF // n, WIDTH // n
    cols = FF // 8
    half_width = WIDTH // 2
    VS, sem = pltpu.VMEM, pltpu.SemaphoreType.DMA
    shape = jax.ShapeDtypeStruct
    return pl.pallas_call(
        ffn_kernel,
        out_shape=(
            shape((4, BLOCK, WIDTH), bf16),
            shape((8, ROWS, WIDTH), bf16),
            shape((ROWS, WIDTH), f32),
            shape((ROWS, WIDTH), f32),
            shape((4, 2, ROWS, WIDTH), bf16),
            shape((1, WIDTH), f32),
            shape((T, 2, seg, half_width), bf16),
            shape((T, cols, 4 * each), bf16),
        ),
        in_specs=vspecs(1) + any_specs(2) + vspecs(1) + any_specs(4) + vspecs(1),
        out_specs=tuple(vspecs(8)),
        scratch_shapes=[
            VS((4, BLOCK, WIDTH), bf16),
            VS((4, BLOCK, WIDTH), bf16),
            VS((WIDTH, WIDTH), bf16),
            VS((WIDTH, cols), bf16),
            VS((WIDTH, cols), bf16),
            VS((cols, WIDTH), bf16),
            VS((4, BLOCK, WIDTH), bf16),
            VS((4, BLOCK, cols), bf16),
            VS((4, BLOCK, cols), bf16),
            VS((4, BLOCK, cols), bf16),
            VS((2, ROWS, WIDTH), f32),
            VS((4, 2, ROWS, WIDTH), bf16),
            VS((4, ROWS, WIDTH), bf16),
            VS((3, ROWS, WIDTH), bf16),
            VS((3, ROWS, WIDTH), bf16),
            VS((T, 2, seg, half_width), bf16),
            VS((T, cols, 4 * each), bf16),
            VS((ROWS, WIDTH), bf16),
            sem((6,)),
            sem((3, 4)),
            sem((3, 4)),
            sem((4, 4)),
            sem((4, 4)),
            sem((7,)),
            sem((7,)),
            sem((7,)),
            sem((7,)),
            sem((3, T - 1)),
            sem((3, T - 1)),
            sem((3,)),
        ],
        compiler_params=pltpu.CompilerParams(
            collective_id=cid, has_side_effects=True, vmem_limit_bytes=60 * 2**20
        ),
        name="feed_forward",
    )(att, x_all, c_all, own_c, w_out, w_gate, w_up, w_down, gain)


def root_mean_norm(rows, gain):
    return (
        rows * lax.rsqrt(jnp.mean(rows * rows, axis=-1, keepdims=True) + epsilon) * gain
    )


def rotary(rows, cosine, sine):
    halfway = rows.shape[-1] // 2
    leading = rows[..., :halfway]
    trailing = rows[..., halfway:]
    return jnp.concatenate(
        [leading * cosine - trailing * sine, leading * sine + trailing * cosine], axis=-1
    )


SWAP = [(0, 1), (1, 0)]


def halves(f, own, other, axis):
    return jnp.where(
        f == 0,
        jnp.concatenate([own, other], axis=axis),
        jnp.concatenate([other, own], axis=axis),
    )


def local(
    hidden_in,
    doc_lengths,
    attn_gain,
    query_gain,
    key_norm_gain,
    ffn_gain,
    query_proj,
    key_weight,
    value_weight,
    attn_proj,
    gate_proj,
    up_proj,
    down_proj,
    out_cotangent,
):
    n_ctx = lax.axis_size("ctx")
    M = n_ctx // 8
    T = 2 * M
    z, m, core, f = who()
    head = slot(z, core)
    tokens = 8 * ROWS
    span = n_ctx // 4 * ROWS
    segment = FF // n_ctx
    columns = M * segment
    half_width = WIDTH // 2
    each = WIDTH // n_ctx

    heads_own = jnp.concatenate(
        [
            lax.dynamic_slice(query_proj, (0, head * 128), (half_width, 128)),
            lax.dynamic_slice(key_weight, (0, head * 64), (half_width, 64)),
            lax.dynamic_slice(value_weight, (0, head * 64), (half_width, 64)),
        ],
        axis=1,
    ).astype(bf16)
    first = z * (n_ctx // 4) + core
    gate_own, up_own = [
        jnp.concatenate(
            [
                lax.dynamic_slice(w, (0, (first + 2 * mm) * segment), (half_width, segment))
                for mm in range(M)
            ],
            axis=1,
        ).astype(bf16)
        for w in (gate_proj, up_proj)
    ]
    down_own = jnp.concatenate(
        [
            lax.dynamic_slice(
                down_proj, ((first + 2 * mm) * segment - f * (FF // 2), 0), (segment, WIDTH)
            )
            for mm in range(M)
        ],
        axis=0,
    ).astype(bf16)
    out_own = attn_proj.astype(bf16)

    def swap(v):
        return lax.ppermute(v, "fsdp", SWAP)

    w_heads = halves(f, heads_own, swap(heads_own), 0)
    x_rows = gather8(hidden_in[0], 1)
    gate_own, up_own, down_own, out_own, cotangent, x_rows = lax.optimization_barrier(
        (gate_own, up_own, down_own, out_own, out_cotangent[0], x_rows)
    )
    w_out = halves(f, out_own, swap(out_own), 0)
    w_gate = halves(f, gate_own, swap(gate_own), 0)
    w_up = halves(f, up_own, swap(up_own), 0)
    x_all = x_rows.reshape(tokens, WIDTH).astype(f32)
    w_down = jnp.where(f == z // 2, down_own, swap(down_own))

    starts = jnp.cumsum(doc_lengths[0]) - doc_lengths[0]
    token_index = (
        jnp.arange(4, dtype=jnp.int32)[:, None] * span
        + m * BLOCK
        + jnp.arange(BLOCK, dtype=jnp.int32)[None, :]
    ).reshape(tokens, 1)
    after = token_index >= starts[None, :]
    begins = jnp.max(jnp.where(after, starts[None, :], 0), axis=1, keepdims=True)
    place = token_index - begins
    freqs = rope_base ** (-2.0 * jnp.arange(32, dtype=f32) / 64)
    angles = place.astype(f32) * freqs[None, :]
    cosine = jnp.cos(angles)[:, None, :]
    sine = jnp.sin(angles)[:, None, :]

    normed = root_mean_norm(x_all, attn_gain).astype(bf16)
    stacked = dot(normed, w_heads)

    def rotate(q_in, k_in, q_gain, k_gain):
        q_out = (
            rotary(root_mean_norm(q_in.reshape(tokens, 2, HEAD_SIZE), q_gain), cosine, sine)
            * HEAD_SIZE ** (-0.5)
        )
        k_out = rotary(root_mean_norm(k_in.reshape(tokens, 1, HEAD_SIZE), k_gain), cosine, sine)
        return q_out.reshape(tokens, 128), k_out.reshape(tokens, 64)

    (q_rot, k_rot), heads_back = jax.vjp(
        rotate, stacked[:, :128], stacked[:, 128:192], query_gain, key_norm_gain
    )
    q_rows = q_rot.astype(bf16)
    kv_rows = jnp.concatenate([k_rot, stacked[:, 192:]], axis=1).astype(bf16)
    kv_all = across(kv_rows, False, True, 2)
    m_arr = jnp.full((1,), m, jnp.int32)
    summed, totals = attend(m_arr, q_rows, kv_all, begins, span)
    att_own = (summed / totals).astype(bf16).reshape(4, BLOCK, 128)
    c_rows = gather8(cotangent, 15)
    attended, branch, grad_middle, own, down_parts, ffn_gain_part, glu_got, down_got = feed_forward(
        att_own,
        x_rows.reshape(4, BLOCK, WIDTH),
        c_rows.reshape(4, BLOCK, WIDTH),
        cotangent,
        w_out,
        w_gate,
        w_up,
        w_down,
        ffn_gain[None],
        4,
    )
    attended = attended.reshape(tokens, WIDTH)
    branch = branch.reshape(tokens, WIDTH)
    ffn_gain_part = ffn_gain_part[0]
    output = own + scatter8(down_parts.reshape(8, ROWS, WIDTH), 5)

    w_out_head = lax.dynamic_slice(w_out, (head * 128, 0), (128, WIDTH))
    grad_mixed = back_product(branch, w_out_head)
    grad_summed = (grad_mixed / totals).astype(bf16)
    weighted = (grad_mixed * summed / (totals * totals)).reshape(tokens, 2, 64)
    delta = jnp.broadcast_to(
        jnp.sum(weighted, axis=2, keepdims=True), (tokens, 2, 64)
    ).reshape(tokens, 128)
    grad_q, dkv = attend_back(m_arr, q_rows, kv_all, begins, grad_summed, delta, span)
    dkv = jnp.sum(across(dkv, False, False, 6).astype(f32), axis=0)
    gq_pre, gk_pre, q_gain_part, k_gain_part = heads_back((grad_q, dkv[:, :64]))
    grad_stacked = jnp.concatenate([gq_pre, gk_pre, dkv[:, 64:]], axis=1).astype(bf16)
    part_normed = back_product(grad_stacked, w_heads).reshape(8, ROWS, WIDTH).astype(bf16)
    grad_normed = scatter8(part_normed, 7)
    _, attn_back = jax.vjp(root_mean_norm, hidden_in[0].astype(f32), attn_gain)
    grad_resid, attn_gain_part = attn_back(grad_normed)
    input_grad = grad_middle + grad_resid

    glu_grad = jnp.sum(glu_got.astype(f32), axis=0)
    down_sum = jnp.sum(down_got.astype(f32), axis=0)
    gate_grad = jnp.transpose(glu_grad[0])
    up_grad = jnp.transpose(glu_grad[1])

    devices = [
        (zz, mm, cc, ff) for zz in range(4) for mm in range(M) for cc in range(2) for ff in range(2)
    ]

    def number(zz, mm, cc, ff):
        return (zz * (n_ctx // 4) + mm * 2 + cc) * 2 + ff

    down_pieces = down_sum.reshape(columns, 2, 2, each)
    rounds = []
    for dz in range(2):
        for dc in range(2):
            piece = lax.dynamic_slice(
                down_pieces, (0, (z + dz) % 2, (core + dc) % 2, 0), (columns, 1, 1, each)
            ).reshape(columns, each)
            perm = [
                (number(zz, mm, cc, ff), number(2 * ff + (zz + dz) % 2, mm, (cc + dc) % 2, zz // 2))
                for zz, mm, cc, ff in devices
            ]
            rounds.append(lax.ppermute(piece, ("ctx", "fsdp"), perm))
    rounds = jnp.stack(rounds).reshape(2, 2, columns, each)
    rounds = jnp.where(z % 2 == 0, rounds, rounds[::-1])
    rounds = jnp.where(core == 0, rounds, rounds[:, ::-1])
    down_grad = jnp.transpose(
        rounds.reshape(2, 2, M, segment, each), (0, 2, 1, 3, 4)
    ).reshape(FF // 2, each)

    branch_columns = lax.dynamic_slice(
        branch.reshape(tokens, 4, M, 2, each), (0, z, 0, core, 0), (tokens, 1, M, 1, each)
    ).reshape(tokens, M * each)
    attn_part = lead_sum(attended, branch_columns).astype(bf16)
    attn_part = jnp.transpose(
        attn_part.reshape(2, half_width, M, each), (2, 0, 1, 3)
    ).reshape(T, half_width, each)
    attn_grad = jnp.sum(across(attn_part, True, False, 11).astype(f32), axis=0)

    heads_part = lead_sum(normed, grad_stacked).astype(bf16)
    qw, kw = 128 // M, 64 // M
    heads_part = jnp.concatenate(
        [
            heads_part[:, :128].reshape(2, half_width, M, qw),
            heads_part[:, 128:192].reshape(2, half_width, M, kw),
            heads_part[:, 192:].reshape(2, half_width, M, kw),
        ],
        axis=3,
    )
    heads_part = jnp.transpose(heads_part, (2, 0, 1, 3)).reshape(T, half_width, 256 // M)
    heads_grad = jnp.sum(across(heads_part, True, False, 12).astype(f32), axis=0)
    perm = [
        (number(zz, mm, cc, ff), number(zz, (cc * M + mm) // 2, (cc * M + mm) % 2, ff))
        for zz, mm, cc, ff in devices
    ]
    heads_grad = lax.ppermute(heads_grad, ("ctx", "fsdp"), perm)
    query_grad = heads_grad[:, :qw]
    key_grad = heads_grad[:, qw : qw + kw]
    value_grad = heads_grad[:, qw + kw :]

    gains = jnp.concatenate([attn_gain_part, ffn_gain_part, q_gain_part, k_gain_part])
    gains = jnp.sum(gather8(gains.reshape(17, 128), 13), axis=0)
    gains = jnp.sum(across(gains, True, True, 14), axis=0).reshape(-1)
    return (
        output[None],
        input_grad[None],
        gains[:WIDTH],
        gains[2 * WIDTH : 2 * WIDTH + 64],
        gains[2 * WIDTH + 64 :],
        gains[WIDTH : 2 * WIDTH],
        query_grad,
        key_grad,
        value_grad,
        attn_grad,
        gate_grad,
        up_grad,
        down_grad,
    )


def solution(mesh):
    in_specs = (
        P("fsdp", "ctx", None),
        P("fsdp", None),
        P(),
        P(),
        P(),
        P(),
        P("fsdp", None),
        P("fsdp", None),
        P("fsdp", None),
        P("fsdp", None),
        P("fsdp", None),
        P("fsdp", None),
        P("fsdp", None),
        P("fsdp", "ctx", None),
    )
    out_specs = (
        P("fsdp", "ctx", None),
        P("fsdp", "ctx", None),
        P(),
        P(),
        P(),
        P(),
        P("fsdp", "ctx"),
        P("fsdp", "ctx"),
        P("fsdp", "ctx"),
        P("fsdp", "ctx"),
        P("fsdp", "ctx"),
        P("fsdp", "ctx"),
        P("fsdp", "ctx"),
    )
    return jax.shard_map(local, mesh=mesh, in_specs=in_specs, out_specs=out_specs, check_vma=False)
```

```python
import functools
import math

import jax
import jax.numpy as jnp
from jax import lax
from jax.experimental import pallas as pl
from jax.experimental.pallas import tpu as pltpu
from jax.sharding import PartitionSpec as P

QUERY_HEADS = 16
KEY_VALUE_HEADS = 8
HEAD_SIZE = 64
FF = 4608
WIDTH = 1024
ROWS = 128

epsilon = 1e-05
rope_base = 1000000.0
MESH = pl.DeviceIdType.MESH
ANY = pl.ANY
bf16 = jnp.bfloat16
f32 = jnp.float32


def who():
    n = lax.axis_size("ctx")
    c = lax.axis_index("ctx")
    f = lax.axis_index("fsdp")
    q = n // 4
    return c // q, (c % q) // 2, c % 2, f


def dev(z, m, core, f):
    return (z * (lax.axis_size("ctx") // 4) + m * 2 + core, f)


def slot(z, core):
    return z * 2 + core


def enter(peers):
    bar = pltpu.get_barrier_semaphore()
    for p in peers:
        pl.semaphore_signal(bar, inc=1, device_id=p, device_id_type=MESH)
    pl.semaphore_wait(bar, len(peers))


def rcopy(src, dst, s, r, to):
    return pltpu.make_async_remote_copy(
        src_ref=src, dst_ref=dst, send_sem=s, recv_sem=r, device_id=to, device_id_type=MESH
    )


def comm_params(cid):
    return pltpu.CompilerParams(collective_id=cid, has_side_effects=True)


def any_specs(n):
    return [pl.BlockSpec(memory_space=ANY)] * n


def gather8_kernel(x_ref, o_ref, ss, rs, ls):
    z, m, core, f = who()
    sib = dev(z, m, 1 - core, f)
    peers = [dev((z + s) % 4, m, core, f) for s in (1, 2, 3)]
    me = slot(z, core)
    own = pltpu.make_async_copy(x_ref, o_ref.at[me], ls)
    own.start()
    enter([sib] + peers)
    first = []
    for k in (1, 0, 2):
        cp = rcopy(x_ref, o_ref.at[me], ss.at[k], rs.at[k], peers[k])
        cp.start()
        first.append((k, cp))
    cp0 = rcopy(x_ref, o_ref.at[me], ss.at[3], rs.at[3], sib)
    cp0.start()
    fw = []
    for k, cp in first:
        sl = slot((z + 3 - k) % 4, core)
        cp.wait_recv()
        cp = rcopy(o_ref.at[sl], o_ref.at[sl], ss.at[4 + k], rs.at[4 + k], sib)
        cp.start()
        fw.append(cp)
    for cp in fw + [cp0]:
        cp.wait_recv()
    for cp in [cp for _, cp in first] + [cp0] + fw:
        cp.wait_send()
    own.wait()


def gather8(x, cid):
    return pl.pallas_call(
        gather8_kernel,
        out_shape=jax.ShapeDtypeStruct((8,) + x.shape, x.dtype),
        in_specs=any_specs(1),
        out_specs=any_specs(1)[0],
        scratch_shapes=[
            pltpu.SemaphoreType.DMA((7,)),
            pltpu.SemaphoreType.DMA((7,)),
            pltpu.SemaphoreType.DMA,
        ],
        compiler_params=comm_params(cid),
        name="gather8_%d" % cid,
    )(x)


def across_kernel(both, same, x_ref, o_ref, ss, rs, ls):
    z, m, core, f = who()
    M = lax.axis_size("ctx") // 8
    count = M * 2 if both else M
    me = m * 2 + f if both else m
    others = [(me + s) % count for s in range(1, count)]
    peers = [dev(z, o // 2, core, o % 2) if both else dev(z, o, core, f) for o in others]

    def src(k):
        return x_ref if same else x_ref.at[k]

    own = pltpu.make_async_copy(src(me), o_ref.at[me], ls)
    own.start()
    enter(peers)
    cps = []
    for s in range(count - 1):
        cp = rcopy(src(others[s]), o_ref.at[me], ss.at[s], rs.at[s], peers[s])
        cp.start()
        cps.append(cp)
    for cp in cps:
        cp.wait_recv()
    for cp in cps:
        cp.wait_send()
    own.wait()


def across(x, both, same, cid):
    shp = x.shape if same else x.shape[1:]
    count = lax.axis_size("ctx") // (4 if both else 8)
    return pl.pallas_call(
        functools.partial(across_kernel, both, same),
        out_shape=jax.ShapeDtypeStruct((count,) + shp, x.dtype),
        in_specs=any_specs(1),
        out_specs=any_specs(1)[0],
        scratch_shapes=[
            pltpu.SemaphoreType.DMA((count - 1,)),
            pltpu.SemaphoreType.DMA((count - 1,)),
            pltpu.SemaphoreType.DMA,
        ],
        compiler_params=comm_params(cid),
        name="across_%d" % cid,
    )(x)


def scatter8_kernel(x_ref, o_ref, a, b, s_buf, d, ls, s1, r1, s2, r2):
    z, m, core, f = who()
    sib = dev(z, m, 1 - core, f)
    to = [(z + s) % 4 for s in (1, 2, 3, 0)]
    peers = [dev(zz, m, core, f) for zz in to[:3]]
    loads = []
    for k in range(4):
        cp = pltpu.make_async_copy(x_ref.at[slot(to[k], core)], a.at[k], ls.at[k])
        cp.start()
        loads.append(cp)
    enter([sib] + peers)
    ones = []
    for k in range(4):
        cp = rcopy(x_ref.at[slot(to[k], 1 - core)], b.at[k], s1.at[k], r1.at[k], sib)
        cp.start()
        ones.append(cp)
    twos = []
    for k in range(3):
        loads[k].wait()
        ones[k].wait_recv()
        s_buf[k] = (a[k].astype(f32) + b[k].astype(f32)).astype(s_buf.dtype)
        cp = rcopy(s_buf.at[k], d.at[k], s2.at[k], r2.at[k], peers[k])
        cp.start()
        twos.append(cp)
    loads[3].wait()
    ones[3].wait_recv()
    total = a[3].astype(f32) + b[3].astype(f32)
    for k in range(3):
        twos[k].wait_recv()
        total = total + d[k].astype(f32)
    o_ref[...] = total
    for cp in ones + twos:
        cp.wait_send()


def scatter8(x, cid):
    shp = x.shape[1:]
    return pl.pallas_call(
        scatter8_kernel,
        out_shape=jax.ShapeDtypeStruct(shp, f32),
        in_specs=any_specs(1),
        out_specs=pl.BlockSpec(memory_space=pltpu.VMEM),
        scratch_shapes=[
            pltpu.VMEM((4,) + shp, x.dtype),
            pltpu.VMEM((4,) + shp, x.dtype),
            pltpu.VMEM((3,) + shp, x.dtype),
            pltpu.VMEM((3,) + shp, x.dtype),
            pltpu.SemaphoreType.DMA((4,)),
            pltpu.SemaphoreType.DMA((4,)),
            pltpu.SemaphoreType.DMA((4,)),
            pltpu.SemaphoreType.DMA((3,)),
            pltpu.SemaphoreType.DMA((3,)),
        ],
        compiler_params=comm_params(cid),
        name="scatter8_%d" % cid,
    )(x)


def back_product(left, right):
    return lax.dot_general(
        left, right, (((1,), (1,)), ((), ())), preferred_element_type=f32
    )


def lead_sum(left, right):
    return lax.dot_general(
        left, right, (((0,), (0,)), ((), ())), preferred_element_type=f32
    )


def dot(left, right):
    return jnp.dot(left, right, preferred_element_type=f32)


BLOCK = 2 * ROWS


def block_weights(q, k, begin, z, m, mm, span):
    keys = (z + 1) * BLOCK
    key = lax.broadcasted_iota(jnp.int32, (1, keys), 1)
    key = key // BLOCK * span + key % BLOCK + mm * BLOCK
    token = z * span + m * BLOCK + lax.broadcasted_iota(jnp.int32, (BLOCK, 1), 0)
    e = jnp.exp(back_product(q, k))
    return jnp.where((key >= begin) & (key <= token), e, 0.0)


def attend_kernel(span, m_ref, q_ref, kv_ref, begin_ref, sum_ref, tot_ref):
    m = m_ref[0]
    for z in range(4):
        rows = slice(z * BLOCK, (z + 1) * BLOCK)
        keys = (z + 1) * BLOCK
        for h in range(2):
            lanes = slice(h * 64, h * 64 + 64)
            acc = jnp.zeros((BLOCK, 64), f32)
            tot = jnp.zeros((BLOCK, 1), f32)
            q = q_ref[rows, lanes]

            def step(mm, carry):
                acc, tot = carry
                e = block_weights(q, kv_ref[mm, :keys, :64], begin_ref[rows, :], z, m, mm, span)
                acc = acc + dot(e.astype(bf16), kv_ref[mm, :keys, 64:])
                return acc, tot + jnp.sum(e, axis=1, keepdims=True)

            acc, tot = lax.fori_loop(0, kv_ref.shape[0], step, (acc, tot))
            sum_ref[rows, lanes] = acc
            tot_ref[rows, lanes] = jnp.broadcast_to(tot, (BLOCK, 64))


VM = pltpu.VMEM


def vspecs(n):
    return [pl.BlockSpec(memory_space=VM)] * n


def attend(m, q, kv, begin, span):
    n = q.shape[0]
    return pl.pallas_call(
        functools.partial(attend_kernel, span),
        out_shape=(jax.ShapeDtypeStruct((n, 128), f32), jax.ShapeDtypeStruct((n, 128), f32)),
        in_specs=[pl.BlockSpec(memory_space=pltpu.SMEM)] + vspecs(3),
        out_specs=tuple(vspecs(2)),
        cost_estimate=pl.CostEstimate(flops=2**31, bytes_accessed=2**22, transcendentals=2**22),
        compiler_params=pltpu.CompilerParams(vmem_limit_bytes=40 * 2**20),
        name="attend",
    )(m, q, kv, begin)


def attend_back_kernel(span, m_ref, q_ref, kv_ref, begin_ref, g_ref, delta_ref, dq_ref, dkv_ref, acc_ref):
    m = m_ref[0]
    dq_ref[...] = jnp.zeros_like(dq_ref)

    def step(mm, _):
        acc_ref[...] = jnp.zeros_like(acc_ref)
        for z in range(4):
            rows = slice(z * BLOCK, (z + 1) * BLOCK)
            keys = (z + 1) * BLOCK
            for h in range(2):
                lanes = slice(h * 64, h * 64 + 64)
                q = q_ref[rows, lanes]
                g = g_ref[rows, lanes]
                k = kv_ref[mm, :keys, :64]
                v = kv_ref[mm, :keys, 64:]
                e = block_weights(q, k, begin_ref[rows, :], z, m, mm, span)
                dp = back_product(g, v)
                ds = (e * (dp - delta_ref[rows, h * 64 : h * 64 + 1])).astype(bf16)
                dq_ref[rows, lanes] += dot(ds, k)
                acc_ref[:keys, :64] += lead_sum(ds, q)
                acc_ref[:keys, 64:] += lead_sum(e.astype(bf16), g)
        dkv_ref[mm] = acc_ref[...].astype(dkv_ref.dtype)
        return 0

    lax.fori_loop(0, kv_ref.shape[0], step, 0)


def attend_back(m, q, kv, begin, g, delta, span):
    n = q.shape[0]
    return pl.pallas_call(
        functools.partial(attend_back_kernel, span),
        out_shape=(jax.ShapeDtypeStruct((n, 128), f32), jax.ShapeDtypeStruct(kv.shape, bf16)),
        in_specs=[pl.BlockSpec(memory_space=pltpu.SMEM)] + vspecs(5),
        out_specs=tuple(vspecs(2)),
        scratch_shapes=[pltpu.VMEM((n, 128), f32)],
        cost_estimate=pl.CostEstimate(flops=2**33, bytes_accessed=2**23, transcendentals=2**22),
        compiler_params=pltpu.CompilerParams(vmem_limit_bytes=48 * 2**20),
        name="attend_back",
    )(m, q, kv, begin, g, delta)


def begin_of(token, doc_ref):
    begin = jnp.zeros(token.shape, jnp.int32)
    start = doc_ref[0, 0]
    for d in range(1, doc_ref.shape[1]):
        begin = jnp.where(token >= start, start, begin)
        start = start + doc_ref[0, d]
    return begin


def turn(v):
    lane = lax.broadcasted_iota(jnp.int32, v.shape, 1)
    n = v.shape[1]
    return jnp.where(lane % 64 < 32, pltpu.roll(v, n - 32, 1), pltpu.roll(v, 32, 1))


def head_scale(v):
    sq = v * v
    if v.shape[1] == 64:
        return lax.rsqrt(jnp.mean(sq, axis=1, keepdims=True) + epsilon)
    low = lax.broadcasted_iota(jnp.int32, v.shape, 1) < 64
    a = jnp.sum(jnp.where(low, sq, 0.0), axis=1, keepdims=True)
    b = jnp.sum(jnp.where(low, 0.0, sq), axis=1, keepdims=True)
    return lax.rsqrt(jnp.where(low, a, b) * (1.0 / 64) + epsilon)


def front_kernel(
    doc_ref, x_ref, c_hbm, wh_ref, wg_hbm, wu_hbm, wd_hbm, wo_hbm, again_ref, qgain_ref, kgain_ref,
    x_all, c_all, w_heads, w_gate, w_up, w_down, w_out, q_rows, kv_all, att, summed, totals,
    stacked, normed, cosine, sine,
    s_x, r_x, s_c, r_c, s_h, r_h, s_w, r_w, s_v, r_v, s_o, r_o, s_k, r_k, l_s,
):
    z, m, core, f = who()
    M = lax.axis_size("ctx") // 8
    span = lax.axis_size("ctx") // 4 * ROWS
    half_width = WIDTH // 2
    sib = dev(z, m, 1 - core, f)
    zpeers = [dev((z + s) % 4, m, core, f) for s in (1, 2, 3)]
    hm = m % 2
    pair = dev(z, m, core, 1 - f)
    beside = dev(z, m + 1 - 2 * hm, core, f)
    mpeers = [dev(z, (m + s) % M, core, f) for s in range(1, M)]
    me = slot(z, core)
    owner = f == z // 2

    stay = [
        pltpu.make_async_copy(c_hbm, c_all.at[me], l_s.at[0]),
        pltpu.make_async_copy(wg_hbm, w_gate.at[pl.ds(f * half_width, half_width)], l_s.at[1]),
        pltpu.make_async_copy(wu_hbm, w_up.at[pl.ds(f * half_width, half_width)], l_s.at[2]),
        pltpu.make_async_copy(wo_hbm, w_out.at[pl.ds(f * half_width, half_width)], l_s.at[3]),
    ]
    for cp in stay:
        cp.start()
    stay_down = pltpu.make_async_copy(wd_hbm, w_down, l_s.at[4])

    @pl.when(owner)
    def _():
        stay_down.start()

    enter([sib, pair] + zpeers + mpeers)

    def gather(src, dst, ss, rs, k):
        if k < 3:
            return rcopy(src, dst.at[me], ss.at[k], rs.at[k], zpeers[k])
        if k == 3:
            return rcopy(src, dst.at[me], ss.at[k], rs.at[k], sib)
        j = slot((z + 3 - (k - 4)) % 4, core)
        return rcopy(dst.at[j], dst.at[j], ss.at[k], rs.at[k], sib)

    def x_copy(k):
        return gather(x_ref, x_all, s_x, r_x, k)

    def c_copy(k):
        return gather(c_hbm, c_all, s_c, r_c, k)

    for k in (1, 0, 2, 3):
        x_copy(k).start()
    head_rows = pl.ds(f * half_width, half_width)
    heads_copy = rcopy(wh_ref, w_heads.at[head_rows], s_h.at[0], r_h.at[0], pair)
    heads_copy.start()

    quarter = half_width // 2
    eighth = half_width // 4
    cols = wd_hbm.shape[0]

    def w_copy(k, stage):
        src, dst = ((wg_hbm, w_gate), (wu_hbm, w_up), (wd_hbm, w_down), (wo_hbm, w_out))[k]
        base = 0 if k == 2 else (f if stage == 0 else 1 - f) * half_width
        size = (quarter, quarter, cols // 2, eighth)[k]
        part = hm * 2 + core if k == 3 else hm
        place = dst.at[pl.ds(pl.multiple_of(base + part * size, 8), size)]
        if stage == 0:
            here = src.at[pl.ds(pl.multiple_of(part * size, 8), size)]
            return rcopy(here, place, s_w.at[k], r_w.at[k], pair)
        return rcopy(place, place, s_v.at[k], r_v.at[k], beside)

    def out_copy(k):
        part = (hm if k == 0 else 1 - hm) * 2 + core
        base = (1 - f) * half_width
        place = w_out.at[pl.ds(pl.multiple_of(base + part * eighth, 8), eighth)]
        return rcopy(place, place, s_o.at[k], r_o.at[k], sib)

    for k in (0, 1, 3):
        w_copy(k, 0).start()

    @pl.when(owner)
    def _():
        w_copy(2, 0).start()

    w_heads[head_rows] = wh_ref[...]
    x_all[me] = x_ref[...]

    lane = lax.broadcasted_iota(jnp.int32, (1, 128), 1) % 32
    freq = jnp.exp(lane.astype(f32) * (-2.0 / 64 * math.log(rope_base)))
    sign = jnp.where(lax.broadcasted_iota(jnp.int32, (1, 128), 1) % 64 < 32, -1.0, 1.0)

    def tokens_of(zz):
        return zz * span + m * BLOCK + lax.broadcasted_iota(jnp.int32, (BLOCK, 1), 0)

    def table(zz, _):
        rows = pl.ds(pl.multiple_of(zz * BLOCK, BLOCK), BLOCK)
        token = tokens_of(zz)
        place = (token - begin_of(token, doc_ref)).astype(f32)
        angle = place * freq
        cosine[rows, :] = jnp.cos(angle)
        sine[rows, :] = jnp.sin(angle) * sign
        return 0

    lax.fori_loop(0, 4, table, 0)
    for k in range(3):
        x_copy(k).wait_recv()
        x_copy(k + 4).start()
    for k in (1, 0, 2, 3):
        c_copy(k).start()
    heads_copy.wait_recv()

    def kv_copy(b, s):
        rows = pl.ds(pl.multiple_of(b * BLOCK, BLOCK), BLOCK)
        place = kv_all.at[m, rows]
        return rcopy(place, place, s_k.at[b, s], r_k.at[b, s], mpeers[s])

    again = again_ref[...]
    qgain = qgain_ref[...]
    kgain = kgain_ref[...]

    for k in range(3, 7):
        x_copy(k).wait_recv()

    def project(b, _):
        rows = pl.ds(pl.multiple_of(b * BLOCK, BLOCK), BLOCK)
        x = jnp.concatenate([x_all[2 * b], x_all[2 * b + 1]], axis=0).astype(f32)
        nb = (
            x * lax.rsqrt(jnp.mean(x * x, axis=-1, keepdims=True) + epsilon) * again
        ).astype(bf16)
        normed[rows, :] = nb
        st = dot(nb, w_heads[...])
        stacked[rows, :] = st
        co = cosine[rows, :]
        si = sine[rows, :]
        q = st[:, :128]
        q = q * head_scale(q) * qgain
        q_rows[rows, :] = ((q * co + turn(q) * si) * HEAD_SIZE ** (-0.5)).astype(bf16)
        kv = st[:, 128:]
        low = lax.broadcasted_iota(jnp.int32, kv.shape, 1) < 64
        k = kv * head_scale(kv) * kgain
        kv_all[m, rows, :] = jnp.where(low, k * co + turn(k) * si, kv).astype(bf16)
        for s in range(M - 1):
            kv_copy(b, s).start()
        return 0

    lax.fori_loop(0, 4, project, 0)
    for k in range(2):
        w_copy(k, 0).wait_recv()
        w_copy(k, 1).start()

    summed[...] = jnp.zeros_like(summed)
    totals[...] = jnp.zeros_like(totals)

    def attend(s, _):
        mm = (m + M - s) % M

        @pl.when(s > 0)
        def _():
            for b in range(4):
                rows = pl.ds(b * BLOCK, BLOCK)
                place = kv_all.at[mm, rows]
                rcopy(place, place, s_k.at[b, s - 1], r_k.at[b, s - 1], sib).wait_recv()

        for zz in range(4):
            rows = slice(zz * BLOCK, (zz + 1) * BLOCK)
            keys = (zz + 1) * BLOCK
            begin = begin_of(tokens_of(zz), doc_ref)
            for h in range(2):
                lanes = slice(h * 64, h * 64 + 64)
                e = block_weights(
                    q_rows[rows, lanes], kv_all[mm, :keys, :64], begin, zz, m, mm, span
                )
                summed[rows, lanes] += dot(e.astype(bf16), kv_all[mm, :keys, 64:])
                totals[rows, lanes] += jnp.broadcast_to(
                    jnp.sum(e, axis=1, keepdims=True), (BLOCK, 64)
                )
        return 0

    lax.fori_loop(0, M, attend, 0)
    for b in range(4):
        rows = slice(b * BLOCK, (b + 1) * BLOCK)
        att[b] = (summed[rows, :] / totals[rows, :]).astype(bf16)

    w_copy(3, 0).wait_recv()
    w_copy(3, 1).start()
    out_copy(0).start()

    @pl.when(jnp.logical_not(owner))
    def _():
        w_copy(2, 0).wait_recv()
        w_copy(2, 1).start()

    for k in range(3):
        c_copy(k).wait_recv()
        c_copy(k + 4).start()

    def w_got(k):
        dst = (w_gate, w_up, w_down, w_out)[k]
        base = 0 if k == 2 else (1 - f) * half_width
        size = (quarter, quarter, cols // 2, eighth)[k]
        part = (1 - hm) * 2 + core if k == 3 else 1 - hm
        place = dst.at[pl.ds(pl.multiple_of(base + part * size, 8), size)]
        return rcopy(place, place, s_v.at[k], r_v.at[k], beside)

    w_got(3).wait_recv()
    out_copy(1).start()
    for k in range(2):
        w_got(k).wait_recv()

    @pl.when(jnp.logical_not(owner))
    def _():
        w_got(2).wait_recv()
        w_copy(2, 1).wait_send()

    @pl.when(owner)
    def _():
        stay_down.wait()
        w_copy(2, 0).wait_send()

    for k in range(3, 7):
        c_copy(k).wait_recv()
    for k in range(2):
        out_copy(k).wait_recv()
    for cp in stay:
        cp.wait()
    heads_copy.wait_send()
    for k in range(7):
        x_copy(k).wait_send()
        c_copy(k).wait_send()
    for k in (0, 1, 3):
        w_copy(k, 0).wait_send()
        w_copy(k, 1).wait_send()
    for k in range(2):
        out_copy(k).wait_send()
    for b in range(4):
        for s in range(M - 1):
            kv_copy(b, s).wait_send()


def front(docs, x, c, wh, wg, wu, wd, wo, again, qgain, kgain, cid):
    n = lax.axis_size("ctx")
    M = n // 8
    cols = FF // 8
    tokens = 8 * ROWS
    sem = pltpu.SemaphoreType.DMA
    shape = jax.ShapeDtypeStruct
    return pl.pallas_call(
        front_kernel,
        out_shape=(
            shape((8, ROWS, WIDTH), bf16),
            shape((8, ROWS, WIDTH), bf16),
            shape((WIDTH, 256), bf16),
            shape((WIDTH, cols), bf16),
            shape((WIDTH, cols), bf16),
            shape((cols, WIDTH), bf16),
            shape((WIDTH, WIDTH), bf16),
            shape((tokens, 128), bf16),
            shape((M, tokens, 128), bf16),
            shape((4, BLOCK, 128), bf16),
            shape((tokens, 128), f32),
            shape((tokens, 128), f32),
            shape((tokens, 256), f32),
            shape((tokens, WIDTH), bf16),
            shape((tokens, 128), f32),
            shape((tokens, 128), f32),
        ),
        in_specs=[pl.BlockSpec(memory_space=pltpu.SMEM)]
        + vspecs(1) + any_specs(1) + vspecs(1) + any_specs(4) + vspecs(3),
        out_specs=tuple(vspecs(1) + any_specs(1) + vspecs(1) + any_specs(4) + vspecs(9)),
        scratch_shapes=[
            sem((7,)), sem((7,)), sem((7,)), sem((7,)), sem((1,)), sem((1,)),
            sem((4,)), sem((4,)), sem((4,)), sem((4,)), sem((2,)), sem((2,)),
            sem((4, M - 1)), sem((4, M - 1)), sem((5,)),
        ],
        compiler_params=pltpu.CompilerParams(
            collective_id=cid, has_side_effects=True, vmem_limit_bytes=60 * 2**20
        ),
        name="front",
    )(docs, x, c, wh, wg, wu, wd, wo, again, qgain, kgain)


def ffn_kernel(
    att_ref, x_hbm, c_hbm, own_c_ref, wo_hbm, wg_hbm, wu_hbm, wd_hbm, gain_ref,
    att_all, branch_ref, gmid_ref, mid_ref, dpart_ref, gpart_ref, glu_rx, down_rx,
    x_v, c_v, wo_v, wg_v, wu_v, wd_v, normed, hid, gg, gu, mid_b, p_out, p_sib, p_sum, p_rx,
    glu_tx, down_tx, br_own,
    ld, s_att, r_att, s_sib, r_sib, s_rs, r_rs, s_br, r_br, s_x, r_x, l_x,
):
    z, m, core, f = who()
    M = lax.axis_size("ctx") // 8
    T = 2 * M
    seg = glu_tx.shape[2]
    each = WIDTH // lax.axis_size("ctx")
    half_width = WIDTH // 2
    sib = dev(z, m, 1 - core, f)
    zs = [(z + s) % 4 for s in (1, 2, 3)]
    zpeers = [dev(zz, m, core, f) for zz in zs]
    group = m * 2 + f
    others = [(group + s) % T for s in range(1, T)]
    tpeers = [dev(z, o // 2, core, o % 2) for o in others]

    loads = []
    for k, (a, b) in enumerate(
        ((wo_hbm, wo_v), (x_hbm, x_v), (wg_hbm, wg_v), (wu_hbm, wu_v), (c_hbm, c_v), (wd_hbm, wd_v))
    ):
        cp = pltpu.make_async_copy(a, b, ld.at[k])
        cp.start()
        loads.append(cp)
    enter([sib] + zpeers + tpeers)

    def lanes(j):
        return pl.ds(pl.multiple_of(j * 128, 128), 128)

    me = slot(z, core)

    def send_att(s, i):
        b = (zs[s] + 1 + i) % 4
        return rcopy(
            att_ref.at[b], att_all.at[b, :, lanes(me)], s_att.at[s, i], r_att.at[s, i], zpeers[s]
        )

    def got_att(s, i):
        b = (z + 1 + i) % 4
        j = slot((z + 3 - s) % 4, core)
        return rcopy(
            att_ref.at[b], att_all.at[b, :, lanes(j)], s_att.at[s, i], r_att.at[s, i], zpeers[s]
        )

    def sib_att(k, i):
        b = (z + 1 + i) % 4
        j = me if k == 3 else slot((z + 3 - k) % 4, core)
        src = att_ref.at[b] if k == 3 else att_all.at[b, :, lanes(j)]
        return rcopy(src, att_all.at[b, :, lanes(j)], s_sib.at[k, i], r_sib.at[k, i], sib)

    def from_sib(k, i):
        b = (z + 1 + i) % 4
        j = slot(z, 1 - core) if k == 3 else slot((z + 3 - k) % 4, 1 - core)
        return rcopy(att_ref.at[b], att_all.at[b, :, lanes(j)], s_sib.at[k, i], r_sib.at[k, i], sib)

    for i in range(4):
        for s in (1, 0, 2):
            send_att(s, i).start()
        sib_att(3, i).start()
    for b in range(4):
        att_all[b, :, lanes(me)] = att_ref[b]

    def forward(i):
        for s in range(3):
            got_att(s, i).wait_recv()
            sib_att(s, i).start()

    def p_copy(i):
        return rcopy(p_out.at[i, 1 - core], p_sib.at[i], s_rs.at[i], r_rs.at[i], sib)

    def rs_copy(i):
        return rcopy(p_sum.at[i], p_rx.at[i], s_rs.at[4 + i], r_rs.at[4 + i], zpeers[i])

    def reduce_block(i):
        p_copy(i).wait_recv()
        p_sum[i] = (p_out[i, core].astype(f32) + p_sib[i].astype(f32)).astype(bf16)
        rs_copy(i).start()

    forward(0)
    gain = gain_ref[...]
    for cp in loads:
        cp.wait()
    for i in range(4):
        b = (z + 1 + i) % 4
        for k in range(4):
            from_sib(k, i).wait_recv()
        mid = x_v[b].astype(f32) + dot(att_all[b], wo_v[...])
        nb = (
            mid * lax.rsqrt(jnp.mean(mid * mid, axis=-1, keepdims=True) + epsilon) * gain
        ).astype(bf16)
        normed[b] = nb
        if i == 3:
            mid_b[0] = mid[:ROWS]
            mid_b[1] = mid[ROWS:]
        if i < 3:
            forward(i + 1)
        gate = dot(nb, wg_v[...])
        up = dot(nb, wu_v[...])
        sig = 1.0 / (1.0 + jnp.exp(-gate))
        silu = gate * sig
        hb = (silu * up).astype(bf16)
        hid[b] = hb
        gh = back_product(c_v[b], wd_v[...])
        ggb = (gh * up * (sig * (1.0 + gate * (1.0 - sig)))).astype(bf16)
        gub = (gh * silu).astype(bf16)
        gg[b] = ggb
        gu[b] = gub
        pb = (back_product(ggb, wg_v[...]) + back_product(gub, wu_v[...])).astype(bf16)
        p_out[i, 0] = pb[:ROWS]
        p_out[i, 1] = pb[ROWS:]
        p_copy(i).start()
        if i > 0:
            reduce_block(i - 1)
        db = dot(hb, wd_v[...]).astype(bf16)
        dpart_ref[b, 0] = db[:ROWS]
        dpart_ref[b, 1] = db[ROWS:]

    def x_copy(which, s):
        tx, rx = (glu_tx, glu_rx) if which < 2 else (down_tx, down_rx)
        if which < 2:
            src, dst = tx.at[others[s], which], rx.at[group, which]
        else:
            src, dst = tx.at[others[s]], rx.at[group]
        return rcopy(src, dst, s_x.at[which, s], r_x.at[which, s], tpeers[s])

    def x_own(which):
        if which < 2:
            return pltpu.make_async_copy(
                glu_tx.at[group, which], glu_rx.at[group, which], l_x.at[which]
            )
        return pltpu.make_async_copy(down_tx.at[group], down_rx.at[group], l_x.at[which])

    def flat(ref):
        return ref[...].reshape(8 * ROWS, ref.shape[-1])

    def glu_grads(which):
        prod = lead_sum(flat((gg, gu)[which]), flat(normed)).astype(bf16)
        for mm in range(M):
            for ff in range(2):
                glu_tx[mm * 2 + ff, which] = prod[
                    mm * seg : (mm + 1) * seg, ff * half_width : (ff + 1) * half_width
                ]
        for s in range(T - 1):
            x_copy(which, s).start()
        x_own(which).start()

    def down_grads():
        prod = lead_sum(flat(hid), flat(c_v))
        for mm in range(M):
            for ff in range(2):
                down_tx[mm * 2 + ff] = jnp.concatenate(
                    [
                        prod[:, blk * each : (blk + 1) * each]
                        for zl in range(2)
                        for cc in range(2)
                        for blk in [(2 * ff + zl) * 2 * M + mm * 2 + cc]
                    ],
                    axis=1,
                ).astype(bf16)
        for s in range(T - 1):
            x_copy(2, s).start()
        x_own(2).start()

    glu_grads(0)

    p_copy(3).wait_recv()
    dy = p_out[3, core].astype(f32) + p_sib[3].astype(f32)
    for i in range(3):
        rs_copy(i).wait_recv()
        dy = dy + p_rx[i].astype(f32)
    mid = mid_b[core]
    r = lax.rsqrt(jnp.mean(mid * mid, axis=-1, keepdims=True) + epsilon)
    gdy = gain * dy
    dv = r * gdy - mid * (r * r * r) * jnp.mean(mid * gdy, axis=-1, keepdims=True)
    gmid = own_c_ref[...].astype(f32) + dv
    gmid_ref[...] = gmid
    mid_ref[...] = mid
    gpart_ref[...] = jnp.sum(dy * mid * r, axis=0, keepdims=True)
    br_own[...] = gmid.astype(bf16)
    branch_ref[me] = br_own[...]

    def br_copy(k):
        if k < 3:
            return rcopy(br_own, branch_ref.at[me], s_br.at[k], r_br.at[k], zpeers[k])
        j = me if k == 3 else slot((z + 3 - (k - 4)) % 4, core)
        return rcopy(
            br_own if k == 3 else branch_ref.at[j], branch_ref.at[j], s_br.at[k], r_br.at[k], sib
        )

    for k in (1, 0, 2, 3):
        br_copy(k).start()
    glu_grads(1)
    down_grads()
    for k in range(3):
        br_copy(k).wait_recv()
        br_copy(k + 4).start()
    for k in range(3, 7):
        br_copy(k).wait_recv()
    for which in range(3):
        x_own(which).wait()
        for s in range(T - 1):
            x_copy(which, s).wait_recv()
    for i in range(4):
        for s in range(3):
            send_att(s, i).wait_send()
        for k in range(4):
            sib_att(k, i).wait_send()
        p_copy(i).wait_send()
    for i in range(3):
        rs_copy(i).wait_send()
    for k in range(7):
        br_copy(k).wait_send()
    for which in range(3):
        for s in range(T - 1):
            x_copy(which, s).wait_send()


def feed_forward(att, x_all, c_all, own_c, w_out, w_gate, w_up, w_down, gain, cid):
    n = lax.axis_size("ctx")
    T, seg, each = n // 4, FF // n, WIDTH // n
    cols = FF // 8
    half_width = WIDTH // 2
    VS, sem = pltpu.VMEM, pltpu.SemaphoreType.DMA
    shape = jax.ShapeDtypeStruct
    return pl.pallas_call(
        ffn_kernel,
        out_shape=(
            shape((4, BLOCK, WIDTH), bf16),
            shape((8, ROWS, WIDTH), bf16),
            shape((ROWS, WIDTH), f32),
            shape((ROWS, WIDTH), f32),
            shape((4, 2, ROWS, WIDTH), bf16),
            shape((1, WIDTH), f32),
            shape((T, 2, seg, half_width), bf16),
            shape((T, cols, 4 * each), bf16),
        ),
        in_specs=vspecs(1) + any_specs(2) + vspecs(1) + any_specs(4) + vspecs(1),
        out_specs=tuple(vspecs(8)),
        scratch_shapes=[
            VS((4, BLOCK, WIDTH), bf16),
            VS((4, BLOCK, WIDTH), bf16),
            VS((WIDTH, WIDTH), bf16),
            VS((WIDTH, cols), bf16),
            VS((WIDTH, cols), bf16),
            VS((cols, WIDTH), bf16),
            VS((4, BLOCK, WIDTH), bf16),
            VS((4, BLOCK, cols), bf16),
            VS((4, BLOCK, cols), bf16),
            VS((4, BLOCK, cols), bf16),
            VS((2, ROWS, WIDTH), f32),
            VS((4, 2, ROWS, WIDTH), bf16),
            VS((4, ROWS, WIDTH), bf16),
            VS((3, ROWS, WIDTH), bf16),
            VS((3, ROWS, WIDTH), bf16),
            VS((T, 2, seg, half_width), bf16),
            VS((T, cols, 4 * each), bf16),
            VS((ROWS, WIDTH), bf16),
            sem((6,)),
            sem((3, 4)),
            sem((3, 4)),
            sem((4, 4)),
            sem((4, 4)),
            sem((7,)),
            sem((7,)),
            sem((7,)),
            sem((7,)),
            sem((3, T - 1)),
            sem((3, T - 1)),
            sem((3,)),
        ],
        compiler_params=pltpu.CompilerParams(
            collective_id=cid, has_side_effects=True, vmem_limit_bytes=60 * 2**20
        ),
        name="feed_forward",
    )(att, x_all, c_all, own_c, w_out, w_gate, w_up, w_down, gain)


def root_mean_norm(rows, gain):
    return (
        rows * lax.rsqrt(jnp.mean(rows * rows, axis=-1, keepdims=True) + epsilon) * gain
    )


def rotary(rows, cosine, sine):
    halfway = rows.shape[-1] // 2
    leading = rows[..., :halfway]
    trailing = rows[..., halfway:]
    return jnp.concatenate(
        [leading * cosine - trailing * sine, leading * sine + trailing * cosine], axis=-1
    )


SWAP = [(0, 1), (1, 0)]


def halves(f, own, other, axis):
    return jnp.where(
        f == 0,
        jnp.concatenate([own, other], axis=axis),
        jnp.concatenate([other, own], axis=axis),
    )


def local(
    hidden_in,
    doc_lengths,
    attn_gain,
    query_gain,
    key_norm_gain,
    ffn_gain,
    query_proj,
    key_weight,
    value_weight,
    attn_proj,
    gate_proj,
    up_proj,
    down_proj,
    out_cotangent,
):
    n_ctx = lax.axis_size("ctx")
    M = n_ctx // 8
    T = 2 * M
    z, m, core, f = who()
    head = slot(z, core)
    tokens = 8 * ROWS
    span = n_ctx // 4 * ROWS
    segment = FF // n_ctx
    columns = M * segment
    half_width = WIDTH // 2
    each = WIDTH // n_ctx

    heads_own = jnp.concatenate(
        [
            lax.dynamic_slice(query_proj, (0, head * 128), (half_width, 128)),
            lax.dynamic_slice(key_weight, (0, head * 64), (half_width, 64)),
            lax.dynamic_slice(value_weight, (0, head * 64), (half_width, 64)),
        ],
        axis=1,
    ).astype(bf16)
    first = z * (n_ctx // 4) + core
    gate_own, up_own = [
        jnp.concatenate(
            [
                lax.dynamic_slice(w, (0, (first + 2 * mm) * segment), (half_width, segment))
                for mm in range(M)
            ],
            axis=1,
        ).astype(bf16)
        for w in (gate_proj, up_proj)
    ]
    down_own = jnp.concatenate(
        [
            lax.dynamic_slice(
                down_proj, ((first + 2 * mm) * segment - f * (FF // 2), 0), (segment, WIDTH)
            )
            for mm in range(M)
        ],
        axis=0,
    ).astype(bf16)
    out_own = attn_proj.astype(bf16)

    cotangent = out_cotangent[0]
    (
        x_rows, c_rows, w_heads, w_gate, w_up, w_down, w_out, q_rows, kv_all, att_own, summed, totals,
        stacked, normed, cos_table, sin_table,
    ) = front(
        doc_lengths,
        hidden_in[0],
        cotangent,
        heads_own,
        gate_own,
        up_own,
        down_own,
        out_own,
        attn_gain[None],
        jnp.tile(query_gain, 2)[None],
        jnp.concatenate([key_norm_gain, jnp.ones((64,), f32)])[None],
        1,
    )
    starts = jnp.cumsum(doc_lengths[0]) - doc_lengths[0]
    token_index = (
        jnp.arange(4, dtype=jnp.int32)[:, None] * span
        + m * BLOCK
        + jnp.arange(BLOCK, dtype=jnp.int32)[None, :]
    ).reshape(tokens, 1)
    after = token_index >= starts[None, :]
    begins = jnp.max(jnp.where(after, starts[None, :], 0), axis=1, keepdims=True)
    cosine = cos_table[:, None, :32]
    sine = sin_table[:, None, 32:64]

    def rotate(q_in, k_in, q_gain, k_gain):
        q_out = (
            rotary(root_mean_norm(q_in.reshape(tokens, 2, HEAD_SIZE), q_gain), cosine, sine)
            * HEAD_SIZE ** (-0.5)
        )
        k_out = rotary(root_mean_norm(k_in.reshape(tokens, 1, HEAD_SIZE), k_gain), cosine, sine)
        return q_out.reshape(tokens, 128), k_out.reshape(tokens, 64)

    _, heads_back = jax.vjp(
        rotate, stacked[:, :128], stacked[:, 128:192], query_gain, key_norm_gain
    )
    m_arr = jnp.full((1,), m, jnp.int32)
    attended, branch, grad_middle, own, down_parts, ffn_gain_part, glu_got, down_got = feed_forward(
        att_own,
        x_rows.reshape(4, BLOCK, WIDTH),
        c_rows.reshape(4, BLOCK, WIDTH),
        cotangent,
        w_out,
        w_gate,
        w_up,
        w_down,
        ffn_gain[None],
        4,
    )
    attended = attended.reshape(tokens, WIDTH)
    branch = branch.reshape(tokens, WIDTH)
    ffn_gain_part = ffn_gain_part[0]
    output = own + scatter8(down_parts.reshape(8, ROWS, WIDTH), 5)

    w_out_head = lax.dynamic_slice(w_out, (head * 128, 0), (128, WIDTH))
    grad_mixed = back_product(branch, w_out_head)
    grad_summed = (grad_mixed / totals).astype(bf16)
    weighted = (grad_mixed * summed / (totals * totals)).reshape(tokens, 2, 64)
    delta = jnp.broadcast_to(
        jnp.sum(weighted, axis=2, keepdims=True), (tokens, 2, 64)
    ).reshape(tokens, 128)
    grad_q, dkv = attend_back(m_arr, q_rows, kv_all, begins, grad_summed, delta, span)
    dkv = jnp.sum(across(dkv, False, False, 6).astype(f32), axis=0)
    gq_pre, gk_pre, q_gain_part, k_gain_part = heads_back((grad_q, dkv[:, :64]))
    grad_stacked = jnp.concatenate([gq_pre, gk_pre, dkv[:, 64:]], axis=1).astype(bf16)
    part_normed = back_product(grad_stacked, w_heads).reshape(8, ROWS, WIDTH).astype(bf16)
    grad_normed = scatter8(part_normed, 7)
    _, attn_back = jax.vjp(root_mean_norm, hidden_in[0].astype(f32), attn_gain)
    grad_resid, attn_gain_part = attn_back(grad_normed)
    input_grad = grad_middle + grad_resid

    glu_grad = jnp.sum(glu_got.astype(f32), axis=0)
    down_sum = jnp.sum(down_got.astype(f32), axis=0)
    gate_grad = jnp.transpose(glu_grad[0])
    up_grad = jnp.transpose(glu_grad[1])

    devices = [
        (zz, mm, cc, ff) for zz in range(4) for mm in range(M) for cc in range(2) for ff in range(2)
    ]

    def number(zz, mm, cc, ff):
        return (zz * (n_ctx // 4) + mm * 2 + cc) * 2 + ff

    down_pieces = down_sum.reshape(columns, 2, 2, each)
    rounds = []
    for dz in range(2):
        for dc in range(2):
            piece = lax.dynamic_slice(
                down_pieces, (0, (z + dz) % 2, (core + dc) % 2, 0), (columns, 1, 1, each)
            ).reshape(columns, each)
            perm = [
                (number(zz, mm, cc, ff), number(2 * ff + (zz + dz) % 2, mm, (cc + dc) % 2, zz // 2))
                for zz, mm, cc, ff in devices
            ]
            rounds.append(lax.ppermute(piece, ("ctx", "fsdp"), perm))
    rounds = jnp.stack(rounds).reshape(2, 2, columns, each)
    rounds = jnp.where(z % 2 == 0, rounds, rounds[::-1])
    rounds = jnp.where(core == 0, rounds, rounds[:, ::-1])
    down_grad = jnp.transpose(
        rounds.reshape(2, 2, M, segment, each), (0, 2, 1, 3, 4)
    ).reshape(FF // 2, each)

    branch_columns = lax.dynamic_slice(
        branch.reshape(tokens, 4, M, 2, each), (0, z, 0, core, 0), (tokens, 1, M, 1, each)
    ).reshape(tokens, M * each)
    attn_part = lead_sum(attended, branch_columns).astype(bf16)
    attn_part = jnp.transpose(
        attn_part.reshape(2, half_width, M, each), (2, 0, 1, 3)
    ).reshape(T, half_width, each)
    attn_grad = jnp.sum(across(attn_part, True, False, 11).astype(f32), axis=0)

    heads_part = lead_sum(normed, grad_stacked).astype(bf16)
    qw, kw = 128 // M, 64 // M
    heads_part = jnp.concatenate(
        [
            heads_part[:, :128].reshape(2, half_width, M, qw),
            heads_part[:, 128:192].reshape(2, half_width, M, kw),
            heads_part[:, 192:].reshape(2, half_width, M, kw),
        ],
        axis=3,
    )
    heads_part = jnp.transpose(heads_part, (2, 0, 1, 3)).reshape(T, half_width, 256 // M)
    heads_grad = jnp.sum(across(heads_part, True, False, 12).astype(f32), axis=0)
    perm = [
        (number(zz, mm, cc, ff), number(zz, (cc * M + mm) // 2, (cc * M + mm) % 2, ff))
        for zz, mm, cc, ff in devices
    ]
    heads_grad = lax.ppermute(heads_grad, ("ctx", "fsdp"), perm)
    query_grad = heads_grad[:, :qw]
    key_grad = heads_grad[:, qw : qw + kw]
    value_grad = heads_grad[:, qw + kw :]

    gains = jnp.concatenate([attn_gain_part, ffn_gain_part, q_gain_part, k_gain_part])
    gains = jnp.sum(gather8(gains.reshape(17, 128), 13), axis=0)
    gains = jnp.sum(across(gains, True, True, 14), axis=0).reshape(-1)
    return (
        output[None],
        input_grad[None],
        gains[:WIDTH],
        gains[2 * WIDTH : 2 * WIDTH + 64],
        gains[2 * WIDTH + 64 :],
        gains[WIDTH : 2 * WIDTH],
        query_grad,
        key_grad,
        value_grad,
        attn_grad,
        gate_grad,
        up_grad,
        down_grad,
    )


def solution(mesh):
    in_specs = (
        P("fsdp", "ctx", None),
        P("fsdp", None),
        P(),
        P(),
        P(),
        P(),
        P("fsdp", None),
        P("fsdp", None),
        P("fsdp", None),
        P("fsdp", None),
        P("fsdp", None),
        P("fsdp", None),
        P("fsdp", None),
        P("fsdp", "ctx", None),
    )
    out_specs = (
        P("fsdp", "ctx", None),
        P("fsdp", "ctx", None),
        P(),
        P(),
        P(),
        P(),
        P("fsdp", "ctx"),
        P("fsdp", "ctx"),
        P("fsdp", "ctx"),
        P("fsdp", "ctx"),
        P("fsdp", "ctx"),
        P("fsdp", "ctx"),
        P("fsdp", "ctx"),
    )
    return jax.shard_map(local, mesh=mesh, in_specs=in_specs, out_specs=out_specs, check_vma=False)
```

```python
import functools
import math

import jax
import jax.numpy as jnp
from jax import lax
from jax.experimental import pallas as pl
from jax.experimental.pallas import tpu as pltpu
from jax.sharding import PartitionSpec as P

QUERY_HEADS = 16
KEY_VALUE_HEADS = 8
HEAD_SIZE = 64
FF = 4608
WIDTH = 1024
ROWS = 128

epsilon = 1e-05
rope_base = 1000000.0
MESH = pl.DeviceIdType.MESH
ANY = pl.ANY
bf16 = jnp.bfloat16
f32 = jnp.float32


def who():
    n = lax.axis_size("ctx")
    c = lax.axis_index("ctx")
    f = lax.axis_index("fsdp")
    q = n // 4
    return c // q, (c % q) // 2, c % 2, f


def dev(z, m, core, f):
    return (z * (lax.axis_size("ctx") // 4) + m * 2 + core, f)


def slot(z, core):
    return z * 2 + core


def enter(peers):
    bar = pltpu.get_barrier_semaphore()
    for p in peers:
        pl.semaphore_signal(bar, inc=1, device_id=p, device_id_type=MESH)
    pl.semaphore_wait(bar, len(peers))


def rcopy(src, dst, s, r, to):
    return pltpu.make_async_remote_copy(
        src_ref=src, dst_ref=dst, send_sem=s, recv_sem=r, device_id=to, device_id_type=MESH
    )


def comm_params(cid):
    return pltpu.CompilerParams(collective_id=cid, has_side_effects=True)


def any_specs(n):
    return [pl.BlockSpec(memory_space=ANY)] * n


def gather8_kernel(x_ref, o_ref, ss, rs, ls):
    z, m, core, f = who()
    sib = dev(z, m, 1 - core, f)
    peers = [dev((z + s) % 4, m, core, f) for s in (1, 2, 3)]
    me = slot(z, core)
    own = pltpu.make_async_copy(x_ref, o_ref.at[me], ls)
    own.start()
    enter([sib] + peers)
    first = []
    for k in (1, 0, 2):
        cp = rcopy(x_ref, o_ref.at[me], ss.at[k], rs.at[k], peers[k])
        cp.start()
        first.append((k, cp))
    cp0 = rcopy(x_ref, o_ref.at[me], ss.at[3], rs.at[3], sib)
    cp0.start()
    fw = []
    for k, cp in first:
        sl = slot((z + 3 - k) % 4, core)
        cp.wait_recv()
        cp = rcopy(o_ref.at[sl], o_ref.at[sl], ss.at[4 + k], rs.at[4 + k], sib)
        cp.start()
        fw.append(cp)
    for cp in fw + [cp0]:
        cp.wait_recv()
    for cp in [cp for _, cp in first] + [cp0] + fw:
        cp.wait_send()
    own.wait()


def gather8(x, cid):
    return pl.pallas_call(
        gather8_kernel,
        out_shape=jax.ShapeDtypeStruct((8,) + x.shape, x.dtype),
        in_specs=any_specs(1),
        out_specs=any_specs(1)[0],
        scratch_shapes=[
            pltpu.SemaphoreType.DMA((7,)),
            pltpu.SemaphoreType.DMA((7,)),
            pltpu.SemaphoreType.DMA,
        ],
        compiler_params=comm_params(cid),
        name="gather8_%d" % cid,
    )(x)


def across_kernel(both, same, x_ref, o_ref, ss, rs, ls):
    z, m, core, f = who()
    M = lax.axis_size("ctx") // 8
    count = M * 2 if both else M
    me = m * 2 + f if both else m
    others = [(me + s) % count for s in range(1, count)]
    peers = [dev(z, o // 2, core, o % 2) if both else dev(z, o, core, f) for o in others]

    def src(k):
        return x_ref if same else x_ref.at[k]

    own = pltpu.make_async_copy(src(me), o_ref.at[me], ls)
    own.start()
    enter(peers)
    cps = []
    for s in range(count - 1):
        cp = rcopy(src(others[s]), o_ref.at[me], ss.at[s], rs.at[s], peers[s])
        cp.start()
        cps.append(cp)
    for cp in cps:
        cp.wait_recv()
    for cp in cps:
        cp.wait_send()
    own.wait()


def across(x, both, same, cid):
    shp = x.shape if same else x.shape[1:]
    count = lax.axis_size("ctx") // (4 if both else 8)
    return pl.pallas_call(
        functools.partial(across_kernel, both, same),
        out_shape=jax.ShapeDtypeStruct((count,) + shp, x.dtype),
        in_specs=any_specs(1),
        out_specs=any_specs(1)[0],
        scratch_shapes=[
            pltpu.SemaphoreType.DMA((count - 1,)),
            pltpu.SemaphoreType.DMA((count - 1,)),
            pltpu.SemaphoreType.DMA,
        ],
        compiler_params=comm_params(cid),
        name="across_%d" % cid,
    )(x)


def scatter8_kernel(x_ref, o_ref, a, b, s_buf, d, ls, s1, r1, s2, r2):
    z, m, core, f = who()
    sib = dev(z, m, 1 - core, f)
    to = [(z + s) % 4 for s in (1, 2, 3, 0)]
    peers = [dev(zz, m, core, f) for zz in to[:3]]
    loads = []
    for k in range(4):
        cp = pltpu.make_async_copy(x_ref.at[slot(to[k], core)], a.at[k], ls.at[k])
        cp.start()
        loads.append(cp)
    enter([sib] + peers)
    ones = []
    for k in range(4):
        cp = rcopy(x_ref.at[slot(to[k], 1 - core)], b.at[k], s1.at[k], r1.at[k], sib)
        cp.start()
        ones.append(cp)
    twos = []
    for k in range(3):
        loads[k].wait()
        ones[k].wait_recv()
        s_buf[k] = (a[k].astype(f32) + b[k].astype(f32)).astype(s_buf.dtype)
        cp = rcopy(s_buf.at[k], d.at[k], s2.at[k], r2.at[k], peers[k])
        cp.start()
        twos.append(cp)
    loads[3].wait()
    ones[3].wait_recv()
    total = a[3].astype(f32) + b[3].astype(f32)
    for k in range(3):
        twos[k].wait_recv()
        total = total + d[k].astype(f32)
    o_ref[...] = total
    for cp in ones + twos:
        cp.wait_send()


def scatter8(x, cid):
    shp = x.shape[1:]
    return pl.pallas_call(
        scatter8_kernel,
        out_shape=jax.ShapeDtypeStruct(shp, f32),
        in_specs=any_specs(1),
        out_specs=pl.BlockSpec(memory_space=pltpu.VMEM),
        scratch_shapes=[
            pltpu.VMEM((4,) + shp, x.dtype),
            pltpu.VMEM((4,) + shp, x.dtype),
            pltpu.VMEM((3,) + shp, x.dtype),
            pltpu.VMEM((3,) + shp, x.dtype),
            pltpu.SemaphoreType.DMA((4,)),
            pltpu.SemaphoreType.DMA((4,)),
            pltpu.SemaphoreType.DMA((4,)),
            pltpu.SemaphoreType.DMA((3,)),
            pltpu.SemaphoreType.DMA((3,)),
        ],
        compiler_params=comm_params(cid),
        name="scatter8_%d" % cid,
    )(x)


def back_product(left, right):
    return lax.dot_general(
        left, right, (((1,), (1,)), ((), ())), preferred_element_type=f32
    )


def lead_sum(left, right):
    return lax.dot_general(
        left, right, (((0,), (0,)), ((), ())), preferred_element_type=f32
    )


def dot(left, right):
    return jnp.dot(left, right, preferred_element_type=f32)


BLOCK = 2 * ROWS


def block_weights(q, k, begin, z, m, mm, span):
    keys = (z + 1) * BLOCK
    key = lax.broadcasted_iota(jnp.int32, (1, keys), 1)
    key = key // BLOCK * span + key % BLOCK + mm * BLOCK
    token = z * span + m * BLOCK + lax.broadcasted_iota(jnp.int32, (BLOCK, 1), 0)
    e = jnp.exp(back_product(q, k))
    return jnp.where((key >= begin) & (key <= token), e, 0.0)


def attend_kernel(span, m_ref, q_ref, kv_ref, begin_ref, sum_ref, tot_ref):
    m = m_ref[0]
    for z in range(4):
        rows = slice(z * BLOCK, (z + 1) * BLOCK)
        keys = (z + 1) * BLOCK
        for h in range(2):
            lanes = slice(h * 64, h * 64 + 64)
            acc = jnp.zeros((BLOCK, 64), f32)
            tot = jnp.zeros((BLOCK, 1), f32)
            q = q_ref[rows, lanes]

            def step(mm, carry):
                acc, tot = carry
                e = block_weights(q, kv_ref[mm, :keys, :64], begin_ref[rows, :], z, m, mm, span)
                acc = acc + dot(e.astype(bf16), kv_ref[mm, :keys, 64:])
                return acc, tot + jnp.sum(e, axis=1, keepdims=True)

            acc, tot = lax.fori_loop(0, kv_ref.shape[0], step, (acc, tot))
            sum_ref[rows, lanes] = acc
            tot_ref[rows, lanes] = jnp.broadcast_to(tot, (BLOCK, 64))


VM = pltpu.VMEM


def vspecs(n):
    return [pl.BlockSpec(memory_space=VM)] * n


def attend(m, q, kv, begin, span):
    n = q.shape[0]
    return pl.pallas_call(
        functools.partial(attend_kernel, span),
        out_shape=(jax.ShapeDtypeStruct((n, 128), f32), jax.ShapeDtypeStruct((n, 128), f32)),
        in_specs=[pl.BlockSpec(memory_space=pltpu.SMEM)] + vspecs(3),
        out_specs=tuple(vspecs(2)),
        cost_estimate=pl.CostEstimate(flops=2**31, bytes_accessed=2**22, transcendentals=2**22),
        compiler_params=pltpu.CompilerParams(vmem_limit_bytes=40 * 2**20),
        name="attend",
    )(m, q, kv, begin)


def attend_back_kernel(span, m_ref, q_ref, kv_ref, begin_ref, g_ref, delta_ref, dq_ref, dkv_ref, acc_ref):
    m = m_ref[0]
    dq_ref[...] = jnp.zeros_like(dq_ref)

    def step(mm, _):
        acc_ref[...] = jnp.zeros_like(acc_ref)
        for z in range(4):
            rows = slice(z * BLOCK, (z + 1) * BLOCK)
            keys = (z + 1) * BLOCK
            for h in range(2):
                lanes = slice(h * 64, h * 64 + 64)
                q = q_ref[rows, lanes]
                g = g_ref[rows, lanes]
                k = kv_ref[mm, :keys, :64]
                v = kv_ref[mm, :keys, 64:]
                e = block_weights(q, k, begin_ref[rows, :], z, m, mm, span)
                dp = back_product(g, v)
                ds = (e * (dp - delta_ref[rows, h * 64 : h * 64 + 1])).astype(bf16)
                dq_ref[rows, lanes] += dot(ds, k)
                acc_ref[:keys, :64] += lead_sum(ds, q)
                acc_ref[:keys, 64:] += lead_sum(e.astype(bf16), g)
        dkv_ref[mm] = acc_ref[...].astype(dkv_ref.dtype)
        return 0

    lax.fori_loop(0, kv_ref.shape[0], step, 0)


def attend_back(m, q, kv, begin, g, delta, span):
    n = q.shape[0]
    return pl.pallas_call(
        functools.partial(attend_back_kernel, span),
        out_shape=(jax.ShapeDtypeStruct((n, 128), f32), jax.ShapeDtypeStruct(kv.shape, bf16)),
        in_specs=[pl.BlockSpec(memory_space=pltpu.SMEM)] + vspecs(5),
        out_specs=tuple(vspecs(2)),
        scratch_shapes=[pltpu.VMEM((n, 128), f32)],
        cost_estimate=pl.CostEstimate(flops=2**33, bytes_accessed=2**23, transcendentals=2**22),
        compiler_params=pltpu.CompilerParams(vmem_limit_bytes=48 * 2**20),
        name="attend_back",
    )(m, q, kv, begin, g, delta)


def begin_of(token, doc_ref):
    begin = jnp.zeros(token.shape, jnp.int32)
    start = doc_ref[0, 0]
    for d in range(1, doc_ref.shape[1]):
        begin = jnp.where(token >= start, start, begin)
        start = start + doc_ref[0, d]
    return begin


def turn(v):
    lane = lax.broadcasted_iota(jnp.int32, v.shape, 1)
    n = v.shape[1]
    return jnp.where(lane % 64 < 32, pltpu.roll(v, n - 32, 1), pltpu.roll(v, 32, 1))


def head_scale(v):
    sq = v * v
    if v.shape[1] == 64:
        return lax.rsqrt(jnp.mean(sq, axis=1, keepdims=True) + epsilon)
    low = lax.broadcasted_iota(jnp.int32, v.shape, 1) < 64
    a = jnp.sum(jnp.where(low, sq, 0.0), axis=1, keepdims=True)
    b = jnp.sum(jnp.where(low, 0.0, sq), axis=1, keepdims=True)
    return lax.rsqrt(jnp.where(low, a, b) * (1.0 / 64) + epsilon)


def front_kernel(
    doc_ref, x_ref, c_ref, wh_ref, wg_hbm, wu_hbm, wd_hbm, wo_hbm, again_ref, qgain_ref, kgain_ref,
    x_all, c_all, w_heads, w_gate, w_up, w_down, w_out, q_rows, kv_all, att, summed, totals,
    stacked, normed, cosine, sine,
    s_x, r_x, s_c, r_c, s_h, r_h, s_w, r_w, s_v, r_v, s_o, r_o, s_k, r_k, l_s,
):
    z, m, core, f = who()
    M = lax.axis_size("ctx") // 8
    span = lax.axis_size("ctx") // 4 * ROWS
    half_width = WIDTH // 2
    sib = dev(z, m, 1 - core, f)
    zpeers = [dev((z + s) % 4, m, core, f) for s in (1, 2, 3)]
    hm = m % 2
    pair = dev(z, m, core, 1 - f)
    beside = dev(z, m + 1 - 2 * hm, core, f)
    mpeers = [dev(z, (m + s) % M, core, f) for s in range(1, M)]
    me = slot(z, core)
    owner = f == z // 2

    stay = pltpu.make_async_copy(c_ref, c_all.at[me], l_s.at[0])
    stay.start()

    enter([sib, pair] + zpeers + mpeers)

    def gather(src, dst, ss, rs, k):
        if k < 3:
            return rcopy(src, dst.at[me], ss.at[k], rs.at[k], zpeers[k])
        if k == 3:
            return rcopy(src, dst.at[me], ss.at[k], rs.at[k], sib)
        j = slot((z + 3 - (k - 4)) % 4, core)
        return rcopy(dst.at[j], dst.at[j], ss.at[k], rs.at[k], sib)

    def x_copy(k):
        return gather(x_ref, x_all, s_x, r_x, k)

    def c_copy(k):
        return gather(c_ref, c_all, s_c, r_c, k)

    for k in (1, 0, 2, 3):
        x_copy(k).start()
    head_rows = pl.ds(f * half_width, half_width)
    heads_copy = rcopy(wh_ref, w_heads.at[head_rows], s_h.at[0], r_h.at[0], pair)
    heads_copy.start()

    quarter = half_width // 2
    eighth = half_width // 4
    cols = wd_hbm.shape[0]

    def w_copy(k, stage):
        src, dst = ((wg_hbm, w_gate), (wu_hbm, w_up), (wd_hbm, w_down), (wo_hbm, w_out))[k]
        size = (quarter, quarter, cols // 2, eighth)[k]
        part = hm * 2 + core if k == 3 else hm
        place = dst.at[pl.ds(pl.multiple_of(part * size, 8), size)]
        if stage == 0:
            here = src.at[pl.ds(pl.multiple_of(part * size, 8), size)]
            return rcopy(here, place, s_w.at[k], r_w.at[k], pair)
        return rcopy(place, place, s_v.at[k], r_v.at[k], beside)

    def out_copy(k):
        part = (hm if k == 0 else 1 - hm) * 2 + core
        place = w_out.at[pl.ds(pl.multiple_of(part * eighth, 8), eighth)]
        return rcopy(place, place, s_o.at[k], r_o.at[k], sib)

    for k in (0, 1, 3):
        w_copy(k, 0).start()

    @pl.when(owner)
    def _():
        w_copy(2, 0).start()

    w_heads[head_rows] = wh_ref[...]
    x_all[me] = x_ref[...]

    lane = lax.broadcasted_iota(jnp.int32, (1, 128), 1) % 32
    freq = jnp.exp(lane.astype(f32) * (-2.0 / 64 * math.log(rope_base)))
    sign = jnp.where(lax.broadcasted_iota(jnp.int32, (1, 128), 1) % 64 < 32, -1.0, 1.0)

    def tokens_of(zz):
        return zz * span + m * BLOCK + lax.broadcasted_iota(jnp.int32, (BLOCK, 1), 0)

    def table(zz, _):
        rows = pl.ds(pl.multiple_of(zz * BLOCK, BLOCK), BLOCK)
        token = tokens_of(zz)
        place = (token - begin_of(token, doc_ref)).astype(f32)
        angle = place * freq
        cosine[rows, :] = jnp.cos(angle)
        sine[rows, :] = jnp.sin(angle) * sign
        return 0

    lax.fori_loop(0, 4, table, 0)
    for k in range(3):
        x_copy(k).wait_recv()
        x_copy(k + 4).start()
    for k in (1, 0, 2, 3):
        c_copy(k).start()
    heads_copy.wait_recv()

    def kv_copy(b, s):
        rows = pl.ds(pl.multiple_of(b * BLOCK, BLOCK), BLOCK)
        place = kv_all.at[m, rows]
        return rcopy(place, place, s_k.at[b, s], r_k.at[b, s], mpeers[s])

    again = again_ref[...]
    qgain = qgain_ref[...]
    kgain = kgain_ref[...]

    for k in range(3, 7):
        x_copy(k).wait_recv()

    def project(b, _):
        rows = pl.ds(pl.multiple_of(b * BLOCK, BLOCK), BLOCK)
        x = jnp.concatenate([x_all[2 * b], x_all[2 * b + 1]], axis=0).astype(f32)
        nb = (
            x * lax.rsqrt(jnp.mean(x * x, axis=-1, keepdims=True) + epsilon) * again
        ).astype(bf16)
        normed[rows, :] = nb
        st = dot(nb, w_heads[...])
        stacked[rows, :] = st
        co = cosine[rows, :]
        si = sine[rows, :]
        q = st[:, :128]
        q = q * head_scale(q) * qgain
        q_rows[rows, :] = ((q * co + turn(q) * si) * HEAD_SIZE ** (-0.5)).astype(bf16)
        kv = st[:, 128:]
        low = lax.broadcasted_iota(jnp.int32, kv.shape, 1) < 64
        k = kv * head_scale(kv) * kgain
        kv_all[m, rows, :] = jnp.where(low, k * co + turn(k) * si, kv).astype(bf16)
        for s in range(M - 1):
            kv_copy(b, s).start()
        return 0

    lax.fori_loop(0, 4, project, 0)
    for k in range(2):
        w_copy(k, 0).wait_recv()
        w_copy(k, 1).start()

    summed[...] = jnp.zeros_like(summed)
    totals[...] = jnp.zeros_like(totals)

    def attend(s, _):
        mm = (m + M - s) % M

        @pl.when(s > 0)
        def _():
            for b in range(4):
                rows = pl.ds(b * BLOCK, BLOCK)
                place = kv_all.at[mm, rows]
                rcopy(place, place, s_k.at[b, s - 1], r_k.at[b, s - 1], sib).wait_recv()

        for zz in range(4):
            rows = slice(zz * BLOCK, (zz + 1) * BLOCK)
            keys = (zz + 1) * BLOCK
            begin = begin_of(tokens_of(zz), doc_ref)
            for h in range(2):
                lanes = slice(h * 64, h * 64 + 64)
                e = block_weights(
                    q_rows[rows, lanes], kv_all[mm, :keys, :64], begin, zz, m, mm, span
                )
                summed[rows, lanes] += dot(e.astype(bf16), kv_all[mm, :keys, 64:])
                totals[rows, lanes] += jnp.broadcast_to(
                    jnp.sum(e, axis=1, keepdims=True), (BLOCK, 64)
                )
        return 0

    lax.fori_loop(0, M, attend, 0)
    for b in range(4):
        rows = slice(b * BLOCK, (b + 1) * BLOCK)
        att[b] = (summed[rows, :] / totals[rows, :]).astype(bf16)

    w_copy(3, 0).wait_recv()
    w_copy(3, 1).start()
    out_copy(0).start()

    @pl.when(jnp.logical_not(owner))
    def _():
        w_copy(2, 0).wait_recv()
        w_copy(2, 1).start()

    for k in range(3):
        c_copy(k).wait_recv()
        c_copy(k + 4).start()

    def w_got(k):
        dst = (w_gate, w_up, w_down, w_out)[k]
        size = (quarter, quarter, cols // 2, eighth)[k]
        part = (1 - hm) * 2 + core if k == 3 else 1 - hm
        place = dst.at[pl.ds(pl.multiple_of(part * size, 8), size)]
        return rcopy(place, place, s_v.at[k], r_v.at[k], beside)

    w_got(3).wait_recv()
    out_copy(1).start()
    for k in range(2):
        w_got(k).wait_recv()

    @pl.when(jnp.logical_not(owner))
    def _():
        w_got(2).wait_recv()
        w_copy(2, 1).wait_send()

    @pl.when(owner)
    def _():
        w_copy(2, 0).wait_send()

    for k in range(3, 7):
        c_copy(k).wait_recv()
    for k in range(2):
        out_copy(k).wait_recv()
    stay.wait()
    heads_copy.wait_send()
    for k in range(7):
        x_copy(k).wait_send()
        c_copy(k).wait_send()
    for k in (0, 1, 3):
        w_copy(k, 0).wait_send()
        w_copy(k, 1).wait_send()
    for k in range(2):
        out_copy(k).wait_send()
    for b in range(4):
        for s in range(M - 1):
            kv_copy(b, s).wait_send()


def front(docs, x, c, wh, wg, wu, wd, wo, again, qgain, kgain, cid):
    n = lax.axis_size("ctx")
    M = n // 8
    cols = FF // 8
    tokens = 8 * ROWS
    sem = pltpu.SemaphoreType.DMA
    shape = jax.ShapeDtypeStruct
    return pl.pallas_call(
        front_kernel,
        out_shape=(
            shape((8, ROWS, WIDTH), bf16),
            shape((8, ROWS, WIDTH), bf16),
            shape((WIDTH, 256), bf16),
            shape((WIDTH // 2, cols), bf16),
            shape((WIDTH // 2, cols), bf16),
            shape((cols, WIDTH), bf16),
            shape((WIDTH // 2, WIDTH), bf16),
            shape((tokens, 128), bf16),
            shape((M, tokens, 128), bf16),
            shape((4, BLOCK, 128), bf16),
            shape((tokens, 128), f32),
            shape((tokens, 128), f32),
            shape((tokens, 256), f32),
            shape((tokens, WIDTH), bf16),
            shape((tokens, 128), f32),
            shape((tokens, 128), f32),
        ),
        in_specs=[pl.BlockSpec(memory_space=pltpu.SMEM)]
        + vspecs(3) + any_specs(4) + vspecs(3),
        out_specs=tuple(vspecs(1) + any_specs(1) + vspecs(1) + any_specs(4) + vspecs(9)),
        scratch_shapes=[
            sem((7,)), sem((7,)), sem((7,)), sem((7,)), sem((1,)), sem((1,)),
            sem((4,)), sem((4,)), sem((4,)), sem((4,)), sem((2,)), sem((2,)),
            sem((4, M - 1)), sem((4, M - 1)), sem((5,)),
        ],
        compiler_params=pltpu.CompilerParams(
            collective_id=cid, has_side_effects=True, vmem_limit_bytes=60 * 2**20
        ),
        name="front",
    )(docs, x, c, wh, wg, wu, wd, wo, again, qgain, kgain)


def ffn_kernel(
    att_ref, x_hbm, c_hbm, own_c_ref, wo_own, wg_own, wu_own, wd_own, wo_got, wg_got, wu_got, wd_got,
    gain_ref,
    att_all, branch_ref, gmid_ref, mid_ref, dpart_ref, gpart_ref, glu_rx, down_rx,
    x_v, c_v, wo_v, wg_v, wu_v, wd_v, normed, hid, gg, gu, mid_b, p_out, p_sib, p_sum, p_rx,
    glu_tx, down_tx, br_own,
    ld, s_att, r_att, s_sib, r_sib, s_rs, r_rs, s_br, r_br, s_x, r_x, l_x,
):
    z, m, core, f = who()
    M = lax.axis_size("ctx") // 8
    T = 2 * M
    seg = glu_tx.shape[2]
    each = WIDTH // lax.axis_size("ctx")
    half_width = WIDTH // 2
    sib = dev(z, m, 1 - core, f)
    zs = [(z + s) % 4 for s in (1, 2, 3)]
    zpeers = [dev(zz, m, core, f) for zz in zs]
    group = m * 2 + f
    others = [(group + s) % T for s in range(1, T)]
    tpeers = [dev(z, o // 2, core, o % 2) for o in others]

    mine = pl.ds(pl.multiple_of(f * half_width, half_width), half_width)
    yours = pl.ds(pl.multiple_of((1 - f) * half_width, half_width), half_width)
    loads = [
        pltpu.make_async_copy(a, b, ld.at[k])
        for k, (a, b) in enumerate(
            (
                (wo_own, wo_v.at[mine]),
                (wo_got, wo_v.at[yours]),
                (x_hbm, x_v),
                (wg_own, wg_v.at[mine]),
                (wg_got, wg_v.at[yours]),
                (wu_own, wu_v.at[mine]),
                (wu_got, wu_v.at[yours]),
                (c_hbm, c_v),
            )
        )
    ]
    for cp in loads:
        cp.start()
    owner = f == z // 2

    @pl.when(owner)
    def _():
        pltpu.make_async_copy(wd_own, wd_v, ld.at[8]).start()

    @pl.when(jnp.logical_not(owner))
    def _():
        pltpu.make_async_copy(wd_got, wd_v, ld.at[8]).start()

    loads.append(pltpu.make_async_copy(wd_own, wd_v, ld.at[8]))
    enter([sib] + zpeers + tpeers)

    def lanes(j):
        return pl.ds(pl.multiple_of(j * 128, 128), 128)

    me = slot(z, core)

    def send_att(s, i):
        b = (zs[s] + 1 + i) % 4
        return rcopy(
            att_ref.at[b], att_all.at[b, :, lanes(me)], s_att.at[s, i], r_att.at[s, i], zpeers[s]
        )

    def got_att(s, i):
        b = (z + 1 + i) % 4
        j = slot((z + 3 - s) % 4, core)
        return rcopy(
            att_ref.at[b], att_all.at[b, :, lanes(j)], s_att.at[s, i], r_att.at[s, i], zpeers[s]
        )

    def sib_att(k, i):
        b = (z + 1 + i) % 4
        j = me if k == 3 else slot((z + 3 - k) % 4, core)
        src = att_ref.at[b] if k == 3 else att_all.at[b, :, lanes(j)]
        return rcopy(src, att_all.at[b, :, lanes(j)], s_sib.at[k, i], r_sib.at[k, i], sib)

    def from_sib(k, i):
        b = (z + 1 + i) % 4
        j = slot(z, 1 - core) if k == 3 else slot((z + 3 - k) % 4, 1 - core)
        return rcopy(att_ref.at[b], att_all.at[b, :, lanes(j)], s_sib.at[k, i], r_sib.at[k, i], sib)

    for i in range(4):
        for s in (1, 0, 2):
            send_att(s, i).start()
        sib_att(3, i).start()
    for b in range(4):
        att_all[b, :, lanes(me)] = att_ref[b]

    def forward(i):
        for s in range(3):
            got_att(s, i).wait_recv()
            sib_att(s, i).start()

    def p_copy(i):
        return rcopy(p_out.at[i, 1 - core], p_sib.at[i], s_rs.at[i], r_rs.at[i], sib)

    def rs_copy(i):
        return rcopy(p_sum.at[i], p_rx.at[i], s_rs.at[4 + i], r_rs.at[4 + i], zpeers[i])

    def reduce_block(i):
        p_copy(i).wait_recv()
        p_sum[i] = (p_out[i, core].astype(f32) + p_sib[i].astype(f32)).astype(bf16)
        rs_copy(i).start()

    forward(0)
    gain = gain_ref[...]
    for cp in loads:
        cp.wait()
    for i in range(4):
        b = (z + 1 + i) % 4
        for k in range(4):
            from_sib(k, i).wait_recv()
        mid = x_v[b].astype(f32) + dot(att_all[b], wo_v[...])
        nb = (
            mid * lax.rsqrt(jnp.mean(mid * mid, axis=-1, keepdims=True) + epsilon) * gain
        ).astype(bf16)
        normed[b] = nb
        if i == 3:
            mid_b[0] = mid[:ROWS]
            mid_b[1] = mid[ROWS:]
        if i < 3:
            forward(i + 1)
        gate = dot(nb, wg_v[...])
        up = dot(nb, wu_v[...])
        sig = 1.0 / (1.0 + jnp.exp(-gate))
        silu = gate * sig
        hb = (silu * up).astype(bf16)
        hid[b] = hb
        gh = back_product(c_v[b], wd_v[...])
        ggb = (gh * up * (sig * (1.0 + gate * (1.0 - sig)))).astype(bf16)
        gub = (gh * silu).astype(bf16)
        gg[b] = ggb
        gu[b] = gub
        pb = (back_product(ggb, wg_v[...]) + back_product(gub, wu_v[...])).astype(bf16)
        p_out[i, 0] = pb[:ROWS]
        p_out[i, 1] = pb[ROWS:]
        p_copy(i).start()
        if i > 0:
            reduce_block(i - 1)
        db = dot(hb, wd_v[...]).astype(bf16)
        dpart_ref[b, 0] = db[:ROWS]
        dpart_ref[b, 1] = db[ROWS:]

    def x_copy(which, s):
        tx, rx = (glu_tx, glu_rx) if which < 2 else (down_tx, down_rx)
        if which < 2:
            src, dst = tx.at[others[s], which], rx.at[group, which]
        else:
            src, dst = tx.at[others[s]], rx.at[group]
        return rcopy(src, dst, s_x.at[which, s], r_x.at[which, s], tpeers[s])

    def x_own(which):
        if which < 2:
            return pltpu.make_async_copy(
                glu_tx.at[group, which], glu_rx.at[group, which], l_x.at[which]
            )
        return pltpu.make_async_copy(down_tx.at[group], down_rx.at[group], l_x.at[which])

    def flat(ref):
        return ref[...].reshape(8 * ROWS, ref.shape[-1])

    def glu_grads(which):
        prod = lead_sum(flat((gg, gu)[which]), flat(normed)).astype(bf16)
        for mm in range(M):
            for ff in range(2):
                glu_tx[mm * 2 + ff, which] = prod[
                    mm * seg : (mm + 1) * seg, ff * half_width : (ff + 1) * half_width
                ]
        for s in range(T - 1):
            x_copy(which, s).start()
        x_own(which).start()

    def down_grads():
        prod = lead_sum(flat(hid), flat(c_v))
        for mm in range(M):
            for ff in range(2):
                down_tx[mm * 2 + ff] = jnp.concatenate(
                    [
                        prod[:, blk * each : (blk + 1) * each]
                        for zl in range(2)
                        for cc in range(2)
                        for blk in [(2 * ff + zl) * 2 * M + mm * 2 + cc]
                    ],
                    axis=1,
                ).astype(bf16)
        for s in range(T - 1):
            x_copy(2, s).start()
        x_own(2).start()

    glu_grads(0)

    p_copy(3).wait_recv()
    dy = p_out[3, core].astype(f32) + p_sib[3].astype(f32)
    for i in range(3):
        rs_copy(i).wait_recv()
        dy = dy + p_rx[i].astype(f32)
    mid = mid_b[core]
    r = lax.rsqrt(jnp.mean(mid * mid, axis=-1, keepdims=True) + epsilon)
    gdy = gain * dy
    dv = r * gdy - mid * (r * r * r) * jnp.mean(mid * gdy, axis=-1, keepdims=True)
    gmid = own_c_ref[...].astype(f32) + dv
    gmid_ref[...] = gmid
    mid_ref[...] = mid
    gpart_ref[...] = jnp.sum(dy * mid * r, axis=0, keepdims=True)
    br_own[...] = gmid.astype(bf16)
    branch_ref[me] = br_own[...]

    def br_copy(k):
        if k < 3:
            return rcopy(br_own, branch_ref.at[me], s_br.at[k], r_br.at[k], zpeers[k])
        j = me if k == 3 else slot((z + 3 - (k - 4)) % 4, core)
        return rcopy(
            br_own if k == 3 else branch_ref.at[j], branch_ref.at[j], s_br.at[k], r_br.at[k], sib
        )

    for k in (1, 0, 2, 3):
        br_copy(k).start()
    glu_grads(1)
    down_grads()
    for k in range(3):
        br_copy(k).wait_recv()
        br_copy(k + 4).start()
    for k in range(3, 7):
        br_copy(k).wait_recv()
    for which in range(3):
        x_own(which).wait()
        for s in range(T - 1):
            x_copy(which, s).wait_recv()
    for i in range(4):
        for s in range(3):
            send_att(s, i).wait_send()
        for k in range(4):
            sib_att(k, i).wait_send()
        p_copy(i).wait_send()
    for i in range(3):
        rs_copy(i).wait_send()
    for k in range(7):
        br_copy(k).wait_send()
    for which in range(3):
        for s in range(T - 1):
            x_copy(which, s).wait_send()


def feed_forward(att, x_all, c_all, own_c, own_weights, got_weights, gain, cid):
    n = lax.axis_size("ctx")
    T, seg, each = n // 4, FF // n, WIDTH // n
    cols = FF // 8
    half_width = WIDTH // 2
    VS, sem = pltpu.VMEM, pltpu.SemaphoreType.DMA
    shape = jax.ShapeDtypeStruct
    return pl.pallas_call(
        ffn_kernel,
        out_shape=(
            shape((4, BLOCK, WIDTH), bf16),
            shape((8, ROWS, WIDTH), bf16),
            shape((ROWS, WIDTH), f32),
            shape((ROWS, WIDTH), f32),
            shape((4, 2, ROWS, WIDTH), bf16),
            shape((1, WIDTH), f32),
            shape((T, 2, seg, half_width), bf16),
            shape((T, cols, 4 * each), bf16),
        ),
        in_specs=vspecs(1) + any_specs(2) + vspecs(1) + any_specs(8) + vspecs(1),
        out_specs=tuple(vspecs(8)),
        scratch_shapes=[
            VS((4, BLOCK, WIDTH), bf16),
            VS((4, BLOCK, WIDTH), bf16),
            VS((WIDTH, WIDTH), bf16),
            VS((WIDTH, cols), bf16),
            VS((WIDTH, cols), bf16),
            VS((cols, WIDTH), bf16),
            VS((4, BLOCK, WIDTH), bf16),
            VS((4, BLOCK, cols), bf16),
            VS((4, BLOCK, cols), bf16),
            VS((4, BLOCK, cols), bf16),
            VS((2, ROWS, WIDTH), f32),
            VS((4, 2, ROWS, WIDTH), bf16),
            VS((4, ROWS, WIDTH), bf16),
            VS((3, ROWS, WIDTH), bf16),
            VS((3, ROWS, WIDTH), bf16),
            VS((T, 2, seg, half_width), bf16),
            VS((T, cols, 4 * each), bf16),
            VS((ROWS, WIDTH), bf16),
            sem((9,)),
            sem((3, 4)),
            sem((3, 4)),
            sem((4, 4)),
            sem((4, 4)),
            sem((7,)),
            sem((7,)),
            sem((7,)),
            sem((7,)),
            sem((3, T - 1)),
            sem((3, T - 1)),
            sem((3,)),
        ],
        compiler_params=pltpu.CompilerParams(
            collective_id=cid, has_side_effects=True, vmem_limit_bytes=60 * 2**20
        ),
        name="feed_forward",
    )(att, x_all, c_all, own_c, *own_weights, *got_weights, gain)


def back_kernel(
    doc_ref, branch_ref, att_ref, wo_own, wo_got, q_rows, kv_all, summed, totals, stacked, cosine, sine,
    normed, w_heads, dpart, mid_ref, gmid_ref, x_ref, again_ref, qgain_ref, kgain_ref, fpart_ref,
    out_ref, igrad_ref, gains_ref, heads_ref, attn_ref,
    wo_v, g_v, delta_v, dq_v, dkv_acc, dkv_tx, dkv_rx, gs_v,
    d_sib, d_sum, d_rx, p_part, p_sib, p_sum, p_rx, h_tx, h_rx, a_tx, a_rx, gn_tx, gn_rx, gt_tx, gt_rx,
    ld, s_d, r_d, s_p, r_p, s_k, r_k, s_h, r_h, l_h, s_a, r_a, l_a, s_g, r_g, s_t, r_t,
):
    z, m, core, f = who()
    M = lax.axis_size("ctx") // 8
    T = 2 * M
    span = lax.axis_size("ctx") // 4 * ROWS
    each = WIDTH // lax.axis_size("ctx")
    half_width = WIDTH // 2
    sib = dev(z, m, 1 - core, f)
    zs = [(z + s) % 4 for s in (1, 2, 3)]
    zpeers = [dev(zz, m, core, f) for zz in zs]
    cross = [dev(zz, m, 1 - core, f) for zz in zs]
    mpeers = [dev(z, (m + s) % M, core, f) for s in range(1, M)]
    group = m * 2 + f
    others = [(group + s) % T for s in range(1, T)]
    tpeers = [dev(z, o // 2, core, o % 2) for o in others]
    owner = f == z // 2
    head = slot(z, core)
    me = head

    pieces = [(group + s) % T for s in range(T)]
    rest_to = [core * M + p // 2 for p in pieces]
    piece_to = [dev(z, rr // 2, rr % 2, p % 2) for rr, p in zip(rest_to, pieces)]
    to_self = [(rr == m * 2 + core) & (p % 2 == f) for rr, p in zip(rest_to, pieces)]
    rest = m * 2 + core
    core_from = rest // M
    sources = [(group + s) % T for s in range(T)]
    piece_from = [dev(z, o // 2, core_from, o % 2) for o in sources]
    from_self = [(core_from == core) & (o == group) for o in sources]

    cp_own = pltpu.make_async_copy(
        wo_own.at[pl.ds(pl.multiple_of(head % 4 * 128, 128), 128)], wo_v, ld.at[0]
    )
    cp_got = pltpu.make_async_copy(
        wo_got.at[pl.ds(pl.multiple_of(head % 4 * 128, 128), 128)], wo_v, ld.at[0]
    )

    @pl.when(owner)
    def _():
        cp_own.start()

    @pl.when(jnp.logical_not(owner))
    def _():
        cp_got.start()

    bar = pltpu.get_barrier_semaphore()
    fixed = [sib] + zpeers + cross + tpeers
    for p in fixed:
        pl.semaphore_signal(bar, inc=1, device_id=p, device_id_type=MESH)
    for s in range(T):

        @pl.when(jnp.logical_not(from_self[s]))
        def _(s=s):
            pl.semaphore_signal(bar, inc=1, device_id=piece_from[s], device_id_type=MESH)

    pl.semaphore_wait(bar, len(fixed) + T - jnp.where(core_from == core, 1, 0))

    def sib_copy(part, buf, ss, rs, i):
        b = (z + 1 + i) % 4
        return rcopy(part.at[b, 1 - core], buf.at[i], ss.at[i], rs.at[i], sib)

    def z_copy(sums, rx, ss, rs, i):
        return rcopy(sums.at[i], rx.at[i], ss.at[4 + i], rs.at[4 + i], zpeers[i])

    def pass_on(part, buf, sums, rx, ss, rs, i):
        sib_copy(part, buf, ss, rs, i).wait_recv()
        b = (z + 1 + i) % 4
        sums[i] = (part[b, core].astype(f32) + buf[i].astype(f32)).astype(bf16)
        z_copy(sums, rx, ss, rs, i).start()

    def total_of(part, buf, rx, sums, ss, rs):
        sib_copy(part, buf, ss, rs, 3).wait_recv()
        total = part[z, core].astype(f32) + buf[3].astype(f32)
        for i in range(3):
            z_copy(sums, rx, ss, rs, i).wait_recv()
            total = total + rx[i].astype(f32)
        return total

    D = (dpart, d_sib, d_sum, d_rx, s_d, r_d)
    for i in range(4):
        sib_copy(dpart, d_sib, s_d, r_d, i).start()

    @pl.when(owner)
    def _():
        cp_own.wait()

    @pl.when(jnp.logical_not(owner))
    def _():
        cp_got.wait()

    def block_rows(b):
        return pl.ds(pl.multiple_of(b * BLOCK, BLOCK), BLOCK)

    def mixed(b, _):
        rows = block_rows(b)
        br = jnp.concatenate([branch_ref[2 * b], branch_ref[2 * b + 1]], axis=0)
        gm = back_product(br, wo_v[...])
        inv = 1.0 / totals[rows, :]
        g_v[rows, :] = (gm * inv).astype(bf16)
        w = gm * summed[rows, :] * (inv * inv)
        low = lax.broadcasted_iota(jnp.int32, w.shape, 1) < 64
        a = jnp.sum(jnp.where(low, w, 0.0), axis=1, keepdims=True)
        c = jnp.sum(jnp.where(low, 0.0, w), axis=1, keepdims=True)
        delta_v[rows, :] = jnp.where(low, a, c)
        return 0

    lax.fori_loop(0, 4, mixed, 0)
    for i in range(3):
        pass_on(*D[:4], s_d, r_d, i)

    dq_v[...] = jnp.zeros_like(dq_v)

    def kv_copy(s):
        return rcopy(dkv_tx.at[s], dkv_rx.at[s], s_k.at[s], r_k.at[s], mpeers[s])

    def attend(s, _):
        mm = (m + 1 + s) % M
        dkv_acc[...] = jnp.zeros_like(dkv_acc)
        for zz in range(4):
            rows = slice(zz * BLOCK, (zz + 1) * BLOCK)
            keys = (zz + 1) * BLOCK
            token = zz * span + m * BLOCK + lax.broadcasted_iota(jnp.int32, (BLOCK, 1), 0)
            begin = begin_of(token, doc_ref)
            for h in range(2):
                lanes = slice(h * 64, h * 64 + 64)
                q = q_rows[rows, lanes]
                g = g_v[rows, lanes]
                k = kv_all[mm, :keys, :64]
                v = kv_all[mm, :keys, 64:]
                e = block_weights(q, k, begin, zz, m, mm, span)
                dp = back_product(g, v)
                ds = (e * (dp - delta_v[rows, h * 64 : h * 64 + 1])).astype(bf16)
                dq_v[rows, lanes] += dot(ds, k)
                dkv_acc[:keys, :64] += lead_sum(ds, q)
                dkv_acc[:keys, 64:] += lead_sum(e.astype(bf16), g)

        @pl.when(s < M - 1)
        def _():
            dkv_tx[s] = dkv_acc[...].astype(bf16)

            for ss in range(M - 1):

                @pl.when(s == ss)
                def _(ss=ss):
                    kv_copy(ss).start()

        return 0

    lax.fori_loop(0, M, attend, 0)

    strip = jnp.concatenate(
        [branch_ref[j, :, pl.ds(pl.multiple_of(z * 256, 128), 256)] for j in range(8)], axis=0
    )
    strip = jnp.concatenate(
        [
            jnp.where(
                core == 0,
                strip[:, 2 * mm * each : (2 * mm + 1) * each],
                strip[:, (2 * mm + 1) * each : (2 * mm + 2) * each],
            )
            for mm in range(M)
        ],
        axis=1,
    )
    prod = lead_sum(att_ref[...].reshape(8 * ROWS, WIDTH), strip).astype(bf16)
    for mm in range(M):
        for ff in range(2):
            a_tx[mm * 2 + ff] = prod[
                ff * half_width : (ff + 1) * half_width, mm * each : (mm + 1) * each
            ]

    def a_copy(s):
        return rcopy(a_tx.at[others[s]], a_rx.at[group], s_a.at[s], r_a.at[s], tpeers[s])

    for s in range(M - 1):
        kv_copy(s).wait_recv()
    for s in range(T - 1):
        a_copy(s).start()
    a_own = pltpu.make_async_copy(a_tx.at[group], a_rx.at[group], l_a.at[0])
    a_own.start()

    qgain = qgain_ref[...]
    kgain = kgain_ref[...]

    def head_mean(v):
        low = lax.broadcasted_iota(jnp.int32, v.shape, 1) < 64
        a = jnp.sum(jnp.where(low, v, 0.0), axis=1, keepdims=True)
        c = jnp.sum(jnp.where(low, 0.0, v), axis=1, keepdims=True)
        return jnp.where(low, a, c) * (1.0 / 64)

    def heads_back(i, carry):
        qg, kg = carry
        b = (z + 1 + i) % 4
        rows = block_rows(b)
        co = cosine[rows, :]
        si = sine[rows, :]

        def through(v, dy, gain):
            dy = dy * co - turn(dy) * si
            r = head_scale(v)
            gdy = gain * dy
            dv = r * gdy - v * (r * r * r) * head_mean(v * gdy)
            return dv, jnp.sum(dy * v * r, axis=0, keepdims=True)

        st = stacked[rows, :]
        dq, qpart = through(st[:, :128], dq_v[rows, :] * HEAD_SIZE ** (-0.5), qgain)
        dkv = dkv_acc[rows, :]
        for s in range(M - 1):
            dkv = dkv + dkv_rx[s, rows, :].astype(f32)
        dk, kpart = through(st[:, 128:], dkv, kgain)
        low = lax.broadcasted_iota(jnp.int32, dkv.shape, 1) < 64
        gs = jnp.concatenate([dq, jnp.where(low, dk, dkv)], axis=1).astype(bf16)
        gs_v[rows, :] = gs
        pb = back_product(gs, w_heads[...]).astype(bf16)
        p_part[b, 0] = pb[:ROWS]
        p_part[b, 1] = pb[ROWS:]
        sib_copy(p_part, p_sib, s_p, r_p, i).start()
        return qg + qpart, kg + kpart

    zero = jnp.zeros((1, 128), f32)
    qg, kg = lax.fori_loop(0, 4, heads_back, (zero, zero))
    for i in range(3):
        pass_on(p_part, p_sib, p_sum, p_rx, s_p, r_p, i)

    prod = lead_sum(normed[...], gs_v[...]).astype(bf16)
    qw, kw = 128 // M, 64 // M
    for i in range(M):
        for ff in range(2):
            rows = slice(ff * half_width, (ff + 1) * half_width)
            h_tx[i * 2 + ff] = jnp.concatenate(
                [
                    prod[rows, i * qw : (i + 1) * qw],
                    prod[rows, 128 + i * kw : 128 + (i + 1) * kw],
                    prod[rows, 192 + i * kw : 192 + (i + 1) * kw],
                ],
                axis=1,
            )

    def h_copy(s):
        return rcopy(
            h_tx.at[pieces[s]], h_rx.at[group], s_h.at[s], r_h.at[group], piece_to[s]
        )

    def h_own(s):
        return pltpu.make_async_copy(h_tx.at[pieces[s]], h_rx.at[group], l_h.at[0])

    def h_got(s):
        return rcopy(
            h_tx.at[pieces[s]], h_rx.at[sources[s]], s_h.at[s], r_h.at[sources[s]], piece_from[s]
        )

    for s in range(T):

        @pl.when(to_self[s])
        def _(s=s):
            h_own(s).start()

        @pl.when(jnp.logical_not(to_self[s]))
        def _(s=s):
            h_copy(s).start()

    out_ref[...] = mid_ref[...] + total_of(dpart, d_sib, d_rx, d_sum, s_d, r_d)
    dy = total_of(p_part, p_sib, p_rx, p_sum, s_p, r_p)
    x = x_ref[...].astype(f32)
    r = lax.rsqrt(jnp.mean(x * x, axis=-1, keepdims=True) + epsilon)
    gdy = again_ref[...] * dy
    dv = r * gdy - x * (r * r * r) * jnp.mean(x * gdy, axis=-1, keepdims=True)
    igrad_ref[...] = gmid_ref[...] + dv

    gn_tx[0:1, :] = jnp.sum(dy * x * r, axis=0, keepdims=True)
    gn_tx[1:2, :] = fpart_ref[...]
    gn_tx[2:3, :] = jnp.concatenate(
        [qg, kg, jnp.zeros((1, WIDTH - 256), f32)], axis=1
    )
    gpeers = [sib] + zpeers + cross

    def g_copy(k):
        return rcopy(gn_tx, gn_rx.at[k], s_g.at[k], r_g.at[k], gpeers[k])

    for k in range(7):
        g_copy(k).start()
    total = gn_tx[...]
    for k in range(7):
        g_copy(k).wait_recv()
    for k in range(7):
        total = total + gn_rx[k]
    gt_tx[...] = total

    def t_copy(s):
        return rcopy(gt_tx, gt_rx.at[s], s_t.at[s], r_t.at[s], tpeers[s])

    for s in range(T - 1):
        t_copy(s).start()

    for s in range(T):

        @pl.when(from_self[s])
        def _(s=s):
            pltpu.make_async_copy(h_tx.at[0], h_rx.at[group], l_h.at[0]).wait()

        @pl.when(jnp.logical_not(from_self[s]))
        def _(s=s):
            h_got(s).wait_recv()

    for s in range(T - 1):
        a_copy(s).wait_recv()
    a_own.wait()
    hsum = h_rx[0].astype(f32)
    asum = a_rx[0].astype(f32)
    for k in range(1, T):
        hsum = hsum + h_rx[k].astype(f32)
        asum = asum + a_rx[k].astype(f32)
    heads_ref[...] = hsum
    attn_ref[...] = asum

    for s in range(T - 1):
        t_copy(s).wait_recv()
        total = total + gt_rx[s]
    gains_ref[...] = total

    for i in range(4):
        sib_copy(dpart, d_sib, s_d, r_d, i).wait_send()
        sib_copy(p_part, p_sib, s_p, r_p, i).wait_send()
    for i in range(3):
        z_copy(d_sum, d_rx, s_d, r_d, i).wait_send()
        z_copy(p_sum, p_rx, s_p, r_p, i).wait_send()
    for s in range(M - 1):
        kv_copy(s).wait_send()
    for s in range(T):

        @pl.when(jnp.logical_not(to_self[s]))
        def _(s=s):
            h_copy(s).wait_send()

    for s in range(T - 1):
        a_copy(s).wait_send()
        t_copy(s).wait_send()
    for k in range(7):
        g_copy(k).wait_send()


def back(*args, cid):
    n = lax.axis_size("ctx")
    M, T, each = n // 8, n // 4, WIDTH // n
    tokens = 8 * ROWS
    half_width = WIDTH // 2
    VS, sem = pltpu.VMEM, pltpu.SemaphoreType.DMA
    shape = jax.ShapeDtypeStruct
    part = (ROWS, WIDTH)
    return pl.pallas_call(
        back_kernel,
        out_shape=(
            shape(part, f32),
            shape(part, f32),
            shape((3, WIDTH), f32),
            shape((half_width, 256 // M), f32),
            shape((half_width, each), f32),
        ),
        in_specs=[pl.BlockSpec(memory_space=pltpu.SMEM)] + vspecs(2) + any_specs(2) + vspecs(17),
        out_specs=tuple(vspecs(5)),
        scratch_shapes=[
            VS((128, WIDTH), bf16),
            VS((tokens, 128), bf16),
            VS((tokens, 128), f32),
            VS((tokens, 128), f32),
            VS((tokens, 128), f32),
            VS((M - 1, tokens, 128), bf16),
            VS((M - 1, tokens, 128), bf16),
            VS((tokens, 256), bf16),
            VS((4,) + part, bf16),
            VS((3,) + part, bf16),
            VS((3,) + part, bf16),
            VS((4, 2) + part, bf16),
            VS((4,) + part, bf16),
            VS((3,) + part, bf16),
            VS((3,) + part, bf16),
            VS((T, half_width, 256 // M), bf16),
            VS((T, half_width, 256 // M), bf16),
            VS((T, half_width, each), bf16),
            VS((T, half_width, each), bf16),
            VS((3, WIDTH), f32),
            VS((7, 3, WIDTH), f32),
            VS((3, WIDTH), f32),
            VS((T - 1, 3, WIDTH), f32),
            sem((1,)),
            sem((7,)), sem((7,)), sem((7,)), sem((7,)),
            sem((M - 1,)), sem((M - 1,)),
            sem((T,)), sem((T,)), sem((1,)),
            sem((T - 1,)), sem((T - 1,)), sem((1,)),
            sem((7,)), sem((7,)),
            sem((T - 1,)), sem((T - 1,)),
        ],
        compiler_params=pltpu.CompilerParams(
            collective_id=cid, has_side_effects=True, vmem_limit_bytes=60 * 2**20
        ),
        name="back",
    )(*args)


def root_mean_norm(rows, gain):
    return (
        rows * lax.rsqrt(jnp.mean(rows * rows, axis=-1, keepdims=True) + epsilon) * gain
    )


def rotary(rows, cosine, sine):
    halfway = rows.shape[-1] // 2
    leading = rows[..., :halfway]
    trailing = rows[..., halfway:]
    return jnp.concatenate(
        [leading * cosine - trailing * sine, leading * sine + trailing * cosine], axis=-1
    )


SWAP = [(0, 1), (1, 0)]


def halves(f, own, other, axis):
    return jnp.where(
        f == 0,
        jnp.concatenate([own, other], axis=axis),
        jnp.concatenate([other, own], axis=axis),
    )


def local(
    hidden_in,
    doc_lengths,
    attn_gain,
    query_gain,
    key_norm_gain,
    ffn_gain,
    query_proj,
    key_weight,
    value_weight,
    attn_proj,
    gate_proj,
    up_proj,
    down_proj,
    out_cotangent,
):
    n_ctx = lax.axis_size("ctx")
    M = n_ctx // 8
    T = 2 * M
    z, m, core, f = who()
    head = slot(z, core)
    tokens = 8 * ROWS
    span = n_ctx // 4 * ROWS
    segment = FF // n_ctx
    columns = M * segment
    half_width = WIDTH // 2
    each = WIDTH // n_ctx

    heads_own = jnp.concatenate(
        [
            lax.dynamic_slice(query_proj, (0, head * 128), (half_width, 128)),
            lax.dynamic_slice(key_weight, (0, head * 64), (half_width, 64)),
            lax.dynamic_slice(value_weight, (0, head * 64), (half_width, 64)),
        ],
        axis=1,
    ).astype(bf16)
    first = z * (n_ctx // 4) + core
    gate_own, up_own = [
        jnp.concatenate(
            [
                lax.dynamic_slice(w, (0, (first + 2 * mm) * segment), (half_width, segment))
                for mm in range(M)
            ],
            axis=1,
        ).astype(bf16)
        for w in (gate_proj, up_proj)
    ]
    down_own = jnp.concatenate(
        [
            lax.dynamic_slice(
                down_proj, ((first + 2 * mm) * segment - f * (FF // 2), 0), (segment, WIDTH)
            )
            for mm in range(M)
        ],
        axis=0,
    ).astype(bf16)
    out_own = attn_proj.astype(bf16)

    cotangent = out_cotangent[0]
    q_gain = jnp.tile(query_gain, 2)[None]
    k_gain = jnp.concatenate([key_norm_gain, jnp.ones((64,), f32)])[None]
    (
        x_rows, c_rows, w_heads, w_gate, w_up, w_down, w_out, q_rows, kv_all, att_own, summed, totals,
        stacked, normed, cos_table, sin_table,
    ) = front(
        doc_lengths,
        hidden_in[0],
        cotangent,
        heads_own,
        gate_own,
        up_own,
        down_own,
        out_own,
        attn_gain[None],
        q_gain,
        k_gain,
        1,
    )
    attended, branch, grad_middle, own, down_parts, ffn_gain_part, glu_got, down_got = feed_forward(
        att_own,
        x_rows.reshape(4, BLOCK, WIDTH),
        c_rows.reshape(4, BLOCK, WIDTH),
        cotangent,
        (out_own, gate_own, up_own, down_own),
        (w_out, w_gate, w_up, w_down),
        ffn_gain[None],
        4,
    )
    output, input_grad, gains, heads_grad, attn_grad = back(
        doc_lengths,
        branch,
        attended,
        out_own,
        w_out,
        q_rows,
        kv_all,
        summed,
        totals,
        stacked,
        cos_table,
        sin_table,
        normed,
        w_heads,
        down_parts,
        own,
        grad_middle,
        hidden_in[0],
        attn_gain[None],
        q_gain,
        k_gain,
        ffn_gain_part,
        cid=7,
    )

    glu_grad = jnp.sum(glu_got.astype(f32), axis=0)
    down_sum = jnp.sum(down_got.astype(f32), axis=0)
    gate_grad = jnp.transpose(glu_grad[0])
    up_grad = jnp.transpose(glu_grad[1])

    devices = [
        (zz, mm, cc, ff) for zz in range(4) for mm in range(M) for cc in range(2) for ff in range(2)
    ]

    def number(zz, mm, cc, ff):
        return (zz * (n_ctx // 4) + mm * 2 + cc) * 2 + ff

    down_pieces = down_sum.reshape(columns, 2, 2, each)
    rounds = []
    for dz in range(2):
        for dc in range(2):
            piece = lax.dynamic_slice(
                down_pieces, (0, (z + dz) % 2, (core + dc) % 2, 0), (columns, 1, 1, each)
            ).reshape(columns, each)
            perm = [
                (number(zz, mm, cc, ff), number(2 * ff + (zz + dz) % 2, mm, (cc + dc) % 2, zz // 2))
                for zz, mm, cc, ff in devices
            ]
            rounds.append(lax.ppermute(piece, ("ctx", "fsdp"), perm))
    rounds = jnp.stack(rounds).reshape(2, 2, columns, each)
    rounds = jnp.where(z % 2 == 0, rounds, rounds[::-1])
    rounds = jnp.where(core == 0, rounds, rounds[:, ::-1])
    down_grad = jnp.transpose(
        rounds.reshape(2, 2, M, segment, each), (0, 2, 1, 3, 4)
    ).reshape(FF // 2, each)

    qw, kw = 128 // M, 64 // M
    query_grad = heads_grad[:, :qw]
    key_grad = heads_grad[:, qw : qw + kw]
    value_grad = heads_grad[:, qw + kw :]

    return (
        output[None],
        input_grad[None],
        gains[0],
        gains[2, :64] + gains[2, 64:128],
        gains[2, 128:192],
        gains[1],
        query_grad,
        key_grad,
        value_grad,
        attn_grad,
        gate_grad,
        up_grad,
        down_grad,
    )


def solution(mesh):
    in_specs = (
        P("fsdp", "ctx", None),
        P("fsdp", None),
        P(),
        P(),
        P(),
        P(),
        P("fsdp", None),
        P("fsdp", None),
        P("fsdp", None),
        P("fsdp", None),
        P("fsdp", None),
        P("fsdp", None),
        P("fsdp", None),
        P("fsdp", "ctx", None),
    )
    out_specs = (
        P("fsdp", "ctx", None),
        P("fsdp", "ctx", None),
        P(),
        P(),
        P(),
        P(),
        P("fsdp", "ctx"),
        P("fsdp", "ctx"),
        P("fsdp", "ctx"),
        P("fsdp", "ctx"),
        P("fsdp", "ctx"),
        P("fsdp", "ctx"),
        P("fsdp", "ctx"),
    )
    return jax.shard_map(local, mesh=mesh, in_specs=in_specs, out_specs=out_specs, check_vma=False)
```

```python
import functools
import math

import jax
import jax.numpy as jnp
from jax import lax
from jax.experimental import pallas as pl
from jax.experimental.pallas import tpu as pltpu
from jax.sharding import PartitionSpec as P

QUERY_HEADS = 16
KEY_VALUE_HEADS = 8
HEAD_SIZE = 64
FF = 4608
WIDTH = 1024
ROWS = 128

epsilon = 1e-05
rope_base = 1000000.0
MESH = pl.DeviceIdType.MESH
ANY = pl.ANY
bf16 = jnp.bfloat16
f32 = jnp.float32


def who():
    n = lax.axis_size("ctx")
    c = lax.axis_index("ctx")
    f = lax.axis_index("fsdp")
    q = n // 4
    return c // q, (c % q) // 2, c % 2, f


def dev(z, m, core, f):
    return (z * (lax.axis_size("ctx") // 4) + m * 2 + core, f)


def slot(z, core):
    return z * 2 + core


def enter(peers):
    bar = pltpu.get_barrier_semaphore()
    for p in peers:
        pl.semaphore_signal(bar, inc=1, device_id=p, device_id_type=MESH)
    pl.semaphore_wait(bar, len(peers))


def rcopy(src, dst, s, r, to):
    return pltpu.make_async_remote_copy(
        src_ref=src, dst_ref=dst, send_sem=s, recv_sem=r, device_id=to, device_id_type=MESH
    )


def comm_params(cid):
    return pltpu.CompilerParams(collective_id=cid, has_side_effects=True)


def any_specs(n):
    return [pl.BlockSpec(memory_space=ANY)] * n


def line_of(z):
    return z + 1 - 2 * (z % 2), 2 - z // 2, 3 - 3 * (z // 2), 1 - ((z + 1) // 2) % 2


def packed(v):
    rows, cols = v.shape
    n = 128 // cols
    size = rows // n
    return jnp.concatenate([v[g * size : (g + 1) * size] for g in range(n)], axis=1)


class Gather:
    def __init__(self, src, dst, ss, rs):
        z, m, core, f = who()
        partner, middle, end, self.at_end = line_of(z)
        self.src, self.dst, self.ss, self.rs = src, dst, ss, rs
        self.me = slot(z, core)
        self.slots = [slot(zz, core) for zz in (partner, middle, end)]
        self.partner = dev(partner, m, core, f)
        self.middle = dev(middle, m, core, f)
        self.sib = dev(z, m, 1 - core, f)

    def copy(self, k):
        src, dst, ss, rs = self.src, self.dst, self.ss.at[k], self.rs
        if k == 0:
            return rcopy(src, dst.at[self.me], ss, rs.at[0], self.partner)
        if k == 1:
            return rcopy(src, dst.at[self.me], ss, rs.at[1 + self.at_end], self.middle)
        if k == 3:
            return rcopy(src, dst.at[self.me], ss, rs.at[3], self.sib)
        if k < 7:
            j = self.slots[k - 4]
            return rcopy(dst.at[j], dst.at[j], ss, rs.at[k], self.sib)
        j = self.slots[k - 6]
        return rcopy(dst.at[j], dst.at[j], ss, rs.at[k - 6], self.partner)

    def own(self):
        for k in (1, 0, 3):
            self.copy(k).start()

    def take(self, kind):
        j = self.slots[kind]
        rcopy(
            self.dst.at[j], self.dst.at[j], self.ss.at[0], self.rs.at[kind], self.partner
        ).wait_recv()
        if kind > 0:

            @pl.when(self.at_end == 0)
            def _():
                self.copy(6 + kind).start()

        self.copy(4 + kind).start()

    def rest(self):
        for k in range(3, 7):
            self.copy(k).wait_recv()

    def sent(self):
        for k in (0, 1, 3, 4, 5, 6):
            self.copy(k).wait_send()

        @pl.when(self.at_end == 0)
        def _():
            self.copy(7).wait_send()
            self.copy(8).wait_send()


class Scatter:
    def __init__(self, part, buf, sums, relay, rx, ss, rs):
        z, m, self.core, f = who()
        core = self.core
        partner, middle, end, self.at_end = line_of(z)
        self.z = z
        self.part, self.buf, self.sums, self.relay_buf, self.rx = part, buf, sums, relay, rx
        self.ss, self.rs = ss, rs
        self.order = [end, middle, partner, z]
        self.sib = dev(z, m, 1 - core, f)
        self.to = [dev(zz, m, core, f) for zz in self.order[:3]]

    def sibling(self, i):
        return rcopy(
            self.part.at[self.order[i], 1 - self.core],
            self.buf.at[i],
            self.ss.at[i],
            self.rs.at[i],
            self.sib,
        )

    def copy(self, i, at_end):
        if i == 2:
            return rcopy(
                self.sums.at[2], self.rx.at[0], self.ss.at[6], self.rs.at[4], self.to[2]
            )
        if at_end:
            return rcopy(
                self.sums.at[i], self.relay_buf.at[i], self.ss.at[4 + i], self.rs.at[6 + i], self.to[2]
            )
        return rcopy(self.sums.at[i], self.rx.at[1], self.ss.at[4 + i], self.rs.at[5], self.to[i])

    def pass_on(self, i):
        self.sibling(i).wait_recv()
        self.sums[i] = (
            self.part[self.order[i], self.core].astype(f32) + self.buf[i].astype(f32)
        ).astype(bf16)
        if i == 2:
            self.copy(2, True).start()
        else:

            @pl.when(self.at_end == 1)
            def _():
                self.copy(i, True).start()

    def relay(self, i):
        @pl.when(self.at_end == 0)
        def _():
            self.copy(i, True).wait_recv()
            self.sums[i] = (
                self.sums[i].astype(f32) + self.relay_buf[i].astype(f32)
            ).astype(bf16)
            self.copy(i, False).start()

    def total(self):
        self.sibling(3).wait_recv()
        total = self.part[self.z, self.core].astype(f32) + self.buf[3].astype(f32)
        self.copy(2, True).wait_recv()
        total = total + self.rx[0].astype(f32)
        self.copy(0, False).wait_recv()
        return total + self.rx[1].astype(f32)

    def sent(self):
        for i in range(4):
            self.sibling(i).wait_send()
        for i in range(3):
            self.copy(i, False).wait_send()


def scatter_scratch():
    part = (ROWS, WIDTH)
    return [
        pltpu.VMEM((4,) + part, bf16),
        pltpu.VMEM((3,) + part, bf16),
        pltpu.VMEM((2,) + part, bf16),
        pltpu.VMEM((2,) + part, bf16),
        pltpu.SemaphoreType.DMA((7,)),
        pltpu.SemaphoreType.DMA((8,)),
    ]


def back_product(left, right):
    return lax.dot_general(
        left, right, (((1,), (1,)), ((), ())), preferred_element_type=f32
    )


def lead_sum(left, right):
    return lax.dot_general(
        left, right, (((0,), (0,)), ((), ())), preferred_element_type=f32
    )


def dot(left, right):
    return jnp.dot(left, right, preferred_element_type=f32)


BLOCK = 2 * ROWS


def block_weights(q, k, begin, z, m, mm, span):
    keys = (z + 1) * BLOCK
    key = lax.broadcasted_iota(jnp.int32, (1, keys), 1)
    key = key // BLOCK * span + key % BLOCK + mm * BLOCK
    token = z * span + m * BLOCK + lax.broadcasted_iota(jnp.int32, (BLOCK, 1), 0)
    e = jnp.exp(back_product(q, k))
    return jnp.where((key >= begin) & (key <= token), e, 0.0)


VM = pltpu.VMEM


def vspecs(n):
    return [pl.BlockSpec(memory_space=VM)] * n


def begin_of(token, doc_ref):
    begin = jnp.zeros(token.shape, jnp.int32)
    start = doc_ref[0, 0]
    for d in range(1, doc_ref.shape[1]):
        begin = jnp.where(token >= start, start, begin)
        start = start + doc_ref[0, d]
    return begin


def turn(v):
    lane = lax.broadcasted_iota(jnp.int32, v.shape, 1)
    n = v.shape[1]
    return jnp.where(lane % 64 < 32, pltpu.roll(v, n - 32, 1), pltpu.roll(v, 32, 1))


def head_scale(v):
    sq = v * v
    if v.shape[1] == 64:
        return lax.rsqrt(jnp.mean(sq, axis=1, keepdims=True) + epsilon)
    low = lax.broadcasted_iota(jnp.int32, v.shape, 1) < 64
    a = jnp.sum(jnp.where(low, sq, 0.0), axis=1, keepdims=True)
    b = jnp.sum(jnp.where(low, 0.0, sq), axis=1, keepdims=True)
    return lax.rsqrt(jnp.where(low, a, b) * (1.0 / 64) + epsilon)


def front_kernel(
    doc_ref, x_ref, c_ref, wh_ref, wg_hbm, wu_hbm, wd_hbm, wo_hbm, again_ref, qgain_ref, kgain_ref,
    x_all, c_all, w_heads, w_gate, w_up, w_down, w_out, q_rows, kv_all, att, summed, totals,
    stacked, normed, cosine, sine,
    s_x, r_x, s_c, r_c, s_h, r_h, s_w, r_w, s_v, r_v, s_o, r_o, s_k, r_k, l_s,
):
    z, m, core, f = who()
    M = lax.axis_size("ctx") // 8
    span = lax.axis_size("ctx") // 4 * ROWS
    half_width = WIDTH // 2
    sib = dev(z, m, 1 - core, f)
    zpeers = [dev((z + s) % 4, m, core, f) for s in (1, 2, 3)]
    hm = m % 2
    pair = dev(z, m, core, 1 - f)
    beside = dev(z, m + 1 - 2 * hm, core, f)
    mpeers = [dev(z, (m + s) % M, core, f) for s in range(1, M)]
    me = slot(z, core)
    owner = f == z // 2

    stay = pltpu.make_async_copy(c_ref, c_all.at[me], l_s.at[0])
    stay.start()

    enter([sib, pair] + zpeers + mpeers)

    gx = Gather(x_ref, x_all, s_x, r_x)
    gc = Gather(c_ref, c_all, s_c, r_c)
    gx.own()
    head_rows = pl.ds(f * half_width, half_width)
    heads_copy = rcopy(wh_ref, w_heads.at[head_rows], s_h.at[0], r_h.at[0], pair)
    heads_copy.start()

    quarter = half_width // 2
    eighth = half_width // 4
    cols = wd_hbm.shape[0]

    def w_copy(k, stage):
        src, dst = ((wg_hbm, w_gate), (wu_hbm, w_up), (wd_hbm, w_down), (wo_hbm, w_out))[k]
        size = (quarter, quarter, cols // 2, eighth)[k]
        part = hm * 2 + core if k == 3 else hm
        place = dst.at[pl.ds(pl.multiple_of(part * size, 8), size)]
        if stage == 0:
            here = src.at[pl.ds(pl.multiple_of(part * size, 8), size)]
            return rcopy(here, place, s_w.at[k], r_w.at[k], pair)
        return rcopy(place, place, s_v.at[k], r_v.at[k], beside)

    def out_copy(k):
        part = (hm if k == 0 else 1 - hm) * 2 + core
        place = w_out.at[pl.ds(pl.multiple_of(part * eighth, 8), eighth)]
        return rcopy(place, place, s_o.at[k], r_o.at[k], sib)

    @pl.when(owner)
    def _():
        w_copy(2, 0).start()

    w_heads[head_rows] = wh_ref[...]
    x_all[me] = x_ref[...]

    lane = lax.broadcasted_iota(jnp.int32, (1, 128), 1) % 32
    freq = jnp.exp(lane.astype(f32) * (-2.0 / 64 * math.log(rope_base)))
    sign = jnp.where(lax.broadcasted_iota(jnp.int32, (1, 128), 1) % 64 < 32, -1.0, 1.0)

    def tokens_of(zz):
        return zz * span + m * BLOCK + lax.broadcasted_iota(jnp.int32, (BLOCK, 1), 0)

    def table(zz, _):
        rows = pl.ds(pl.multiple_of(zz * BLOCK, BLOCK), BLOCK)
        token = tokens_of(zz)
        place = (token - begin_of(token, doc_ref)).astype(f32)
        angle = place * freq
        cosine[rows, :] = jnp.cos(angle)
        sine[rows, :] = jnp.sin(angle) * sign
        return 0

    lax.fori_loop(0, 4, table, 0)
    for k in (0, 1, 3):
        w_copy(k, 0).start()
    for kind in (0, 1, 2):
        gx.take(kind)
    gc.own()
    heads_copy.wait_recv()

    def kv_copy(b, s):
        rows = pl.ds(pl.multiple_of(b * BLOCK, BLOCK), BLOCK)
        place = kv_all.at[m, rows]
        return rcopy(place, place, s_k.at[b, s], r_k.at[b, s], mpeers[s])

    again = again_ref[...]
    qgain = qgain_ref[...]
    kgain = kgain_ref[...]

    gx.rest()

    def project(b, _):
        rows = pl.ds(pl.multiple_of(b * BLOCK, BLOCK), BLOCK)
        x = jnp.concatenate([x_all[2 * b], x_all[2 * b + 1]], axis=0).astype(f32)
        nb = (
            x * lax.rsqrt(jnp.mean(x * x, axis=-1, keepdims=True) + epsilon) * again
        ).astype(bf16)
        normed[rows, :] = nb
        st = dot(nb, w_heads[...])
        stacked[rows, :] = st
        co = cosine[rows, :]
        si = sine[rows, :]
        q = st[:, :128]
        q = q * head_scale(q) * qgain
        q_rows[rows, :] = ((q * co + turn(q) * si) * HEAD_SIZE ** (-0.5)).astype(bf16)
        kv = st[:, 128:]
        low = lax.broadcasted_iota(jnp.int32, kv.shape, 1) < 64
        k = kv * head_scale(kv) * kgain
        kv_all[m, rows, :] = jnp.where(low, k * co + turn(k) * si, kv).astype(bf16)
        for s in range(M - 1):
            kv_copy(b, s).start()
        return 0

    lax.fori_loop(0, 4, project, 0)

    @pl.when(jnp.logical_not(owner))
    def _():
        w_copy(2, 0).wait_recv()
        w_copy(2, 1).start()

    w_copy(0, 0).wait_recv()
    w_copy(0, 1).start()

    summed[...] = jnp.zeros_like(summed)
    totals[...] = jnp.zeros_like(totals)

    def attend(s, _):
        mm = (m + M - s) % M

        @pl.when(s > 0)
        def _():
            for b in range(4):
                rows = pl.ds(b * BLOCK, BLOCK)
                place = kv_all.at[mm, rows]
                rcopy(place, place, s_k.at[b, s - 1], r_k.at[b, s - 1], sib).wait_recv()

        @pl.when(s == 1)
        def _():
            w_copy(1, 0).wait_recv()
            w_copy(1, 1).start()
            w_copy(3, 0).wait_recv()
            w_copy(3, 1).start()
            out_copy(0).start()

        for zz in range(4):
            rows = slice(zz * BLOCK, (zz + 1) * BLOCK)
            keys = (zz + 1) * BLOCK
            begin = begin_of(tokens_of(zz), doc_ref)
            for h in range(2):
                lanes = slice(h * 64, h * 64 + 64)
                e = block_weights(
                    q_rows[rows, lanes], kv_all[mm, :keys, :64], begin, zz, m, mm, span
                )
                summed[rows, lanes] += dot(e.astype(bf16), kv_all[mm, :keys, 64:])
                totals[rows, lanes] += jnp.broadcast_to(
                    jnp.sum(e, axis=1, keepdims=True), (BLOCK, 64)
                )
        return 0

    lax.fori_loop(0, M, attend, 0)
    for b in range(4):
        rows = slice(b * BLOCK, (b + 1) * BLOCK)
        att[b] = (summed[rows, :] / totals[rows, :]).astype(bf16)

    for kind in (0, 1, 2):
        gc.take(kind)

    def w_got(k):
        dst = (w_gate, w_up, w_down, w_out)[k]
        size = (quarter, quarter, cols // 2, eighth)[k]
        part = (1 - hm) * 2 + core if k == 3 else 1 - hm
        place = dst.at[pl.ds(pl.multiple_of(part * size, 8), size)]
        return rcopy(place, place, s_v.at[k], r_v.at[k], beside)

    w_got(3).wait_recv()
    out_copy(1).start()
    for k in range(2):
        w_got(k).wait_recv()

    @pl.when(jnp.logical_not(owner))
    def _():
        w_got(2).wait_recv()
        w_copy(2, 1).wait_send()

    @pl.when(owner)
    def _():
        w_copy(2, 0).wait_send()

    gc.rest()
    for k in range(2):
        out_copy(k).wait_recv()
    stay.wait()
    heads_copy.wait_send()
    gx.sent()
    gc.sent()
    for k in (0, 1, 3):
        w_copy(k, 0).wait_send()
        w_copy(k, 1).wait_send()
    for k in range(2):
        out_copy(k).wait_send()
    for b in range(4):
        for s in range(M - 1):
            kv_copy(b, s).wait_send()


def front(docs, x, c, wh, wg, wu, wd, wo, again, qgain, kgain, cid):
    n = lax.axis_size("ctx")
    M = n // 8
    cols = FF // 8
    tokens = 8 * ROWS
    sem = pltpu.SemaphoreType.DMA
    shape = jax.ShapeDtypeStruct
    return pl.pallas_call(
        front_kernel,
        out_shape=(
            shape((8, ROWS, WIDTH), bf16),
            shape((8, ROWS, WIDTH), bf16),
            shape((WIDTH, 256), bf16),
            shape((WIDTH // 2, cols), bf16),
            shape((WIDTH // 2, cols), bf16),
            shape((cols, WIDTH), bf16),
            shape((WIDTH // 2, WIDTH), bf16),
            shape((tokens, 128), bf16),
            shape((M, tokens, 128), bf16),
            shape((4, BLOCK, 128), bf16),
            shape((tokens, 128), f32),
            shape((tokens, 128), f32),
            shape((tokens, 256), f32),
            shape((tokens, WIDTH), bf16),
            shape((tokens, 128), f32),
            shape((tokens, 128), f32),
        ),
        in_specs=[pl.BlockSpec(memory_space=pltpu.SMEM)]
        + vspecs(3) + any_specs(4) + vspecs(3),
        out_specs=tuple(vspecs(1) + any_specs(1) + vspecs(1) + any_specs(4) + vspecs(9)),
        scratch_shapes=[
            sem((9,)), sem((7,)), sem((9,)), sem((7,)), sem((1,)), sem((1,)),
            sem((4,)), sem((4,)), sem((4,)), sem((4,)), sem((2,)), sem((2,)),
            sem((4, M - 1)), sem((4, M - 1)), sem((5,)),
        ],
        compiler_params=pltpu.CompilerParams(
            collective_id=cid, has_side_effects=True, vmem_limit_bytes=60 * 2**20
        ),
        name="front",
    )(docs, x, c, wh, wg, wu, wd, wo, again, qgain, kgain)


def ffn_kernel(
    att_ref, x_hbm, c_hbm, own_c_ref, wo_own, wg_own, wu_own, wd_own, wo_got, wg_got, wu_got, wd_got,
    gain_ref,
    att_all, branch_ref, gmid_ref, mid_ref, dpart_ref, gpart_ref, gate_rx, down_rx, up_tx,
    x_v, c_v, wo_v, wg_v, wu_v, wd_v, normed, hid, gg, gu, mid_b, p_out,
    p_sib, p_sum, p_relay, p_rx, s_rs, r_rs,
    gate_tx, down_tx, br_own,
    ld, s_att, r_att, s_pass, s_sib, r_sib, s_br, r_br, s_x, r_x, l_x,
):
    z, m, core, f = who()
    M = lax.axis_size("ctx") // 8
    T = 2 * M
    seg = gate_tx.shape[1]
    each = WIDTH // lax.axis_size("ctx")
    half_width = WIDTH // 2
    sib = dev(z, m, 1 - core, f)
    zs = [(z + s) % 4 for s in (1, 2, 3)]
    zpeers = [dev(zz, m, core, f) for zz in zs]
    group = m * 2 + f
    others = [(group + s) % T for s in range(1, T)]
    tpeers = [dev(z, o // 2, core, o % 2) for o in others]

    mine = pl.ds(pl.multiple_of(f * half_width, half_width), half_width)
    yours = pl.ds(pl.multiple_of((1 - f) * half_width, half_width), half_width)
    loads = [
        pltpu.make_async_copy(a, b, ld.at[k])
        for k, (a, b) in enumerate(
            (
                (wo_own, wo_v.at[mine]),
                (wo_got, wo_v.at[yours]),
                (x_hbm, x_v),
                (wg_own, wg_v.at[mine]),
                (wg_got, wg_v.at[yours]),
                (wu_own, wu_v.at[mine]),
                (wu_got, wu_v.at[yours]),
                (c_hbm, c_v),
            )
        )
    ]
    for cp in loads:
        cp.start()
    owner = f == z // 2

    @pl.when(owner)
    def _():
        pltpu.make_async_copy(wd_own, wd_v, ld.at[8]).start()

    @pl.when(jnp.logical_not(owner))
    def _():
        pltpu.make_async_copy(wd_got, wd_v, ld.at[8]).start()

    loads.append(pltpu.make_async_copy(wd_own, wd_v, ld.at[8]))
    enter([sib] + zpeers + tpeers)

    def lanes(j):
        return pl.ds(pl.multiple_of(j * 128, 128), 128)

    me = slot(z, core)

    partner, middle, end, at_end = line_of(z)
    order = [end, middle, partner, z]
    to_partner = [end, middle, z, partner]
    to_middle = [3 * (z // 2), 1 + z // 2, end, middle]
    from_slot = [slot(zz, core) for zz in (partner, middle, end)]
    to_p, to_m = dev(partner, m, core, f), dev(middle, m, core, f)

    def att_copy(k, i):
        if k == 0:
            b = to_partner[i]
            return rcopy(
                att_ref.at[b], att_all.at[b, :, lanes(me)], s_att.at[0, i], r_att.at[0, i], to_p
            )
        if k == 1:
            b = to_middle[i]
            return rcopy(
                att_ref.at[b],
                att_all.at[b, :, lanes(me)],
                s_att.at[1, i],
                r_att.at[1 + at_end, i],
                to_m,
            )
        place = att_all.at[order[i], :, lanes(from_slot[k - 1])]
        return rcopy(place, place, s_pass.at[k - 2, i], r_att.at[k - 1, (0, 1, 3, 2)[i]], to_p)

    def sib_att(k, i):
        b = order[i]
        j = me if k == 3 else from_slot[k]
        src = att_ref.at[b] if k == 3 else att_all.at[b, :, lanes(j)]
        return rcopy(src, att_all.at[b, :, lanes(j)], s_sib.at[k, i], r_sib.at[k, i], sib)

    for i in range(4):
        att_copy(1, i).start()
        att_copy(0, i).start()
        sib_att(3, i).start()
    for b in range(4):
        att_all[b, :, lanes(me)] = att_ref[b]

    def forward(i):
        for k in range(3):
            place = att_all.at[order[i], :, lanes(from_slot[k])]
            rcopy(place, place, s_att.at[0, i], r_att.at[k, i], to_p).wait_recv()
            if k > 0:

                @pl.when(at_end == 0)
                def _(k=k):
                    att_copy(k + 1, i).start()

            sib_att(k, i).start()

    sc = Scatter(p_out, p_sib, p_sum, p_relay, p_rx, s_rs, r_rs)

    forward(0)
    gain = gain_ref[...]
    for cp in loads:
        cp.wait()
    for i in range(4):
        b = order[i]
        for k in range(4):
            sib_att(k, i).wait_recv()
        mid = x_v[b].astype(f32) + dot(att_all[b], wo_v[...])
        nb = (
            mid * lax.rsqrt(jnp.mean(mid * mid, axis=-1, keepdims=True) + epsilon) * gain
        ).astype(bf16)
        normed[b] = nb
        if i == 3:
            mid_b[0] = mid[:ROWS]
            mid_b[1] = mid[ROWS:]
        for ii in ((1,), (2, 3), (), ())[i]:
            forward(ii)
        gate = dot(nb, wg_v[...])
        up = dot(nb, wu_v[...])
        sig = 1.0 / (1.0 + jnp.exp(-gate))
        silu = gate * sig
        hb = (silu * up).astype(bf16)
        hid[b] = hb
        gh = back_product(c_v[b], wd_v[...])
        ggb = (gh * up * (sig * (1.0 + gate * (1.0 - sig)))).astype(bf16)
        gub = (gh * silu).astype(bf16)
        gg[b] = ggb
        gu[b] = gub
        pb = (back_product(ggb, wg_v[...]) + back_product(gub, wu_v[...])).astype(bf16)
        p_out[b, 0] = pb[:ROWS]
        p_out[b, 1] = pb[ROWS:]
        sc.sibling(i).start()
        if i > 0:
            sc.pass_on(i - 1)
        if i > 1:
            sc.relay(i - 2)
        db = dot(hb, wd_v[...]).astype(bf16)
        dpart_ref[b, 0] = db[:ROWS]
        dpart_ref[b, 1] = db[ROWS:]

    def x_copy(which, s):
        tx, rx = ((gate_tx, gate_rx), (down_tx, down_rx))[which]
        return rcopy(
            tx.at[others[s]], rx.at[group], s_x.at[which, s], r_x.at[which, s], tpeers[s]
        )

    def x_own(which):
        tx, rx = ((gate_tx, gate_rx), (down_tx, down_rx))[which]
        return pltpu.make_async_copy(tx.at[group], rx.at[group], l_x.at[which])

    def send_grads(which):
        for s in range(T - 1):
            x_copy(which, s).start()
        x_own(which).start()

    def flat(ref):
        return ref[...].reshape(8 * ROWS, ref.shape[-1])

    def glu_grads(grads, tx):
        prod = lead_sum(flat(grads), flat(normed)).astype(bf16)
        for mm in range(M):
            for ff in range(2):
                tx[mm * 2 + ff] = prod[
                    mm * seg : (mm + 1) * seg, ff * half_width : (ff + 1) * half_width
                ]

    def down_grads():
        prod = lead_sum(flat(hid), flat(c_v))
        for mm in range(M):
            for ff in range(2):
                down_tx[mm * 2 + ff] = jnp.concatenate(
                    [
                        prod[:, blk * each : (blk + 1) * each]
                        for zl in range(2)
                        for cc in range(2)
                        for blk in [(2 * zl + ff) * 2 * M + mm * 2 + cc]
                    ],
                    axis=1,
                ).astype(bf16)
    down_grads()
    send_grads(1)
    glu_grads(gg, gate_tx)
    send_grads(0)

    dy = sc.total()
    mid = mid_b[core]
    r = lax.rsqrt(jnp.mean(mid * mid, axis=-1, keepdims=True) + epsilon)
    gdy = gain * dy
    dv = r * gdy - mid * (r * r * r) * jnp.mean(mid * gdy, axis=-1, keepdims=True)
    gmid = own_c_ref[...].astype(f32) + dv
    gmid_ref[...] = gmid
    mid_ref[...] = mid
    gpart_ref[...] = jnp.sum(dy * mid * r, axis=0, keepdims=True)
    br_own[...] = gmid.astype(bf16)
    branch_ref[me] = br_own[...]

    gb = Gather(br_own, branch_ref, s_br, r_br)
    gb.own()
    glu_grads(gu, up_tx)
    for kind in (0, 1, 2):
        gb.take(kind)
    gb.rest()
    for which in range(2):
        x_own(which).wait()
        for s in range(T - 1):
            x_copy(which, s).wait_recv()
    for i in range(4):
        for k in range(2):
            att_copy(k, i).wait_send()
        for k in range(4):
            sib_att(k, i).wait_send()

        @pl.when(at_end == 0)
        def _(i=i):
            att_copy(2, i).wait_send()
            att_copy(3, i).wait_send()

    sc.sent()
    gb.sent()
    for which in range(2):
        for s in range(T - 1):
            x_copy(which, s).wait_send()


def feed_forward(att, x_all, c_all, own_c, own_weights, got_weights, gain, cid):
    n = lax.axis_size("ctx")
    T, seg, each = n // 4, FF // n, WIDTH // n
    cols = FF // 8
    half_width = WIDTH // 2
    VS, sem = pltpu.VMEM, pltpu.SemaphoreType.DMA
    shape = jax.ShapeDtypeStruct
    return pl.pallas_call(
        ffn_kernel,
        out_shape=(
            shape((4, BLOCK, WIDTH), bf16),
            shape((8, ROWS, WIDTH), bf16),
            shape((ROWS, WIDTH), f32),
            shape((ROWS, WIDTH), f32),
            shape((4, 2, ROWS, WIDTH), bf16),
            shape((1, WIDTH), f32),
            shape((T, seg, half_width), bf16),
            shape((T, cols, 4 * each), bf16),
            shape((T, seg, half_width), bf16),
        ),
        in_specs=vspecs(1) + any_specs(2) + vspecs(1) + any_specs(8) + vspecs(1),
        out_specs=tuple(vspecs(9)),
        scratch_shapes=[
            VS((4, BLOCK, WIDTH), bf16),
            VS((4, BLOCK, WIDTH), bf16),
            VS((WIDTH, WIDTH), bf16),
            VS((WIDTH, cols), bf16),
            VS((WIDTH, cols), bf16),
            VS((cols, WIDTH), bf16),
            VS((4, BLOCK, WIDTH), bf16),
            VS((4, BLOCK, cols), bf16),
            VS((4, BLOCK, cols), bf16),
            VS((4, BLOCK, cols), bf16),
            VS((2, ROWS, WIDTH), f32),
            VS((4, 2, ROWS, WIDTH), bf16),
            *scatter_scratch(),
            VS((T, seg, half_width), bf16),
            VS((T, cols, 4 * each), bf16),
            VS((ROWS, WIDTH), bf16),
            sem((9,)),
            sem((2, 4)),
            sem((3, 4)),
            sem((2, 4)),
            sem((4, 4)),
            sem((4, 4)),
            sem((9,)),
            sem((7,)),
            sem((2, T - 1)),
            sem((2, T - 1)),
            sem((2,)),
        ],
        compiler_params=pltpu.CompilerParams(
            collective_id=cid, has_side_effects=True, vmem_limit_bytes=60 * 2**20
        ),
        name="feed_forward",
    )(att, x_all, c_all, own_c, *own_weights, *got_weights, gain)


def back_kernel(
    doc_ref, branch_ref, att_ref, wo_own, wo_got, q_rows, kv_all, summed, totals, stacked, cosine, sine,
    normed, w_heads, dpart, mid_ref, gmid_ref, x_ref, x_all, again_ref, qgain_ref, kgain_ref, fpart_ref,
    gate_rx, down_rx, up_tx,
    out_ref, igrad_ref, gains_ref, heads_ref, attn_ref, gate_ref, up_ref, down_ref,
    wo_v, g_v, delta_v, dq_v, dkv_acc, dkv_tx, dkv_rx, gs_v,
    d_sib, d_sum, d_relay, d_rx, s_d, r_d, p_sib, p_sum, p_relay, p_rx, s_p, r_p, p_part,
    h_tx, h_rx, a_tx, a_rx, gn_tx, gn_rx, gt_tx, gt_rx, up_rx, w_tx, w_rx,
    ld, s_k, r_k, s_h, r_h, l_h, s_a, r_a, l_a, s_g, r_g, s_t, r_t, s_u, r_u, s_w, r_w,
):
    z, m, core, f = who()
    M = lax.axis_size("ctx") // 8
    T = 2 * M
    span = lax.axis_size("ctx") // 4 * ROWS
    each = WIDTH // lax.axis_size("ctx")
    half_width = WIDTH // 2
    sib = dev(z, m, 1 - core, f)
    zs = [(z + s) % 4 for s in (1, 2, 3)]
    zpeers = [dev(zz, m, core, f) for zz in zs]
    cross = [dev(zz, m, 1 - core, f) for zz in zs]
    mpeers = [dev(z, (m + s) % M, core, f) for s in range(1, M)]
    group = m * 2 + f
    others = [(group + s) % T for s in range(1, T)]
    tpeers = [dev(z, o // 2, core, o % 2) for o in others]
    owner = f == z // 2
    head = slot(z, core)
    me = head

    pieces = [(group + s) % T for s in range(T)]
    rest_to = [core * M + p // 2 for p in pieces]
    piece_to = [dev(z, rr // 2, rr % 2, p % 2) for rr, p in zip(rest_to, pieces)]
    to_self = [(rr == m * 2 + core) & (p % 2 == f) for rr, p in zip(rest_to, pieces)]
    rest = m * 2 + core
    core_from = rest // M
    sources = [(group + s) % T for s in range(T)]
    piece_from = [dev(z, o // 2, core_from, o % 2) for o in sources]
    from_self = [(core_from == core) & (o == group) for o in sources]

    cp_own = pltpu.make_async_copy(
        wo_own.at[pl.ds(pl.multiple_of(head % 4 * 128, 128), 128)], wo_v, ld.at[0]
    )
    cp_got = pltpu.make_async_copy(
        wo_got.at[pl.ds(pl.multiple_of(head % 4 * 128, 128), 128)], wo_v, ld.at[0]
    )

    @pl.when(owner)
    def _():
        cp_own.start()

    @pl.when(jnp.logical_not(owner))
    def _():
        cp_got.start()

    bar = pltpu.get_barrier_semaphore()
    fixed = [sib] + zpeers + cross + tpeers
    for p in fixed:
        pl.semaphore_signal(bar, inc=1, device_id=p, device_id_type=MESH)
    for s in range(T):

        @pl.when(jnp.logical_not(from_self[s]))
        def _(s=s):
            pl.semaphore_signal(bar, inc=1, device_id=piece_from[s], device_id_type=MESH)

    place = [(zl, cc) for zl in range(2) for cc in range(2)]
    place_dev = [dev(2 * zl + f, m, cc, z // 2) for zl, cc in place]
    place_self = [owner & (z == 2 * zl + f) & (core == cc) for zl, cc in place]
    place_from = [dev(2 * f + zb, m, cc, z % 2) for zb, cc in place]
    from_me = [owner & (z == 2 * f + zb) & (z % 2 == f) & (core == cc) for zb, cc in place]
    for k in range(4):

        @pl.when(jnp.logical_not(from_me[k]))
        def _(k=k):
            pl.semaphore_signal(bar, inc=1, device_id=place_from[k], device_id_type=MESH)

    pl.semaphore_wait(
        bar,
        len(fixed)
        + T
        + 4
        - jnp.where(core_from == core, 1, 0)
        - jnp.where(owner & (z % 2 == f), 1, 0),
    )

    sd = Scatter(dpart, d_sib, d_sum, d_relay, d_rx, s_d, r_d)
    sp = Scatter(p_part, p_sib, p_sum, p_relay, p_rx, s_p, r_p)
    for i in range(4):
        sd.sibling(i).start()

    def u_copy(s):
        return rcopy(up_tx.at[others[s]], up_rx.at[group], s_u.at[s], r_u.at[s], tpeers[s])

    for s in range(T - 1):
        u_copy(s).start()

    @pl.when(owner)
    def _():
        cp_own.wait()

    @pl.when(jnp.logical_not(owner))
    def _():
        cp_got.wait()

    def block_rows(b):
        return pl.ds(pl.multiple_of(b * BLOCK, BLOCK), BLOCK)

    def mixed(b, _):
        rows = block_rows(b)
        br = jnp.concatenate([branch_ref[2 * b], branch_ref[2 * b + 1]], axis=0)
        gm = back_product(br, wo_v[...])
        inv = 1.0 / totals[rows, :]
        g_v[rows, :] = (gm * inv).astype(bf16)
        w = gm * summed[rows, :] * (inv * inv)
        low = lax.broadcasted_iota(jnp.int32, w.shape, 1) < 64
        a = jnp.sum(jnp.where(low, w, 0.0), axis=1, keepdims=True)
        c = jnp.sum(jnp.where(low, 0.0, w), axis=1, keepdims=True)
        delta_v[rows, :] = jnp.where(low, a, c)
        return 0

    lax.fori_loop(0, 4, mixed, 0)
    for i in range(3):
        sd.pass_on(i)

    total = down_rx[0].astype(f32)
    for k in range(1, T):
        total = total + down_rx[k].astype(f32)
    for k in range(4):
        w_tx[k] = packed(total[:, k * each : (k + 1) * each]).astype(bf16)
    here = z % 2 * 2 + core

    def w_copy(k):
        return rcopy(w_tx.at[k], w_rx.at[here], s_w.at[k], r_w.at[here], place_dev[k])

    for k in range(4):

        @pl.when(jnp.logical_not(place_self[k]))
        def _(k=k):
            w_copy(k).start()

        @pl.when(place_self[k])
        def _(k=k):
            w_rx[here] = w_tx[k]

    for i in range(2):
        sd.relay(i)

    dq_v[...] = jnp.zeros_like(dq_v)

    def kv_copy(s):
        return rcopy(dkv_tx.at[s], dkv_rx.at[s], s_k.at[s], r_k.at[s], mpeers[s])

    def attend(s, _):
        mm = (m + 1 + s) % M
        dkv_acc[...] = jnp.zeros_like(dkv_acc)
        for zz in range(4):
            rows = slice(zz * BLOCK, (zz + 1) * BLOCK)
            keys = (zz + 1) * BLOCK
            token = zz * span + m * BLOCK + lax.broadcasted_iota(jnp.int32, (BLOCK, 1), 0)
            begin = begin_of(token, doc_ref)
            for h in range(2):
                lanes = slice(h * 64, h * 64 + 64)
                q = q_rows[rows, lanes]
                g = g_v[rows, lanes]
                k = kv_all[mm, :keys, :64]
                v = kv_all[mm, :keys, 64:]
                e = block_weights(q, k, begin, zz, m, mm, span)
                dp = back_product(g, v)
                ds = (e * (dp - delta_v[rows, h * 64 : h * 64 + 1])).astype(bf16)
                dq_v[rows, lanes] += dot(ds, k)
                dkv_acc[:keys, :64] += lead_sum(ds, q)
                dkv_acc[:keys, 64:] += lead_sum(e.astype(bf16), g)

        @pl.when(s < M - 1)
        def _():
            dkv_tx[s] = dkv_acc[...].astype(bf16)

            for ss in range(M - 1):

                @pl.when(s == ss)
                def _(ss=ss):
                    kv_copy(ss).start()

        return 0

    lax.fori_loop(0, M, attend, 0)

    def over_groups(rx):
        total = rx[0].astype(f32)
        for k in range(1, T):
            total = total + rx[k].astype(f32)
        return total

    gate_ref[...] = jnp.transpose(over_groups(gate_rx))

    strip = jnp.concatenate(
        [branch_ref[j, :, pl.ds(pl.multiple_of(z * 256, 128), 256)] for j in range(8)], axis=0
    )
    strip = jnp.concatenate(
        [
            jnp.where(
                core == 0,
                strip[:, 2 * mm * each : (2 * mm + 1) * each],
                strip[:, (2 * mm + 1) * each : (2 * mm + 2) * each],
            )
            for mm in range(M)
        ],
        axis=1,
    )
    prod = lead_sum(att_ref[...].reshape(8 * ROWS, WIDTH), strip).astype(bf16)
    for mm in range(M):
        for ff in range(2):
            a_tx[mm * 2 + ff] = packed(
                prod[ff * half_width : (ff + 1) * half_width, mm * each : (mm + 1) * each]
            )

    def a_copy(s):
        return rcopy(a_tx.at[others[s]], a_rx.at[group], s_a.at[s], r_a.at[s], tpeers[s])

    for s in range(M - 1):
        kv_copy(s).wait_recv()
    for s in range(T - 1):
        a_copy(s).start()
    a_own = pltpu.make_async_copy(a_tx.at[group], a_rx.at[group], l_a.at[0])
    a_own.start()

    qgain = qgain_ref[...]
    kgain = kgain_ref[...]

    def head_mean(v):
        low = lax.broadcasted_iota(jnp.int32, v.shape, 1) < 64
        a = jnp.sum(jnp.where(low, v, 0.0), axis=1, keepdims=True)
        c = jnp.sum(jnp.where(low, 0.0, v), axis=1, keepdims=True)
        return jnp.where(low, a, c) * (1.0 / 64)

    def heads_back(i, carry):
        qg, kg, ag = carry
        b = jnp.where(i == 0, sp.order[0], jnp.where(i == 1, sp.order[1], jnp.where(i == 2, sp.order[2], z)))
        rows = block_rows(b)
        co = cosine[rows, :]
        si = sine[rows, :]

        def through(v, dy, gain):
            dy = dy * co - turn(dy) * si
            r = head_scale(v)
            gdy = gain * dy
            dv = r * gdy - v * (r * r * r) * head_mean(v * gdy)
            return dv, jnp.sum(dy * v * r, axis=0, keepdims=True)

        st = stacked[rows, :]
        dq, qpart = through(st[:, :128], dq_v[rows, :] * HEAD_SIZE ** (-0.5), qgain)
        dkv = dkv_acc[rows, :]
        for s in range(M - 1):
            dkv = dkv + dkv_rx[s, rows, :].astype(f32)
        dk, kpart = through(st[:, 128:], dkv, kgain)
        low = lax.broadcasted_iota(jnp.int32, dkv.shape, 1) < 64
        gs = jnp.concatenate([dq, jnp.where(low, dk, dkv)], axis=1).astype(bf16)
        gs_v[rows, :] = gs
        pb = back_product(gs, w_heads[...])
        xb = jnp.concatenate([x_all[2 * b], x_all[2 * b + 1]], axis=0).astype(f32)
        rb = lax.rsqrt(jnp.mean(xb * xb, axis=-1, keepdims=True) + epsilon)
        ag = ag + jnp.sum(pb * (xb * rb), axis=0, keepdims=True)
        pb = pb.astype(bf16)
        p_part[b, 0] = pb[:ROWS]
        p_part[b, 1] = pb[ROWS:]
        rcopy(
            p_part.at[b, 1 - core], p_sib.at[i], s_p.at[i], r_p.at[i], sib
        ).start()
        return qg + qpart, kg + kpart, ag

    zero = jnp.zeros((1, 128), f32)
    qg, kg, ag = lax.fori_loop(
        0, 4, heads_back, (zero, zero, jnp.zeros((1, WIDTH), f32))
    )
    for i in range(3):
        sp.pass_on(i)

    def stack(row):
        return jnp.concatenate([row[:, k * 128 : (k + 1) * 128] for k in range(8)], axis=0)

    gn_tx[0:8, :] = stack(ag)
    gn_tx[8:16, :] = stack(fpart_ref[...])
    gn_tx[16:24, :] = jnp.concatenate([qg, kg, jnp.zeros((6, 128), f32)], axis=0)
    gpeers = [sib] + zpeers + cross

    def g_copy(k):
        return rcopy(gn_tx, gn_rx.at[k], s_g.at[k], r_g.at[k], gpeers[k])

    for k in range(7):
        g_copy(k).start()

    prod = lead_sum(normed[...], gs_v[...]).astype(bf16)
    qw, kw = 128 // M, 64 // M
    for i in range(M):
        for ff in range(2):
            rows = slice(ff * half_width, (ff + 1) * half_width)
            h_tx[i * 2 + ff] = jnp.concatenate(
                [
                    prod[rows, i * qw : (i + 1) * qw],
                    prod[rows, 128 + i * kw : 128 + (i + 1) * kw],
                    prod[rows, 192 + i * kw : 192 + (i + 1) * kw],
                ],
                axis=1,
            )

    def h_copy(s):
        return rcopy(
            h_tx.at[pieces[s]], h_rx.at[group], s_h.at[s], r_h.at[group], piece_to[s]
        )

    def h_own(s):
        return pltpu.make_async_copy(h_tx.at[pieces[s]], h_rx.at[group], l_h.at[0])

    def h_got(s):
        return rcopy(
            h_tx.at[pieces[s]], h_rx.at[sources[s]], s_h.at[s], r_h.at[sources[s]], piece_from[s]
        )

    for s in range(T):

        @pl.when(to_self[s])
        def _(s=s):
            h_own(s).start()

        @pl.when(jnp.logical_not(to_self[s]))
        def _(s=s):
            h_copy(s).start()

    for i in range(2):
        sp.relay(i)
    gains = gn_tx[...]
    for k in range(7):
        g_copy(k).wait_recv()
    for k in range(7):
        gains = gains + gn_rx[k]
    gt_tx[...] = gains

    def t_copy(s):
        return rcopy(gt_tx, gt_rx.at[s], s_t.at[s], r_t.at[s], tpeers[s])

    for s in range(T - 1):
        t_copy(s).start()


    for s in range(T - 1):
        u_copy(s).wait_recv()
    up_rx[group] = up_tx[group]
    up_ref[...] = jnp.transpose(over_groups(up_rx))
    for k in range(4):

        @pl.when(jnp.logical_not(from_me[k]))
        def _(k=k):
            rcopy(w_tx.at[k], w_rx.at[k], s_w.at[k], r_w.at[k], place_from[k]).wait_recv()

    seg = gate_rx.shape[1]
    for zl in range(2):
        for cc in range(2):
            for mm in range(M):
                at = ((zl * M + mm) * 2 + cc) * seg
                down_ref[at : at + seg, :] = w_rx[
                    zl * 2 + cc, :, mm * each : (mm + 1) * each
                ].astype(f32)

    out_ref[...] = mid_ref[...] + sd.total()
    dy = sp.total()
    x = x_ref[...].astype(f32)
    r = lax.rsqrt(jnp.mean(x * x, axis=-1, keepdims=True) + epsilon)
    gdy = again_ref[...] * dy
    dv = r * gdy - x * (r * r * r) * jnp.mean(x * gdy, axis=-1, keepdims=True)
    igrad_ref[...] = gmid_ref[...] + dv

    for s in range(T):

        @pl.when(from_self[s])
        def _(s=s):
            pltpu.make_async_copy(h_tx.at[0], h_rx.at[group], l_h.at[0]).wait()

        @pl.when(jnp.logical_not(from_self[s]))
        def _(s=s):
            h_got(s).wait_recv()

    for s in range(T - 1):
        a_copy(s).wait_recv()
    a_own.wait()
    hsum = h_rx[0].astype(f32)
    asum = a_rx[0].astype(f32)
    for k in range(1, T):
        hsum = hsum + h_rx[k].astype(f32)
        asum = asum + a_rx[k].astype(f32)
    heads_ref[...] = hsum
    size = asum.shape[0]
    for g in range(128 // each):
        attn_ref[g * size : (g + 1) * size, :] = asum[:, g * each : (g + 1) * each]

    for s in range(T - 1):
        t_copy(s).wait_recv()
        gains = gains + gt_rx[s]
    gains_ref[...] = gains

    sd.sent()
    sp.sent()
    for k in range(4):

        @pl.when(jnp.logical_not(place_self[k]))
        def _(k=k):
            w_copy(k).wait_send()

    for s in range(T - 1):
        u_copy(s).wait_send()
    for s in range(M - 1):
        kv_copy(s).wait_send()
    for s in range(T):

        @pl.when(jnp.logical_not(to_self[s]))
        def _(s=s):
            h_copy(s).wait_send()

    for s in range(T - 1):
        a_copy(s).wait_send()
        t_copy(s).wait_send()
    for k in range(7):
        g_copy(k).wait_send()


def back(*args, cid):
    n = lax.axis_size("ctx")
    M, T, each = n // 8, n // 4, WIDTH // n
    tokens = 8 * ROWS
    half_width = WIDTH // 2
    VS, sem = pltpu.VMEM, pltpu.SemaphoreType.DMA
    shape = jax.ShapeDtypeStruct
    part = (ROWS, WIDTH)
    return pl.pallas_call(
        back_kernel,
        out_shape=(
            shape(part, f32),
            shape(part, f32),
            shape((24, 128), f32),
            shape((half_width, 256 // M), f32),
            shape((half_width, each), f32),
            shape((half_width, FF // n), f32),
            shape((half_width, FF // n), f32),
            shape((FF // 2, each), f32),
        ),
        in_specs=[pl.BlockSpec(memory_space=pltpu.SMEM)] + vspecs(2) + any_specs(2) + vspecs(21),
        out_specs=tuple(vspecs(8)),
        scratch_shapes=[
            VS((128, WIDTH), bf16),
            VS((tokens, 128), bf16),
            VS((tokens, 128), f32),
            VS((tokens, 128), f32),
            VS((tokens, 128), f32),
            VS((M - 1, tokens, 128), bf16),
            VS((M - 1, tokens, 128), bf16),
            VS((tokens, 256), bf16),
            *scatter_scratch(),
            *scatter_scratch(),
            VS((4, 2) + part, bf16),
            VS((T, half_width, 256 // M), bf16),
            VS((T, half_width, 256 // M), bf16),
            VS((T, half_width * each // 128, 128), bf16),
            VS((T, half_width * each // 128, 128), bf16),
            VS((24, 128), f32),
            VS((7, 24, 128), f32),
            VS((24, 128), f32),
            VS((T - 1, 24, 128), f32),
            VS((T, FF // n, half_width), bf16),
            VS((4, FF // 8 * each // 128, 128), bf16),
            VS((4, FF // 8 * each // 128, 128), bf16),
            sem((1,)),
            sem((M - 1,)), sem((M - 1,)),
            sem((T,)), sem((T,)), sem((1,)),
            sem((T - 1,)), sem((T - 1,)), sem((1,)),
            sem((7,)), sem((7,)),
            sem((T - 1,)), sem((T - 1,)),
            sem((T - 1,)), sem((T - 1,)),
            sem((4,)), sem((4,)),
        ],
        compiler_params=pltpu.CompilerParams(
            collective_id=cid, has_side_effects=True, vmem_limit_bytes=60 * 2**20
        ),
        name="back",
    )(*args)


def root_mean_norm(rows, gain):
    return (
        rows * lax.rsqrt(jnp.mean(rows * rows, axis=-1, keepdims=True) + epsilon) * gain
    )


def rotary(rows, cosine, sine):
    halfway = rows.shape[-1] // 2
    leading = rows[..., :halfway]
    trailing = rows[..., halfway:]
    return jnp.concatenate(
        [leading * cosine - trailing * sine, leading * sine + trailing * cosine], axis=-1
    )


SWAP = [(0, 1), (1, 0)]


def halves(f, own, other, axis):
    return jnp.where(
        f == 0,
        jnp.concatenate([own, other], axis=axis),
        jnp.concatenate([other, own], axis=axis),
    )


def local(
    hidden_in,
    doc_lengths,
    attn_gain,
    query_gain,
    key_norm_gain,
    ffn_gain,
    query_proj,
    key_weight,
    value_weight,
    attn_proj,
    gate_proj,
    up_proj,
    down_proj,
    out_cotangent,
):
    n_ctx = lax.axis_size("ctx")
    M = n_ctx // 8
    T = 2 * M
    z, m, core, f = who()
    head = slot(z, core)
    tokens = 8 * ROWS
    span = n_ctx // 4 * ROWS
    segment = FF // n_ctx
    columns = M * segment
    half_width = WIDTH // 2
    each = WIDTH // n_ctx

    heads_own = jnp.concatenate(
        [
            lax.dynamic_slice(query_proj, (0, head * 128), (half_width, 128)),
            lax.dynamic_slice(key_weight, (0, head * 64), (half_width, 64)),
            lax.dynamic_slice(value_weight, (0, head * 64), (half_width, 64)),
        ],
        axis=1,
    ).astype(bf16)
    first = z * (n_ctx // 4) + core
    gate_own, up_own = [
        jnp.concatenate(
            [
                lax.dynamic_slice(w, (0, (first + 2 * mm) * segment), (half_width, segment))
                for mm in range(M)
            ],
            axis=1,
        ).astype(bf16)
        for w in (gate_proj, up_proj)
    ]
    down_own = jnp.concatenate(
        [
            lax.dynamic_slice(
                down_proj, ((first + 2 * mm) * segment - f * (FF // 2), 0), (segment, WIDTH)
            )
            for mm in range(M)
        ],
        axis=0,
    ).astype(bf16)
    out_own = attn_proj.astype(bf16)

    cotangent = out_cotangent[0]
    q_gain = jnp.tile(query_gain, 2)[None]
    k_gain = jnp.concatenate([key_norm_gain, jnp.ones((64,), f32)])[None]
    (
        x_rows, c_rows, w_heads, w_gate, w_up, w_down, w_out, q_rows, kv_all, att_own, summed, totals,
        stacked, normed, cos_table, sin_table,
    ) = front(
        doc_lengths,
        hidden_in[0],
        cotangent,
        heads_own,
        gate_own,
        up_own,
        down_own,
        out_own,
        attn_gain[None],
        q_gain,
        k_gain,
        1,
    )
    attended, branch, grad_middle, own, down_parts, ffn_gain_part, gate_got, down_got, up_give = feed_forward(
        att_own,
        x_rows.reshape(4, BLOCK, WIDTH),
        c_rows.reshape(4, BLOCK, WIDTH),
        cotangent,
        (out_own, gate_own, up_own, down_own),
        (w_out, w_gate, w_up, w_down),
        ffn_gain[None],
        4,
    )
    output, input_grad, gains, heads_grad, attn_grad, gate_grad, up_grad, down_grad = back(
        doc_lengths,
        branch,
        attended,
        out_own,
        w_out,
        q_rows,
        kv_all,
        summed,
        totals,
        stacked,
        cos_table,
        sin_table,
        normed,
        w_heads,
        down_parts,
        own,
        grad_middle,
        hidden_in[0],
        x_rows,
        attn_gain[None],
        q_gain,
        k_gain,
        ffn_gain_part,
        gate_got,
        down_got,
        up_give,
        cid=7,
    )

    qw, kw = 128 // M, 64 // M
    query_grad = heads_grad[:, :qw]
    key_grad = heads_grad[:, qw : qw + kw]
    value_grad = heads_grad[:, qw + kw :]

    return (
        output[None],
        input_grad[None],
        gains[:8].reshape(WIDTH),
        gains[16, :64] + gains[16, 64:],
        gains[17, :64],
        gains[8:16].reshape(WIDTH),
        query_grad,
        key_grad,
        value_grad,
        attn_grad,
        gate_grad,
        up_grad,
        down_grad,
    )


def solution(mesh):
    in_specs = (
        P("fsdp", "ctx", None),
        P("fsdp", None),
        P(),
        P(),
        P(),
        P(),
        P("fsdp", None),
        P("fsdp", None),
        P("fsdp", None),
        P("fsdp", None),
        P("fsdp", None),
        P("fsdp", None),
        P("fsdp", None),
        P("fsdp", "ctx", None),
    )
    out_specs = (
        P("fsdp", "ctx", None),
        P("fsdp", "ctx", None),
        P(),
        P(),
        P(),
        P(),
        P("fsdp", "ctx"),
        P("fsdp", "ctx"),
        P("fsdp", "ctx"),
        P("fsdp", "ctx"),
        P("fsdp", "ctx"),
        P("fsdp", "ctx"),
        P("fsdp", "ctx"),
    )
    return jax.shard_map(local, mesh=mesh, in_specs=in_specs, out_specs=out_specs, check_vma=False)
```

```python
import functools
import math

import jax
import jax.numpy as jnp
from jax import lax
from jax.experimental import pallas as pl
from jax.experimental.pallas import tpu as pltpu
from jax.sharding import PartitionSpec as P

QUERY_HEADS = 16
KEY_VALUE_HEADS = 8
HEAD_SIZE = 64
FF = 4608
WIDTH = 1024
ROWS = 128

epsilon = 1e-05
rope_base = 1000000.0
MESH = pl.DeviceIdType.MESH
ANY = pl.ANY
VMEM_LIMIT = 64 * 2**20 - 2**17
bf16 = jnp.bfloat16
f32 = jnp.float32


def who():
    n = lax.axis_size("ctx")
    c = lax.axis_index("ctx")
    f = lax.axis_index("fsdp")
    q = n // 4
    return c // q, (c % q) // 2, c % 2, f


def dev(z, m, core, f):
    return (z * (lax.axis_size("ctx") // 4) + m * 2 + core, f)


def slot(z, core):
    return z * 2 + core


def enter(peers):
    bar = pltpu.get_barrier_semaphore()
    for p in peers:
        pl.semaphore_signal(bar, inc=1, device_id=p, device_id_type=MESH)
    pl.semaphore_wait(bar, len(peers))


def rcopy(src, dst, s, r, to):
    return pltpu.make_async_remote_copy(
        src_ref=src, dst_ref=dst, send_sem=s, recv_sem=r, device_id=to, device_id_type=MESH
    )


def comm_params(cid):
    return pltpu.CompilerParams(collective_id=cid, has_side_effects=True)


def any_specs(n):
    return [pl.BlockSpec(memory_space=ANY)] * n


def line_of(z):
    return z + 1 - 2 * (z % 2), 2 - z // 2, 3 - 3 * (z // 2), 1 - ((z + 1) // 2) % 2


def packed(v):
    rows, cols = v.shape
    n = max(1, 128 // cols)
    size = rows // n
    return jnp.concatenate([v[g * size : (g + 1) * size] for g in range(n)], axis=1)


def unpacked(v, cols):
    n = max(1, 128 // cols)
    return jnp.concatenate([v[:, g * cols : (g + 1) * cols] for g in range(n)], axis=0)


class Gather:
    def __init__(self, src, dst, ss, rs):
        z, m, core, f = who()
        partner, middle, end, self.at_end = line_of(z)
        self.src, self.dst, self.ss, self.rs = src, dst, ss, rs
        self.me = slot(z, core)
        self.slots = [slot(zz, core) for zz in (partner, middle, end)]
        self.partner = dev(partner, m, core, f)
        self.middle = dev(middle, m, core, f)
        self.sib = dev(z, m, 1 - core, f)

    def copy(self, k):
        src, dst, ss, rs = self.src, self.dst, self.ss.at[k], self.rs
        if k == 0:
            return rcopy(src, dst.at[self.me], ss, rs.at[0], self.partner)
        if k == 1:
            return rcopy(src, dst.at[self.me], ss, rs.at[1 + self.at_end], self.middle)
        if k == 3:
            return rcopy(src, dst.at[self.me], ss, rs.at[3], self.sib)
        if k < 7:
            j = self.slots[k - 4]
            return rcopy(dst.at[j], dst.at[j], ss, rs.at[k], self.sib)
        j = self.slots[k - 6]
        return rcopy(dst.at[j], dst.at[j], ss, rs.at[k - 6], self.partner)

    def own(self):
        for k in (1, 0, 3):
            self.copy(k).start()

    def take(self, kind):
        j = self.slots[kind]
        rcopy(
            self.dst.at[j], self.dst.at[j], self.ss.at[0], self.rs.at[kind], self.partner
        ).wait_recv()
        if kind > 0:

            @pl.when(self.at_end == 0)
            def _():
                self.copy(6 + kind).start()

        self.copy(4 + kind).start()

    def rest(self):
        for k in range(3, 7):
            self.copy(k).wait_recv()

    def sent(self):
        for k in (0, 1, 3, 4, 5, 6):
            self.copy(k).wait_send()

        @pl.when(self.at_end == 0)
        def _():
            self.copy(7).wait_send()
            self.copy(8).wait_send()


class Scatter:
    def __init__(self, part, buf, sums, relay, rx, ss, rs):
        z, m, self.core, f = who()
        core = self.core
        partner, middle, end, self.at_end = line_of(z)
        self.z = z
        self.part, self.buf, self.sums, self.relay_buf, self.rx = part, buf, sums, relay, rx
        self.ss, self.rs = ss, rs
        self.order = [end, middle, partner, z]
        self.sib = dev(z, m, 1 - core, f)
        self.to = [dev(zz, m, core, f) for zz in self.order[:3]]

    def sibling(self, i):
        return rcopy(
            self.part.at[self.order[i], 1 - self.core],
            self.buf.at[i],
            self.ss.at[i],
            self.rs.at[i],
            self.sib,
        )

    def copy(self, i, at_end):
        if i == 2:
            return rcopy(
                self.sums.at[2], self.rx.at[0], self.ss.at[6], self.rs.at[4], self.to[2]
            )
        if at_end:
            return rcopy(
                self.sums.at[i], self.relay_buf.at[i], self.ss.at[4 + i], self.rs.at[6 + i], self.to[2]
            )
        return rcopy(self.sums.at[i], self.rx.at[1], self.ss.at[4 + i], self.rs.at[5], self.to[i])

    def pass_on(self, i):
        self.sibling(i).wait_recv()
        self.sums[i] = (
            self.part[self.order[i], self.core].astype(f32) + self.buf[i].astype(f32)
        ).astype(bf16)
        if i == 2:
            self.copy(2, True).start()
        else:

            @pl.when(self.at_end == 1)
            def _():
                self.copy(i, True).start()

    def relay(self, i):
        @pl.when(self.at_end == 0)
        def _():
            self.copy(i, True).wait_recv()
            self.sums[i] = (
                self.sums[i].astype(f32) + self.relay_buf[i].astype(f32)
            ).astype(bf16)
            self.copy(i, False).start()

    def total(self):
        self.sibling(3).wait_recv()
        total = self.part[self.z, self.core].astype(f32) + self.buf[3].astype(f32)
        self.copy(2, True).wait_recv()
        total = total + self.rx[0].astype(f32)
        self.copy(0, False).wait_recv()
        return total + self.rx[1].astype(f32)

    def sent(self):
        for i in range(4):
            self.sibling(i).wait_send()
        for i in range(3):
            self.copy(i, False).wait_send()


def scatter_scratch():
    part = (ROWS, WIDTH)
    return [
        pltpu.VMEM((4,) + part, bf16),
        pltpu.VMEM((3,) + part, bf16),
        pltpu.VMEM((2,) + part, bf16),
        pltpu.VMEM((2,) + part, bf16),
        pltpu.SemaphoreType.DMA((7,)),
        pltpu.SemaphoreType.DMA((8,)),
    ]


def back_product(left, right):
    return lax.dot_general(
        left, right, (((1,), (1,)), ((), ())), preferred_element_type=f32
    )


def lead_sum(left, right):
    return lax.dot_general(
        left, right, (((0,), (0,)), ((), ())), preferred_element_type=f32
    )


def dot(left, right):
    return jnp.dot(left, right, preferred_element_type=f32)


BLOCK = 2 * ROWS


def block_weights(q, k, begin, z, m, mm, span):
    keys = (z + 1) * BLOCK
    key = lax.broadcasted_iota(jnp.int32, (1, keys), 1)
    key = key // BLOCK * span + key % BLOCK + mm * BLOCK
    token = z * span + m * BLOCK + lax.broadcasted_iota(jnp.int32, (BLOCK, 1), 0)
    e = jnp.exp(back_product(q, k))
    return jnp.where((key >= begin) & (key <= token), e, 0.0)


VM = pltpu.VMEM


def vspecs(n):
    return [pl.BlockSpec(memory_space=VM)] * n


def begin_of(token, doc_ref):
    begin = jnp.zeros(token.shape, jnp.int32)
    start = doc_ref[0, 0]
    for d in range(1, doc_ref.shape[1]):
        begin = jnp.where(token >= start, start, begin)
        start = start + doc_ref[0, d]
    return begin


def turn(v):
    lane = lax.broadcasted_iota(jnp.int32, v.shape, 1)
    n = v.shape[1]
    return jnp.where(lane % 64 < 32, pltpu.roll(v, n - 32, 1), pltpu.roll(v, 32, 1))


def head_scale(v):
    sq = v * v
    if v.shape[1] == 64:
        return lax.rsqrt(jnp.mean(sq, axis=1, keepdims=True) + epsilon)
    low = lax.broadcasted_iota(jnp.int32, v.shape, 1) < 64
    a = jnp.sum(jnp.where(low, sq, 0.0), axis=1, keepdims=True)
    b = jnp.sum(jnp.where(low, 0.0, sq), axis=1, keepdims=True)
    return lax.rsqrt(jnp.where(low, a, b) * (1.0 / 64) + epsilon)


def block_kernel(
    doc_ref, x_ref, c_ref, wh_own, wg_own, wu_own, wd_own, wo_own,
    again_ref, qgain_ref, kgain_ref, fgain_ref,
    out_ref, igrad_ref, gains_ref, heads_ref, attn_ref, gate_ref, up_ref, down_ref,
    x_all, c_all, w_heads, wg_v, wu_v, wd_v, wo_v, q_rows, kv_all, att, summed, totals,
    stacked, normed, cosine, sine,
    att_all, branch, gmid_v, dpart, nffn, hid, gg, gu, mid_b, p_out, gate_tx, gate_rx, down_tx, down_rx,
    up_tx, up_rx, br_own,
    a_sib, a_sum, a_relay, a_rx, s_a, r_a, d_sib, d_sum, d_relay, d_rx, s_d, r_d,
    s_p, r_p,
    g_v, dkv_acc, dkv_rx, gs_v,
    h_tx, h_rx, ap_tx, ap_rx, gn_tx, gn_rx, gt_tx, gt_rx, w_tx, w_rx,
    s_x0, r_x0, s_c, r_c, s_h0, r_h0, s_w0, r_w0, s_v, r_v, s_o, r_o, s_k, r_k, ld,
    s_att, r_att, s_pass, s_sib, r_sib, s_br, r_br, s_x, r_x,
    s_dk, r_dk, s_h, r_h, s_ap, r_ap, s_g, r_g, s_t, r_t, s_w, r_w,
):
    z, m, core, f = who()
    M = lax.axis_size("ctx") // 8
    T = 2 * M
    span = lax.axis_size("ctx") // 4 * ROWS
    each = WIDTH // lax.axis_size("ctx")
    seg = FF // lax.axis_size("ctx")
    half_width = WIDTH // 2
    partner, middle, end, at_end = line_of(z)
    sib = dev(z, m, 1 - core, f)
    zs = [(z + s) % 4 for s in (1, 2, 3)]
    zpeers = [dev(zz, m, core, f) for zz in zs]
    cross = [dev(zz, m, 1 - core, f) for zz in zs]
    hm = m % 2
    pair = dev(z, m, core, 1 - f)
    beside = dev(z, m + 1 - 2 * hm, core, f)
    mpeers = [dev(z, (m + s) % M, core, f) for s in range(1, M)]
    group = m * 2 + f
    others = [(group + s) % T for s in range(1, T)]
    tpeers = [dev(z, o // 2, core, o % 2) for o in others]
    owner = f == z // 2
    me = slot(z, core)

    pieces = [(group + s) % T for s in range(T)]
    rest_to = [core * M + p // 2 for p in pieces]
    piece_to = [dev(z, rr // 2, rr % 2, p % 2) for rr, p in zip(rest_to, pieces)]
    to_self = [(rr == m * 2 + core) & (p % 2 == f) for rr, p in zip(rest_to, pieces)]
    rest = m * 2 + core
    core_from = rest // M
    sources = [(group + s) % T for s in range(T)]
    piece_from = [dev(z, o // 2, core_from, o % 2) for o in sources]
    from_self = [(core_from == core) & (o == group) for o in sources]

    mine = pl.ds(pl.multiple_of(f * half_width, half_width), half_width)
    load_heads = pltpu.make_async_copy(wh_own, w_heads.at[mine], ld.at[0])
    load_out = pltpu.make_async_copy(wo_own, wo_v.at[mine], ld.at[1])
    load_gate = pltpu.make_async_copy(wg_own, wg_v.at[mine], ld.at[2])
    load_up = pltpu.make_async_copy(wu_own, wu_v.at[mine], ld.at[3])
    load_down = pltpu.make_async_copy(wd_own, wd_v, ld.at[4])
    for cp in (load_heads, load_out, load_gate, load_up):
        cp.start()

    @pl.when(owner)
    def _():
        load_down.start()

    bar = pltpu.get_barrier_semaphore()
    fixed = [sib] + zpeers + cross + tpeers
    for p in fixed:
        pl.semaphore_signal(bar, inc=1, device_id=p, device_id_type=MESH)
    for s in range(T):

        @pl.when(jnp.logical_not(from_self[s]))
        def _(s=s):
            pl.semaphore_signal(bar, inc=1, device_id=piece_from[s], device_id_type=MESH)

    place = [(zl, cc) for zl in range(2) for cc in range(2)]
    place_dev = [dev(2 * zl + f, m, cc, z // 2) for zl, cc in place]
    place_self = [owner & (z == 2 * zl + f) & (core == cc) for zl, cc in place]
    place_from = [dev(2 * f + zb, m, cc, z % 2) for zb, cc in place]
    from_me = [owner & (z == 2 * f + zb) & (z % 2 == f) & (core == cc) for zb, cc in place]
    for k in range(4):

        @pl.when(jnp.logical_not(from_me[k]))
        def _(k=k):
            pl.semaphore_signal(bar, inc=1, device_id=place_from[k], device_id_type=MESH)

    pl.semaphore_wait(
        bar,
        len(fixed)
        + T
        + 4
        - jnp.where(core_from == core, 1, 0)
        - jnp.where(owner & (z % 2 == f), 1, 0),
    )

    def lane_block(j):
        return pl.ds(pl.multiple_of(j * 128, 128), 128)

    def front():
        gx = Gather(x_ref, x_all, s_x0, r_x0)
        gc = Gather(c_ref, c_all, s_c, r_c)
        gx.own()
        head_rows = pl.ds(f * half_width, half_width)
        heads_copy = rcopy(wh_own, w_heads.at[head_rows], s_h0.at[0], r_h0.at[0], pair)
        heads_copy.start()

        quarter = half_width // 2
        eighth = half_width // 4
        cols = wd_own.shape[0]

        def w_copy(k, stage):
            src, dst = ((wg_own, wg_v), (wu_own, wu_v), (wd_own, wd_v), (wo_own, wo_v))[k]
            base = 0 if k == 2 else (f if stage == 0 else 1 - f) * half_width
            size = (quarter, quarter, cols // 2, eighth)[k]
            part = hm * 2 + core if k == 3 else hm
            place = dst.at[pl.ds(pl.multiple_of(base + part * size, 8), size)]
            if stage == 0:
                here = src.at[pl.ds(pl.multiple_of(part * size, 8), size)]
                return rcopy(here, place, s_w0.at[k], r_w0.at[k], pair)
            return rcopy(place, place, s_v.at[k], r_v.at[k], beside)

        def out_copy(k):
            part = (hm if k == 0 else 1 - hm) * 2 + core
            base = (1 - f) * half_width
            place = wo_v.at[pl.ds(pl.multiple_of(base + part * eighth, 8), eighth)]
            return rcopy(place, place, s_o.at[k], r_o.at[k], sib)

        w_copy(0, 0).start()
        x_all[me] = x_ref[...]
        c_all[me] = c_ref[...]

        lane = lax.broadcasted_iota(jnp.int32, (1, 128), 1) % 32
        freq = jnp.exp(lane.astype(f32) * (-2.0 / 64 * math.log(rope_base)))
        sign = jnp.where(lax.broadcasted_iota(jnp.int32, (1, 128), 1) % 64 < 32, -1.0, 1.0)

        def tokens_of(zz):
            return zz * span + m * BLOCK + lax.broadcasted_iota(jnp.int32, (BLOCK, 1), 0)

        def table(zz, _):
            rows = pl.ds(pl.multiple_of(zz * BLOCK, BLOCK), BLOCK)
            token = tokens_of(zz)
            place = (token - begin_of(token, doc_ref)).astype(f32)
            angle = place * freq
            cosine[rows, :] = jnp.cos(angle)
            sine[rows, :] = jnp.sin(angle) * sign
            return 0

        lax.fori_loop(0, 4, table, 0)
        for k in (1, 3):
            w_copy(k, 0).start()
        for kind in (0, 1, 2):
            gx.take(kind)
        gc.own()

        @pl.when(owner)
        def _():
            w_copy(2, 0).start()

        heads_copy.wait_recv()

        def kv_copy(b, s):
            rows = pl.ds(pl.multiple_of(b * BLOCK, BLOCK), BLOCK)
            place = kv_all.at[m, rows]
            return rcopy(place, place, s_k.at[b, s], r_k.at[b, s], mpeers[s])

        again = again_ref[...]
        qgain = qgain_ref[...]
        kgain = kgain_ref[...]

        gx.rest()
        load_heads.wait()
        for k in range(2):
            w_copy(k, 0).wait_recv()
            w_copy(k, 1).start()

        def project(b, _):
            rows = pl.ds(pl.multiple_of(b * BLOCK, BLOCK), BLOCK)
            x = jnp.concatenate([x_all[2 * b], x_all[2 * b + 1]], axis=0).astype(f32)
            nb = (
                x * lax.rsqrt(jnp.mean(x * x, axis=-1, keepdims=True) + epsilon) * again
            ).astype(bf16)
            normed[rows, :] = nb
            st = dot(nb, w_heads[...])
            stacked[rows, :] = st
            co = cosine[rows, :]
            si = sine[rows, :]
            q = st[:, :128]
            q = q * head_scale(q) * qgain
            q_rows[rows, :] = ((q * co + turn(q) * si) * HEAD_SIZE ** (-0.5)).astype(bf16)
            kv = st[:, 128:]
            low = lax.broadcasted_iota(jnp.int32, kv.shape, 1) < 64
            k = kv * head_scale(kv) * kgain
            kv_all[m, rows, :] = jnp.where(low, k * co + turn(k) * si, kv).astype(bf16)
            for s in range(M - 1):
                kv_copy(b, s).start()
            return 0

        lax.fori_loop(0, 4, project, 0)

        w_copy(3, 0).wait_recv()
        w_copy(3, 1).start()
        out_copy(0).start()

        @pl.when(at_end == 0)
        def _():
            for kind in (0, 1, 2):
                gc.take(kind)

        summed[...] = jnp.zeros_like(summed)
        totals[...] = jnp.zeros_like(totals)

        def attend(s, _):
            mm = (m + M - s) % M

            @pl.when(s > 0)
            def _():
                for b in range(4):
                    rows = pl.ds(b * BLOCK, BLOCK)
                    place = kv_all.at[mm, rows]
                    rcopy(place, place, s_k.at[b, s - 1], r_k.at[b, s - 1], sib).wait_recv()

            @pl.when((s == 1) & jnp.logical_not(owner))
            def _():
                w_copy(2, 0).wait_recv()
                w_copy(2, 1).start()

            for zz in range(4):
                rows = slice(zz * BLOCK, (zz + 1) * BLOCK)
                keys = (zz + 1) * BLOCK
                begin = begin_of(tokens_of(zz), doc_ref)
                for h in range(2):
                    lanes = slice(h * 64, h * 64 + 64)
                    e = block_weights(
                        q_rows[rows, lanes], kv_all[mm, :keys, :64], begin, zz, m, mm, span
                    )
                    summed[rows, lanes] += dot(e.astype(bf16), kv_all[mm, :keys, 64:])
                    totals[rows, lanes] += jnp.broadcast_to(
                        jnp.sum(e, axis=1, keepdims=True), (BLOCK, 64)
                    )
            return 0

        lax.fori_loop(0, M, attend, 0)
        for b in range(4):
            rows = slice(b * BLOCK, (b + 1) * BLOCK)
            att[b] = (summed[rows, :] / totals[rows, :]).astype(bf16)

        def w_got(k):
            dst = (wg_v, wu_v, wd_v, wo_v)[k]
            base = 0 if k == 2 else (1 - f) * half_width
            size = (quarter, quarter, cols // 2, eighth)[k]
            part = (1 - hm) * 2 + core if k == 3 else 1 - hm
            place = dst.at[pl.ds(pl.multiple_of(base + part * size, 8), size)]
            return rcopy(place, place, s_v.at[k], r_v.at[k], beside)

        def ends_take():
            @pl.when(at_end == 1)
            def _():
                for kind in (0, 1, 2):
                    gc.take(kind)

        def out_ready():
            w_got(3).wait_recv()
            out_copy(1).start()
            load_out.wait()
            for k in range(2):
                out_copy(k).wait_recv()

        def glu_ready():
            for k in range(2):
                w_got(k).wait_recv()
            load_gate.wait()
            load_up.wait()

        def rest_ready():
            gc.rest()

            @pl.when(owner)
            def _():
                load_down.wait()

            @pl.when(jnp.logical_not(owner))
            def _():
                w_got(2).wait_recv()

        def sent():
            heads_copy.wait_send()
            gx.sent()
            gc.sent()
            for k in (0, 1, 3):
                w_copy(k, 0).wait_send()
                w_copy(k, 1).wait_send()

            @pl.when(owner)
            def _():
                w_copy(2, 0).wait_send()

            @pl.when(jnp.logical_not(owner))
            def _():
                w_copy(2, 1).wait_send()

            for k in range(2):
                out_copy(k).wait_send()
            for b in range(4):
                for s in range(M - 1):
                    kv_copy(b, s).wait_send()

        return sent, ends_take, out_ready, glu_ready, rest_ready

    front_sent, ends_take, out_ready, glu_ready, rest_ready = front()

    def feed_forward():
        def lanes(j):
            return pl.ds(pl.multiple_of(j * 128, 128), 128)

        order = [end, middle, partner, z]
        to_partner = [end, middle, z, partner]
        to_middle = [3 * (z // 2), 1 + z // 2, end, middle]
        from_slot = [slot(zz, core) for zz in (partner, middle, end)]
        to_p, to_m = dev(partner, m, core, f), dev(middle, m, core, f)

        def att_copy(k, i):
            if k == 0:
                b = to_partner[i]
                return rcopy(
                    att.at[b], att_all.at[b, :, lanes(me)], s_att.at[0, i], r_att.at[0, i], to_p
                )
            if k == 1:
                b = to_middle[i]
                return rcopy(
                    att.at[b],
                    att_all.at[b, :, lanes(me)],
                    s_att.at[1, i],
                    r_att.at[1 + at_end, i],
                    to_m,
                )
            place = att_all.at[order[i], :, lanes(from_slot[k - 1])]
            return rcopy(place, place, s_pass.at[k - 2, i], r_att.at[k - 1, (0, 1, 3, 2)[i]], to_p)

        def sib_att(k, i):
            b = order[i]
            j = me if k == 3 else from_slot[k]
            src = att.at[b] if k == 3 else att_all.at[b, :, lanes(j)]
            return rcopy(src, att_all.at[b, :, lanes(j)], s_sib.at[k, i], r_sib.at[k, i], sib)

        for i in range(4):
            att_copy(1, i).start()
            att_copy(0, i).start()
            sib_att(3, i).start()
        for b in range(4):
            att_all[b, :, lanes(me)] = att[b]

        def forward(i):
            for k in range(3):
                place = att_all.at[order[i], :, lanes(from_slot[k])]
                rcopy(place, place, s_att.at[0, i], r_att.at[k, i], to_p).wait_recv()
                if k > 0:

                    @pl.when(at_end == 0)
                    def _(k=k):
                        att_copy(k + 1, i).start()

                sib_att(k, i).start()

        ends_take()
        sc = Scatter(p_out, a_sib, a_sum, a_relay, a_rx, s_a, r_a)

        forward(0)
        gain = fgain_ref[...]

        def pair_of(ref, b):
            return jnp.concatenate([ref[2 * b], ref[2 * b + 1]], axis=0)

        for i in range(4):
            b = order[i]
            for k in range(4):
                sib_att(k, i).wait_recv()
            if i == 0:
                out_ready()
            mid = pair_of(x_all, b).astype(f32) + dot(att_all[b], wo_v[...])
            nb = (
                mid * lax.rsqrt(jnp.mean(mid * mid, axis=-1, keepdims=True) + epsilon) * gain
            ).astype(bf16)
            nffn[b] = nb
            if i == 3:
                mid_b[0] = mid[:ROWS]
                mid_b[1] = mid[ROWS:]
            for ii in ((1,), (2, 3), (), ())[i]:
                forward(ii)
            if i == 0:
                glu_ready()
            gate = dot(nb, wg_v[...])
            up = dot(nb, wu_v[...])
            sig = 1.0 / (1.0 + jnp.exp(-gate))
            silu = gate * sig
            hb = (silu * up).astype(bf16)
            hid[b] = hb
            if i == 0:
                rest_ready()
            gh = back_product(pair_of(c_all, b), wd_v[...])
            ggb = (gh * up * (sig * (1.0 + gate * (1.0 - sig)))).astype(bf16)
            gub = (gh * silu).astype(bf16)
            gg[b] = ggb
            gu[b] = gub
            pb = (back_product(ggb, wg_v[...]) + back_product(gub, wu_v[...])).astype(bf16)
            p_out[b, 0] = pb[:ROWS]
            p_out[b, 1] = pb[ROWS:]
            sc.sibling(i).start()
            if i > 0:
                sc.pass_on(i - 1)
            if i > 1:
                sc.relay(i - 2)
            db = dot(hb, wd_v[...]).astype(bf16)
            dpart[b, 0] = db[:ROWS]
            dpart[b, 1] = db[ROWS:]

        def x_copy(which, s):
            tx, rx = ((gate_tx, gate_rx), (down_tx, down_rx), (up_tx, up_rx))[which]
            return rcopy(
                tx.at[others[s]], rx.at[group], s_x.at[which, s], r_x.at[which, s], tpeers[s]
            )

        def send_grads(which):
            tx, rx = ((gate_tx, gate_rx), (down_tx, down_rx), (up_tx, up_rx))[which]
            for s in range(T - 1):
                x_copy(which, s).start()
            rx[group] = tx[group]

        def got_grads(which):
            for s in range(T - 1):
                x_copy(which, s).wait_recv()

        def flat(ref):
            return ref[...].reshape(8 * ROWS, ref.shape[-1])

        def glu_grads(grads, tx):
            prod = lead_sum(flat(grads), flat(nffn)).astype(bf16)
            for mm in range(M):
                for ff in range(2):
                    tx[mm * 2 + ff] = prod[
                        mm * seg : (mm + 1) * seg, ff * half_width : (ff + 1) * half_width
                    ]

        def down_grads():
            prod = lead_sum(flat(hid), flat(c_all))
            for mm in range(M):
                for ff in range(2):
                    piece = jnp.concatenate(
                        [
                            prod[:, blk * each : (blk + 1) * each]
                            for zl in range(2)
                            for cc in range(2)
                            for blk in [(2 * zl + ff) * 2 * M + mm * 2 + cc]
                        ],
                        axis=1,
                    )
                    down_tx[mm * 2 + ff] = packed(piece).astype(bf16)

        down_grads()
        send_grads(1)
        glu_grads(gg, gate_tx)
        send_grads(0)

        dy = sc.total()
        mid = mid_b[core]
        r = lax.rsqrt(jnp.mean(mid * mid, axis=-1, keepdims=True) + epsilon)
        gdy = gain * dy
        dv = r * gdy - mid * (r * r * r) * jnp.mean(mid * gdy, axis=-1, keepdims=True)
        gmid = c_ref[...].astype(f32) + dv
        gmid_v[...] = gmid
        ffn_part = jnp.sum(dy * mid * r, axis=0, keepdims=True)
        br_own[...] = gmid.astype(bf16)
        branch[me] = br_own[...]

        gb = Gather(br_own, branch, s_br, r_br)
        gb.own()
        glu_grads(gu, up_tx)
        send_grads(2)
        for kind in (0, 1, 2):
            gb.take(kind)
        gb.rest()

        def sent():
            for i in range(4):
                for k in range(2):
                    att_copy(k, i).wait_send()
                for k in range(4):
                    sib_att(k, i).wait_send()

                @pl.when(at_end == 0)
                def _(i=i):
                    att_copy(2, i).wait_send()
                    att_copy(3, i).wait_send()

            gb.sent()
            for which in range(3):
                for s in range(T - 1):
                    x_copy(which, s).wait_send()

        sc.sent()
        return sent, got_grads, ffn_part

    ffn_sent, got_grads, ffn_part = feed_forward()

    def back():
        sd = Scatter(dpart, d_sib, d_sum, d_relay, d_rx, s_d, r_d)
        sp = Scatter(p_out, a_sib, a_sum, a_relay, a_rx, s_p, r_p)
        for i in range(4):
            sd.sibling(i).start()

        def block_rows(b):
            return pl.ds(pl.multiple_of(b * BLOCK, BLOCK), BLOCK)

        def mixed(b, _):
            rows = block_rows(b)
            br = jnp.concatenate([branch[2 * b], branch[2 * b + 1]], axis=0)
            gm = back_product(br, wo_v[pl.ds(pl.multiple_of(me * 128, 128), 128), :])
            inv = 1.0 / totals[rows, :]
            g_v[rows, :] = (gm * inv).astype(bf16)
            w = gm * summed[rows, :] * (inv * inv)
            low = lax.broadcasted_iota(jnp.int32, w.shape, 1) < 64
            a = jnp.sum(jnp.where(low, w, 0.0), axis=1, keepdims=True)
            c = jnp.sum(jnp.where(low, 0.0, w), axis=1, keepdims=True)
            totals[rows, :] = jnp.where(low, a, c)
            return 0

        lax.fori_loop(0, 4, mixed, 0)
        for i in range(3):
            sd.pass_on(i)

        got_grads(1)
        total = down_rx[0].astype(f32)
        for k in range(1, T):
            total = total + down_rx[k].astype(f32)
        total = unpacked(total, 4 * each)
        for k in range(4):
            w_tx[k] = packed(total[:, k * each : (k + 1) * each]).astype(bf16)
        here = z % 2 * 2 + core

        def w_copy(k):
            return rcopy(w_tx.at[k], w_rx.at[here], s_w.at[k], r_w.at[here], place_dev[k])

        for k in range(4):

            @pl.when(jnp.logical_not(place_self[k]))
            def _(k=k):
                w_copy(k).start()

            @pl.when(place_self[k])
            def _(k=k):
                w_rx[here] = w_tx[k]

        for i in range(2):
            sd.relay(i)

        summed[...] = jnp.zeros_like(summed)

        def kv_copy(s):
            return rcopy(
                nffn.at[:, :, lane_block(s)], dkv_rx.at[s], s_dk.at[s], r_dk.at[s], mpeers[s]
            )

        def attend(s, _):
            mm = (m + 1 + s) % M
            dkv_acc[...] = jnp.zeros_like(dkv_acc)
            for zz in range(4):
                rows = slice(zz * BLOCK, (zz + 1) * BLOCK)
                keys = (zz + 1) * BLOCK
                token = zz * span + m * BLOCK + lax.broadcasted_iota(jnp.int32, (BLOCK, 1), 0)
                begin = begin_of(token, doc_ref)
                for h in range(2):
                    lanes = slice(h * 64, h * 64 + 64)
                    q = q_rows[rows, lanes]
                    g = g_v[rows, lanes]
                    k = kv_all[mm, :keys, :64]
                    v = kv_all[mm, :keys, 64:]
                    e = block_weights(q, k, begin, zz, m, mm, span)
                    dp = back_product(g, v)
                    ds = (e * (dp - totals[rows, h * 64 : h * 64 + 1])).astype(bf16)
                    summed[rows, lanes] += dot(ds, k)
                    dkv_acc[:keys, :64] += lead_sum(ds, q)
                    dkv_acc[:keys, 64:] += lead_sum(e.astype(bf16), g)

            @pl.when(s < M - 1)
            def _():
                nffn[:, :, lane_block(s)] = dkv_acc[...].astype(bf16).reshape(4, BLOCK, 128)

                for ss in range(M - 1):

                    @pl.when(s == ss)
                    def _(ss=ss):
                        kv_copy(ss).start()

            return 0

        lax.fori_loop(0, M, attend, 0)

        def over_groups(rx):
            total = rx[0].astype(f32)
            for k in range(1, T):
                total = total + rx[k].astype(f32)
            return total

        got_grads(0)
        gate_ref[...] = jnp.transpose(over_groups(gate_rx))

        strip = jnp.concatenate(
            [branch[j, :, pl.ds(pl.multiple_of(z * 256, 128), 256)] for j in range(8)], axis=0
        )
        strip = jnp.concatenate(
            [
                jnp.where(
                    core == 0,
                    strip[:, 2 * mm * each : (2 * mm + 1) * each],
                    strip[:, (2 * mm + 1) * each : (2 * mm + 2) * each],
                )
                for mm in range(M)
            ],
            axis=1,
        )
        prod = lead_sum(att_all[...].reshape(8 * ROWS, WIDTH), strip).astype(bf16)
        for mm in range(M):
            for ff in range(2):
                ap_tx[mm * 2 + ff] = packed(
                    prod[ff * half_width : (ff + 1) * half_width, mm * each : (mm + 1) * each]
                )

        def a_copy(s):
            return rcopy(ap_tx.at[others[s]], ap_rx.at[group], s_ap.at[s], r_ap.at[s], tpeers[s])

        for s in range(M - 1):
            kv_copy(s).wait_recv()
        for s in range(T - 1):
            a_copy(s).start()
        ap_rx[group] = ap_tx[group]

        qgain = qgain_ref[...]
        kgain = kgain_ref[...]

        def head_mean(v):
            low = lax.broadcasted_iota(jnp.int32, v.shape, 1) < 64
            a = jnp.sum(jnp.where(low, v, 0.0), axis=1, keepdims=True)
            c = jnp.sum(jnp.where(low, 0.0, v), axis=1, keepdims=True)
            return jnp.where(low, a, c) * (1.0 / 64)

        def heads_back(i, carry):
            qg, kg, ag = carry
            b = jnp.where(i == 0, sp.order[0], jnp.where(i == 1, sp.order[1], jnp.where(i == 2, sp.order[2], z)))
            rows = block_rows(b)
            co = cosine[rows, :]
            si = sine[rows, :]

            def through(v, dy, gain):
                dy = dy * co - turn(dy) * si
                r = head_scale(v)
                gdy = gain * dy
                dv = r * gdy - v * (r * r * r) * head_mean(v * gdy)
                return dv, jnp.sum(dy * v * r, axis=0, keepdims=True)

            st = stacked[rows, :]
            dq, qpart = through(st[:, :128], summed[rows, :] * HEAD_SIZE ** (-0.5), qgain)
            dkv = dkv_acc[rows, :]
            for s in range(M - 1):
                dkv = dkv + dkv_rx[s, b].astype(f32)
            dk, kpart = through(st[:, 128:], dkv, kgain)
            low = lax.broadcasted_iota(jnp.int32, dkv.shape, 1) < 64
            gs = jnp.concatenate([dq, jnp.where(low, dk, dkv)], axis=1).astype(bf16)
            gs_v[rows, :] = gs
            pb = back_product(gs, w_heads[...])
            xb = jnp.concatenate([x_all[2 * b], x_all[2 * b + 1]], axis=0).astype(f32)
            rb = lax.rsqrt(jnp.mean(xb * xb, axis=-1, keepdims=True) + epsilon)
            ag = ag + jnp.sum(pb * (xb * rb), axis=0, keepdims=True)
            pb = pb.astype(bf16)
            p_out[b, 0] = pb[:ROWS]
            p_out[b, 1] = pb[ROWS:]
            rcopy(
                p_out.at[b, 1 - core], a_sib.at[i], s_p.at[i], r_p.at[i], sib
            ).start()
            return qg + qpart, kg + kpart, ag

        zero = jnp.zeros((1, 128), f32)
        qg, kg, ag = lax.fori_loop(
            0, 4, heads_back, (zero, zero, jnp.zeros((1, WIDTH), f32))
        )
        for i in range(3):
            sp.pass_on(i)

        def stack(row):
            return jnp.concatenate([row[:, k * 128 : (k + 1) * 128] for k in range(8)], axis=0)

        gn_tx[0:8, :] = stack(ag)
        gn_tx[8:16, :] = stack(ffn_part)
        gn_tx[16:24, :] = jnp.concatenate([qg, kg, jnp.zeros((6, 128), f32)], axis=0)
        gpeers = [sib] + zpeers + cross

        def g_copy(k):
            return rcopy(gn_tx, gn_rx.at[k], s_g.at[k], r_g.at[k], gpeers[k])

        for k in range(7):
            g_copy(k).start()

        prod = lead_sum(normed[...], gs_v[...]).astype(bf16)
        qw, kw = 128 // M, 64 // M
        for i in range(M):
            for ff in range(2):
                rows = slice(ff * half_width, (ff + 1) * half_width)
                h_tx[i * 2 + ff] = packed(
                    jnp.concatenate(
                        [
                            prod[rows, i * qw : (i + 1) * qw],
                            prod[rows, 128 + i * kw : 128 + (i + 1) * kw],
                            prod[rows, 192 + i * kw : 192 + (i + 1) * kw],
                        ],
                        axis=1,
                    )
                )

        def h_copy(s):
            return rcopy(
                h_tx.at[pieces[s]], h_rx.at[group], s_h.at[s], r_h.at[group], piece_to[s]
            )

        def h_got(s):
            return rcopy(
                h_tx.at[pieces[s]], h_rx.at[sources[s]], s_h.at[s], r_h.at[sources[s]], piece_from[s]
            )

        for s in range(T):

            @pl.when(to_self[s])
            def _(s=s):
                h_rx[group] = h_tx[pieces[s]]

            @pl.when(jnp.logical_not(to_self[s]))
            def _(s=s):
                h_copy(s).start()

        for i in range(2):
            sp.relay(i)
        gains = gn_tx[...]
        for k in range(7):
            g_copy(k).wait_recv()
        for k in range(7):
            gains = gains + gn_rx[k]
        gt_tx[...] = gains

        def t_copy(s):
            return rcopy(gt_tx, gt_rx.at[s], s_t.at[s], r_t.at[s], tpeers[s])

        for s in range(T - 1):
            t_copy(s).start()


        got_grads(2)
        up_ref[...] = jnp.transpose(over_groups(up_rx))
        for k in range(4):

            @pl.when(jnp.logical_not(from_me[k]))
            def _(k=k):
                rcopy(w_tx.at[k], w_rx.at[k], s_w.at[k], r_w.at[k], place_from[k]).wait_recv()

        seg = gate_rx.shape[1]
        for zl in range(2):
            for cc in range(2):
                for mm in range(M):
                    at = ((zl * M + mm) * 2 + cc) * seg
                    down_ref[at : at + seg, :] = w_rx[
                        zl * 2 + cc, :, mm * each : (mm + 1) * each
                    ].astype(f32)

        out_ref[...] = mid_b[core] + sd.total()
        dy = sp.total()
        x = x_ref[...].astype(f32)
        r = lax.rsqrt(jnp.mean(x * x, axis=-1, keepdims=True) + epsilon)
        gdy = again_ref[...] * dy
        dv = r * gdy - x * (r * r * r) * jnp.mean(x * gdy, axis=-1, keepdims=True)
        igrad_ref[...] = gmid_v[...] + dv

        for s in range(T):

            @pl.when(jnp.logical_not(from_self[s]))
            def _(s=s):
                h_got(s).wait_recv()

        for s in range(T - 1):
            a_copy(s).wait_recv()
        hsum = h_rx[0].astype(f32)
        asum = ap_rx[0].astype(f32)
        for k in range(1, T):
            hsum = hsum + h_rx[k].astype(f32)
            asum = asum + ap_rx[k].astype(f32)
        heads_ref[...] = unpacked(hsum, 256 // M)
        size = asum.shape[0]
        for g in range(128 // each):
            attn_ref[g * size : (g + 1) * size, :] = asum[:, g * each : (g + 1) * each]

        for s in range(T - 1):
            t_copy(s).wait_recv()
            gains = gains + gt_rx[s]
        gains_ref[...] = gains

        sd.sent()
        sp.sent()
        for k in range(4):

            @pl.when(jnp.logical_not(place_self[k]))
            def _(k=k):
                w_copy(k).wait_send()

        for s in range(M - 1):
            kv_copy(s).wait_send()
        for s in range(T):

            @pl.when(jnp.logical_not(to_self[s]))
            def _(s=s):
                h_copy(s).wait_send()

        for s in range(T - 1):
            a_copy(s).wait_send()
            t_copy(s).wait_send()
        for k in range(7):
            g_copy(k).wait_send()

    back()
    front_sent()
    ffn_sent()


def block(*args, cid):
    n = lax.axis_size("ctx")
    M, T, seg, each = n // 8, n // 4, FF // n, WIDTH // n
    cols = FF // 8
    tokens = 8 * ROWS
    half_width = WIDTH // 2
    part = (ROWS, WIDTH)
    VS, sem = pltpu.VMEM, pltpu.SemaphoreType.DMA
    shape = jax.ShapeDtypeStruct

    def sems(*shapes):
        return [sem(v) for v in shapes]

    return pl.pallas_call(
        block_kernel,
        out_shape=(
            shape(part, f32),
            shape(part, f32),
            shape((24, 128), f32),
            shape((half_width, 256 // M), f32),
            shape((half_width, each), f32),
            shape((half_width, seg), f32),
            shape((half_width, seg), f32),
            shape((FF // 2, each), f32),
        ),
        in_specs=[pl.BlockSpec(memory_space=pltpu.SMEM)] + vspecs(2) + any_specs(5) + vspecs(4),
        out_specs=tuple(vspecs(8)),
        scratch_shapes=[
            VS((8,) + part, bf16),
            VS((8,) + part, bf16),
            VS((WIDTH, 256), bf16),
            VS((WIDTH, cols), bf16),
            VS((WIDTH, cols), bf16),
            VS((cols, WIDTH), bf16),
            VS((WIDTH, WIDTH), bf16),
            VS((tokens, 128), bf16),
            VS((M, tokens, 128), bf16),
            VS((4, BLOCK, 128), bf16),
            VS((tokens, 128), f32),
            VS((tokens, 128), f32),
            VS((tokens, 256), f32),
            VS((tokens, WIDTH), bf16),
            VS((tokens, 128), f32),
            VS((tokens, 128), f32),
            VS((4, BLOCK, WIDTH), bf16),
            VS((8,) + part, bf16),
            VS(part, f32),
            VS((4, 2) + part, bf16),
            VS((4, BLOCK, WIDTH), bf16),
            VS((4, BLOCK, cols), bf16),
            VS((4, BLOCK, cols), bf16),
            VS((4, BLOCK, cols), bf16),
            VS((2,) + part, f32),
            VS((4, 2) + part, bf16),
            VS((T, seg, half_width), bf16),
            VS((T, seg, half_width), bf16),
            *[VS((T, cols * 4 * each // max(128, 4 * each), max(128, 4 * each)), bf16)] * 2,
            VS((T, seg, half_width), bf16),
            VS((T, seg, half_width), bf16),
            VS(part, bf16),
            *scatter_scratch(),
            *scatter_scratch(),
            *scatter_scratch()[4:],
            VS((tokens, 128), bf16),
            VS((tokens, 128), f32),
            VS((M - 1, 4, BLOCK, 128), bf16),
            VS((tokens, 256), bf16),
            *[VS((T, half_width * 2 // M, 128), bf16)] * 2,
            VS((T, half_width * each // 128, 128), bf16),
            VS((T, half_width * each // 128, 128), bf16),
            VS((24, 128), f32),
            VS((7, 24, 128), f32),
            VS((24, 128), f32),
            VS((T - 1, 24, 128), f32),
            VS((4, cols * each // 128, 128), bf16),
            VS((4, cols * each // 128, 128), bf16),
            *sems((9,), (7,), (9,), (7,), (1,), (1,), (4,), (4,), (4,), (4,), (2,), (2,)),
            *sems((4, M - 1), (4, M - 1), (5,)),
            *sems((2, 4), (3, 4), (2, 4), (4, 4), (4, 4), (9,), (7,), (3, T - 1), (3, T - 1)),
            *sems((M - 1,), (M - 1,), (T,), (T,), (T - 1,), (T - 1,), (7,), (7,)),
            *sems((T - 1,), (T - 1,), (4,), (4,)),
        ],
        compiler_params=pltpu.CompilerParams(
            collective_id=cid, has_side_effects=True, vmem_limit_bytes=VMEM_LIMIT
        ),
        name="block",
    )(*args)


def root_mean_norm(rows, gain):
    return (
        rows * lax.rsqrt(jnp.mean(rows * rows, axis=-1, keepdims=True) + epsilon) * gain
    )


def rotary(rows, cosine, sine):
    halfway = rows.shape[-1] // 2
    leading = rows[..., :halfway]
    trailing = rows[..., halfway:]
    return jnp.concatenate(
        [leading * cosine - trailing * sine, leading * sine + trailing * cosine], axis=-1
    )


SWAP = [(0, 1), (1, 0)]


def halves(f, own, other, axis):
    return jnp.where(
        f == 0,
        jnp.concatenate([own, other], axis=axis),
        jnp.concatenate([other, own], axis=axis),
    )


def local(
    hidden_in,
    doc_lengths,
    attn_gain,
    query_gain,
    key_norm_gain,
    ffn_gain,
    query_proj,
    key_weight,
    value_weight,
    attn_proj,
    gate_proj,
    up_proj,
    down_proj,
    out_cotangent,
):
    n_ctx = lax.axis_size("ctx")
    M = n_ctx // 8
    T = 2 * M
    z, m, core, f = who()
    head = slot(z, core)
    tokens = 8 * ROWS
    span = n_ctx // 4 * ROWS
    segment = FF // n_ctx
    columns = M * segment
    half_width = WIDTH // 2
    each = WIDTH // n_ctx

    heads_own = jnp.concatenate(
        [
            lax.dynamic_slice(query_proj, (0, head * 128), (half_width, 128)),
            lax.dynamic_slice(key_weight, (0, head * 64), (half_width, 64)),
            lax.dynamic_slice(value_weight, (0, head * 64), (half_width, 64)),
        ],
        axis=1,
    ).astype(bf16)
    first = z * (n_ctx // 4) + core
    gate_own, up_own = [
        jnp.concatenate(
            [
                lax.dynamic_slice(w, (0, (first + 2 * mm) * segment), (half_width, segment))
                for mm in range(M)
            ],
            axis=1,
        ).astype(bf16)
        for w in (gate_proj, up_proj)
    ]
    down_own = jnp.concatenate(
        [
            lax.dynamic_slice(
                down_proj, ((first + 2 * mm) * segment - f * (FF // 2), 0), (segment, WIDTH)
            )
            for mm in range(M)
        ],
        axis=0,
    ).astype(bf16)
    out_own = attn_proj.astype(bf16)

    cotangent = out_cotangent[0]
    q_gain = jnp.tile(query_gain, 2)[None]
    k_gain = jnp.concatenate([key_norm_gain, jnp.ones((64,), f32)])[None]
    output, input_grad, gains, heads_grad, attn_grad, gate_grad, up_grad, down_grad = block(
        doc_lengths,
        hidden_in[0],
        cotangent,
        heads_own,
        gate_own,
        up_own,
        down_own,
        out_own,
        attn_gain[None],
        q_gain,
        k_gain,
        ffn_gain[None],
        cid=1,
    )
    qw, kw = 128 // M, 64 // M
    query_grad = heads_grad[:, :qw]
    key_grad = heads_grad[:, qw : qw + kw]
    value_grad = heads_grad[:, qw + kw :]

    return (
        output[None],
        input_grad[None],
        gains[:8].reshape(WIDTH),
        gains[16, :64] + gains[16, 64:],
        gains[17, :64],
        gains[8:16].reshape(WIDTH),
        query_grad,
        key_grad,
        value_grad,
        attn_grad,
        gate_grad,
        up_grad,
        down_grad,
    )


def solution(mesh):
    in_specs = (
        P("fsdp", "ctx", None),
        P("fsdp", None),
        P(),
        P(),
        P(),
        P(),
        P("fsdp", None),
        P("fsdp", None),
        P("fsdp", None),
        P("fsdp", None),
        P("fsdp", None),
        P("fsdp", None),
        P("fsdp", None),
        P("fsdp", "ctx", None),
    )
    out_specs = (
        P("fsdp", "ctx", None),
        P("fsdp", "ctx", None),
        P(),
        P(),
        P(),
        P(),
        P("fsdp", "ctx"),
        P("fsdp", "ctx"),
        P("fsdp", "ctx"),
        P("fsdp", "ctx"),
        P("fsdp", "ctx"),
        P("fsdp", "ctx"),
        P("fsdp", "ctx"),
    )
    return jax.shard_map(local, mesh=mesh, in_specs=in_specs, out_specs=out_specs, check_vma=False)
```

```python
import functools
import math

import jax
import jax.numpy as jnp
from jax import lax
from jax.experimental import pallas as pl
from jax.experimental.pallas import tpu as pltpu
from jax.sharding import PartitionSpec as P

QUERY_HEADS = 16
KEY_VALUE_HEADS = 8
HEAD_SIZE = 64
FF = 4608
WIDTH = 1024
ROWS = 128

epsilon = 1e-05
rope_base = 1000000.0
MESH = pl.DeviceIdType.MESH
ANY = pl.ANY
VMEM_LIMIT = 64 * 2**20 - 2**17
bf16 = jnp.bfloat16
f32 = jnp.float32


def who():
    n = lax.axis_size("ctx")
    c = lax.axis_index("ctx")
    f = lax.axis_index("fsdp")
    q = n // 4
    return c // q, (c % q) // 2, c % 2, f


def dev(z, m, core, f):
    return (z * (lax.axis_size("ctx") // 4) + m * 2 + core, f)


def slot(z, core):
    return z * 2 + core


def enter(peers):
    bar = pltpu.get_barrier_semaphore()
    for p in peers:
        pl.semaphore_signal(bar, inc=1, device_id=p, device_id_type=MESH)
    pl.semaphore_wait(bar, len(peers))


def rcopy(src, dst, s, r, to):
    return pltpu.make_async_remote_copy(
        src_ref=src, dst_ref=dst, send_sem=s, recv_sem=r, device_id=to, device_id_type=MESH
    )


def comm_params(cid):
    return pltpu.CompilerParams(collective_id=cid, has_side_effects=True)


def any_specs(n):
    return [pl.BlockSpec(memory_space=ANY)] * n


def line_of(z):
    return z + 1 - 2 * (z % 2), 2 - z // 2, 3 - 3 * (z // 2), 1 - ((z + 1) // 2) % 2


class Gather:
    def __init__(self, src, dst, ss, rs):
        z, m, core, f = who()
        partner, middle, end, self.at_end = line_of(z)
        self.src, self.dst, self.ss, self.rs = src, dst, ss, rs
        self.me = slot(z, core)
        self.slots = [slot(zz, core) for zz in (partner, middle, end)]
        self.partner = dev(partner, m, core, f)
        self.middle = dev(middle, m, core, f)
        self.sib = dev(z, m, 1 - core, f)

    def copy(self, k):
        src, dst, ss, rs = self.src, self.dst, self.ss.at[k], self.rs
        if k == 0:
            return rcopy(src, dst.at[self.me], ss, rs.at[0], self.partner)
        if k == 1:
            return rcopy(src, dst.at[self.me], ss, rs.at[1 + self.at_end], self.middle)
        if k == 3:
            return rcopy(src, dst.at[self.me], ss, rs.at[3], self.sib)
        if k < 7:
            j = self.slots[k - 4]
            return rcopy(dst.at[j], dst.at[j], ss, rs.at[k], self.sib)
        j = self.slots[k - 6]
        return rcopy(dst.at[j], dst.at[j], ss, rs.at[k - 6], self.partner)

    def own(self):
        for k in (1, 0, 3):
            self.copy(k).start()

    def take(self, kind):
        j = self.slots[kind]
        rcopy(
            self.dst.at[j], self.dst.at[j], self.ss.at[0], self.rs.at[kind], self.partner
        ).wait_recv()
        if kind > 0:

            @pl.when(self.at_end == 0)
            def _():
                self.copy(6 + kind).start()

        self.copy(4 + kind).start()

    def rest(self):
        for k in range(3, 7):
            self.copy(k).wait_recv()

    def sent(self):
        for k in (0, 1, 3, 4, 5, 6):
            self.copy(k).wait_send()

        @pl.when(self.at_end == 0)
        def _():
            self.copy(7).wait_send()
            self.copy(8).wait_send()


class Scatter:
    def __init__(self, part, buf, sums, relay, rx, ss, rs):
        z, m, self.core, f = who()
        core = self.core
        partner, middle, end, self.at_end = line_of(z)
        self.z = z
        self.part, self.buf, self.sums, self.relay_buf, self.rx = part, buf, sums, relay, rx
        self.ss, self.rs = ss, rs
        self.order = [end, middle, partner, z]
        self.sib = dev(z, m, 1 - core, f)
        self.to = [dev(zz, m, core, f) for zz in self.order[:3]]

    def sibling(self, i):
        return rcopy(
            self.part.at[self.order[i], 1 - self.core],
            self.buf.at[i],
            self.ss.at[i],
            self.rs.at[i],
            self.sib,
        )

    def copy(self, i, at_end):
        if i == 2:
            return rcopy(
                self.sums.at[2], self.rx.at[0], self.ss.at[6], self.rs.at[4], self.to[2]
            )
        if at_end:
            return rcopy(
                self.sums.at[i], self.relay_buf.at[i], self.ss.at[4 + i], self.rs.at[6 + i], self.to[2]
            )
        return rcopy(self.sums.at[i], self.rx.at[1], self.ss.at[4 + i], self.rs.at[5], self.to[i])

    def pass_on(self, i):
        self.sibling(i).wait_recv()
        self.sums[i] = (
            self.part[self.order[i], self.core].astype(f32) + self.buf[i].astype(f32)
        ).astype(bf16)
        if i == 2:
            self.copy(2, True).start()
        else:

            @pl.when(self.at_end == 1)
            def _():
                self.copy(i, True).start()

    def relay(self, i):
        @pl.when(self.at_end == 0)
        def _():
            self.copy(i, True).wait_recv()
            self.sums[i] = (
                self.sums[i].astype(f32) + self.relay_buf[i].astype(f32)
            ).astype(bf16)
            self.copy(i, False).start()

    def total(self):
        self.sibling(3).wait_recv()
        total = self.part[self.z, self.core].astype(f32) + self.buf[3].astype(f32)
        self.copy(2, True).wait_recv()
        total = total + self.rx[0].astype(f32)
        self.copy(0, False).wait_recv()
        return total + self.rx[1].astype(f32)

    def sent(self):
        for i in range(4):
            self.sibling(i).wait_send()
        for i in range(3):
            self.copy(i, False).wait_send()


def scatter_scratch():
    part = (ROWS, WIDTH)
    return [
        pltpu.VMEM((4,) + part, bf16),
        pltpu.VMEM((3,) + part, bf16),
        pltpu.VMEM((2,) + part, bf16),
        pltpu.VMEM((2,) + part, bf16),
        pltpu.SemaphoreType.DMA((7,)),
        pltpu.SemaphoreType.DMA((8,)),
    ]


def back_product(left, right):
    return lax.dot_general(
        left, right, (((1,), (1,)), ((), ())), preferred_element_type=f32
    )


def lead_sum(left, right):
    return lax.dot_general(
        left, right, (((0,), (0,)), ((), ())), preferred_element_type=f32
    )


def dot(left, right):
    return jnp.dot(left, right, preferred_element_type=f32)


BLOCK = 2 * ROWS


def block_weights(q, k, begin, z, m, mm, span):
    keys = (z + 1) * BLOCK
    key = lax.broadcasted_iota(jnp.int32, (1, keys), 1)
    key = key // BLOCK * span + key % BLOCK + mm * BLOCK
    token = z * span + m * BLOCK + lax.broadcasted_iota(jnp.int32, (BLOCK, 1), 0)
    e = jnp.exp(back_product(q, k))
    return jnp.where((key >= begin) & (key <= token), e, 0.0)


VM = pltpu.VMEM


def vspecs(n):
    return [pl.BlockSpec(memory_space=VM)] * n


def begin_of(token, doc_ref):
    begin = jnp.zeros(token.shape, jnp.int32)
    start = doc_ref[0, 0]
    for d in range(1, doc_ref.shape[1]):
        begin = jnp.where(token >= start, start, begin)
        start = start + doc_ref[0, d]
    return begin


def turn(v):
    lane = lax.broadcasted_iota(jnp.int32, v.shape, 1)
    n = v.shape[1]
    return jnp.where(lane % 64 < 32, pltpu.roll(v, n - 32, 1), pltpu.roll(v, 32, 1))


def head_scale(v):
    sq = v * v
    if v.shape[1] == 64:
        return lax.rsqrt(jnp.mean(sq, axis=1, keepdims=True) + epsilon)
    low = lax.broadcasted_iota(jnp.int32, v.shape, 1) < 64
    a = jnp.sum(jnp.where(low, sq, 0.0), axis=1, keepdims=True)
    b = jnp.sum(jnp.where(low, 0.0, sq), axis=1, keepdims=True)
    return lax.rsqrt(jnp.where(low, a, b) * (1.0 / 64) + epsilon)


def block_kernel(
    doc_ref, x_ref, c_ref, wh_own, wg_own, wu_own, wd_own, wo_own,
    again_ref, qgain_ref, kgain_ref, fgain_ref,
    out_ref, igrad_ref, gains_ref, heads_ref, attn_ref, gate_ref, up_ref, down_ref,
    x_all, c_all, w_heads, wg_v, wu_v, wd_v, wo_v, q_rows, kv_all, att, summed, totals,
    stacked, normed, cosine, sine,
    att_all, branch, gmid_v, dpart, nffn, hid, gg, gu, mid_b, p_out, gate_tx, gate_rx, down_tx, down_rx,
    up_tx, up_rx, br_own,
    a_sib, a_sum, a_relay, a_rx, s_a, r_a, d_sib, d_sum, d_relay, d_rx, s_d, r_d,
    s_p, r_p,
    g_v, dkv_acc, dkv_rx, gs_v,
    h_tx, h_rx, ap_tx, ap_rx, gn_tx, gn_rx, gt_tx, gt_rx, w_tx, w_rx,
    s_x0, r_x0, s_c, r_c, s_h0, r_h0, s_w0, r_w0, s_v, r_v, s_o, r_o, s_k, r_k, ld,
    s_att, r_att, s_pass, s_sib, r_sib, s_br, r_br, s_x, r_x,
    s_dk, r_dk, s_h, r_h, s_ap, r_ap, s_g, r_g, s_t, r_t, s_w, r_w,
):
    z, m, core, f = who()
    M = lax.axis_size("ctx") // 8
    T = 2 * M
    span = lax.axis_size("ctx") // 4 * ROWS
    each = WIDTH // lax.axis_size("ctx")
    seg = FF // lax.axis_size("ctx")
    half_width = WIDTH // 2
    partner, middle, end, at_end = line_of(z)
    sib = dev(z, m, 1 - core, f)
    zs = [(z + s) % 4 for s in (1, 2, 3)]
    zpeers = [dev(zz, m, core, f) for zz in zs]
    cross = [dev(zz, m, 1 - core, f) for zz in zs]
    hm = m % 2
    pair = dev(z, m, core, 1 - f)
    beside = dev(z, m + 1 - 2 * hm, core, f)
    mpeers = [dev(z, (m + s) % M, core, f) for s in range(1, M)]
    group = m * 2 + f
    others = [(group + s) % T for s in range(1, T)]
    tpeers = [dev(z, o // 2, core, o % 2) for o in others]
    owner = f == z // 2
    me = slot(z, core)

    pieces = [(group + s) % T for s in range(T)]
    rest_to = [core * M + p // 2 for p in pieces]
    piece_to = [dev(z, rr // 2, rr % 2, p % 2) for rr, p in zip(rest_to, pieces)]
    to_self = [(rr == m * 2 + core) & (p % 2 == f) for rr, p in zip(rest_to, pieces)]
    rest = m * 2 + core
    core_from = rest // M
    sources = [(group + s) % T for s in range(T)]
    piece_from = [dev(z, o // 2, core_from, o % 2) for o in sources]
    from_self = [(core_from == core) & (o == group) for o in sources]

    mine = pl.ds(pl.multiple_of(f * half_width, half_width), half_width)
    load_heads = pltpu.make_async_copy(wh_own, w_heads.at[mine], ld.at[0])
    load_out = pltpu.make_async_copy(wo_own, wo_v.at[mine], ld.at[1])
    load_gate = pltpu.make_async_copy(wg_own, wg_v.at[mine], ld.at[2])
    load_up = pltpu.make_async_copy(wu_own, wu_v.at[mine], ld.at[3])
    load_down = pltpu.make_async_copy(wd_own, wd_v, ld.at[4])
    for cp in (load_heads, load_out, load_gate, load_up):
        cp.start()

    @pl.when(owner)
    def _():
        load_down.start()

    bar = pltpu.get_barrier_semaphore()
    fixed = [sib] + zpeers + cross + tpeers
    for p in fixed:
        pl.semaphore_signal(bar, inc=1, device_id=p, device_id_type=MESH)
    for s in range(T):

        @pl.when(jnp.logical_not(from_self[s]))
        def _(s=s):
            pl.semaphore_signal(bar, inc=1, device_id=piece_from[s], device_id_type=MESH)

    place = [(zl, cc) for zl in range(2) for cc in range(2)]
    place_dev = [dev(2 * zl + f, m, cc, z // 2) for zl, cc in place]
    place_self = [owner & (z == 2 * zl + f) & (core == cc) for zl, cc in place]
    place_from = [dev(2 * f + zb, m, cc, z % 2) for zb, cc in place]
    from_me = [owner & (z == 2 * f + zb) & (z % 2 == f) & (core == cc) for zb, cc in place]
    for k in range(4):

        @pl.when(jnp.logical_not(from_me[k]))
        def _(k=k):
            pl.semaphore_signal(bar, inc=1, device_id=place_from[k], device_id_type=MESH)

    pl.semaphore_wait(
        bar,
        len(fixed)
        + T
        + 4
        - jnp.where(core_from == core, 1, 0)
        - jnp.where(owner & (z % 2 == f), 1, 0),
    )

    def lane_block(j):
        return pl.ds(pl.multiple_of(j * 128, 128), 128)

    def front():
        gx = Gather(x_ref, x_all, s_x0, r_x0)
        gc = Gather(c_ref, c_all, s_c, r_c)
        gx.own()
        head_rows = pl.ds(f * half_width, half_width)
        heads_copy = rcopy(wh_own, w_heads.at[head_rows], s_h0.at[0], r_h0.at[0], pair)
        heads_copy.start()

        quarter = half_width // 2
        eighth = half_width // 4
        cols = wd_own.shape[0]

        def w_copy(k, stage):
            src, dst = ((wg_own, wg_v), (wu_own, wu_v), (wd_own, wd_v), (wo_own, wo_v))[k]
            base = 0 if k == 2 else (f if stage == 0 else 1 - f) * half_width
            size = (quarter, quarter, cols // 2, eighth)[k]
            part = hm * 2 + core if k == 3 else hm
            place = dst.at[pl.ds(pl.multiple_of(base + part * size, 8), size)]
            if stage == 0:
                here = src.at[pl.ds(pl.multiple_of(part * size, 8), size)]
                return rcopy(here, place, s_w0.at[k], r_w0.at[k], pair)
            return rcopy(place, place, s_v.at[k], r_v.at[k], beside)

        def out_copy(k):
            part = (hm if k == 0 else 1 - hm) * 2 + core
            base = (1 - f) * half_width
            place = wo_v.at[pl.ds(pl.multiple_of(base + part * eighth, 8), eighth)]
            return rcopy(place, place, s_o.at[k], r_o.at[k], sib)

        w_copy(0, 0).start()
        x_all[me] = x_ref[...]
        c_all[me] = c_ref[...]

        lane = lax.broadcasted_iota(jnp.int32, (1, 128), 1) % 32
        freq = jnp.exp(lane.astype(f32) * (-2.0 / 64 * math.log(rope_base)))
        sign = jnp.where(lax.broadcasted_iota(jnp.int32, (1, 128), 1) % 64 < 32, -1.0, 1.0)

        def tokens_of(zz):
            return zz * span + m * BLOCK + lax.broadcasted_iota(jnp.int32, (BLOCK, 1), 0)

        def table(zz, _):
            rows = pl.ds(pl.multiple_of(zz * BLOCK, BLOCK), BLOCK)
            token = tokens_of(zz)
            place = (token - begin_of(token, doc_ref)).astype(f32)
            angle = place * freq
            cosine[rows, :] = jnp.cos(angle)
            sine[rows, :] = jnp.sin(angle) * sign
            return 0

        lax.fori_loop(0, 4, table, 0)
        for k in (1, 3):
            w_copy(k, 0).start()
        for kind in (0, 1, 2):
            gx.take(kind)
        gc.own()

        @pl.when(owner)
        def _():
            w_copy(2, 0).start()

        heads_copy.wait_recv()

        def kv_copy(b, s):
            rows = pl.ds(pl.multiple_of(b * BLOCK, BLOCK), BLOCK)
            place = kv_all.at[m, rows]
            return rcopy(place, place, s_k.at[b, s], r_k.at[b, s], mpeers[s])

        again = again_ref[...]
        qgain = qgain_ref[...]
        kgain = kgain_ref[...]

        gx.rest()
        load_heads.wait()
        for k in range(2):
            w_copy(k, 0).wait_recv()
            w_copy(k, 1).start()

        def project(b, _):
            rows = pl.ds(pl.multiple_of(b * BLOCK, BLOCK), BLOCK)
            x = jnp.concatenate([x_all[2 * b], x_all[2 * b + 1]], axis=0).astype(f32)
            nb = (
                x * lax.rsqrt(jnp.mean(x * x, axis=-1, keepdims=True) + epsilon) * again
            ).astype(bf16)
            normed[rows, :] = nb
            st = dot(nb, w_heads[...])
            stacked[rows, :] = st
            co = cosine[rows, :]
            si = sine[rows, :]
            q = st[:, :128]
            q = q * head_scale(q) * qgain
            q_rows[rows, :] = ((q * co + turn(q) * si) * HEAD_SIZE ** (-0.5)).astype(bf16)
            kv = st[:, 128:]
            low = lax.broadcasted_iota(jnp.int32, kv.shape, 1) < 64
            k = kv * head_scale(kv) * kgain
            kv_all[m, rows, :] = jnp.where(low, k * co + turn(k) * si, kv).astype(bf16)
            for s in range(M - 1):
                kv_copy(b, s).start()
            return 0

        lax.fori_loop(0, 4, project, 0)

        w_copy(3, 0).wait_recv()
        w_copy(3, 1).start()
        out_copy(0).start()

        @pl.when(at_end == 0)
        def _():
            for kind in (0, 1, 2):
                gc.take(kind)

        summed[...] = jnp.zeros_like(summed)
        totals[...] = jnp.zeros_like(totals)

        def attend(s, _):
            mm = (m + M - s) % M

            @pl.when(s > 0)
            def _():
                for b in range(4):
                    rows = pl.ds(b * BLOCK, BLOCK)
                    place = kv_all.at[mm, rows]
                    rcopy(place, place, s_k.at[b, s - 1], r_k.at[b, s - 1], sib).wait_recv()

            @pl.when((s == 1) & jnp.logical_not(owner))
            def _():
                w_copy(2, 0).wait_recv()
                w_copy(2, 1).start()

            for zz in range(4):
                rows = slice(zz * BLOCK, (zz + 1) * BLOCK)
                keys = (zz + 1) * BLOCK
                begin = begin_of(tokens_of(zz), doc_ref)
                for h in range(2):
                    lanes = slice(h * 64, h * 64 + 64)
                    e = block_weights(
                        q_rows[rows, lanes], kv_all[mm, :keys, :64], begin, zz, m, mm, span
                    )
                    summed[rows, lanes] += dot(e.astype(bf16), kv_all[mm, :keys, 64:])
                    totals[rows, lanes] += jnp.broadcast_to(
                        jnp.sum(e, axis=1, keepdims=True), (BLOCK, 64)
                    )
            return 0

        lax.fori_loop(0, M, attend, 0)
        for b in range(4):
            rows = slice(b * BLOCK, (b + 1) * BLOCK)
            att[b] = (summed[rows, :] / totals[rows, :]).astype(bf16)

        def w_got(k):
            dst = (wg_v, wu_v, wd_v, wo_v)[k]
            base = 0 if k == 2 else (1 - f) * half_width
            size = (quarter, quarter, cols // 2, eighth)[k]
            part = (1 - hm) * 2 + core if k == 3 else 1 - hm
            place = dst.at[pl.ds(pl.multiple_of(base + part * size, 8), size)]
            return rcopy(place, place, s_v.at[k], r_v.at[k], beside)

        def ends_take():
            @pl.when(at_end == 1)
            def _():
                for kind in (0, 1, 2):
                    gc.take(kind)

        def out_ready():
            w_got(3).wait_recv()
            out_copy(1).start()
            load_out.wait()
            for k in range(2):
                out_copy(k).wait_recv()

        def glu_ready():
            for k in range(2):
                w_got(k).wait_recv()
            load_gate.wait()
            load_up.wait()

        def rest_ready():
            gc.rest()

            @pl.when(owner)
            def _():
                load_down.wait()

            @pl.when(jnp.logical_not(owner))
            def _():
                w_got(2).wait_recv()

        def sent():
            heads_copy.wait_send()
            gx.sent()
            gc.sent()
            for k in (0, 1, 3):
                w_copy(k, 0).wait_send()
                w_copy(k, 1).wait_send()

            @pl.when(owner)
            def _():
                w_copy(2, 0).wait_send()

            @pl.when(jnp.logical_not(owner))
            def _():
                w_copy(2, 1).wait_send()

            for k in range(2):
                out_copy(k).wait_send()
            for b in range(4):
                for s in range(M - 1):
                    kv_copy(b, s).wait_send()

        return sent, ends_take, out_ready, glu_ready, rest_ready

    front_sent, ends_take, out_ready, glu_ready, rest_ready = front()

    def feed_forward():
        def lanes(j):
            return pl.ds(pl.multiple_of(j * 128, 128), 128)

        order = [end, middle, partner, z]
        to_partner = [end, middle, z, partner]
        to_middle = [3 * (z // 2), 1 + z // 2, end, middle]
        from_slot = [slot(zz, core) for zz in (partner, middle, end)]
        to_p, to_m = dev(partner, m, core, f), dev(middle, m, core, f)

        def att_copy(k, i):
            if k == 0:
                b = to_partner[i]
                return rcopy(
                    att.at[b], att_all.at[b, :, lanes(me)], s_att.at[0, i], r_att.at[0, i], to_p
                )
            if k == 1:
                b = to_middle[i]
                return rcopy(
                    att.at[b],
                    att_all.at[b, :, lanes(me)],
                    s_att.at[1, i],
                    r_att.at[1 + at_end, i],
                    to_m,
                )
            place = att_all.at[order[i], :, lanes(from_slot[k - 1])]
            return rcopy(place, place, s_pass.at[k - 2, i], r_att.at[k - 1, (0, 1, 3, 2)[i]], to_p)

        def sib_att(k, i):
            b = order[i]
            j = me if k == 3 else from_slot[k]
            src = att.at[b] if k == 3 else att_all.at[b, :, lanes(j)]
            return rcopy(src, att_all.at[b, :, lanes(j)], s_sib.at[k, i], r_sib.at[k, i], sib)

        for i in range(4):
            att_copy(1, i).start()
            att_copy(0, i).start()
            sib_att(3, i).start()
        for b in range(4):
            att_all[b, :, lanes(me)] = att[b]

        def forward(i):
            for k in range(3):
                place = att_all.at[order[i], :, lanes(from_slot[k])]
                rcopy(place, place, s_att.at[0, i], r_att.at[k, i], to_p).wait_recv()
                if k > 0:

                    @pl.when(at_end == 0)
                    def _(k=k):
                        att_copy(k + 1, i).start()

                sib_att(k, i).start()

        ends_take()
        sc = Scatter(p_out, a_sib, a_sum, a_relay, a_rx, s_a, r_a)

        forward(0)
        gain = fgain_ref[...]

        def pair_of(ref, b):
            return jnp.concatenate([ref[2 * b], ref[2 * b + 1]], axis=0)

        for i in range(4):
            b = order[i]
            for k in range(4):
                sib_att(k, i).wait_recv()
            if i == 0:
                out_ready()
            mid = pair_of(x_all, b).astype(f32) + dot(att_all[b], wo_v[...])
            nb = (
                mid * lax.rsqrt(jnp.mean(mid * mid, axis=-1, keepdims=True) + epsilon) * gain
            ).astype(bf16)
            nffn[b] = nb
            if i == 3:
                mid_b[0] = mid[:ROWS]
                mid_b[1] = mid[ROWS:]
            for ii in ((1,), (2, 3), (), ())[i]:
                forward(ii)
            if i == 0:
                glu_ready()
            gate = dot(nb, wg_v[...])
            up = dot(nb, wu_v[...])
            sig = 1.0 / (1.0 + jnp.exp(-gate))
            silu = gate * sig
            hb = (silu * up).astype(bf16)
            hid[b] = hb
            if i == 0:
                rest_ready()
            gh = back_product(pair_of(c_all, b), wd_v[...])
            ggb = (gh * up * (sig * (1.0 + gate * (1.0 - sig)))).astype(bf16)
            gub = (gh * silu).astype(bf16)
            gg[b] = ggb
            gu[b] = gub
            pb = (back_product(ggb, wg_v[...]) + back_product(gub, wu_v[...])).astype(bf16)
            p_out[b, 0] = pb[:ROWS]
            p_out[b, 1] = pb[ROWS:]
            sc.sibling(i).start()
            if i > 0:
                sc.pass_on(i - 1)
            if i > 1:
                sc.relay(i - 2)
            db = dot(hb, wd_v[...]).astype(bf16)
            dpart[b, 0] = db[:ROWS]
            dpart[b, 1] = db[ROWS:]

        def x_copy(which, s):
            tx, rx = ((gate_tx, gate_rx), (down_tx, down_rx), (up_tx, up_rx))[which]
            return rcopy(
                tx.at[others[s]], rx.at[group], s_x.at[which, s], r_x.at[which, s], tpeers[s]
            )

        def send_grads(which):
            tx, rx = ((gate_tx, gate_rx), (down_tx, down_rx), (up_tx, up_rx))[which]
            for s in range(T - 1):
                x_copy(which, s).start()
            rx[group] = tx[group]

        def got_grads(which):
            for s in range(T - 1):
                x_copy(which, s).wait_recv()

        def flat(ref):
            return ref[...].reshape(8 * ROWS, ref.shape[-1])

        def glu_grads(grads, tx):
            prod = lead_sum(flat(grads), flat(nffn)).astype(bf16)
            for mm in range(M):
                for ff in range(2):
                    tx[mm * 2 + ff] = prod[
                        mm * seg : (mm + 1) * seg, ff * half_width : (ff + 1) * half_width
                    ]

        def down_grads():
            prod = lead_sum(flat(c_all), flat(hid))
            for mm in range(M):
                for ff in range(2):
                    down_tx[mm * 2 + ff] = jnp.concatenate(
                        [
                            prod[blk * each : (blk + 1) * each]
                            for zl in range(2)
                            for cc in range(2)
                            for blk in [(2 * zl + ff) * 2 * M + mm * 2 + cc]
                        ],
                        axis=0,
                    ).astype(bf16)

        down_grads()
        send_grads(1)
        glu_grads(gg, gate_tx)
        send_grads(0)

        dy = sc.total()
        mid = mid_b[core]
        r = lax.rsqrt(jnp.mean(mid * mid, axis=-1, keepdims=True) + epsilon)
        gdy = gain * dy
        dv = r * gdy - mid * (r * r * r) * jnp.mean(mid * gdy, axis=-1, keepdims=True)
        gmid = c_ref[...].astype(f32) + dv
        gmid_v[...] = gmid
        ffn_part = jnp.sum(dy * mid * r, axis=0, keepdims=True)
        br_own[...] = gmid.astype(bf16)
        branch[me] = br_own[...]

        gb = Gather(br_own, branch, s_br, r_br)
        gb.own()
        glu_grads(gu, up_tx)
        send_grads(2)
        for kind in (0, 1, 2):
            gb.take(kind)
        gb.rest()

        def sent():
            for i in range(4):
                for k in range(2):
                    att_copy(k, i).wait_send()
                for k in range(4):
                    sib_att(k, i).wait_send()

                @pl.when(at_end == 0)
                def _(i=i):
                    att_copy(2, i).wait_send()
                    att_copy(3, i).wait_send()

            gb.sent()
            for which in range(3):
                for s in range(T - 1):
                    x_copy(which, s).wait_send()

        sc.sent()
        return sent, got_grads, ffn_part

    ffn_sent, got_grads, ffn_part = feed_forward()

    def back():
        sd = Scatter(dpart, d_sib, d_sum, d_relay, d_rx, s_d, r_d)
        sp = Scatter(p_out, a_sib, a_sum, a_relay, a_rx, s_p, r_p)
        for i in range(4):
            sd.sibling(i).start()

        def block_rows(b):
            return pl.ds(pl.multiple_of(b * BLOCK, BLOCK), BLOCK)

        def mixed(b, _):
            rows = block_rows(b)
            br = jnp.concatenate([branch[2 * b], branch[2 * b + 1]], axis=0)
            gm = back_product(br, wo_v[pl.ds(pl.multiple_of(me * 128, 128), 128), :])
            inv = 1.0 / totals[rows, :]
            g_v[rows, :] = (gm * inv).astype(bf16)
            w = gm * summed[rows, :] * (inv * inv)
            low = lax.broadcasted_iota(jnp.int32, w.shape, 1) < 64
            a = jnp.sum(jnp.where(low, w, 0.0), axis=1, keepdims=True)
            c = jnp.sum(jnp.where(low, 0.0, w), axis=1, keepdims=True)
            totals[rows, :] = jnp.where(low, a, c)
            return 0

        lax.fori_loop(0, 4, mixed, 0)
        for i in range(3):
            sd.pass_on(i)

        got_grads(1)
        total = down_rx[0].astype(f32)
        for k in range(1, T):
            total = total + down_rx[k].astype(f32)
        for k in range(4):
            w_tx[k] = total[k * each : (k + 1) * each].astype(bf16)
        here = z % 2 * 2 + core

        def w_copy(k):
            return rcopy(w_tx.at[k], w_rx.at[here], s_w.at[k], r_w.at[here], place_dev[k])

        for k in range(4):

            @pl.when(jnp.logical_not(place_self[k]))
            def _(k=k):
                w_copy(k).start()

            @pl.when(place_self[k])
            def _(k=k):
                w_rx[here] = w_tx[k]

        for i in range(2):
            sd.relay(i)

        summed[...] = jnp.zeros_like(summed)

        def kv_copy(s):
            return rcopy(
                nffn.at[:, :, lane_block(s)], dkv_rx.at[s], s_dk.at[s], r_dk.at[s], mpeers[s]
            )

        def attend(s, _):
            mm = (m + 1 + s) % M
            dkv_acc[...] = jnp.zeros_like(dkv_acc)
            for zz in range(4):
                rows = slice(zz * BLOCK, (zz + 1) * BLOCK)
                keys = (zz + 1) * BLOCK
                token = zz * span + m * BLOCK + lax.broadcasted_iota(jnp.int32, (BLOCK, 1), 0)
                begin = begin_of(token, doc_ref)
                for h in range(2):
                    lanes = slice(h * 64, h * 64 + 64)
                    q = q_rows[rows, lanes]
                    g = g_v[rows, lanes]
                    k = kv_all[mm, :keys, :64]
                    v = kv_all[mm, :keys, 64:]
                    e = block_weights(q, k, begin, zz, m, mm, span)
                    dp = back_product(g, v)
                    ds = (e * (dp - totals[rows, h * 64 : h * 64 + 1])).astype(bf16)
                    summed[rows, lanes] += dot(ds, k)
                    dkv_acc[:keys, :64] += lead_sum(ds, q)
                    dkv_acc[:keys, 64:] += lead_sum(e.astype(bf16), g)

            @pl.when(s < M - 1)
            def _():
                nffn[:, :, lane_block(s)] = dkv_acc[...].astype(bf16).reshape(4, BLOCK, 128)

                for ss in range(M - 1):

                    @pl.when(s == ss)
                    def _(ss=ss):
                        kv_copy(ss).start()

            return 0

        lax.fori_loop(0, M, attend, 0)

        def over_groups(rx):
            total = rx[0].astype(f32)
            for k in range(1, T):
                total = total + rx[k].astype(f32)
            return total

        got_grads(0)
        gate_ref[...] = over_groups(gate_rx)

        strip = jnp.concatenate(
            [branch[j, :, pl.ds(pl.multiple_of(z * 256, 128), 256)] for j in range(8)], axis=0
        )
        strip = jnp.concatenate(
            [
                jnp.where(
                    core == 0,
                    strip[:, 2 * mm * each : (2 * mm + 1) * each],
                    strip[:, (2 * mm + 1) * each : (2 * mm + 2) * each],
                )
                for mm in range(M)
            ],
            axis=1,
        )
        prod = lead_sum(strip, att_all[...].reshape(8 * ROWS, WIDTH))
        for mm in range(M):
            for ff in range(2):
                ap_tx[mm * 2 + ff] = prod[
                    mm * each : (mm + 1) * each, ff * half_width : (ff + 1) * half_width
                ].astype(bf16)

        def a_copy(s):
            return rcopy(ap_tx.at[others[s]], ap_rx.at[group], s_ap.at[s], r_ap.at[s], tpeers[s])

        for s in range(M - 1):
            kv_copy(s).wait_recv()
        for s in range(T - 1):
            a_copy(s).start()
        ap_rx[group] = ap_tx[group]

        qgain = qgain_ref[...]
        kgain = kgain_ref[...]

        def head_mean(v):
            low = lax.broadcasted_iota(jnp.int32, v.shape, 1) < 64
            a = jnp.sum(jnp.where(low, v, 0.0), axis=1, keepdims=True)
            c = jnp.sum(jnp.where(low, 0.0, v), axis=1, keepdims=True)
            return jnp.where(low, a, c) * (1.0 / 64)

        def heads_back(i, carry):
            qg, kg, ag = carry
            b = jnp.where(i == 0, sp.order[0], jnp.where(i == 1, sp.order[1], jnp.where(i == 2, sp.order[2], z)))
            rows = block_rows(b)
            co = cosine[rows, :]
            si = sine[rows, :]

            def through(v, dy, gain):
                dy = dy * co - turn(dy) * si
                r = head_scale(v)
                gdy = gain * dy
                dv = r * gdy - v * (r * r * r) * head_mean(v * gdy)
                return dv, jnp.sum(dy * v * r, axis=0, keepdims=True)

            st = stacked[rows, :]
            dq, qpart = through(st[:, :128], summed[rows, :] * HEAD_SIZE ** (-0.5), qgain)
            dkv = dkv_acc[rows, :]
            for s in range(M - 1):
                dkv = dkv + dkv_rx[s, b].astype(f32)
            dk, kpart = through(st[:, 128:], dkv, kgain)
            low = lax.broadcasted_iota(jnp.int32, dkv.shape, 1) < 64
            gs = jnp.concatenate([dq, jnp.where(low, dk, dkv)], axis=1).astype(bf16)
            gs_v[rows, :] = gs
            pb = back_product(gs, w_heads[...])
            xb = jnp.concatenate([x_all[2 * b], x_all[2 * b + 1]], axis=0).astype(f32)
            rb = lax.rsqrt(jnp.mean(xb * xb, axis=-1, keepdims=True) + epsilon)
            ag = ag + jnp.sum(pb * (xb * rb), axis=0, keepdims=True)
            pb = pb.astype(bf16)
            p_out[b, 0] = pb[:ROWS]
            p_out[b, 1] = pb[ROWS:]
            rcopy(
                p_out.at[b, 1 - core], a_sib.at[i], s_p.at[i], r_p.at[i], sib
            ).start()
            return qg + qpart, kg + kpart, ag

        zero = jnp.zeros((1, 128), f32)
        qg, kg, ag = lax.fori_loop(
            0, 4, heads_back, (zero, zero, jnp.zeros((1, WIDTH), f32))
        )
        for i in range(3):
            sp.pass_on(i)

        def stack(row):
            return jnp.concatenate([row[:, k * 128 : (k + 1) * 128] for k in range(8)], axis=0)

        gn_tx[0:8, :] = stack(ag)
        gn_tx[8:16, :] = stack(ffn_part)
        gn_tx[16:24, :] = jnp.concatenate([qg, kg, jnp.zeros((6, 128), f32)], axis=0)
        gpeers = [sib] + zpeers + cross

        def g_copy(k):
            return rcopy(gn_tx, gn_rx.at[k], s_g.at[k], r_g.at[k], gpeers[k])

        for k in range(7):
            g_copy(k).start()

        prod = lead_sum(gs_v[...], normed[...])
        qw, kw = 128 // M, 64 // M
        for i in range(M):
            piece = jnp.concatenate(
                [
                    prod[i * qw : (i + 1) * qw],
                    prod[128 + i * kw : 128 + (i + 1) * kw],
                    prod[192 + i * kw : 192 + (i + 1) * kw],
                ],
                axis=0,
            ).astype(bf16)
            for ff in range(2):
                h_tx[i * 2 + ff] = piece[:, ff * half_width : (ff + 1) * half_width]

        def h_copy(s):
            return rcopy(
                h_tx.at[pieces[s]], h_rx.at[group], s_h.at[s], r_h.at[group], piece_to[s]
            )

        def h_got(s):
            return rcopy(
                h_tx.at[pieces[s]], h_rx.at[sources[s]], s_h.at[s], r_h.at[sources[s]], piece_from[s]
            )

        for s in range(T):

            @pl.when(to_self[s])
            def _(s=s):
                h_rx[group] = h_tx[pieces[s]]

            @pl.when(jnp.logical_not(to_self[s]))
            def _(s=s):
                h_copy(s).start()

        for i in range(2):
            sp.relay(i)
        gains = gn_tx[...]
        for k in range(7):
            g_copy(k).wait_recv()
        for k in range(7):
            gains = gains + gn_rx[k]
        gt_tx[...] = gains

        def t_copy(s):
            return rcopy(gt_tx, gt_rx.at[s], s_t.at[s], r_t.at[s], tpeers[s])

        for s in range(T - 1):
            t_copy(s).start()


        got_grads(2)
        up_ref[...] = over_groups(up_rx)
        for k in range(4):

            @pl.when(jnp.logical_not(from_me[k]))
            def _(k=k):
                rcopy(w_tx.at[k], w_rx.at[k], s_w.at[k], r_w.at[k], place_from[k]).wait_recv()

        down_ref[...] = jnp.concatenate(
            [
                w_rx[zl * 2 + cc, :, mm * seg : (mm + 1) * seg].astype(f32)
                for zl in range(2)
                for mm in range(M)
                for cc in range(2)
            ],
            axis=1,
        )

        out_ref[...] = mid_b[core] + sd.total()
        dy = sp.total()
        x = x_ref[...].astype(f32)
        r = lax.rsqrt(jnp.mean(x * x, axis=-1, keepdims=True) + epsilon)
        gdy = again_ref[...] * dy
        dv = r * gdy - x * (r * r * r) * jnp.mean(x * gdy, axis=-1, keepdims=True)
        igrad_ref[...] = gmid_v[...] + dv

        for s in range(T):

            @pl.when(jnp.logical_not(from_self[s]))
            def _(s=s):
                h_got(s).wait_recv()

        for s in range(T - 1):
            a_copy(s).wait_recv()
        hsum = h_rx[0].astype(f32)
        asum = ap_rx[0].astype(f32)
        for k in range(1, T):
            hsum = hsum + h_rx[k].astype(f32)
            asum = asum + ap_rx[k].astype(f32)
        heads_ref[...] = hsum
        attn_ref[...] = asum

        for s in range(T - 1):
            t_copy(s).wait_recv()
            gains = gains + gt_rx[s]
        gains_ref[...] = gains

        sd.sent()
        sp.sent()
        for k in range(4):

            @pl.when(jnp.logical_not(place_self[k]))
            def _(k=k):
                w_copy(k).wait_send()

        for s in range(M - 1):
            kv_copy(s).wait_send()
        for s in range(T):

            @pl.when(jnp.logical_not(to_self[s]))
            def _(s=s):
                h_copy(s).wait_send()

        for s in range(T - 1):
            a_copy(s).wait_send()
            t_copy(s).wait_send()
        for k in range(7):
            g_copy(k).wait_send()

    back()
    front_sent()
    ffn_sent()


def block(*args, cid):
    n = lax.axis_size("ctx")
    M, T, seg, each = n // 8, n // 4, FF // n, WIDTH // n
    cols = FF // 8
    tokens = 8 * ROWS
    half_width = WIDTH // 2
    part = (ROWS, WIDTH)
    VS, sem = pltpu.VMEM, pltpu.SemaphoreType.DMA
    shape = jax.ShapeDtypeStruct

    def sems(*shapes):
        return [sem(v) for v in shapes]

    return pl.pallas_call(
        block_kernel,
        out_shape=(
            shape(part, f32),
            shape(part, f32),
            shape((24, 128), f32),
            shape((256 // M, half_width), f32),
            shape((each, half_width), f32),
            shape((seg, half_width), f32),
            shape((seg, half_width), f32),
            shape((each, FF // 2), f32),
        ),
        in_specs=[pl.BlockSpec(memory_space=pltpu.SMEM)] + vspecs(2) + any_specs(5) + vspecs(4),
        out_specs=tuple(vspecs(8)),
        scratch_shapes=[
            VS((8,) + part, bf16),
            VS((8,) + part, bf16),
            VS((WIDTH, 256), bf16),
            VS((WIDTH, cols), bf16),
            VS((WIDTH, cols), bf16),
            VS((cols, WIDTH), bf16),
            VS((WIDTH, WIDTH), bf16),
            VS((tokens, 128), bf16),
            VS((M, tokens, 128), bf16),
            VS((4, BLOCK, 128), bf16),
            VS((tokens, 128), f32),
            VS((tokens, 128), f32),
            VS((tokens, 256), f32),
            VS((tokens, WIDTH), bf16),
            VS((tokens, 128), f32),
            VS((tokens, 128), f32),
            VS((4, BLOCK, WIDTH), bf16),
            VS((8,) + part, bf16),
            VS(part, f32),
            VS((4, 2) + part, bf16),
            VS((4, BLOCK, WIDTH), bf16),
            VS((4, BLOCK, cols), bf16),
            VS((4, BLOCK, cols), bf16),
            VS((4, BLOCK, cols), bf16),
            VS((2,) + part, f32),
            VS((4, 2) + part, bf16),
            VS((T, seg, half_width), bf16),
            VS((T, seg, half_width), bf16),
            *[VS((T, 4 * each, cols), bf16)] * 2,
            VS((T, seg, half_width), bf16),
            VS((T, seg, half_width), bf16),
            VS(part, bf16),
            *scatter_scratch(),
            *scatter_scratch(),
            *scatter_scratch()[4:],
            VS((tokens, 128), bf16),
            VS((tokens, 128), f32),
            VS((M - 1, 4, BLOCK, 128), bf16),
            VS((tokens, 256), bf16),
            *[VS((T, 256 // M, half_width), bf16)] * 2,
            *[VS((T, each, half_width), bf16)] * 2,
            VS((24, 128), f32),
            VS((7, 24, 128), f32),
            VS((24, 128), f32),
            VS((T - 1, 24, 128), f32),
            *[VS((4, each, cols), bf16)] * 2,
            *sems((9,), (7,), (9,), (7,), (1,), (1,), (4,), (4,), (4,), (4,), (2,), (2,)),
            *sems((4, M - 1), (4, M - 1), (5,)),
            *sems((2, 4), (3, 4), (2, 4), (4, 4), (4, 4), (9,), (7,), (3, T - 1), (3, T - 1)),
            *sems((M - 1,), (M - 1,), (T,), (T,), (T - 1,), (T - 1,), (7,), (7,)),
            *sems((T - 1,), (T - 1,), (4,), (4,)),
        ],
        compiler_params=pltpu.CompilerParams(
            collective_id=cid, has_side_effects=True, vmem_limit_bytes=VMEM_LIMIT
        ),
        name="block",
    )(*args)


def finish_kernel(out, igrad, heads, attn, gate, up, down, *refs):
    outs, (s_in, s_out), bufs = refs[:9], refs[16:], refs[9:16]
    qw = heads.shape[0] // 2
    kw = qw // 2
    loads = []
    for k, (a, b) in enumerate(zip((out, igrad, heads, attn, gate, up, down), bufs)):
        cp = pltpu.make_async_copy(a, b, s_in.at[k])
        cp.start()
        loads.append(cp)
    o_out, o_igrad, o_query, o_key, o_value, o_attn, o_gate, o_up, o_down = outs
    b_out, b_igrad, b_heads, b_attn, b_gate, b_up, b_down = bufs
    stores = []
    for k, (load, a, b) in enumerate(
        (
            (4, b_gate, o_gate),
            (5, b_up, o_up),
            (6, b_down, o_down),
            (0, b_out, o_out),
            (1, b_igrad, o_igrad),
            (3, b_attn, o_attn),
            (2, b_heads.at[:qw], o_query),
            (None, b_heads.at[qw : qw + kw], o_key),
            (None, b_heads.at[qw + kw :], o_value),
        )
    ):
        if load is not None:
            loads[load].wait()
        cp = pltpu.make_async_copy(a, b, s_out.at[k])
        cp.start()
        stores.append(cp)
    for cp in stores:
        cp.wait()


def finish(*parts):
    out, igrad, heads, attn, gate, up, down = parts
    qw, kw = heads.shape[0] // 2, heads.shape[0] // 4
    shape = jax.ShapeDtypeStruct
    shapes = [
        out.shape, igrad.shape, (qw, heads.shape[1]), (kw, heads.shape[1]), (kw, heads.shape[1]),
        attn.shape, gate.shape, up.shape, down.shape,
    ]
    return pl.pallas_call(
        finish_kernel,
        out_shape=tuple(shape(v, f32) for v in shapes),
        in_specs=any_specs(7),
        out_specs=tuple(any_specs(9)),
        scratch_shapes=[pltpu.VMEM(v.shape, f32) for v in parts]
        + [pltpu.SemaphoreType.DMA((7,)), pltpu.SemaphoreType.DMA((9,))],
        compiler_params=pltpu.CompilerParams(vmem_limit_bytes=VMEM_LIMIT),
        name="finish",
    )(*parts)


def root_mean_norm(rows, gain):
    return (
        rows * lax.rsqrt(jnp.mean(rows * rows, axis=-1, keepdims=True) + epsilon) * gain
    )


def rotary(rows, cosine, sine):
    halfway = rows.shape[-1] // 2
    leading = rows[..., :halfway]
    trailing = rows[..., halfway:]
    return jnp.concatenate(
        [leading * cosine - trailing * sine, leading * sine + trailing * cosine], axis=-1
    )


SWAP = [(0, 1), (1, 0)]


def halves(f, own, other, axis):
    return jnp.where(
        f == 0,
        jnp.concatenate([own, other], axis=axis),
        jnp.concatenate([other, own], axis=axis),
    )


def local(
    hidden_in,
    doc_lengths,
    attn_gain,
    query_gain,
    key_norm_gain,
    ffn_gain,
    query_proj,
    key_weight,
    value_weight,
    attn_proj,
    gate_proj,
    up_proj,
    down_proj,
    out_cotangent,
):
    n_ctx = lax.axis_size("ctx")
    M = n_ctx // 8
    T = 2 * M
    z, m, core, f = who()
    head = slot(z, core)
    tokens = 8 * ROWS
    span = n_ctx // 4 * ROWS
    segment = FF // n_ctx
    columns = M * segment
    half_width = WIDTH // 2
    each = WIDTH // n_ctx

    heads_own = jnp.concatenate(
        [
            lax.dynamic_slice(query_proj, (0, head * 128), (half_width, 128)),
            lax.dynamic_slice(key_weight, (0, head * 64), (half_width, 64)),
            lax.dynamic_slice(value_weight, (0, head * 64), (half_width, 64)),
        ],
        axis=1,
    ).astype(bf16)
    first = z * (n_ctx // 4) + core
    gate_own, up_own = [
        jnp.concatenate(
            [
                lax.dynamic_slice(w, (0, (first + 2 * mm) * segment), (half_width, segment))
                for mm in range(M)
            ],
            axis=1,
        ).astype(bf16)
        for w in (gate_proj, up_proj)
    ]
    down_own = jnp.concatenate(
        [
            lax.dynamic_slice(
                down_proj, ((first + 2 * mm) * segment - f * (FF // 2), 0), (segment, WIDTH)
            )
            for mm in range(M)
        ],
        axis=0,
    ).astype(bf16)
    out_own = attn_proj.astype(bf16)

    cotangent = out_cotangent[0]
    q_gain = jnp.tile(query_gain, 2)[None]
    k_gain = jnp.concatenate([key_norm_gain, jnp.ones((64,), f32)])[None]
    out, igrad, gains, heads, attn, gate, up, down = block(
        doc_lengths,
        hidden_in[0],
        cotangent,
        heads_own,
        gate_own,
        up_own,
        down_own,
        out_own,
        attn_gain[None],
        q_gain,
        k_gain,
        ffn_gain[None],
        cid=1,
    )
    out, igrad, query, key, value, attn, gate, up, down = finish(
        out, igrad, heads, attn, gate, up, down
    )
    return (
        out[None],
        igrad[None],
        gains[:8].reshape(WIDTH),
        gains[16, :64] + gains[16, 64:],
        gains[17, :64],
        gains[8:16].reshape(WIDTH),
        query.T,
        key.T,
        value.T,
        attn.T,
        gate.T,
        up.T,
        down.T,
    )


def solution(mesh):
    in_specs = (
        P("fsdp", "ctx", None),
        P("fsdp", None),
        P(),
        P(),
        P(),
        P(),
        P("fsdp", None),
        P("fsdp", None),
        P("fsdp", None),
        P("fsdp", None),
        P("fsdp", None),
        P("fsdp", None),
        P("fsdp", None),
        P("fsdp", "ctx", None),
    )
    out_specs = (
        P("fsdp", "ctx", None),
        P("fsdp", "ctx", None),
        P(),
        P(),
        P(),
        P(),
        P("fsdp", "ctx"),
        P("fsdp", "ctx"),
        P("fsdp", "ctx"),
        P("fsdp", "ctx"),
        P("fsdp", "ctx"),
        P("fsdp", "ctx"),
        P("fsdp", "ctx"),
    )
    return jax.shard_map(local, mesh=mesh, in_specs=in_specs, out_specs=out_specs, check_vma=False)
```

```python
import functools
import math

import jax
import jax.numpy as jnp
from jax import lax
from jax.experimental import pallas as pl
from jax.experimental.pallas import tpu as pltpu
from jax.sharding import PartitionSpec as P

QUERY_HEADS = 16
KEY_VALUE_HEADS = 8
HEAD_SIZE = 64
FF = 4608
WIDTH = 1024
ROWS = 128

epsilon = 1e-05
rope_base = 1000000.0
MESH = pl.DeviceIdType.MESH
ANY = pl.ANY
VMEM_LIMIT = 64 * 2**20 - 2**17
bf16 = jnp.bfloat16
f32 = jnp.float32


def who():
    n = lax.axis_size("ctx")
    c = lax.axis_index("ctx")
    f = lax.axis_index("fsdp")
    q = n // 4
    return c // q, (c % q) // 2, c % 2, f


def dev(z, m, core, f):
    return (z * (lax.axis_size("ctx") // 4) + m * 2 + core, f)


def slot(z, core):
    return z * 2 + core


def enter(peers):
    bar = pltpu.get_barrier_semaphore()
    for p in peers:
        pl.semaphore_signal(bar, inc=1, device_id=p, device_id_type=MESH)
    pl.semaphore_wait(bar, len(peers))


def rcopy(src, dst, s, r, to):
    return pltpu.make_async_remote_copy(
        src_ref=src, dst_ref=dst, send_sem=s, recv_sem=r, device_id=to, device_id_type=MESH
    )


def comm_params(cid):
    return pltpu.CompilerParams(collective_id=cid, has_side_effects=True)


def any_specs(n):
    return [pl.BlockSpec(memory_space=ANY)] * n


def line_of(z):
    return z + 1 - 2 * (z % 2), 2 - z // 2, 3 - 3 * (z // 2), 1 - ((z + 1) // 2) % 2


class Gather:
    def __init__(self, src, dst, ss, rs):
        z, m, core, f = who()
        partner, middle, end, self.at_end = line_of(z)
        self.src, self.dst, self.ss, self.rs = src, dst, ss, rs
        self.me = slot(z, core)
        self.slots = [slot(zz, core) for zz in (partner, middle, end)]
        self.partner = dev(partner, m, core, f)
        self.middle = dev(middle, m, core, f)
        self.sib = dev(z, m, 1 - core, f)

    def copy(self, k):
        src, dst, ss, rs = self.src, self.dst, self.ss.at[k], self.rs
        if k == 0:
            return rcopy(src, dst.at[self.me], ss, rs.at[0], self.partner)
        if k == 1:
            return rcopy(src, dst.at[self.me], ss, rs.at[1 + self.at_end], self.middle)
        if k == 3:
            return rcopy(src, dst.at[self.me], ss, rs.at[3], self.sib)
        if k < 7:
            j = self.slots[k - 4]
            return rcopy(dst.at[j], dst.at[j], ss, rs.at[k], self.sib)
        j = self.slots[k - 6]
        return rcopy(dst.at[j], dst.at[j], ss, rs.at[k - 6], self.partner)

    def own(self):
        for k in (1, 0, 3):
            self.copy(k).start()

    def take(self, kind):
        j = self.slots[kind]
        rcopy(
            self.dst.at[j], self.dst.at[j], self.ss.at[0], self.rs.at[kind], self.partner
        ).wait_recv()
        if kind > 0:

            @pl.when(self.at_end == 0)
            def _():
                self.copy(6 + kind).start()

        self.copy(4 + kind).start()

    def rest(self):
        for k in range(3, 7):
            self.copy(k).wait_recv()

    def sent(self):
        for k in (0, 1, 3, 4, 5, 6):
            self.copy(k).wait_send()

        @pl.when(self.at_end == 0)
        def _():
            self.copy(7).wait_send()
            self.copy(8).wait_send()


class Scatter:
    def __init__(self, part, buf, sums, relay, rx, ss, rs):
        z, m, self.core, f = who()
        core = self.core
        partner, middle, end, self.at_end = line_of(z)
        self.z = z
        self.part, self.buf, self.sums, self.relay_buf, self.rx = part, buf, sums, relay, rx
        self.ss, self.rs = ss, rs
        self.order = [end, middle, partner, z]
        self.sib = dev(z, m, 1 - core, f)
        self.to = [dev(zz, m, core, f) for zz in self.order[:3]]

    def sibling(self, i):
        return rcopy(
            self.part.at[self.order[i], 1 - self.core],
            self.buf.at[i],
            self.ss.at[i],
            self.rs.at[i],
            self.sib,
        )

    def copy(self, i, at_end):
        if i == 2:
            return rcopy(
                self.sums.at[2], self.rx.at[0], self.ss.at[6], self.rs.at[4], self.to[2]
            )
        if at_end:
            return rcopy(
                self.sums.at[i], self.relay_buf.at[i], self.ss.at[4 + i], self.rs.at[6 + i], self.to[2]
            )
        return rcopy(self.sums.at[i], self.rx.at[1], self.ss.at[4 + i], self.rs.at[5], self.to[i])

    def pass_on(self, i):
        self.sibling(i).wait_recv()
        self.sums[i] = (
            self.part[self.order[i], self.core].astype(f32) + self.buf[i].astype(f32)
        ).astype(bf16)
        if i == 2:
            self.copy(2, True).start()
        else:

            @pl.when(self.at_end == 1)
            def _():
                self.copy(i, True).start()

    def relay(self, i):
        @pl.when(self.at_end == 0)
        def _():
            self.copy(i, True).wait_recv()
            self.sums[i] = (
                self.sums[i].astype(f32) + self.relay_buf[i].astype(f32)
            ).astype(bf16)
            self.copy(i, False).start()

    def total(self):
        self.sibling(3).wait_recv()
        total = self.part[self.z, self.core].astype(f32) + self.buf[3].astype(f32)
        self.copy(2, True).wait_recv()
        total = total + self.rx[0].astype(f32)
        self.copy(0, False).wait_recv()
        return total + self.rx[1].astype(f32)

    def sent(self):
        for i in range(4):
            self.sibling(i).wait_send()
        for i in range(3):
            self.copy(i, False).wait_send()


def scatter_scratch():
    part = (ROWS, WIDTH)
    return [
        pltpu.VMEM((4,) + part, bf16),
        pltpu.VMEM((3,) + part, bf16),
        pltpu.VMEM((2,) + part, bf16),
        pltpu.VMEM((2,) + part, bf16),
        pltpu.SemaphoreType.DMA((7,)),
        pltpu.SemaphoreType.DMA((8,)),
    ]


def back_product(left, right):
    return lax.dot_general(
        left, right, (((1,), (1,)), ((), ())), preferred_element_type=f32
    )


def lead_sum(left, right):
    return lax.dot_general(
        left, right, (((0,), (0,)), ((), ())), preferred_element_type=f32
    )


def dot(left, right):
    return jnp.dot(left, right, preferred_element_type=f32)


BLOCK = 2 * ROWS


def block_weights(q, k, begin, z, m, mm, span):
    keys = (z + 1) * BLOCK
    key = lax.broadcasted_iota(jnp.int32, (1, keys), 1)
    key = key // BLOCK * span + key % BLOCK + mm * BLOCK
    token = z * span + m * BLOCK + lax.broadcasted_iota(jnp.int32, (BLOCK, 1), 0)
    e = jnp.exp(back_product(q, k))
    return jnp.where((key >= begin) & (key <= token), e, 0.0)


VM = pltpu.VMEM


def vspecs(n):
    return [pl.BlockSpec(memory_space=VM)] * n


def begin_of(token, doc_ref):
    begin = jnp.zeros(token.shape, jnp.int32)
    start = doc_ref[0, 0]
    for d in range(1, doc_ref.shape[1]):
        begin = jnp.where(token >= start, start, begin)
        start = start + doc_ref[0, d]
    return begin


def turn(v):
    lane = lax.broadcasted_iota(jnp.int32, v.shape, 1)
    n = v.shape[1]
    return jnp.where(lane % 64 < 32, pltpu.roll(v, n - 32, 1), pltpu.roll(v, 32, 1))


def head_scale(v):
    sq = v * v
    if v.shape[1] == 64:
        return lax.rsqrt(jnp.mean(sq, axis=1, keepdims=True) + epsilon)
    low = lax.broadcasted_iota(jnp.int32, v.shape, 1) < 64
    a = jnp.sum(jnp.where(low, sq, 0.0), axis=1, keepdims=True)
    b = jnp.sum(jnp.where(low, 0.0, sq), axis=1, keepdims=True)
    return lax.rsqrt(jnp.where(low, a, b) * (1.0 / 64) + epsilon)


def block_kernel(
    doc_ref, x_ref, c_ref, q_hbm, k_hbm, v_hbm, gate_hbm, up_hbm, down_hbm, out_hbm,
    again_ref, qgain_ref, kgain_ref, fgain_ref,
    out_ref, igrad_ref, gains_ref, heads_ref, attn_ref, gate_ref, up_ref, down_ref,
    x_all, c_all, w_heads, wg_v, wu_v, wd_v, wo_v, q_rows, kv_all, att, summed, totals,
    stacked, normed, cosine, sine,
    att_all, branch, gmid_v, dpart, nffn, hid, gg, gu, mid_b, p_out, gate_tx, gate_rx, down_tx, down_rx,
    up_tx, up_rx, br_own,
    a_sib, a_sum, a_relay, a_rx, s_a, r_a, d_sib, d_sum, d_relay, d_rx, s_d, r_d,
    s_p, r_p,
    g_v, dkv_acc, dkv_rx, gs_v,
    h_tx, h_rx, ap_tx, ap_rx, gn_tx, gn_rx, gt_tx, gt_rx, w_tx, w_rx,
    s_x0, r_x0, s_c, r_c, s_h0, r_h0, s_w0, r_w0, s_v, r_v, s_o, r_o, s_k, r_k, ld,
    s_att, r_att, s_pass, s_sib, r_sib, s_br, r_br, s_x, r_x,
    s_dk, r_dk, s_h, r_h, s_ap, r_ap, s_g, r_g, s_t, r_t, s_w, r_w,
):
    z, m, core, f = who()
    M = lax.axis_size("ctx") // 8
    T = 2 * M
    span = lax.axis_size("ctx") // 4 * ROWS
    each = WIDTH // lax.axis_size("ctx")
    seg = FF // lax.axis_size("ctx")
    half_width = WIDTH // 2
    partner, middle, end, at_end = line_of(z)
    sib = dev(z, m, 1 - core, f)
    zs = [(z + s) % 4 for s in (1, 2, 3)]
    zpeers = [dev(zz, m, core, f) for zz in zs]
    cross = [dev(zz, m, 1 - core, f) for zz in zs]
    hm = m % 2
    pair = dev(z, m, core, 1 - f)
    beside = dev(z, m + 1 - 2 * hm, core, f)
    mpeers = [dev(z, (m + s) % M, core, f) for s in range(1, M)]
    group = m * 2 + f
    others = [(group + s) % T for s in range(1, T)]
    tpeers = [dev(z, o // 2, core, o % 2) for o in others]
    owner = f == z // 2
    me = slot(z, core)
    head = me

    pieces = [(group + s) % T for s in range(T)]
    rest_to = [core * M + p // 2 for p in pieces]
    piece_to = [dev(z, rr // 2, rr % 2, p % 2) for rr, p in zip(rest_to, pieces)]
    to_self = [(rr == m * 2 + core) & (p % 2 == f) for rr, p in zip(rest_to, pieces)]
    rest = m * 2 + core
    core_from = rest // M
    sources = [(group + s) % T for s in range(T)]
    piece_from = [dev(z, o // 2, core_from, o % 2) for o in sources]
    from_self = [(core_from == core) & (o == group) for o in sources]

    stage = [mid_b.at[0], mid_b.at[1], gmid_v, out_ref, igrad_ref]
    cols = M * seg
    wide = -(-(128 - math.gcd(seg, 128) + seg) // 128) * 128
    in_row = WIDTH // wide
    bands = -(-M // in_row)
    high = ROWS // bands
    first_column = [(z * 2 * M + mm * 2 + core) * seg for mm in range(M)]
    window = [v // 128 * 128 for v in first_column]
    window = [v - v // (FF - wide + 128) * 128 for v in window]
    tall = max(d for d in range(8, ROWS + 1, 8) if seg % d == 0)
    base = f * half_width

    def ff_chunk(w, dst, r):
        def parts(buf, i):
            return [
                pltpu.make_async_copy(
                    w.at[pl.ds(r * high, high), pl.ds(pl.multiple_of(window[mm], 128), wide)],
                    buf.at[pl.ds(mm // in_row * high, high), pl.ds(mm % in_row * wide, wide)],
                    ld.at[i % 5, mm],
                )
                for mm in range(M)
            ]

        def use(buf):
            pieces = []
            for mm in range(M):
                v = buf[
                    mm // in_row * high : (mm // in_row + 1) * high,
                    mm % in_row * wide : (mm % in_row + 1) * wide,
                ]
                shift = (wide - (first_column[mm] - window[mm])) % wide
                pieces.append(pltpu.roll(v, shift, 1)[:, :seg])
            rows = pl.ds(pl.multiple_of(base + r * high, high), high)
            dst[rows, :] = jnp.concatenate(pieces, axis=1).astype(bf16)

        return parts, use

    def out_chunk(r):
        def parts(buf, i):
            return [pltpu.make_async_copy(out_hbm.at[pl.ds(r * ROWS, ROWS)], buf, ld.at[i % 5, 0])]

        def use(buf):
            wo_v[pl.ds(pl.multiple_of(base + r * ROWS, ROWS), ROWS), :] = buf[...].astype(bf16)

        return parts, use

    def down_chunk(mm, r):
        def parts(buf, i):
            row = pl.multiple_of(first_column[mm] - f * (FF // 2) + r * tall, 8)
            return [
                pltpu.make_async_copy(
                    down_hbm.at[pl.ds(row, tall)], buf.at[pl.ds(0, tall)], ld.at[i % 5, 0]
                )
            ]

        def use(buf):
            at = mm * seg + r * tall
            wd_v[at : at + tall, :] = buf[:tall, :].astype(bf16)

        return parts, use

    chunks = [ff_chunk(gate_hbm, wg_v, r) for r in range(half_width // high)]
    chunks += [ff_chunk(up_hbm, wu_v, r) for r in range(half_width // high)]
    chunks += [out_chunk(r) for r in range(half_width // ROWS)]
    always = len(chunks)
    chunks += [down_chunk(mm, r) for mm in range(M) for r in range(seg // tall)]

    def fetch(i):
        def go():
            for cp in chunks[i][0](stage[i % 5], i):
                cp.start()

        if i < always:
            go()
        elif i < len(chunks):
            pl.when(owner)(go)

    def take_in(i):
        def go():
            for cp in chunks[i][0](stage[i % 5], i):
                cp.wait()
            chunks[i][1](stage[i % 5])

        if i < always:
            go()
        else:
            pl.when(owner)(go)
        fetch(i + 5)

    half_head = head // 2 * 128
    head_parts = [
        pltpu.make_async_copy(
            q_hbm.at[:, pl.ds(pl.multiple_of(head * 128, 128), 128)],
            stacked.at[pl.ds(0, half_width), pl.ds(0, 128)],
            ld.at[5, 0],
        ),
        pltpu.make_async_copy(
            k_hbm.at[:, pl.ds(pl.multiple_of(half_head, 128), 128)],
            stacked.at[pl.ds(0, half_width), pl.ds(128, 128)],
            ld.at[6, 0],
        ),
        pltpu.make_async_copy(
            v_hbm.at[:, pl.ds(pl.multiple_of(half_head, 128), 128)],
            stacked.at[pl.ds(half_width, half_width), pl.ds(0, 128)],
            ld.at[7, 0],
        ),
    ]
    for cp in head_parts:
        cp.start()
    for i in range(5):
        fetch(i)

    bar = pltpu.get_barrier_semaphore()
    fixed = [sib] + zpeers + cross + tpeers
    for p in fixed:
        pl.semaphore_signal(bar, inc=1, device_id=p, device_id_type=MESH)
    for s in range(T):

        @pl.when(jnp.logical_not(from_self[s]))
        def _(s=s):
            pl.semaphore_signal(bar, inc=1, device_id=piece_from[s], device_id_type=MESH)

    place = [(zl, cc) for zl in range(2) for cc in range(2)]
    place_dev = [dev(2 * zl + f, m, cc, z // 2) for zl, cc in place]
    place_self = [owner & (z == 2 * zl + f) & (core == cc) for zl, cc in place]
    place_from = [dev(2 * f + zb, m, cc, z % 2) for zb, cc in place]
    from_me = [owner & (z == 2 * f + zb) & (z % 2 == f) & (core == cc) for zb, cc in place]
    for k in range(4):

        @pl.when(jnp.logical_not(from_me[k]))
        def _(k=k):
            pl.semaphore_signal(bar, inc=1, device_id=place_from[k], device_id_type=MESH)

    pl.semaphore_wait(
        bar,
        len(fixed)
        + T
        + 4
        - jnp.where(core_from == core, 1, 0)
        - jnp.where(owner & (z % 2 == f), 1, 0),
    )

    def lane_block(j):
        return pl.ds(pl.multiple_of(j * 128, 128), 128)

    def front():
        gx = Gather(x_ref, x_all, s_x0, r_x0)
        gc = Gather(c_ref, c_all, s_c, r_c)
        gx.own()
        head_rows = pl.ds(f * half_width, half_width)
        heads_copy = rcopy(w_heads.at[head_rows], w_heads.at[head_rows], s_h0.at[0], r_h0.at[0], pair)
        for cp in head_parts:
            cp.wait()

        def half_of(v):
            return jnp.where(head % 2 == 0, v[:, :64], v[:, 64:])

        w_heads[head_rows, :] = jnp.concatenate(
            [
                stacked[:half_width, :128],
                half_of(stacked[:half_width, 128:]),
                half_of(stacked[half_width:, :128]),
            ],
            axis=1,
        ).astype(bf16)
        heads_copy.start()
        quarter = half_width // 2
        eighth = half_width // 4

        def w_copy(k, stage):
            dst = (wg_v, wu_v, wd_v, wo_v)[k]
            base = 0 if k == 2 else (f if stage == 0 else 1 - f) * half_width
            size = (quarter, quarter, cols // 2, eighth)[k]
            part = hm * 2 + core if k == 3 else hm
            place = dst.at[pl.ds(pl.multiple_of(base + part * size, 8), size)]
            if stage == 0:
                return rcopy(place, place, s_w0.at[k], r_w0.at[k], pair)
            return rcopy(place, place, s_v.at[k], r_v.at[k], beside)

        def out_copy(k):
            part = (hm if k == 0 else 1 - hm) * 2 + core
            base = (1 - f) * half_width
            place = wo_v.at[pl.ds(pl.multiple_of(base + part * eighth, 8), eighth)]
            return rcopy(place, place, s_o.at[k], r_o.at[k], sib)

        x_all[me] = x_ref[...]
        c_all[me] = c_ref[...]
        each_ff = half_width // high
        for i in range(each_ff):
            take_in(i)
        w_copy(0, 0).start()
        gx.take(0)
        for i in range(each_ff, 2 * each_ff):
            take_in(i)
        w_copy(1, 0).start()
        gx.take(1)
        for i in range(2 * each_ff, always):
            take_in(i)
        w_copy(3, 0).start()
        gx.take(2)
        gc.own()

        lane = lax.broadcasted_iota(jnp.int32, (1, 128), 1) % 32
        freq = jnp.exp(lane.astype(f32) * (-2.0 / 64 * math.log(rope_base)))
        sign = jnp.where(lax.broadcasted_iota(jnp.int32, (1, 128), 1) % 64 < 32, -1.0, 1.0)

        def tokens_of(zz):
            return zz * span + m * BLOCK + lax.broadcasted_iota(jnp.int32, (BLOCK, 1), 0)

        def table(zz, _):
            rows = pl.ds(pl.multiple_of(zz * BLOCK, BLOCK), BLOCK)
            token = tokens_of(zz)
            place = (token - begin_of(token, doc_ref)).astype(f32)
            angle = place * freq
            cosine[rows, :] = jnp.cos(angle)
            sine[rows, :] = jnp.sin(angle) * sign
            return 0

        lax.fori_loop(0, 4, table, 0)
        for i in range(always, len(chunks)):
            take_in(i)

        @pl.when(owner)
        def _():
            w_copy(2, 0).start()

        heads_copy.wait_recv()

        def kv_copy(b, s):
            rows = pl.ds(pl.multiple_of(b * BLOCK, BLOCK), BLOCK)
            place = kv_all.at[m, rows]
            return rcopy(place, place, s_k.at[b, s], r_k.at[b, s], mpeers[s])

        again = again_ref[...]
        qgain = jnp.concatenate([qgain_ref[...]] * 2, axis=1)
        kgain = jnp.concatenate([kgain_ref[...], jnp.ones((1, 64), f32)], axis=1)

        gx.rest()
        for k in range(2):
            w_copy(k, 0).wait_recv()
            w_copy(k, 1).start()

        def project(b, _):
            rows = pl.ds(pl.multiple_of(b * BLOCK, BLOCK), BLOCK)
            x = jnp.concatenate([x_all[2 * b], x_all[2 * b + 1]], axis=0).astype(f32)
            nb = (
                x * lax.rsqrt(jnp.mean(x * x, axis=-1, keepdims=True) + epsilon) * again
            ).astype(bf16)
            normed[rows, :] = nb
            st = dot(nb, w_heads[...])
            stacked[rows, :] = st
            co = cosine[rows, :]
            si = sine[rows, :]
            q = st[:, :128]
            q = q * head_scale(q) * qgain
            q_rows[rows, :] = ((q * co + turn(q) * si) * HEAD_SIZE ** (-0.5)).astype(bf16)
            kv = st[:, 128:]
            low = lax.broadcasted_iota(jnp.int32, kv.shape, 1) < 64
            k = kv * head_scale(kv) * kgain
            kv_all[m, rows, :] = jnp.where(low, k * co + turn(k) * si, kv).astype(bf16)
            for s in range(M - 1):
                kv_copy(b, s).start()
            return 0

        lax.fori_loop(0, 4, project, 0)

        w_copy(3, 0).wait_recv()
        w_copy(3, 1).start()
        out_copy(0).start()

        @pl.when(at_end == 0)
        def _():
            for kind in (0, 1, 2):
                gc.take(kind)

        summed[...] = jnp.zeros_like(summed)
        totals[...] = jnp.zeros_like(totals)

        def attend(s, _):
            mm = (m + M - s) % M

            @pl.when(s > 0)
            def _():
                for b in range(4):
                    rows = pl.ds(b * BLOCK, BLOCK)
                    place = kv_all.at[mm, rows]
                    rcopy(place, place, s_k.at[b, s - 1], r_k.at[b, s - 1], sib).wait_recv()

            @pl.when((s == 1) & jnp.logical_not(owner))
            def _():
                w_copy(2, 0).wait_recv()
                w_copy(2, 1).start()

            for zz in range(4):
                rows = slice(zz * BLOCK, (zz + 1) * BLOCK)
                keys = (zz + 1) * BLOCK
                begin = begin_of(tokens_of(zz), doc_ref)
                for h in range(2):
                    lanes = slice(h * 64, h * 64 + 64)
                    e = block_weights(
                        q_rows[rows, lanes], kv_all[mm, :keys, :64], begin, zz, m, mm, span
                    )
                    summed[rows, lanes] += dot(e.astype(bf16), kv_all[mm, :keys, 64:])
                    totals[rows, lanes] += jnp.broadcast_to(
                        jnp.sum(e, axis=1, keepdims=True), (BLOCK, 64)
                    )
            return 0

        lax.fori_loop(0, M, attend, 0)
        for b in range(4):
            rows = slice(b * BLOCK, (b + 1) * BLOCK)
            att[b] = (summed[rows, :] / totals[rows, :]).astype(bf16)

        def w_got(k):
            dst = (wg_v, wu_v, wd_v, wo_v)[k]
            base = 0 if k == 2 else (1 - f) * half_width
            size = (quarter, quarter, cols // 2, eighth)[k]
            part = (1 - hm) * 2 + core if k == 3 else 1 - hm
            place = dst.at[pl.ds(pl.multiple_of(base + part * size, 8), size)]
            return rcopy(place, place, s_v.at[k], r_v.at[k], beside)

        def ends_take():
            @pl.when(at_end == 1)
            def _():
                for kind in (0, 1, 2):
                    gc.take(kind)

        def out_ready():
            w_got(3).wait_recv()
            out_copy(1).start()
            for k in range(2):
                out_copy(k).wait_recv()

        def glu_ready():
            for k in range(2):
                w_got(k).wait_recv()

        def rest_ready():
            gc.rest()

            @pl.when(jnp.logical_not(owner))
            def _():
                w_got(2).wait_recv()

        def sent():
            heads_copy.wait_send()
            gx.sent()
            gc.sent()
            for k in (0, 1, 3):
                w_copy(k, 0).wait_send()
                w_copy(k, 1).wait_send()

            @pl.when(owner)
            def _():
                w_copy(2, 0).wait_send()

            @pl.when(jnp.logical_not(owner))
            def _():
                w_copy(2, 1).wait_send()

            for k in range(2):
                out_copy(k).wait_send()
            for b in range(4):
                for s in range(M - 1):
                    kv_copy(b, s).wait_send()

        return sent, ends_take, out_ready, glu_ready, rest_ready

    front_sent, ends_take, out_ready, glu_ready, rest_ready = front()

    def feed_forward():
        def lanes(j):
            return pl.ds(pl.multiple_of(j * 128, 128), 128)

        order = [end, middle, partner, z]
        to_partner = [end, middle, z, partner]
        to_middle = [3 * (z // 2), 1 + z // 2, end, middle]
        from_slot = [slot(zz, core) for zz in (partner, middle, end)]
        to_p, to_m = dev(partner, m, core, f), dev(middle, m, core, f)

        def att_copy(k, i):
            if k == 0:
                b = to_partner[i]
                return rcopy(
                    att.at[b], att_all.at[b, :, lanes(me)], s_att.at[0, i], r_att.at[0, i], to_p
                )
            if k == 1:
                b = to_middle[i]
                return rcopy(
                    att.at[b],
                    att_all.at[b, :, lanes(me)],
                    s_att.at[1, i],
                    r_att.at[1 + at_end, i],
                    to_m,
                )
            place = att_all.at[order[i], :, lanes(from_slot[k - 1])]
            return rcopy(place, place, s_pass.at[k - 2, i], r_att.at[k - 1, (0, 1, 3, 2)[i]], to_p)

        def sib_att(k, i):
            b = order[i]
            j = me if k == 3 else from_slot[k]
            src = att.at[b] if k == 3 else att_all.at[b, :, lanes(j)]
            return rcopy(src, att_all.at[b, :, lanes(j)], s_sib.at[k, i], r_sib.at[k, i], sib)

        for i in range(4):
            att_copy(1, i).start()
            att_copy(0, i).start()
            sib_att(3, i).start()
        for b in range(4):
            att_all[b, :, lanes(me)] = att[b]

        def forward(i):
            for k in range(3):
                place = att_all.at[order[i], :, lanes(from_slot[k])]
                rcopy(place, place, s_att.at[0, i], r_att.at[k, i], to_p).wait_recv()
                if k > 0:

                    @pl.when(at_end == 0)
                    def _(k=k):
                        att_copy(k + 1, i).start()

                sib_att(k, i).start()

        ends_take()
        sc = Scatter(p_out, a_sib, a_sum, a_relay, a_rx, s_a, r_a)

        forward(0)
        gain = fgain_ref[...]

        def pair_of(ref, b):
            return jnp.concatenate([ref[2 * b], ref[2 * b + 1]], axis=0)

        for i in range(4):
            b = order[i]
            for k in range(4):
                sib_att(k, i).wait_recv()
            if i == 0:
                out_ready()
            mid = pair_of(x_all, b).astype(f32) + dot(att_all[b], wo_v[...])
            nb = (
                mid * lax.rsqrt(jnp.mean(mid * mid, axis=-1, keepdims=True) + epsilon) * gain
            ).astype(bf16)
            nffn[b] = nb
            if i == 3:
                mid_b[0] = mid[:ROWS]
                mid_b[1] = mid[ROWS:]
            for ii in ((1,), (2, 3), (), ())[i]:
                forward(ii)
            if i == 0:
                glu_ready()
            gate = dot(nb, wg_v[...])
            up = dot(nb, wu_v[...])
            sig = 1.0 / (1.0 + jnp.exp(-gate))
            silu = gate * sig
            hb = (silu * up).astype(bf16)
            hid[b] = hb
            if i == 0:
                rest_ready()
            gh = back_product(pair_of(c_all, b), wd_v[...])
            ggb = (gh * up * (sig * (1.0 + gate * (1.0 - sig)))).astype(bf16)
            gub = (gh * silu).astype(bf16)
            gg[b] = ggb
            gu[b] = gub
            pb = (back_product(ggb, wg_v[...]) + back_product(gub, wu_v[...])).astype(bf16)
            p_out[b, 0] = pb[:ROWS]
            p_out[b, 1] = pb[ROWS:]
            sc.sibling(i).start()
            if i > 0:
                sc.pass_on(i - 1)
            if i > 1:
                sc.relay(i - 2)
            db = dot(hb, wd_v[...]).astype(bf16)
            dpart[b, 0] = db[:ROWS]
            dpart[b, 1] = db[ROWS:]

        def x_copy(which, s):
            tx, rx = ((gate_tx, gate_rx), (down_tx, down_rx), (up_tx, up_rx))[which]
            return rcopy(
                tx.at[others[s]], rx.at[group], s_x.at[which, s], r_x.at[which, s], tpeers[s]
            )

        def send_grads(which):
            tx, rx = ((gate_tx, gate_rx), (down_tx, down_rx), (up_tx, up_rx))[which]
            for s in range(T - 1):
                x_copy(which, s).start()
            rx[group] = tx[group]

        def got_grads(which):
            for s in range(T - 1):
                x_copy(which, s).wait_recv()

        def flat(ref):
            return ref[...].reshape(8 * ROWS, ref.shape[-1])

        def glu_grads(grads, tx):
            prod = lead_sum(flat(grads), flat(nffn)).astype(bf16)
            for mm in range(M):
                for ff in range(2):
                    tx[mm * 2 + ff] = prod[
                        mm * seg : (mm + 1) * seg, ff * half_width : (ff + 1) * half_width
                    ]

        def down_grads():
            prod = lead_sum(flat(c_all), flat(hid))
            for mm in range(M):
                for ff in range(2):
                    down_tx[mm * 2 + ff] = jnp.concatenate(
                        [
                            prod[blk * each : (blk + 1) * each]
                            for zl in range(2)
                            for cc in range(2)
                            for blk in [(2 * zl + ff) * 2 * M + mm * 2 + cc]
                        ],
                        axis=0,
                    ).astype(bf16)

        down_grads()
        send_grads(1)
        glu_grads(gg, gate_tx)
        send_grads(0)

        dy = sc.total()
        mid = mid_b[core]
        r = lax.rsqrt(jnp.mean(mid * mid, axis=-1, keepdims=True) + epsilon)
        gdy = gain * dy
        dv = r * gdy - mid * (r * r * r) * jnp.mean(mid * gdy, axis=-1, keepdims=True)
        gmid = c_ref[...].astype(f32) + dv
        gmid_v[...] = gmid
        ffn_part = jnp.sum(dy * mid * r, axis=0, keepdims=True)
        br_own[...] = gmid.astype(bf16)
        branch[me] = br_own[...]

        gb = Gather(br_own, branch, s_br, r_br)
        gb.own()
        glu_grads(gu, up_tx)
        send_grads(2)
        for kind in (0, 1, 2):
            gb.take(kind)
        gb.rest()

        def sent():
            for i in range(4):
                for k in range(2):
                    att_copy(k, i).wait_send()
                for k in range(4):
                    sib_att(k, i).wait_send()

                @pl.when(at_end == 0)
                def _(i=i):
                    att_copy(2, i).wait_send()
                    att_copy(3, i).wait_send()

            gb.sent()
            for which in range(3):
                for s in range(T - 1):
                    x_copy(which, s).wait_send()

        sc.sent()
        return sent, got_grads, ffn_part

    ffn_sent, got_grads, ffn_part = feed_forward()

    def back():
        sd = Scatter(dpart, d_sib, d_sum, d_relay, d_rx, s_d, r_d)
        sp = Scatter(p_out, a_sib, a_sum, a_relay, a_rx, s_p, r_p)
        for i in range(4):
            sd.sibling(i).start()

        def block_rows(b):
            return pl.ds(pl.multiple_of(b * BLOCK, BLOCK), BLOCK)

        def mixed(b, _):
            rows = block_rows(b)
            br = jnp.concatenate([branch[2 * b], branch[2 * b + 1]], axis=0)
            gm = back_product(br, wo_v[pl.ds(pl.multiple_of(me * 128, 128), 128), :])
            inv = 1.0 / totals[rows, :]
            g_v[rows, :] = (gm * inv).astype(bf16)
            w = gm * summed[rows, :] * (inv * inv)
            low = lax.broadcasted_iota(jnp.int32, w.shape, 1) < 64
            a = jnp.sum(jnp.where(low, w, 0.0), axis=1, keepdims=True)
            c = jnp.sum(jnp.where(low, 0.0, w), axis=1, keepdims=True)
            totals[rows, :] = jnp.where(low, a, c)
            return 0

        lax.fori_loop(0, 4, mixed, 0)
        for i in range(3):
            sd.pass_on(i)

        got_grads(1)
        total = down_rx[0].astype(f32)
        for k in range(1, T):
            total = total + down_rx[k].astype(f32)
        for k in range(4):
            w_tx[k] = total[k * each : (k + 1) * each].astype(bf16)
        here = z % 2 * 2 + core

        def w_copy(k):
            return rcopy(w_tx.at[k], w_rx.at[here], s_w.at[k], r_w.at[here], place_dev[k])

        for k in range(4):

            @pl.when(jnp.logical_not(place_self[k]))
            def _(k=k):
                w_copy(k).start()

            @pl.when(place_self[k])
            def _(k=k):
                w_rx[here] = w_tx[k]

        for i in range(2):
            sd.relay(i)

        summed[...] = jnp.zeros_like(summed)

        def kv_copy(s):
            return rcopy(
                nffn.at[:, :, lane_block(s)], dkv_rx.at[s], s_dk.at[s], r_dk.at[s], mpeers[s]
            )

        def attend(s, _):
            mm = (m + 1 + s) % M
            dkv_acc[...] = jnp.zeros_like(dkv_acc)
            for zz in range(4):
                rows = slice(zz * BLOCK, (zz + 1) * BLOCK)
                keys = (zz + 1) * BLOCK
                token = zz * span + m * BLOCK + lax.broadcasted_iota(jnp.int32, (BLOCK, 1), 0)
                begin = begin_of(token, doc_ref)
                for h in range(2):
                    lanes = slice(h * 64, h * 64 + 64)
                    q = q_rows[rows, lanes]
                    g = g_v[rows, lanes]
                    k = kv_all[mm, :keys, :64]
                    v = kv_all[mm, :keys, 64:]
                    e = block_weights(q, k, begin, zz, m, mm, span)
                    dp = back_product(g, v)
                    ds = (e * (dp - totals[rows, h * 64 : h * 64 + 1])).astype(bf16)
                    summed[rows, lanes] += dot(ds, k)
                    dkv_acc[:keys, :64] += lead_sum(ds, q)
                    dkv_acc[:keys, 64:] += lead_sum(e.astype(bf16), g)

            @pl.when(s < M - 1)
            def _():
                nffn[:, :, lane_block(s)] = dkv_acc[...].astype(bf16).reshape(4, BLOCK, 128)

                for ss in range(M - 1):

                    @pl.when(s == ss)
                    def _(ss=ss):
                        kv_copy(ss).start()

            return 0

        lax.fori_loop(0, M, attend, 0)

        def over_groups(rx):
            total = rx[0].astype(f32)
            for k in range(1, T):
                total = total + rx[k].astype(f32)
            return total

        got_grads(0)
        gate_ref[...] = over_groups(gate_rx)

        strip = jnp.concatenate(
            [branch[j, :, pl.ds(pl.multiple_of(z * 256, 128), 256)] for j in range(8)], axis=0
        )
        strip = jnp.concatenate(
            [
                jnp.where(
                    core == 0,
                    strip[:, 2 * mm * each : (2 * mm + 1) * each],
                    strip[:, (2 * mm + 1) * each : (2 * mm + 2) * each],
                )
                for mm in range(M)
            ],
            axis=1,
        )
        prod = lead_sum(strip, att_all[...].reshape(8 * ROWS, WIDTH))
        for mm in range(M):
            for ff in range(2):
                ap_tx[mm * 2 + ff] = prod[
                    mm * each : (mm + 1) * each, ff * half_width : (ff + 1) * half_width
                ].astype(bf16)

        def a_copy(s):
            return rcopy(ap_tx.at[others[s]], ap_rx.at[group], s_ap.at[s], r_ap.at[s], tpeers[s])

        for s in range(M - 1):
            kv_copy(s).wait_recv()
        for s in range(T - 1):
            a_copy(s).start()
        ap_rx[group] = ap_tx[group]

        qgain = jnp.concatenate([qgain_ref[...]] * 2, axis=1)
        kgain = jnp.concatenate([kgain_ref[...], jnp.ones((1, 64), f32)], axis=1)

        def head_mean(v):
            low = lax.broadcasted_iota(jnp.int32, v.shape, 1) < 64
            a = jnp.sum(jnp.where(low, v, 0.0), axis=1, keepdims=True)
            c = jnp.sum(jnp.where(low, 0.0, v), axis=1, keepdims=True)
            return jnp.where(low, a, c) * (1.0 / 64)

        def heads_back(i, carry):
            qg, kg, ag = carry
            b = jnp.where(i == 0, sp.order[0], jnp.where(i == 1, sp.order[1], jnp.where(i == 2, sp.order[2], z)))
            rows = block_rows(b)
            co = cosine[rows, :]
            si = sine[rows, :]

            def through(v, dy, gain):
                dy = dy * co - turn(dy) * si
                r = head_scale(v)
                gdy = gain * dy
                dv = r * gdy - v * (r * r * r) * head_mean(v * gdy)
                return dv, jnp.sum(dy * v * r, axis=0, keepdims=True)

            st = stacked[rows, :]
            dq, qpart = through(st[:, :128], summed[rows, :] * HEAD_SIZE ** (-0.5), qgain)
            dkv = dkv_acc[rows, :]
            for s in range(M - 1):
                dkv = dkv + dkv_rx[s, b].astype(f32)
            dk, kpart = through(st[:, 128:], dkv, kgain)
            low = lax.broadcasted_iota(jnp.int32, dkv.shape, 1) < 64
            gs = jnp.concatenate([dq, jnp.where(low, dk, dkv)], axis=1).astype(bf16)
            gs_v[rows, :] = gs
            pb = back_product(gs, w_heads[...])
            xb = jnp.concatenate([x_all[2 * b], x_all[2 * b + 1]], axis=0).astype(f32)
            rb = lax.rsqrt(jnp.mean(xb * xb, axis=-1, keepdims=True) + epsilon)
            ag = ag + jnp.sum(pb * (xb * rb), axis=0, keepdims=True)
            pb = pb.astype(bf16)
            p_out[b, 0] = pb[:ROWS]
            p_out[b, 1] = pb[ROWS:]
            rcopy(
                p_out.at[b, 1 - core], a_sib.at[i], s_p.at[i], r_p.at[i], sib
            ).start()
            return qg + qpart, kg + kpart, ag

        zero = jnp.zeros((1, 128), f32)
        qg, kg, ag = lax.fori_loop(
            0, 4, heads_back, (zero, zero, jnp.zeros((1, WIDTH), f32))
        )
        for i in range(3):
            sp.pass_on(i)

        def stack(row):
            return jnp.concatenate([row[:, k * 128 : (k + 1) * 128] for k in range(8)], axis=0)

        gn_tx[0:8, :] = stack(ag)
        gn_tx[8:16, :] = stack(ffn_part)
        gn_tx[16:24, :] = jnp.concatenate([qg, kg, jnp.zeros((6, 128), f32)], axis=0)
        gpeers = [sib] + zpeers + cross

        def g_copy(k):
            return rcopy(gn_tx, gn_rx.at[k], s_g.at[k], r_g.at[k], gpeers[k])

        for k in range(7):
            g_copy(k).start()

        prod = lead_sum(gs_v[...], normed[...])
        qw, kw = 128 // M, 64 // M
        for i in range(M):
            piece = jnp.concatenate(
                [
                    prod[i * qw : (i + 1) * qw],
                    prod[128 + i * kw : 128 + (i + 1) * kw],
                    prod[192 + i * kw : 192 + (i + 1) * kw],
                ],
                axis=0,
            ).astype(bf16)
            for ff in range(2):
                h_tx[i * 2 + ff] = piece[:, ff * half_width : (ff + 1) * half_width]

        def h_copy(s):
            return rcopy(
                h_tx.at[pieces[s]], h_rx.at[group], s_h.at[s], r_h.at[group], piece_to[s]
            )

        def h_got(s):
            return rcopy(
                h_tx.at[pieces[s]], h_rx.at[sources[s]], s_h.at[s], r_h.at[sources[s]], piece_from[s]
            )

        for s in range(T):

            @pl.when(to_self[s])
            def _(s=s):
                h_rx[group] = h_tx[pieces[s]]

            @pl.when(jnp.logical_not(to_self[s]))
            def _(s=s):
                h_copy(s).start()

        for i in range(2):
            sp.relay(i)
        gains = gn_tx[...]
        for k in range(7):
            g_copy(k).wait_recv()
        for k in range(7):
            gains = gains + gn_rx[k]
        gt_tx[...] = gains

        def t_copy(s):
            return rcopy(gt_tx, gt_rx.at[s], s_t.at[s], r_t.at[s], tpeers[s])

        for s in range(T - 1):
            t_copy(s).start()


        got_grads(2)
        up_ref[...] = over_groups(up_rx)
        for k in range(4):

            @pl.when(jnp.logical_not(from_me[k]))
            def _(k=k):
                rcopy(w_tx.at[k], w_rx.at[k], s_w.at[k], r_w.at[k], place_from[k]).wait_recv()

        down_ref[...] = jnp.concatenate(
            [
                w_rx[zl * 2 + cc, :, mm * seg : (mm + 1) * seg].astype(f32)
                for zl in range(2)
                for mm in range(M)
                for cc in range(2)
            ],
            axis=1,
        )

        out_ref[...] = mid_b[core] + sd.total()
        dy = sp.total()
        x = x_ref[...].astype(f32)
        r = lax.rsqrt(jnp.mean(x * x, axis=-1, keepdims=True) + epsilon)
        gdy = again_ref[...] * dy
        dv = r * gdy - x * (r * r * r) * jnp.mean(x * gdy, axis=-1, keepdims=True)
        igrad_ref[...] = gmid_v[...] + dv

        for s in range(T):

            @pl.when(jnp.logical_not(from_self[s]))
            def _(s=s):
                h_got(s).wait_recv()

        for s in range(T - 1):
            a_copy(s).wait_recv()
        hsum = h_rx[0].astype(f32)
        asum = ap_rx[0].astype(f32)
        for k in range(1, T):
            hsum = hsum + h_rx[k].astype(f32)
            asum = asum + ap_rx[k].astype(f32)
        heads_ref[...] = hsum
        attn_ref[...] = asum

        for s in range(T - 1):
            t_copy(s).wait_recv()
            gains = gains + gt_rx[s]
        gains_ref[...] = gains

        sd.sent()
        sp.sent()
        for k in range(4):

            @pl.when(jnp.logical_not(place_self[k]))
            def _(k=k):
                w_copy(k).wait_send()

        for s in range(M - 1):
            kv_copy(s).wait_send()
        for s in range(T):

            @pl.when(jnp.logical_not(to_self[s]))
            def _(s=s):
                h_copy(s).wait_send()

        for s in range(T - 1):
            a_copy(s).wait_send()
            t_copy(s).wait_send()
        for k in range(7):
            g_copy(k).wait_send()

    back()
    front_sent()
    ffn_sent()


def block(*args, cid):
    n = lax.axis_size("ctx")
    M, T, seg, each = n // 8, n // 4, FF // n, WIDTH // n
    cols = FF // 8
    tokens = 8 * ROWS
    half_width = WIDTH // 2
    part = (ROWS, WIDTH)
    VS, sem = pltpu.VMEM, pltpu.SemaphoreType.DMA
    shape = jax.ShapeDtypeStruct

    def sems(*shapes):
        return [sem(v) for v in shapes]

    return pl.pallas_call(
        block_kernel,
        out_shape=(
            shape(part, f32),
            shape(part, f32),
            shape((24, 128), f32),
            shape((256 // M, half_width), f32),
            shape((each, half_width), f32),
            shape((seg, half_width), f32),
            shape((seg, half_width), f32),
            shape((each, FF // 2), f32),
        ),
        in_specs=[pl.BlockSpec(memory_space=pltpu.SMEM)] + vspecs(2) + any_specs(7) + vspecs(4),
        out_specs=tuple(vspecs(8)),
        scratch_shapes=[
            VS((8,) + part, bf16),
            VS((8,) + part, bf16),
            VS((WIDTH, 256), bf16),
            VS((WIDTH, cols), bf16),
            VS((WIDTH, cols), bf16),
            VS((cols, WIDTH), bf16),
            VS((WIDTH, WIDTH), bf16),
            VS((tokens, 128), bf16),
            VS((M, tokens, 128), bf16),
            VS((4, BLOCK, 128), bf16),
            VS((tokens, 128), f32),
            VS((tokens, 128), f32),
            VS((tokens, 256), f32),
            VS((tokens, WIDTH), bf16),
            VS((tokens, 128), f32),
            VS((tokens, 128), f32),
            VS((4, BLOCK, WIDTH), bf16),
            VS((8,) + part, bf16),
            VS(part, f32),
            VS((4, 2) + part, bf16),
            VS((4, BLOCK, WIDTH), bf16),
            VS((4, BLOCK, cols), bf16),
            VS((4, BLOCK, cols), bf16),
            VS((4, BLOCK, cols), bf16),
            VS((2,) + part, f32),
            VS((4, 2) + part, bf16),
            VS((T, seg, half_width), bf16),
            VS((T, seg, half_width), bf16),
            *[VS((T, 4 * each, cols), bf16)] * 2,
            VS((T, seg, half_width), bf16),
            VS((T, seg, half_width), bf16),
            VS(part, bf16),
            *scatter_scratch(),
            *scatter_scratch(),
            *scatter_scratch()[4:],
            VS((tokens, 128), bf16),
            VS((tokens, 128), f32),
            VS((M - 1, 4, BLOCK, 128), bf16),
            VS((tokens, 256), bf16),
            *[VS((T, 256 // M, half_width), bf16)] * 2,
            *[VS((T, each, half_width), bf16)] * 2,
            VS((24, 128), f32),
            VS((7, 24, 128), f32),
            VS((24, 128), f32),
            VS((T - 1, 24, 128), f32),
            *[VS((4, each, cols), bf16)] * 2,
            *sems((9,), (7,), (9,), (7,), (1,), (1,), (4,), (4,), (4,), (4,), (2,), (2,)),
            *sems((4, M - 1), (4, M - 1), (8, M)),
            *sems((2, 4), (3, 4), (2, 4), (4, 4), (4, 4), (9,), (7,), (3, T - 1), (3, T - 1)),
            *sems((M - 1,), (M - 1,), (T,), (T,), (T - 1,), (T - 1,), (7,), (7,)),
            *sems((T - 1,), (T - 1,), (4,), (4,)),
        ],
        compiler_params=pltpu.CompilerParams(
            collective_id=cid, has_side_effects=True, vmem_limit_bytes=VMEM_LIMIT
        ),
        name="block",
    )(*args)


def finish_kernel(out, igrad, heads, attn, gate, up, down, *refs):
    outs, (s_in, s_out), bufs = refs[:9], refs[16:], refs[9:16]
    qw = heads.shape[0] // 2
    kw = qw // 2
    loads = []
    for k, (a, b) in enumerate(zip((out, igrad, heads, attn, gate, up, down), bufs)):
        cp = pltpu.make_async_copy(a, b, s_in.at[k])
        cp.start()
        loads.append(cp)
    o_out, o_igrad, o_query, o_key, o_value, o_attn, o_gate, o_up, o_down = outs
    b_out, b_igrad, b_heads, b_attn, b_gate, b_up, b_down = bufs
    stores = []
    for k, (load, a, b) in enumerate(
        (
            (4, b_gate, o_gate),
            (5, b_up, o_up),
            (6, b_down, o_down),
            (0, b_out, o_out),
            (1, b_igrad, o_igrad),
            (3, b_attn, o_attn),
            (2, b_heads.at[:qw], o_query),
            (None, b_heads.at[qw : qw + kw], o_key),
            (None, b_heads.at[qw + kw :], o_value),
        )
    ):
        if load is not None:
            loads[load].wait()
        cp = pltpu.make_async_copy(a, b, s_out.at[k])
        cp.start()
        stores.append(cp)
    for cp in stores:
        cp.wait()


def finish(*parts):
    out, igrad, heads, attn, gate, up, down = parts
    qw, kw = heads.shape[0] // 2, heads.shape[0] // 4
    shape = jax.ShapeDtypeStruct
    shapes = [
        out.shape, igrad.shape, (qw, heads.shape[1]), (kw, heads.shape[1]), (kw, heads.shape[1]),
        attn.shape, gate.shape, up.shape, down.shape,
    ]
    return pl.pallas_call(
        finish_kernel,
        out_shape=tuple(shape(v, f32) for v in shapes),
        in_specs=any_specs(7),
        out_specs=tuple(any_specs(9)),
        scratch_shapes=[pltpu.VMEM(v.shape, f32) for v in parts]
        + [pltpu.SemaphoreType.DMA((7,)), pltpu.SemaphoreType.DMA((9,))],
        compiler_params=pltpu.CompilerParams(vmem_limit_bytes=VMEM_LIMIT),
        name="finish",
    )(*parts)


def local(
    hidden_in,
    doc_lengths,
    attn_gain,
    query_gain,
    key_norm_gain,
    ffn_gain,
    query_proj,
    key_weight,
    value_weight,
    attn_proj,
    gate_proj,
    up_proj,
    down_proj,
    out_cotangent,
):
    out, igrad, gains, heads, attn, gate, up, down = block(
        doc_lengths,
        hidden_in[0],
        out_cotangent[0],
        query_proj,
        key_weight,
        value_weight,
        gate_proj,
        up_proj,
        down_proj,
        attn_proj,
        attn_gain[None],
        query_gain[None],
        key_norm_gain[None],
        ffn_gain[None],
        cid=1,
    )
    out, igrad, query, key, value, attn, gate, up, down = finish(
        out, igrad, heads, attn, gate, up, down
    )
    return (
        out[None],
        igrad[None],
        gains[:8].reshape(WIDTH),
        gains[16, :64] + gains[16, 64:],
        gains[17, :64],
        gains[8:16].reshape(WIDTH),
        query.T,
        key.T,
        value.T,
        attn.T,
        gate.T,
        up.T,
        down.T,
    )


def solution(mesh):
    in_specs = (
        P("fsdp", "ctx", None),
        P("fsdp", None),
        P(),
        P(),
        P(),
        P(),
        P("fsdp", None),
        P("fsdp", None),
        P("fsdp", None),
        P("fsdp", None),
        P("fsdp", None),
        P("fsdp", None),
        P("fsdp", None),
        P("fsdp", "ctx", None),
    )
    out_specs = (
        P("fsdp", "ctx", None),
        P("fsdp", "ctx", None),
        P(),
        P(),
        P(),
        P(),
        P("fsdp", "ctx"),
        P("fsdp", "ctx"),
        P("fsdp", "ctx"),
        P("fsdp", "ctx"),
        P("fsdp", "ctx"),
        P("fsdp", "ctx"),
        P("fsdp", "ctx"),
    )
    return jax.shard_map(local, mesh=mesh, in_specs=in_specs, out_specs=out_specs, check_vma=False)
```

```python
import functools
import math

import jax
import jax.numpy as jnp
from jax import lax
from jax.experimental import pallas as pl
from jax.experimental.pallas import tpu as pltpu
from jax.sharding import PartitionSpec as P

QUERY_HEADS = 16
KEY_VALUE_HEADS = 8
HEAD_SIZE = 64
FF = 4608
WIDTH = 1024
ROWS = 128

epsilon = 1e-05
rope_base = 1000000.0
MESH = pl.DeviceIdType.MESH
ANY = pl.ANY
VMEM_LIMIT = 64 * 2**20 - 2**17
bf16 = jnp.bfloat16
f32 = jnp.float32


def who():
    n = lax.axis_size("ctx")
    c = lax.axis_index("ctx")
    f = lax.axis_index("fsdp")
    q = n // 4
    return c // q, (c % q) // 2, c % 2, f


def dev(z, m, core, f):
    return (z * (lax.axis_size("ctx") // 4) + m * 2 + core, f)


def slot(z, core):
    return z * 2 + core


def enter(peers):
    bar = pltpu.get_barrier_semaphore()
    for p in peers:
        pl.semaphore_signal(bar, inc=1, device_id=p, device_id_type=MESH)
    pl.semaphore_wait(bar, len(peers))


def rcopy(src, dst, s, r, to):
    return pltpu.make_async_remote_copy(
        src_ref=src, dst_ref=dst, send_sem=s, recv_sem=r, device_id=to, device_id_type=MESH
    )


def comm_params(cid):
    return pltpu.CompilerParams(collective_id=cid, has_side_effects=True)


def any_specs(n):
    return [pl.BlockSpec(memory_space=ANY)] * n


def line_of(z):
    return z + 1 - 2 * (z % 2), 2 - z // 2, 3 - 3 * (z // 2), 1 - ((z + 1) // 2) % 2


class Gather:
    def __init__(self, src, dst, ss, rs):
        z, m, core, f = who()
        partner, middle, end, self.at_end = line_of(z)
        self.src, self.dst, self.ss, self.rs = src, dst, ss, rs
        self.me = slot(z, core)
        self.slots = [slot(zz, core) for zz in (partner, middle, end)]
        self.partner = dev(partner, m, core, f)
        self.middle = dev(middle, m, core, f)
        self.sib = dev(z, m, 1 - core, f)

    def copy(self, k):
        src, dst, ss, rs = self.src, self.dst, self.ss.at[k], self.rs
        if k == 0:
            return rcopy(src, dst.at[self.me], ss, rs.at[0], self.partner)
        if k == 1:
            return rcopy(src, dst.at[self.me], ss, rs.at[1 + self.at_end], self.middle)
        if k == 3:
            return rcopy(src, dst.at[self.me], ss, rs.at[3], self.sib)
        if k < 7:
            j = self.slots[k - 4]
            return rcopy(dst.at[j], dst.at[j], ss, rs.at[k], self.sib)
        j = self.slots[k - 6]
        return rcopy(dst.at[j], dst.at[j], ss, rs.at[k - 6], self.partner)

    def own(self):
        for k in (1, 0, 3):
            self.copy(k).start()

    def take(self, kind):
        j = self.slots[kind]
        rcopy(
            self.dst.at[j], self.dst.at[j], self.ss.at[0], self.rs.at[kind], self.partner
        ).wait_recv()
        if kind > 0:

            @pl.when(self.at_end == 0)
            def _():
                self.copy(6 + kind).start()

        self.copy(4 + kind).start()

    def rest(self):
        for k in range(3, 7):
            self.copy(k).wait_recv()

    def sent(self):
        for k in (0, 1, 3, 4, 5, 6):
            self.copy(k).wait_send()

        @pl.when(self.at_end == 0)
        def _():
            self.copy(7).wait_send()
            self.copy(8).wait_send()


class Scatter:
    def __init__(self, part, buf, sums, relay, rx, ss, rs):
        z, m, self.core, f = who()
        core = self.core
        partner, middle, end, self.at_end = line_of(z)
        self.z = z
        self.part, self.buf, self.sums, self.relay_buf, self.rx = part, buf, sums, relay, rx
        self.ss, self.rs = ss, rs
        self.order = [end, middle, partner, z]
        self.sib = dev(z, m, 1 - core, f)
        self.to = [dev(zz, m, core, f) for zz in self.order[:3]]

    def sibling(self, i):
        return rcopy(
            self.part.at[self.order[i], 1 - self.core],
            self.buf.at[i],
            self.ss.at[i],
            self.rs.at[i],
            self.sib,
        )

    def copy(self, i, at_end):
        if i == 2:
            return rcopy(
                self.sums.at[2], self.rx.at[0], self.ss.at[6], self.rs.at[4], self.to[2]
            )
        if at_end:
            return rcopy(
                self.sums.at[i], self.relay_buf.at[i], self.ss.at[4 + i], self.rs.at[6 + i], self.to[2]
            )
        return rcopy(self.sums.at[i], self.rx.at[1], self.ss.at[4 + i], self.rs.at[5], self.to[i])

    def pass_on(self, i):
        self.sibling(i).wait_recv()
        self.sums[i] = (
            self.part[self.order[i], self.core].astype(f32) + self.buf[i].astype(f32)
        ).astype(bf16)
        if i == 2:
            self.copy(2, True).start()
        else:

            @pl.when(self.at_end == 1)
            def _():
                self.copy(i, True).start()

    def relay(self, i):
        @pl.when(self.at_end == 0)
        def _():
            self.copy(i, True).wait_recv()
            self.sums[i] = (
                self.sums[i].astype(f32) + self.relay_buf[i].astype(f32)
            ).astype(bf16)
            self.copy(i, False).start()

    def total(self):
        self.sibling(3).wait_recv()
        total = self.part[self.z, self.core].astype(f32) + self.buf[3].astype(f32)
        self.copy(2, True).wait_recv()
        total = total + self.rx[0].astype(f32)
        self.copy(0, False).wait_recv()
        return total + self.rx[1].astype(f32)

    def sent(self):
        for i in range(4):
            self.sibling(i).wait_send()
        for i in range(3):
            self.copy(i, False).wait_send()


def scatter_scratch():
    part = (ROWS, WIDTH)
    return [
        pltpu.VMEM((4,) + part, bf16),
        pltpu.VMEM((3,) + part, bf16),
        pltpu.VMEM((2,) + part, bf16),
        pltpu.VMEM((2,) + part, bf16),
        pltpu.SemaphoreType.DMA((7,)),
        pltpu.SemaphoreType.DMA((8,)),
    ]


def back_product(left, right):
    return lax.dot_general(
        left, right, (((1,), (1,)), ((), ())), preferred_element_type=f32
    )


def lead_sum(left, right):
    return lax.dot_general(
        left, right, (((0,), (0,)), ((), ())), preferred_element_type=f32
    )


def dot(left, right):
    return jnp.dot(left, right, preferred_element_type=f32)


BLOCK = 2 * ROWS


def block_weights(q, k, begin, z, m, mm, span):
    keys = (z + 1) * BLOCK
    key = lax.broadcasted_iota(jnp.int32, (1, keys), 1)
    key = key // BLOCK * span + key % BLOCK + mm * BLOCK
    token = z * span + m * BLOCK + lax.broadcasted_iota(jnp.int32, (BLOCK, 1), 0)
    e = jnp.exp(back_product(q, k))
    return jnp.where((key >= begin) & (key <= token), e, 0.0)


VM = pltpu.VMEM


def vspecs(n):
    return [pl.BlockSpec(memory_space=VM)] * n


def begin_of(token, doc_ref):
    begin = jnp.zeros(token.shape, jnp.int32)
    start = doc_ref[0, 0]
    for d in range(1, doc_ref.shape[1]):
        begin = jnp.where(token >= start, start, begin)
        start = start + doc_ref[0, d]
    return begin


def turn(v):
    lane = lax.broadcasted_iota(jnp.int32, v.shape, 1)
    n = v.shape[1]
    return jnp.where(lane % 64 < 32, pltpu.roll(v, n - 32, 1), pltpu.roll(v, 32, 1))


def head_scale(v):
    sq = v * v
    if v.shape[1] == 64:
        return lax.rsqrt(jnp.mean(sq, axis=1, keepdims=True) + epsilon)
    low = lax.broadcasted_iota(jnp.int32, v.shape, 1) < 64
    a = jnp.sum(jnp.where(low, sq, 0.0), axis=1, keepdims=True)
    b = jnp.sum(jnp.where(low, 0.0, sq), axis=1, keepdims=True)
    return lax.rsqrt(jnp.where(low, a, b) * (1.0 / 64) + epsilon)


def block_kernel(
    doc_ref, x_ref, c_ref, q_hbm, k_hbm, v_hbm, gate_hbm, up_hbm, down_hbm, out_hbm,
    again_ref, qgain_ref, kgain_ref, fgain_ref,
    out_ref, igrad_ref, gains_ref, heads_ref, attn_ref, gate_ref, up_ref, down_ref,
    x_all, c_all, w_heads, wg_v, wu_v, wd_v, wo_v, q_rows, kv_all, att, summed, totals,
    stacked, normed, cosine, sine,
    att_all, branch, gmid_v, dpart, nffn, hid, gg, gu, mid_b, p_out, gate_tx, gate_rx, down_tx, down_rx,
    up_tx, up_rx, br_own,
    a_sib, a_sum, a_relay, a_rx, s_a, r_a, d_sib, d_sum, d_relay, d_rx, s_d, r_d,
    s_p, r_p,
    g_v, dkv_acc, dkv_rx, gs_v,
    h_tx, h_rx, ap_tx, ap_rx, gn_tx, gn_rx, gt_tx, gt_rx, w_tx, w_rx,
    s_x0, r_x0, s_c, r_c, s_h0, r_h0, s_w0, r_w0, s_v, r_v, s_o, r_o, s_k, r_k, ld,
    s_att, r_att, s_pass, s_sib, r_sib, s_br, r_br, s_x, r_x,
    s_dk, r_dk, s_h, r_h, s_ap, r_ap, s_g, r_g, s_t, r_t, s_w, r_w,
):
    z, m, core, f = who()
    M = lax.axis_size("ctx") // 8
    T = 2 * M
    span = lax.axis_size("ctx") // 4 * ROWS
    each = WIDTH // lax.axis_size("ctx")
    seg = FF // lax.axis_size("ctx")
    half_width = WIDTH // 2
    partner, middle, end, at_end = line_of(z)
    sib = dev(z, m, 1 - core, f)
    zs = [(z + s) % 4 for s in (1, 2, 3)]
    zpeers = [dev(zz, m, core, f) for zz in zs]
    cross = [dev(zz, m, 1 - core, f) for zz in zs]
    hm = m % 2
    pair = dev(z, m, core, 1 - f)
    beside = dev(z, m + 1 - 2 * hm, core, f)
    mpeers = [dev(z, (m + s) % M, core, f) for s in range(1, M)]
    group = m * 2 + f
    others = [(group + s) % T for s in range(1, T)]
    tpeers = [dev(z, o // 2, core, o % 2) for o in others]
    owner = f == z // 2
    me = slot(z, core)
    head = me

    pieces = [(group + s) % T for s in range(T)]
    rest_to = [core * M + p // 2 for p in pieces]
    piece_to = [dev(z, rr // 2, rr % 2, p % 2) for rr, p in zip(rest_to, pieces)]
    to_self = [(rr == m * 2 + core) & (p % 2 == f) for rr, p in zip(rest_to, pieces)]
    rest = m * 2 + core
    core_from = rest // M
    sources = [(group + s) % T for s in range(T)]
    piece_from = [dev(z, o // 2, core_from, o % 2) for o in sources]
    from_self = [(core_from == core) & (o == group) for o in sources]

    stage = [mid_b.at[0], mid_b.at[1], gmid_v, out_ref, igrad_ref]
    cols = M * seg
    wide = -(-(128 - math.gcd(seg, 128) + seg) // 128) * 128
    in_row = WIDTH // wide
    bands = -(-M // in_row)
    high = ROWS // bands
    first_column = [(z * 2 * M + mm * 2 + core) * seg for mm in range(M)]
    window = [v // 128 * 128 for v in first_column]
    window = [v - v // (FF - wide + 128) * 128 for v in window]
    tall = max(d for d in range(8, ROWS + 1, 8) if seg % d == 0)
    base = f * half_width

    def ff_chunk(w, dst, r):
        def parts(buf, i):
            return [
                pltpu.make_async_copy(
                    w.at[pl.ds(r * high, high), pl.ds(pl.multiple_of(window[mm], 128), wide)],
                    buf.at[pl.ds(mm // in_row * high, high), pl.ds(mm % in_row * wide, wide)],
                    ld.at[i % 5, mm],
                )
                for mm in range(M)
            ]

        def use(buf):
            pieces = []
            for mm in range(M):
                v = buf[
                    mm // in_row * high : (mm // in_row + 1) * high,
                    mm % in_row * wide : (mm % in_row + 1) * wide,
                ]
                shift = (wide - (first_column[mm] - window[mm])) % wide
                pieces.append(pltpu.roll(v, shift, 1)[:, :seg])
            rows = pl.ds(pl.multiple_of(base + r * high, high), high)
            dst[rows, :] = jnp.concatenate(pieces, axis=1).astype(bf16)

        return parts, use

    def out_chunk(r):
        def parts(buf, i):
            return [pltpu.make_async_copy(out_hbm.at[pl.ds(r * ROWS, ROWS)], buf, ld.at[i % 5, 0])]

        def use(buf):
            wo_v[pl.ds(pl.multiple_of(base + r * ROWS, ROWS), ROWS), :] = buf[...].astype(bf16)

        return parts, use

    def down_chunk(mm, r):
        def parts(buf, i):
            row = pl.multiple_of(first_column[mm] - f * (FF // 2) + r * tall, 8)
            return [
                pltpu.make_async_copy(
                    down_hbm.at[pl.ds(row, tall)], buf.at[pl.ds(0, tall)], ld.at[i % 5, 0]
                )
            ]

        def use(buf):
            at = mm * seg + r * tall
            wd_v[at : at + tall, :] = buf[:tall, :].astype(bf16)

        return parts, use

    chunks = [ff_chunk(gate_hbm, wg_v, r) for r in range(half_width // high)]
    chunks += [ff_chunk(up_hbm, wu_v, r) for r in range(half_width // high)]
    chunks += [out_chunk(r) for r in range(half_width // ROWS)]
    always = len(chunks)
    chunks += [down_chunk(mm, r) for mm in range(M) for r in range(seg // tall)]

    def fetch(i):
        def go():
            for cp in chunks[i][0](stage[i % 5], i):
                cp.start()

        if i < always:
            go()
        elif i < len(chunks):
            pl.when(owner)(go)

    def take_in(i):
        def go():
            for cp in chunks[i][0](stage[i % 5], i):
                cp.wait()
            chunks[i][1](stage[i % 5])

        if i < always:
            go()
        else:
            pl.when(owner)(go)
        fetch(i + 5)

    half_head = head // 2 * 128
    head_parts = [
        pltpu.make_async_copy(
            q_hbm.at[:, pl.ds(pl.multiple_of(head * 128, 128), 128)],
            stacked.at[pl.ds(0, half_width), pl.ds(0, 128)],
            ld.at[5, 0],
        ),
        pltpu.make_async_copy(
            k_hbm.at[:, pl.ds(pl.multiple_of(half_head, 128), 128)],
            stacked.at[pl.ds(0, half_width), pl.ds(128, 128)],
            ld.at[6, 0],
        ),
        pltpu.make_async_copy(
            v_hbm.at[:, pl.ds(pl.multiple_of(half_head, 128), 128)],
            stacked.at[pl.ds(half_width, half_width), pl.ds(0, 128)],
            ld.at[7, 0],
        ),
    ]
    for cp in head_parts:
        cp.start()
    for i in range(5):
        fetch(i)

    bar = pltpu.get_barrier_semaphore()
    fixed = [sib] + zpeers + cross + tpeers
    for p in fixed:
        pl.semaphore_signal(bar, inc=1, device_id=p, device_id_type=MESH)
    for s in range(T):

        @pl.when(jnp.logical_not(from_self[s]))
        def _(s=s):
            pl.semaphore_signal(bar, inc=1, device_id=piece_from[s], device_id_type=MESH)

    place = [(zl, cc) for zl in range(2) for cc in range(2)]
    place_dev = [dev(2 * zl + f, m, cc, z // 2) for zl, cc in place]
    place_self = [owner & (z == 2 * zl + f) & (core == cc) for zl, cc in place]
    place_from = [dev(2 * f + zb, m, cc, z % 2) for zb, cc in place]
    from_me = [owner & (z == 2 * f + zb) & (z % 2 == f) & (core == cc) for zb, cc in place]
    for k in range(4):

        @pl.when(jnp.logical_not(from_me[k]))
        def _(k=k):
            pl.semaphore_signal(bar, inc=1, device_id=place_from[k], device_id_type=MESH)

    pl.semaphore_wait(
        bar,
        len(fixed)
        + T
        + 4
        - jnp.where(core_from == core, 1, 0)
        - jnp.where(owner & (z % 2 == f), 1, 0),
    )

    def lane_block(j):
        return pl.ds(pl.multiple_of(j * 128, 128), 128)

    def front():
        gx = Gather(x_ref, x_all, s_x0, r_x0)
        gc = Gather(c_ref, c_all, s_c, r_c)
        gx.own()
        head_rows = pl.ds(f * half_width, half_width)
        heads_copy = rcopy(w_heads.at[head_rows], w_heads.at[head_rows], s_h0.at[0], r_h0.at[0], pair)
        for cp in head_parts:
            cp.wait()

        def half_of(v):
            return jnp.where(head % 2 == 0, v[:, :64], v[:, 64:])

        w_heads[head_rows, :] = jnp.concatenate(
            [
                stacked[:half_width, :128],
                half_of(stacked[:half_width, 128:]),
                half_of(stacked[half_width:, :128]),
            ],
            axis=1,
        ).astype(bf16)
        heads_copy.start()
        quarter = half_width // 2
        eighth = half_width // 4

        def w_copy(k, stage):
            dst = (wg_v, wu_v, wd_v, wo_v)[k]
            base = 0 if k == 2 else (f if stage == 0 else 1 - f) * half_width
            size = (quarter, quarter, cols // 2, eighth)[k]
            part = hm * 2 + core if k == 3 else hm
            place = dst.at[pl.ds(pl.multiple_of(base + part * size, 8), size)]
            if stage == 0:
                return rcopy(place, place, s_w0.at[k], r_w0.at[k], pair)
            return rcopy(place, place, s_v.at[k], r_v.at[k], beside)

        def out_copy(k):
            part = (hm if k == 0 else 1 - hm) * 2 + core
            base = (1 - f) * half_width
            place = wo_v.at[pl.ds(pl.multiple_of(base + part * eighth, 8), eighth)]
            return rcopy(place, place, s_o.at[k], r_o.at[k], sib)

        x_all[me] = x_ref[...]
        c_all[me] = c_ref[...]
        each_ff = half_width // high
        for i in range(each_ff):
            take_in(i)
        w_copy(0, 0).start()
        gx.take(0)
        for i in range(each_ff, 2 * each_ff):
            take_in(i)
        w_copy(1, 0).start()
        gx.take(1)
        for i in range(2 * each_ff, always):
            take_in(i)
        w_copy(3, 0).start()
        gx.take(2)
        gc.own()

        lane = lax.broadcasted_iota(jnp.int32, (1, 128), 1) % 32
        freq = jnp.exp(lane.astype(f32) * (-2.0 / 64 * math.log(rope_base)))
        sign = jnp.where(lax.broadcasted_iota(jnp.int32, (1, 128), 1) % 64 < 32, -1.0, 1.0)

        def tokens_of(zz):
            return zz * span + m * BLOCK + lax.broadcasted_iota(jnp.int32, (BLOCK, 1), 0)

        def table(zz, _):
            rows = pl.ds(pl.multiple_of(zz * BLOCK, BLOCK), BLOCK)
            token = tokens_of(zz)
            place = (token - begin_of(token, doc_ref)).astype(f32)
            angle = place * freq
            cosine[rows, :] = jnp.cos(angle)
            sine[rows, :] = jnp.sin(angle) * sign
            return 0

        lax.fori_loop(0, 4, table, 0)
        for i in range(always, len(chunks)):
            take_in(i)

        @pl.when(owner)
        def _():
            w_copy(2, 0).start()

        heads_copy.wait_recv()

        def kv_copy(b, s):
            rows = pl.ds(pl.multiple_of(b * BLOCK, BLOCK), BLOCK)
            place = kv_all.at[m, rows]
            return rcopy(place, place, s_k.at[b, s], r_k.at[b, s], mpeers[s])

        again = again_ref[...]
        qgain = jnp.concatenate([qgain_ref[...]] * 2, axis=1)
        kgain = jnp.concatenate([kgain_ref[...], jnp.ones((1, 64), f32)], axis=1)

        gx.rest()
        for k in range(2):
            w_copy(k, 0).wait_recv()
            w_copy(k, 1).start()

        def project(b, _):
            rows = pl.ds(pl.multiple_of(b * BLOCK, BLOCK), BLOCK)
            x = jnp.concatenate([x_all[2 * b], x_all[2 * b + 1]], axis=0).astype(f32)
            nb = (
                x * lax.rsqrt(jnp.mean(x * x, axis=-1, keepdims=True) + epsilon) * again
            ).astype(bf16)
            normed[rows, :] = nb
            st = dot(nb, w_heads[...])
            stacked[rows, :] = st
            co = cosine[rows, :]
            si = sine[rows, :]
            q = st[:, :128]
            q = q * head_scale(q) * qgain
            q_rows[rows, :] = ((q * co + turn(q) * si) * HEAD_SIZE ** (-0.5)).astype(bf16)
            kv = st[:, 128:]
            low = lax.broadcasted_iota(jnp.int32, kv.shape, 1) < 64
            k = kv * head_scale(kv) * kgain
            kv_all[m, rows, :] = jnp.where(low, k * co + turn(k) * si, kv).astype(bf16)
            for s in range(M - 1):
                kv_copy(b, s).start()
            return 0

        lax.fori_loop(0, 4, project, 0)

        w_copy(3, 0).wait_recv()
        w_copy(3, 1).start()
        out_copy(0).start()

        @pl.when(at_end == 0)
        def _():
            for kind in (0, 1, 2):
                gc.take(kind)

        summed[...] = jnp.zeros_like(summed)
        totals[...] = jnp.zeros_like(totals)

        def attend(s, _):
            mm = (m + M - s) % M

            @pl.when(s > 0)
            def _():
                for b in range(4):
                    rows = pl.ds(b * BLOCK, BLOCK)
                    place = kv_all.at[mm, rows]
                    rcopy(place, place, s_k.at[b, s - 1], r_k.at[b, s - 1], sib).wait_recv()

            @pl.when((s == 1) & jnp.logical_not(owner))
            def _():
                w_copy(2, 0).wait_recv()
                w_copy(2, 1).start()

            for zz in range(4):
                rows = slice(zz * BLOCK, (zz + 1) * BLOCK)
                keys = (zz + 1) * BLOCK
                begin = begin_of(tokens_of(zz), doc_ref)
                for h in range(2):
                    lanes = slice(h * 64, h * 64 + 64)
                    e = block_weights(
                        q_rows[rows, lanes], kv_all[mm, :keys, :64], begin, zz, m, mm, span
                    )
                    summed[rows, lanes] += dot(e.astype(bf16), kv_all[mm, :keys, 64:])
                    totals[rows, lanes] += jnp.broadcast_to(
                        jnp.sum(e, axis=1, keepdims=True), (BLOCK, 64)
                    )
            return 0

        lax.fori_loop(0, M, attend, 0)
        for b in range(4):
            rows = slice(b * BLOCK, (b + 1) * BLOCK)
            att[b] = (summed[rows, :] / totals[rows, :]).astype(bf16)

        def w_got(k):
            dst = (wg_v, wu_v, wd_v, wo_v)[k]
            base = 0 if k == 2 else (1 - f) * half_width
            size = (quarter, quarter, cols // 2, eighth)[k]
            part = (1 - hm) * 2 + core if k == 3 else 1 - hm
            place = dst.at[pl.ds(pl.multiple_of(base + part * size, 8), size)]
            return rcopy(place, place, s_v.at[k], r_v.at[k], beside)

        def ends_take():
            @pl.when(at_end == 1)
            def _():
                for kind in (0, 1, 2):
                    gc.take(kind)

        def out_ready():
            w_got(3).wait_recv()
            out_copy(1).start()
            for k in range(2):
                out_copy(k).wait_recv()

        def glu_ready():
            for k in range(2):
                w_got(k).wait_recv()

        def rest_ready():
            gc.rest()

            @pl.when(jnp.logical_not(owner))
            def _():
                w_got(2).wait_recv()

        def sent():
            heads_copy.wait_send()
            gx.sent()
            gc.sent()
            for k in (0, 1, 3):
                w_copy(k, 0).wait_send()
                w_copy(k, 1).wait_send()

            @pl.when(owner)
            def _():
                w_copy(2, 0).wait_send()

            @pl.when(jnp.logical_not(owner))
            def _():
                w_copy(2, 1).wait_send()

            for k in range(2):
                out_copy(k).wait_send()
            for b in range(4):
                for s in range(M - 1):
                    kv_copy(b, s).wait_send()

        return sent, ends_take, out_ready, glu_ready, rest_ready

    front_sent, ends_take, out_ready, glu_ready, rest_ready = front()

    def feed_forward():
        def lanes(j):
            return pl.ds(pl.multiple_of(j * 128, 128), 128)

        order = [end, middle, partner, z]
        to_partner = [end, middle, z, partner]
        to_middle = [3 * (z // 2), 1 + z // 2, end, middle]
        from_slot = [slot(zz, core) for zz in (partner, middle, end)]
        to_p, to_m = dev(partner, m, core, f), dev(middle, m, core, f)

        def att_copy(k, i):
            if k == 0:
                b = to_partner[i]
                return rcopy(
                    att.at[b], att_all.at[b, :, lanes(me)], s_att.at[0, i], r_att.at[0, i], to_p
                )
            if k == 1:
                b = to_middle[i]
                return rcopy(
                    att.at[b],
                    att_all.at[b, :, lanes(me)],
                    s_att.at[1, i],
                    r_att.at[1 + at_end, i],
                    to_m,
                )
            place = att_all.at[order[i], :, lanes(from_slot[k - 1])]
            return rcopy(place, place, s_pass.at[k - 2, i], r_att.at[k - 1, (0, 1, 3, 2)[i]], to_p)

        def sib_att(k, i):
            b = order[i]
            j = me if k == 3 else from_slot[k]
            src = att.at[b] if k == 3 else att_all.at[b, :, lanes(j)]
            return rcopy(src, att_all.at[b, :, lanes(j)], s_sib.at[k, i], r_sib.at[k, i], sib)

        for i in range(4):
            att_copy(1, i).start()
            att_copy(0, i).start()
            sib_att(3, i).start()
        for b in range(4):
            att_all[b, :, lanes(me)] = att[b]

        def forward(i):
            for k in range(3):
                place = att_all.at[order[i], :, lanes(from_slot[k])]
                rcopy(place, place, s_att.at[0, i], r_att.at[k, i], to_p).wait_recv()
                if k > 0:

                    @pl.when(at_end == 0)
                    def _(k=k):
                        att_copy(k + 1, i).start()

                sib_att(k, i).start()

        ends_take()
        sc = Scatter(p_out, a_sib, a_sum, a_relay, a_rx, s_a, r_a)

        forward(0)
        gain = fgain_ref[...]

        def pair_of(ref, b):
            return jnp.concatenate([ref[2 * b], ref[2 * b + 1]], axis=0)

        for i in range(4):
            b = order[i]
            for k in range(4):
                sib_att(k, i).wait_recv()
            if i == 0:
                out_ready()
            mid = pair_of(x_all, b).astype(f32) + dot(att_all[b], wo_v[...])
            nb = (
                mid * lax.rsqrt(jnp.mean(mid * mid, axis=-1, keepdims=True) + epsilon) * gain
            ).astype(bf16)
            nffn[b] = nb
            if i == 3:
                mid_b[0] = mid[:ROWS]
                mid_b[1] = mid[ROWS:]
            for ii in ((1,), (2, 3), (), ())[i]:
                forward(ii)
            if i == 0:
                glu_ready()
            gate = dot(nb, wg_v[...])
            up = dot(nb, wu_v[...])
            sig = 1.0 / (1.0 + jnp.exp(-gate))
            silu = gate * sig
            hb = (silu * up).astype(bf16)
            hid[b] = hb
            if i == 0:
                rest_ready()
            gh = back_product(pair_of(c_all, b), wd_v[...])
            ggb = (gh * up * (sig * (1.0 + gate * (1.0 - sig)))).astype(bf16)
            gub = (gh * silu).astype(bf16)
            gg[b] = ggb
            gu[b] = gub
            pb = (back_product(ggb, wg_v[...]) + back_product(gub, wu_v[...])).astype(bf16)
            p_out[b, 0] = pb[:ROWS]
            p_out[b, 1] = pb[ROWS:]
            sc.sibling(i).start()
            if i > 0:
                sc.pass_on(i - 1)
            if i > 1:
                sc.relay(i - 2)
            db = dot(hb, wd_v[...]).astype(bf16)
            dpart[b, 0] = db[:ROWS]
            dpart[b, 1] = db[ROWS:]

        def x_copy(which, s):
            tx, rx = ((gate_tx, gate_rx), (down_tx, down_rx), (up_tx, up_rx))[which]
            return rcopy(
                tx.at[others[s]], rx.at[group], s_x.at[which, s], r_x.at[which, s], tpeers[s]
            )

        def send_grads(which):
            tx, rx = ((gate_tx, gate_rx), (down_tx, down_rx), (up_tx, up_rx))[which]
            for s in range(T - 1):
                x_copy(which, s).start()
            rx[group] = tx[group]

        def got_grads(which):
            for s in range(T - 1):
                x_copy(which, s).wait_recv()

        def flat(ref):
            return ref[...].reshape(8 * ROWS, ref.shape[-1])

        def glu_grads(grads, tx):
            prod = lead_sum(flat(grads), flat(nffn)).astype(bf16)
            for mm in range(M):
                for ff in range(2):
                    tx[mm * 2 + ff] = prod[
                        mm * seg : (mm + 1) * seg, ff * half_width : (ff + 1) * half_width
                    ]

        def down_grads():
            prod = lead_sum(flat(c_all), flat(hid))
            for mm in range(M):
                for ff in range(2):
                    down_tx[mm * 2 + ff] = jnp.concatenate(
                        [
                            prod[blk * each : (blk + 1) * each]
                            for zl in range(2)
                            for cc in range(2)
                            for blk in [(2 * zl + ff) * 2 * M + mm * 2 + cc]
                        ],
                        axis=0,
                    ).astype(bf16)

        down_grads()
        send_grads(1)
        glu_grads(gg, gate_tx)
        send_grads(0)

        dy = sc.total()
        mid = mid_b[core]
        r = lax.rsqrt(jnp.mean(mid * mid, axis=-1, keepdims=True) + epsilon)
        gdy = gain * dy
        dv = r * gdy - mid * (r * r * r) * jnp.mean(mid * gdy, axis=-1, keepdims=True)
        gmid = c_ref[...].astype(f32) + dv
        gmid_v[...] = gmid
        ffn_part = jnp.sum(dy * mid * r, axis=0, keepdims=True)
        br_own[...] = gmid.astype(bf16)
        branch[me] = br_own[...]

        gb = Gather(br_own, branch, s_br, r_br)
        gb.own()
        glu_grads(gu, up_tx)
        send_grads(2)
        for kind in (0, 1, 2):
            gb.take(kind)
        gb.rest()

        def sent():
            for i in range(4):
                for k in range(2):
                    att_copy(k, i).wait_send()
                for k in range(4):
                    sib_att(k, i).wait_send()

                @pl.when(at_end == 0)
                def _(i=i):
                    att_copy(2, i).wait_send()
                    att_copy(3, i).wait_send()

            gb.sent()
            for which in range(3):
                for s in range(T - 1):
                    x_copy(which, s).wait_send()

        sc.sent()
        return sent, got_grads, ffn_part

    ffn_sent, got_grads, ffn_part = feed_forward()

    def back():
        sd = Scatter(dpart, d_sib, d_sum, d_relay, d_rx, s_d, r_d)
        sp = Scatter(p_out, a_sib, a_sum, a_relay, a_rx, s_p, r_p)
        for i in range(4):
            sd.sibling(i).start()

        def block_rows(b):
            return pl.ds(pl.multiple_of(b * BLOCK, BLOCK), BLOCK)

        def mixed(b, _):
            rows = block_rows(b)
            br = jnp.concatenate([branch[2 * b], branch[2 * b + 1]], axis=0)
            gm = back_product(br, wo_v[pl.ds(pl.multiple_of(me * 128, 128), 128), :])
            inv = 1.0 / totals[rows, :]
            g_v[rows, :] = (gm * inv).astype(bf16)
            w = gm * summed[rows, :] * (inv * inv)
            low = lax.broadcasted_iota(jnp.int32, w.shape, 1) < 64
            a = jnp.sum(jnp.where(low, w, 0.0), axis=1, keepdims=True)
            c = jnp.sum(jnp.where(low, 0.0, w), axis=1, keepdims=True)
            totals[rows, :] = jnp.where(low, a, c)
            return 0

        lax.fori_loop(0, 4, mixed, 0)
        for i in range(3):
            sd.pass_on(i)

        got_grads(1)
        total = down_rx[0].astype(f32)
        for k in range(1, T):
            total = total + down_rx[k].astype(f32)
        for k in range(4):
            w_tx[k] = total[k * each : (k + 1) * each].astype(bf16)
        here = z % 2 * 2 + core

        def w_copy(k):
            return rcopy(w_tx.at[k], w_rx.at[here], s_w.at[k], r_w.at[here], place_dev[k])

        for k in range(4):

            @pl.when(jnp.logical_not(place_self[k]))
            def _(k=k):
                w_copy(k).start()

            @pl.when(place_self[k])
            def _(k=k):
                w_rx[here] = w_tx[k]

        for i in range(2):
            sd.relay(i)

        summed[...] = jnp.zeros_like(summed)

        def kv_copy(s):
            return rcopy(
                nffn.at[:, :, lane_block(s)], dkv_rx.at[s], s_dk.at[s], r_dk.at[s], mpeers[s]
            )

        def attend(s, _):
            mm = (m + 1 + s) % M
            dkv_acc[...] = jnp.zeros_like(dkv_acc)
            for zz in range(4):
                rows = slice(zz * BLOCK, (zz + 1) * BLOCK)
                keys = (zz + 1) * BLOCK
                token = zz * span + m * BLOCK + lax.broadcasted_iota(jnp.int32, (BLOCK, 1), 0)
                begin = begin_of(token, doc_ref)
                for h in range(2):
                    lanes = slice(h * 64, h * 64 + 64)
                    q = q_rows[rows, lanes]
                    g = g_v[rows, lanes]
                    k = kv_all[mm, :keys, :64]
                    v = kv_all[mm, :keys, 64:]
                    e = block_weights(q, k, begin, zz, m, mm, span)
                    dp = back_product(g, v)
                    ds = (e * (dp - totals[rows, h * 64 : h * 64 + 1])).astype(bf16)
                    summed[rows, lanes] += dot(ds, k)
                    dkv_acc[:keys, :64] += lead_sum(ds, q)
                    dkv_acc[:keys, 64:] += lead_sum(e.astype(bf16), g)

            @pl.when(s < M - 1)
            def _():
                nffn[:, :, lane_block(s)] = dkv_acc[...].astype(bf16).reshape(4, BLOCK, 128)

                for ss in range(M - 1):

                    @pl.when(s == ss)
                    def _(ss=ss):
                        kv_copy(ss).start()

            return 0

        lax.fori_loop(0, M, attend, 0)

        def over_groups(rx):
            total = rx[0].astype(f32)
            for k in range(1, T):
                total = total + rx[k].astype(f32)
            return total

        got_grads(0)
        gate_ref[...] = over_groups(gate_rx)

        strip = jnp.concatenate(
            [branch[j, :, pl.ds(pl.multiple_of(z * 256, 128), 256)] for j in range(8)], axis=0
        )
        strip = jnp.concatenate(
            [
                jnp.where(
                    core == 0,
                    strip[:, 2 * mm * each : (2 * mm + 1) * each],
                    strip[:, (2 * mm + 1) * each : (2 * mm + 2) * each],
                )
                for mm in range(M)
            ],
            axis=1,
        )
        prod = lead_sum(strip, att_all[...].reshape(8 * ROWS, WIDTH))
        for mm in range(M):
            for ff in range(2):
                ap_tx[mm * 2 + ff] = prod[
                    mm * each : (mm + 1) * each, ff * half_width : (ff + 1) * half_width
                ].astype(bf16)

        def a_copy(s):
            return rcopy(ap_tx.at[others[s]], ap_rx.at[group], s_ap.at[s], r_ap.at[s], tpeers[s])

        for s in range(M - 1):
            kv_copy(s).wait_recv()
        for s in range(T - 1):
            a_copy(s).start()
        ap_rx[group] = ap_tx[group]

        qgain = jnp.concatenate([qgain_ref[...]] * 2, axis=1)
        kgain = jnp.concatenate([kgain_ref[...], jnp.ones((1, 64), f32)], axis=1)

        def head_mean(v):
            low = lax.broadcasted_iota(jnp.int32, v.shape, 1) < 64
            a = jnp.sum(jnp.where(low, v, 0.0), axis=1, keepdims=True)
            c = jnp.sum(jnp.where(low, 0.0, v), axis=1, keepdims=True)
            return jnp.where(low, a, c) * (1.0 / 64)

        def heads_back(i, carry):
            qg, kg, ag = carry
            b = jnp.where(i == 0, sp.order[0], jnp.where(i == 1, sp.order[1], jnp.where(i == 2, sp.order[2], z)))
            rows = block_rows(b)
            co = cosine[rows, :]
            si = sine[rows, :]

            def through(v, dy, gain):
                dy = dy * co - turn(dy) * si
                r = head_scale(v)
                gdy = gain * dy
                dv = r * gdy - v * (r * r * r) * head_mean(v * gdy)
                return dv, jnp.sum(dy * v * r, axis=0, keepdims=True)

            st = stacked[rows, :]
            dq, qpart = through(st[:, :128], summed[rows, :] * HEAD_SIZE ** (-0.5), qgain)
            dkv = dkv_acc[rows, :]
            for s in range(M - 1):
                dkv = dkv + dkv_rx[s, b].astype(f32)
            dk, kpart = through(st[:, 128:], dkv, kgain)
            low = lax.broadcasted_iota(jnp.int32, dkv.shape, 1) < 64
            gs = jnp.concatenate([dq, jnp.where(low, dk, dkv)], axis=1).astype(bf16)
            gs_v[rows, :] = gs
            pb = back_product(gs, w_heads[...])
            xb = jnp.concatenate([x_all[2 * b], x_all[2 * b + 1]], axis=0).astype(f32)
            rb = lax.rsqrt(jnp.mean(xb * xb, axis=-1, keepdims=True) + epsilon)
            ag = ag + jnp.sum(pb * (xb * rb), axis=0, keepdims=True)
            pb = pb.astype(bf16)
            p_out[b, 0] = pb[:ROWS]
            p_out[b, 1] = pb[ROWS:]
            rcopy(
                p_out.at[b, 1 - core], a_sib.at[i], s_p.at[i], r_p.at[i], sib
            ).start()
            return qg + qpart, kg + kpart, ag

        zero = jnp.zeros((1, 128), f32)
        qg, kg, ag = lax.fori_loop(
            0, 4, heads_back, (zero, zero, jnp.zeros((1, WIDTH), f32))
        )
        for i in range(3):
            sp.pass_on(i)

        def stack(row):
            return jnp.concatenate([row[:, k * 128 : (k + 1) * 128] for k in range(8)], axis=0)

        gn_tx[0:8, :] = stack(ag)
        gn_tx[8:16, :] = stack(ffn_part)
        gn_tx[16:24, :] = jnp.concatenate([qg, kg, jnp.zeros((6, 128), f32)], axis=0)
        gpeers = [sib] + zpeers + cross

        def g_copy(k):
            return rcopy(gn_tx, gn_rx.at[k], s_g.at[k], r_g.at[k], gpeers[k])

        for k in range(7):
            g_copy(k).start()

        prod = lead_sum(gs_v[...], normed[...])
        qw, kw = 128 // M, 64 // M
        for i in range(M):
            piece = jnp.concatenate(
                [
                    prod[i * qw : (i + 1) * qw],
                    prod[128 + i * kw : 128 + (i + 1) * kw],
                    prod[192 + i * kw : 192 + (i + 1) * kw],
                ],
                axis=0,
            ).astype(bf16)
            for ff in range(2):
                h_tx[i * 2 + ff] = piece[:, ff * half_width : (ff + 1) * half_width]

        def h_copy(s):
            return rcopy(
                h_tx.at[pieces[s]], h_rx.at[group], s_h.at[s], r_h.at[group], piece_to[s]
            )

        def h_got(s):
            return rcopy(
                h_tx.at[pieces[s]], h_rx.at[sources[s]], s_h.at[s], r_h.at[sources[s]], piece_from[s]
            )

        for s in range(T):

            @pl.when(to_self[s])
            def _(s=s):
                h_rx[group] = h_tx[pieces[s]]

            @pl.when(jnp.logical_not(to_self[s]))
            def _(s=s):
                h_copy(s).start()

        for i in range(2):
            sp.relay(i)
        gains = gn_tx[...]
        for k in range(7):
            g_copy(k).wait_recv()
        for k in range(7):
            gains = gains + gn_rx[k]
        gt_tx[...] = gains

        def t_copy(s):
            return rcopy(gt_tx, gt_rx.at[s], s_t.at[s], r_t.at[s], tpeers[s])

        for s in range(T - 1):
            t_copy(s).start()


        got_grads(2)
        up_ref[...] = over_groups(up_rx)
        for k in range(4):

            @pl.when(jnp.logical_not(from_me[k]))
            def _(k=k):
                rcopy(w_tx.at[k], w_rx.at[k], s_w.at[k], r_w.at[k], place_from[k]).wait_recv()

        down_ref[...] = jnp.concatenate(
            [
                w_rx[zl * 2 + cc, :, mm * seg : (mm + 1) * seg].astype(f32)
                for zl in range(2)
                for mm in range(M)
                for cc in range(2)
            ],
            axis=1,
        )

        out_ref[...] = mid_b[core] + sd.total()
        dy = sp.total()
        x = x_ref[...].astype(f32)
        r = lax.rsqrt(jnp.mean(x * x, axis=-1, keepdims=True) + epsilon)
        gdy = again_ref[...] * dy
        dv = r * gdy - x * (r * r * r) * jnp.mean(x * gdy, axis=-1, keepdims=True)
        igrad_ref[...] = gmid_v[...] + dv

        for s in range(T):

            @pl.when(jnp.logical_not(from_self[s]))
            def _(s=s):
                h_got(s).wait_recv()

        for s in range(T - 1):
            a_copy(s).wait_recv()
        hsum = h_rx[0].astype(f32)
        asum = ap_rx[0].astype(f32)
        for k in range(1, T):
            hsum = hsum + h_rx[k].astype(f32)
            asum = asum + ap_rx[k].astype(f32)
        heads_ref[...] = hsum
        attn_ref[...] = asum

        for s in range(T - 1):
            t_copy(s).wait_recv()
            gains = gains + gt_rx[s]
        gains_ref[...] = gains

        sd.sent()
        sp.sent()
        for k in range(4):

            @pl.when(jnp.logical_not(place_self[k]))
            def _(k=k):
                w_copy(k).wait_send()

        for s in range(M - 1):
            kv_copy(s).wait_send()
        for s in range(T):

            @pl.when(jnp.logical_not(to_self[s]))
            def _(s=s):
                h_copy(s).wait_send()

        for s in range(T - 1):
            a_copy(s).wait_send()
            t_copy(s).wait_send()
        for k in range(7):
            g_copy(k).wait_send()

    back()
    front_sent()
    ffn_sent()


def block(*args, cid):
    n = lax.axis_size("ctx")
    M, T, seg, each = n // 8, n // 4, FF // n, WIDTH // n
    cols = FF // 8
    tokens = 8 * ROWS
    half_width = WIDTH // 2
    part = (ROWS, WIDTH)
    VS, sem = pltpu.VMEM, pltpu.SemaphoreType.DMA
    shape = jax.ShapeDtypeStruct

    def sems(*shapes):
        return [sem(v) for v in shapes]

    return pl.pallas_call(
        block_kernel,
        out_shape=(
            shape(part, f32),
            shape(part, f32),
            shape((24, 128), f32),
            shape((256 // M, half_width), f32),
            shape((each, half_width), f32),
            shape((seg, half_width), f32),
            shape((seg, half_width), f32),
            shape((each, FF // 2), f32),
        ),
        in_specs=[pl.BlockSpec(memory_space=pltpu.SMEM)] + vspecs(2) + any_specs(7) + vspecs(4),
        out_specs=tuple(vspecs(8)),
        scratch_shapes=[
            VS((8,) + part, bf16),
            VS((8,) + part, bf16),
            VS((WIDTH, 256), bf16),
            VS((WIDTH, cols), bf16),
            VS((WIDTH, cols), bf16),
            VS((cols, WIDTH), bf16),
            VS((WIDTH, WIDTH), bf16),
            VS((tokens, 128), bf16),
            VS((M, tokens, 128), bf16),
            VS((4, BLOCK, 128), bf16),
            VS((tokens, 128), f32),
            VS((tokens, 128), f32),
            VS((tokens, 256), f32),
            VS((tokens, WIDTH), bf16),
            VS((tokens, 128), f32),
            VS((tokens, 128), f32),
            VS((4, BLOCK, WIDTH), bf16),
            VS((8,) + part, bf16),
            VS(part, f32),
            VS((4, 2) + part, bf16),
            VS((4, BLOCK, WIDTH), bf16),
            VS((4, BLOCK, cols), bf16),
            VS((4, BLOCK, cols), bf16),
            VS((4, BLOCK, cols), bf16),
            VS((2,) + part, f32),
            VS((4, 2) + part, bf16),
            VS((T, seg, half_width), bf16),
            VS((T, seg, half_width), bf16),
            *[VS((T, 4 * each, cols), bf16)] * 2,
            VS((T, seg, half_width), bf16),
            VS((T, seg, half_width), bf16),
            VS(part, bf16),
            *scatter_scratch(),
            *scatter_scratch(),
            *scatter_scratch()[4:],
            VS((tokens, 128), bf16),
            VS((tokens, 128), f32),
            VS((M - 1, 4, BLOCK, 128), bf16),
            VS((tokens, 256), bf16),
            *[VS((T, 256 // M, half_width), bf16)] * 2,
            *[VS((T, each, half_width), bf16)] * 2,
            VS((24, 128), f32),
            VS((7, 24, 128), f32),
            VS((24, 128), f32),
            VS((T - 1, 24, 128), f32),
            *[VS((4, each, cols), bf16)] * 2,
            *sems((9,), (7,), (9,), (7,), (1,), (1,), (4,), (4,), (4,), (4,), (2,), (2,)),
            *sems((4, M - 1), (4, M - 1), (8, M)),
            *sems((2, 4), (3, 4), (2, 4), (4, 4), (4, 4), (9,), (7,), (3, T - 1), (3, T - 1)),
            *sems((M - 1,), (M - 1,), (T,), (T,), (T - 1,), (T - 1,), (7,), (7,)),
            *sems((T - 1,), (T - 1,), (4,), (4,)),
        ],
        compiler_params=pltpu.CompilerParams(
            collective_id=cid, has_side_effects=True, vmem_limit_bytes=VMEM_LIMIT
        ),
        name="block",
    )(*args)


def finish_kernel(out, igrad, heads, attn, gate, up, down, gains, *refs):
    outs, small, bufs, (s_in, s_out) = refs[:9], refs[9:13], refs[13:21], refs[21:]
    qw = heads.shape[0] // 2
    kw = qw // 2
    loads = []
    for k, (a, b) in enumerate(zip((out, igrad, heads, attn, gate, up, down, gains), bufs)):
        cp = pltpu.make_async_copy(a, b, s_in.at[k])
        cp.start()
        loads.append(cp)
    o_out, o_igrad, o_query, o_key, o_value, o_attn, o_gate, o_up, o_down = outs
    b_out, b_igrad, b_heads, b_attn, b_gate, b_up, b_down, b_gains = bufs
    stores = []
    for k, (load, a, b) in enumerate(
        (
            (4, b_gate, o_gate),
            (5, b_up, o_up),
            (6, b_down, o_down),
            (0, b_out, o_out),
            (1, b_igrad, o_igrad),
            (3, b_attn, o_attn),
            (2, b_heads.at[:qw], o_query),
            (None, b_heads.at[qw : qw + kw], o_key),
            (None, b_heads.at[qw + kw :], o_value),
        )
    ):
        if load is not None:
            loads[load].wait()
        cp = pltpu.make_async_copy(a, b, s_out.at[k])
        cp.start()
        stores.append(cp)
    again, fgain, qgain, kgain = small
    loads[7].wait()
    again[...] = b_gains[:8, :]
    fgain[...] = b_gains[8:16, :]
    qgain[...] = b_gains[16:17, :64] + b_gains[16:17, 64:]
    kgain[...] = b_gains[17:18, :64]
    for cp in stores:
        cp.wait()


def finish(*parts):
    out, igrad, heads, attn, gate, up, down, _ = parts
    qw, kw = heads.shape[0] // 2, heads.shape[0] // 4
    shape = jax.ShapeDtypeStruct
    shapes = [
        out.shape, igrad.shape, (qw, heads.shape[1]), (kw, heads.shape[1]), (kw, heads.shape[1]),
        attn.shape, gate.shape, up.shape, down.shape, (8, 128), (8, 128), (1, 64), (1, 64),
    ]
    return pl.pallas_call(
        finish_kernel,
        out_shape=tuple(shape(v, f32) for v in shapes),
        in_specs=any_specs(8),
        out_specs=tuple(any_specs(9) + vspecs(4)),
        scratch_shapes=[pltpu.VMEM(v.shape, f32) for v in parts]
        + [pltpu.SemaphoreType.DMA((8,)), pltpu.SemaphoreType.DMA((9,))],
        compiler_params=pltpu.CompilerParams(vmem_limit_bytes=VMEM_LIMIT),
        name="finish",
    )(*parts)


def local(
    hidden_in,
    doc_lengths,
    attn_gain,
    query_gain,
    key_norm_gain,
    ffn_gain,
    query_proj,
    key_weight,
    value_weight,
    attn_proj,
    gate_proj,
    up_proj,
    down_proj,
    out_cotangent,
):
    out, igrad, gains, heads, attn, gate, up, down = block(
        doc_lengths,
        hidden_in[0],
        out_cotangent[0],
        query_proj,
        key_weight,
        value_weight,
        gate_proj,
        up_proj,
        down_proj,
        attn_proj,
        attn_gain[None],
        query_gain[None],
        key_norm_gain[None],
        ffn_gain[None],
        cid=1,
    )
    out, igrad, query, key, value, attn, gate, up, down, again, fgain, qgain, kgain = finish(
        out, igrad, heads, attn, gate, up, down, gains
    )
    return (
        out[None],
        igrad[None],
        again.reshape(WIDTH),
        qgain.reshape(HEAD_SIZE),
        kgain.reshape(HEAD_SIZE),
        fgain.reshape(WIDTH),
        query.T,
        key.T,
        value.T,
        attn.T,
        gate.T,
        up.T,
        down.T,
    )


def solution(mesh):
    in_specs = (
        P("fsdp", "ctx", None),
        P("fsdp", None),
        P(),
        P(),
        P(),
        P(),
        P("fsdp", None),
        P("fsdp", None),
        P("fsdp", None),
        P("fsdp", None),
        P("fsdp", None),
        P("fsdp", None),
        P("fsdp", None),
        P("fsdp", "ctx", None),
    )
    out_specs = (
        P("fsdp", "ctx", None),
        P("fsdp", "ctx", None),
        P(),
        P(),
        P(),
        P(),
        P("fsdp", "ctx"),
        P("fsdp", "ctx"),
        P("fsdp", "ctx"),
        P("fsdp", "ctx"),
        P("fsdp", "ctx"),
        P("fsdp", "ctx"),
        P("fsdp", "ctx"),
    )
    return jax.shard_map(local, mesh=mesh, in_specs=in_specs, out_specs=out_specs, check_vma=False)
```
